32 devices in a mesh: fsdp: 4 (over z), ctx: 4 (over x, core), tensor: 2 (over y).
Axes of the slice: x: 2, y: 2, z: 4, core: 2. Of those that a mesh axis runs over, the one named last changes fastest.
Arguments:
- tokens_in: bfloat16 [16384, 2048], P(('fsdp', 'ctx', 'tensor')), may hold values from -6 to 6
- attn_gain: float32 [2048], replicated, may hold values from 0.5 to 1.5
- query_weight: bfloat16 [2048, 2048], P('fsdp', 'tensor'), may hold values from -0.1875 to 0.1875
- key_weight: bfloat16 [2048, 2048], P('fsdp', 'tensor'), may hold values from -0.1875 to 0.1875
- value_weight: bfloat16 [2048, 2048], P('fsdp', 'tensor'), may hold values from -0.125 to 0.125
- output_weight: bfloat16 [2048, 2048], P('fsdp', 'tensor'), may hold values from -1 to 1
- mlp_gain: float32 [2048], replicated, may hold values from 0.5 to 1.5
- gate_weight: bfloat16 [2048, 8192], P('fsdp', 'tensor'), may hold values from -0.125 to 0.125
- up_weight: bfloat16 [2048, 8192], P('fsdp', 'tensor'), may hold values from -0.125 to 0.125
- down_weight: bfloat16 [2048, 8192], P('fsdp', 'tensor'), may hold values from -0.0625 to 0.0625
- seg_lengths: int32 [4, 20], P('fsdp'), may hold values from 1 to 128, 1920 in all within a row
- leaf_parent: int32 [4, 16], P('fsdp'), may hold values from 1 to 4
- cotangent: bfloat16 [16384, 2048], P(('fsdp', 'ctx', 'tensor')), may hold values from -6 to 6
Outputs:
- block_out: bfloat16 [16384, 2048], P(('fsdp', 'ctx', 'tensor'))
- input_grad: bfloat16 [16384, 2048], P(('fsdp', 'ctx', 'tensor'))
- attn_gain_grad: float32 [2048], P(('fsdp', 'ctx', 'tensor'))
- query_grad: float32 [2048, 2048], P(('fsdp', 'ctx'), 'tensor')
- key_grad: float32 [2048, 2048], P(('fsdp', 'ctx'), 'tensor')
- value_grad: float32 [2048, 2048], P(('fsdp', 'ctx'), 'tensor')
- output_grad: float32 [2048, 2048], P(('fsdp', 'ctx'), 'tensor')
- mlp_gain_grad: float32 [2048], P(('fsdp', 'ctx', 'tensor'))
- gate_grad: float32 [2048, 8192], P(('fsdp', 'ctx'), 'tensor')
- up_grad: float32 [2048, 8192], P(('fsdp', 'ctx'), 'tensor')
- down_grad: float32 [2048, 8192], P(('fsdp', 'ctx'), 'tensor')
The draws below stay inside these ranges and needn't reach their ends.
Inputs may be any that keep to these rules, and one draw needn't show every extreme that they name: `seg_lengths`: row t gives the token counts of tree t's 4 branches and then its 16 leaves, which follow its trunk of 2176 tokens in this order; each row sums to 1920 and its largest entry is 128. `leaf_parent`: the branch, numbered 1 to 4, that each leaf hangs from.
All inputs are finite; a program needn't handle non-finite values.
Results may differ from the reference program's by a relative error of at most 0.02.
Values may be sent and summed in bfloat16 or wider, within the bound.
A program may use at most 448 MiB of HBM per device.

```python
import math
import jax
import jax.numpy as jnp
import numpy as np
from jax import lax

D = 2048
HEADS = 32
HEAD_DIM = 64
FF = 8192
TRUNK = 2176
NB = 4
NL = 16
MEAN_SEG = 96
MOST_SEG = 128
NSEG = 20
TREE_LEN = 4096
TREES = 4
TOKENS = 16384
N_CTX = 4


def with_ends(array, own_key, least, high):
    place = [jax.random.randint(jax.random.fold_in(own_key, axis), (), 0, length) for axis, length in enumerate(array.shape)]
    longest = array.shape.index(max(array.shape))
    neighbour = place[:longest] + [(place[longest] + 1) % array.shape[longest]] + place[longest + 1:]
    return array.at[tuple(place)].set(least).at[tuple(neighbour)].set(high)


def block_levels(rng, dims, pieces, low, largest):
    gain = 1.0
    for dim, shards_of in pieces:
        draws = jax.random.uniform(jax.random.fold_in(jax.random.fold_in(rng, 6), dim), (shards_of,), jnp.float32, low / len(pieces), largest / len(pieces))
        gain = gain * jnp.repeat(jnp.exp(draws), dims[dim] // shards_of).reshape((-1,) + (1,) * (len(dims) - 1 - dim))
    return gain


def split_up(count, total, limit, slope):
    loads = [(1 << 20) // math.isqrt(rank ** slope) + 1 for rank in range(2, count + 1)]
    spare, given = total - limit - (count - 1), [1] * (count - 1)
    while spare > 0:
        movable = [i for i in range(count - 1) if given[i] < limit]
        mass, remaining = sum([loads[i] for i in movable]), spare
        for i in movable:
            extra = min(limit - given[i], max(1, remaining * loads[i] // mass), spare)
            given[i] = given[i] + extra
            spare = spare - extra
    return np.array([limit] + given)


def ragged(own_key, number_of, total, most, slope):
    if number_of == 2:
        one = jax.random.randint(own_key, (), max(1, total - most), min(most, total - 1) + 1)
        return jnp.stack([one, total - one])
    lengths = jnp.asarray(split_up(number_of, total, most, slope), jnp.int32)
    twos = (number_of - 1) // 2
    donor, sink = lengths[1:1 + 2 * twos:2], lengths[2:2 + 2 * twos:2]
    slack = jnp.minimum(donor - 1, most - sink)
    moved = jax.random.randint(jax.random.fold_in(own_key, 1), (twos,), 0, 1 << 20) % (slack + 1)
    lengths = lengths.at[1:1 + 2 * twos:2].set(donor - moved).at[2:2 + 2 * twos:2].set(sink + moved)
    return lengths[jax.random.permutation(jax.random.fold_in(own_key, 2), number_of)]


def bell_draw(key, extent, spread, reach, pieces=(), held_as=jnp.bfloat16):
    drawn = jax.random.normal(key, extent, jnp.float32) * spread
    if len(pieces) > 0:
        drawn = block_levels(key, extent, pieces, -0.22, 0.18) * drawn
    return jnp.clip(drawn, min=-reach, max=reach).astype(held_as)


def setup_inputs(seed: int = 0) -> dict:
    splits = jax.random.split(jax.random.key(seed), 14)
    return {
        "tokens_in": bell_draw(splits[0], (TOKENS, D), 1.0, 6.0, ((0, 32),)),
        "attn_gain": jnp.clip(1.0 + 0.1 * jax.random.normal(splits[1], (D,), jnp.float32), 0.5, 1.5),
        "query_weight": bell_draw(splits[2], (D, D), (D // 2) ** -0.5, 0.1875, ((0, 4), (1, 2))),
        "key_weight": bell_draw(splits[3], (D, D), (D // 2) ** -0.5, 0.1875, ((0, 4), (1, 2))),
        "value_weight": bell_draw(splits[4], (D, D), D ** -0.5, 0.125, ((0, 4), (1, 2))),
        "output_weight": bell_draw(splits[5], (D, D), (D // 64) ** -0.5, 1.0, ((0, 4), (1, 2))),
        "mlp_gain": jnp.clip(1.0 + 0.1 * jax.random.normal(splits[6], (D,), jnp.float32), 0.5, 1.5),
        "gate_weight": bell_draw(splits[7], (D, FF), D ** -0.5, 0.125, ((0, 4), (1, 2))),
        "up_weight": bell_draw(splits[8], (D, FF), D ** -0.5, 0.125, ((0, 4), (1, 2))),
        "down_weight": bell_draw(splits[9], (D, FF), FF ** -0.5, 0.0625, ((0, 4), (1, 2))),
        "seg_lengths": jax.vmap(lambda own: ragged(own, NSEG, NSEG * MEAN_SEG, MOST_SEG, 2))(jax.random.split(splits[10], TREES)).reshape((TREES, NSEG)).astype(jnp.int32),
        "leaf_parent": with_ends(jax.random.randint(splits[11], (TREES, NL), 1, NB + 1), jax.random.fold_in(splits[11], 1), 1, NB).astype(jnp.int32),
        "cotangent": bell_draw(splits[12], (TOKENS, D), 1.0, 6.0, ((0, 32),)),
    }


ROPE_BASE = 130000.0
EPSILON = 1e-05
NEG_LARGE = -1e+30

@jax.custom_vjp
def low(v):
    return lax.optimization_barrier(v.astype(jnp.bfloat16)).astype(jnp.float32)

@jax.custom_vjp
def low_back(v):
    return v

def low_keep(v):
    return (low(v), None)

def low_pass(kept, grad):
    return (grad,)

def back_keep(v):
    return (v, None)

def back_low(kept, grad):
    return (low(grad),)
low.defvjp(low_keep, low_pass)
low_back.defvjp(back_keep, back_low)

def pick_table(onehot, table):
    return lax.optimization_barrier(jnp.sum(jnp.where(onehot, table[None, :], 0), axis=1)).astype(jnp.int32)

def tree_tables(lengths_row, parent_row, tree_len):
    lengths_row = lengths_row.astype(jnp.int32)
    parent_row = parent_row.astype(jnp.int32)
    branches = lengths_row.shape[0] - parent_row.shape[0]
    ends = (TRUNK + jnp.cumsum(lengths_row)).astype(jnp.int32)
    starts = (ends - lengths_row).astype(jnp.int32)
    matches = parent_row[:, None] - 1 == jnp.arange(branches, dtype=jnp.int32)[None, :]
    parent_len = lax.optimization_barrier(jnp.sum(jnp.where(matches, lengths_row[None, :branches], 0), axis=1)).astype(jnp.int32)
    zero_one = jnp.zeros((1,), jnp.int32)
    seg_start = jnp.concatenate([zero_one, starts])
    seg_base = jnp.concatenate([zero_one, jnp.full((branches,), TRUNK, jnp.int32), (TRUNK + parent_len).astype(jnp.int32)])
    seg_parent = jnp.concatenate([zero_one, jnp.zeros((branches,), jnp.int32), parent_row])
    positions = jnp.arange(tree_len, dtype=jnp.int32)
    above = lax.optimization_barrier(jnp.sum((ends[None, :] <= positions[:, None]).astype(jnp.int32), axis=1))
    segment = ((positions >= TRUNK).astype(jnp.int32) + above).astype(jnp.int32)
    onehot = segment[:, None] == jnp.arange(seg_start.shape[0], dtype=jnp.int32)[None, :]
    depth = (positions - pick_table(onehot, seg_start) + pick_table(onehot, seg_base)).astype(jnp.int32)
    parent = pick_table(onehot, seg_parent)
    return (segment, parent, depth)

def rotate(values, depth, sign):
    count = values.shape[0]
    width = values.shape[1]
    heads = width // HEAD_DIM
    half = HEAD_DIM // 2
    freqs = jnp.power(ROPE_BASE, -(2.0 * jnp.arange(half, dtype=jnp.float32)) / HEAD_DIM)
    angles = depth.astype(jnp.float32)[:, None] * freqs[None, :]
    cosine = jnp.cos(angles)[:, None, :]
    sine = sign * jnp.sin(angles)[:, None, :]
    shaped = values.reshape(count, heads, HEAD_DIM)
    first = shaped[..., :half]
    second = shaped[..., half:]
    turned = jnp.concatenate([first * cosine - second * sine, second * cosine + first * sine], axis=-1)
    return turned.reshape(count, width)

def normalize(rows):
    return rows * lax.rsqrt(lax.optimization_barrier(jnp.mean(rows * rows, axis=1, keepdims=True)) + EPSILON)

def matmul(left, right):
    return jnp.dot(left, right, precision=lax.Precision.HIGHEST, preferred_element_type=jnp.float32)

def tree_forward(x_rows, attn_gain, query_weight, key_weight, value_weight, output_weight, mlp_gain, gate_weight, up_weight, down_weight, segment, parent, depth):
    piece = TREE_LEN // N_CTX
    score_scale = HEAD_DIM ** (-0.5)
    attn_in = low(normalize(x_rows) * attn_gain[None, :])
    query_pre = low_back(matmul(attn_in, query_weight))
    key_pre = low_back(matmul(attn_in, key_weight))
    value_pre = low_back(matmul(attn_in, value_weight))
    query_rows = low(rotate(query_pre, depth, 1.0))
    key_rows = low(rotate(key_pre, depth, 1.0))
    value_rows = low(value_pre)
    key_heads = key_rows.reshape(TREE_LEN, HEADS, HEAD_DIM)
    value_heads = value_rows.reshape(TREE_LEN, HEADS, HEAD_DIM)
    positions = jnp.arange(TREE_LEN, dtype=jnp.int32)

    def one_block(inputs):
        block_query, block_seg, block_par, block_index = inputs
        raw = jnp.einsum('qhd,khd->hqk', block_query, key_heads, precision=lax.Precision.HIGHEST) * score_scale
        raw = low_back(raw)
        seen = ((segment[None, :] == block_seg[:, None]) | (segment[None, :] == 0) | (segment[None, :] == block_par[:, None])) & (positions[None, :] <= block_index[:, None])
        scores = jnp.where(seen[None], raw, NEG_LARGE)
        probs = low(jnp.exp(scores - jax.nn.logsumexp(scores, axis=2, keepdims=True)))
        return jnp.einsum('hqk,khd->qhd', probs, value_heads, precision=lax.Precision.HIGHEST)
    attended = lax.map(jax.checkpoint(one_block), (query_rows.reshape(N_CTX, piece, HEADS, HEAD_DIM), segment.reshape(N_CTX, piece), parent.reshape(N_CTX, piece), positions.reshape(N_CTX, piece)))
    attn_out = low(low_back(attended.reshape(TREE_LEN, D)))
    mid_rows = x_rows + low_back(matmul(attn_out, output_weight.T))
    mlp_in = low(normalize(mid_rows) * mlp_gain[None, :])
    gate = low_back(matmul(mlp_in, gate_weight))
    up_proj = low_back(matmul(mlp_in, up_weight))
    hidden = low(jax.nn.silu(gate) * up_proj)
    return mid_rows + low_back(matmul(hidden, down_weight.T))

def tables_for(lengths_row, parent_row):
    return tree_tables(lengths_row, parent_row, TREE_LEN)

def reference(tokens_in, attn_gain, query_weight, key_weight, value_weight, output_weight, mlp_gain, gate_weight, up_weight, down_weight, seg_lengths, leaf_parent, cotangent):
    segments, parents, depths = jax.vmap(tables_for)(seg_lengths, leaf_parent)

    def forward_all(x_all, gain_one, w_query, w_key, w_value, w_output, gain_two, w_gate, w_up, w_down):

        def one_tree(inputs):
            rows, segment, parent, depth = inputs
            return tree_forward(rows, gain_one, w_query, w_key, w_value, w_output, gain_two, w_gate, w_up, w_down, segment, parent, depth)
        trees_out = lax.map(jax.checkpoint(one_tree), (x_all.reshape(TREES, TREE_LEN, D), segments, parents, depths))
        return trees_out.reshape(TOKENS, D)
    result, pullback = jax.vjp(forward_all, tokens_in.astype(jnp.float32), attn_gain.astype(jnp.float32), query_weight.astype(jnp.float32), key_weight.astype(jnp.float32), value_weight.astype(jnp.float32), output_weight.astype(jnp.float32), mlp_gain.astype(jnp.float32), gate_weight.astype(jnp.float32), up_weight.astype(jnp.float32), down_weight.astype(jnp.float32))
    grads = pullback(cotangent.astype(jnp.float32))
    return (result.astype(jnp.bfloat16), grads[0].astype(jnp.bfloat16), grads[1], grads[2], grads[3], grads[4], grads[5], grads[6], grads[7], grads[8], grads[9])
```

```python
import functools

import jax
import jax.numpy as jnp
from jax import lax
from jax.experimental import pallas as pl
from jax.experimental.pallas import tpu as pltpu
from jax.sharding import PartitionSpec as P

HEAD_DIM = 64
TRUNK = 2176
MOST_SEG = 128
ROPE_BASE = 130000.0
EPSILON = 1e-05
NEG_LARGE = -1e30
SCALE = HEAD_DIM ** (-0.5)

BQ = 256
BK = 512
GROUP = ("ctx", "tensor")

F32 = jnp.float32
BF16 = jnp.bfloat16


def pick_table(onehot, table):
    return jnp.sum(jnp.where(onehot, table[None, :], 0), axis=1)


def tree_tables(lengths_row, parent_row, tree_len):
    branches = lengths_row.shape[0] - parent_row.shape[0]
    ends = TRUNK + jnp.cumsum(lengths_row)
    starts = ends - lengths_row
    matches = parent_row[:, None] - 1 == jnp.arange(branches, dtype=jnp.int32)[None, :]
    parent_len = jnp.sum(jnp.where(matches, lengths_row[None, :branches], 0), axis=1)
    zero_one = jnp.zeros((1,), jnp.int32)
    seg_start = jnp.concatenate([zero_one, starts])
    seg_base = jnp.concatenate(
        [zero_one, jnp.full((branches,), TRUNK, jnp.int32), TRUNK + parent_len]
    )
    seg_parent = jnp.concatenate([zero_one, jnp.zeros((branches,), jnp.int32), parent_row])
    positions = jnp.arange(tree_len, dtype=jnp.int32)
    above = jnp.sum((ends[None, :] <= positions[:, None]).astype(jnp.int32), axis=1)
    segment = (positions >= TRUNK).astype(jnp.int32) + above
    onehot = segment[:, None] == jnp.arange(seg_start.shape[0], dtype=jnp.int32)[None, :]
    depth = positions - pick_table(onehot, seg_start) + pick_table(onehot, seg_base)
    parent = pick_table(onehot, seg_parent)
    return (segment, parent, depth)


def rope_tables(depth, width):
    half = HEAD_DIM // 2
    lane = jnp.arange(width, dtype=jnp.int32)
    freqs = jnp.power(ROPE_BASE, -(2.0 * (lane % half).astype(F32)) / HEAD_DIM)
    angles = depth.astype(F32)[:, None] * freqs[None, :]
    sign = jnp.where(lane % HEAD_DIM < half, -1.0, 1.0)
    return jnp.cos(angles), jnp.sin(angles) * sign[None, :]


def partner(x):
    half = HEAD_DIM // 2
    width = x.shape[1]
    if width == HEAD_DIM:
        return jnp.concatenate([x[:, half:], x[:, :half]], axis=1)
    lane = lax.broadcasted_iota(jnp.int32, x.shape, 1)
    ahead = pltpu.roll(x, width - half, 1)
    behind = pltpu.roll(x, half, 1)
    return jnp.where(lane % HEAD_DIM < half, ahead, behind)


def head_mask(shape, head):
    lane = lax.broadcasted_iota(jnp.int32, shape, 1)
    return lane // HEAD_DIM == head


def dot_t(a, b):
    return lax.dot_general(a, b, (((1,), (1,)), ((), ())), preferred_element_type=F32)


def dot_n(a, b):
    return lax.dot_general(a, b, (((1,), (0,)), ((), ())), preferred_element_type=F32)


def dot_tn(a, b):
    return lax.dot_general(a, b, (((0,), (0,)), ((), ())), preferred_element_type=F32)


def block_plan(i, tile):
    last_trunk = TRUNK // BK * BK // BQ
    branch_end = TRUNK + 4 * MOST_SEG
    mixed_end = -(-(branch_end + MOST_SEG) // BQ)
    base = TRUNK // BK * BK

    @pl.when(i < last_trunk)
    def _():
        count = (i * BQ) // BK

        @pl.loop(0, count)
        def _(j):
            tile(pl.multiple_of(j * BK, BK), BK, 0)

        tile(pl.multiple_of(count * BK, BK), BK, 1)

    @pl.when(i >= last_trunk)
    def _():
        @pl.loop(0, base // BK)
        def _(j):
            tile(pl.multiple_of(j * BK, BK), BK, 0)

    @pl.when((i >= last_trunk) & (i < mixed_end))
    def _():
        tile(base, mixed_end * BQ - base, 2)

    @pl.when(i >= mixed_end)
    def _():
        tile(base, branch_end - base, 3)
        tile(pl.multiple_of(i * BQ - MOST_SEG, MOST_SEG), BQ + MOST_SEG, 4)


def seen_mask(kind, i, start, width, seg_k, par_seg_q):
    shape = (BQ, width)
    seg_q = par_seg_q[:, 0:1]
    par_q = par_seg_q[:, 1:2]
    if kind == 3:
        return (seg_k == 0) | (seg_k == par_q)
    rows = lax.broadcasted_iota(jnp.int32, shape, 0) + i * BQ
    cols = lax.broadcasted_iota(jnp.int32, shape, 1) + start
    causal = cols <= rows
    if kind == 1:
        return causal
    if kind == 4:
        return causal & (seg_k == seg_q)
    return causal & ((seg_k == 0) | (seg_k == seg_q) | (seg_k == par_q))


def fwd_kernel(
    heads, q_ref, k_ref, v_ref, cos_ref, sin_ref, segk_ref, segq_ref,
    o_ref, lse_ref, qr_ref, kr_ref, vr_ref, m_ref, l_ref, acc_ref,
):
    i = pl.program_id(1)

    @pl.when(i == 0)
    def _():
        @pl.loop(0, k_ref.shape[0] // BK)
        def _(j):
            rows = pl.ds(pl.multiple_of(j * BK, BK), BK)
            k = k_ref[rows, :]
            kr_ref[rows, :] = (k * cos_ref[rows, :] + partner(k) * sin_ref[rows, :]).astype(BF16)
            vr_ref[rows, :] = v_ref[rows, :].astype(BF16)

    rows = pl.ds(pl.multiple_of(i * BQ, BQ), BQ)
    q = q_ref[...]
    q = (q * cos_ref[rows, :] + partner(q) * sin_ref[rows, :]).astype(BF16)
    qr_ref[...] = q
    q = q * jnp.asarray(SCALE, BF16)
    q_heads = [jnp.where(head_mask(q.shape, h), q, jnp.zeros_like(q)) for h in range(heads)]
    m_ref[...] = jnp.full_like(m_ref, NEG_LARGE)
    l_ref[...] = jnp.zeros_like(l_ref)
    acc_ref[...] = jnp.zeros_like(acc_ref)

    def tile(start, width, kind):
        keys = pl.ds(start, width)
        k = kr_ref[keys, :]
        v = vr_ref[keys, :]
        seen = None
        if kind != 0:
            seen = seen_mask(kind, i, start, width, segk_ref[:, keys], segq_ref[...])
        for h in range(heads):
            s = dot_t(q_heads[h], k)
            if seen is not None:
                s = jnp.where(seen, s, NEG_LARGE)
            old = m_ref[h]
            new = jnp.maximum(old, jnp.max(s, axis=1, keepdims=True))
            p = jnp.exp(s - new)
            fade = jnp.exp(old - new)
            l_ref[h] = l_ref[h] * fade + jnp.sum(p, axis=1, keepdims=True)
            acc_ref[h] = acc_ref[h] * fade + dot_n(p.astype(BF16), v)
            m_ref[h] = new

    block_plan(i, tile)
    out = None
    for h in range(heads):
        total = l_ref[h]
        part = acc_ref[h] / total
        out = part if h == 0 else jnp.where(head_mask(part.shape, h), part, out)
        lse_ref[0, :, h : h + 1] = m_ref[h] + jnp.log(total)
    o_ref[...] = out.astype(BF16)


def bwd_kernel(
    heads, q_ref, k_ref, v_ref, o_ref, do_ref, lse_ref, cos_ref, sin_ref, segk_ref, segq_ref,
    dq_ref, dk_ref, dv_ref, dq_acc, dk_acc, dv_acc,
):
    i = pl.program_id(1)

    @pl.when(i == 0)
    def _():
        dk_acc[...] = jnp.zeros_like(dk_acc)
        dv_acc[...] = jnp.zeros_like(dv_acc)

    q = q_ref[...]
    scaled = q * jnp.asarray(SCALE, BF16)
    do = do_ref[...]
    product = do.astype(F32) * o_ref[...].astype(F32)
    zero = jnp.zeros_like(q)
    masks = [head_mask(q.shape, h) for h in range(heads)]
    q_heads = [jnp.where(m, scaled, zero) for m in masks]
    do_heads = [jnp.where(m, do, zero) for m in masks]
    deltas = [jnp.sum(jnp.where(m, product, 0.0), axis=1, keepdims=True) for m in masks]
    lses = [lse_ref[0, :, h : h + 1] for h in range(heads)]
    dq_acc[...] = jnp.zeros_like(dq_acc)

    def tile(start, width, kind):
        keys = pl.ds(start, width)
        k = k_ref[keys, :]
        v = v_ref[keys, :]
        seen = None
        if kind != 0:
            seen = seen_mask(kind, i, start, width, segk_ref[:, keys], segq_ref[...])
        for h in range(heads):
            s = dot_t(q_heads[h], k)
            p = jnp.exp(s - lses[h])
            if seen is not None:
                p = jnp.where(seen, p, 0.0)
            dp = dot_t(do_heads[h], v)
            ds = (p * (dp - deltas[h])).astype(BF16)
            dv_acc[keys, :] += dot_tn(p.astype(BF16), do_heads[h])
            dk_acc[keys, :] += dot_tn(ds, q_heads[h])
            dq_acc[h] += dot_n(ds, k)

    block_plan(i, tile)
    dq = dq_acc[0]
    for h in range(1, heads):
        dq = jnp.where(masks[h], dq_acc[h], dq)
    dq = dq * SCALE
    rows = pl.ds(pl.multiple_of(i * BQ, BQ), BQ)
    dq_ref[...] = (dq * cos_ref[rows, :] - partner(dq) * sin_ref[rows, :]).astype(BF16)

    @pl.when(i == pl.num_programs(1) - 1)
    def _():
        @pl.loop(0, dk_acc.shape[0] // BK)
        def _(j):
            rows = pl.ds(pl.multiple_of(j * BK, BK), BK)
            dk = dk_acc[rows, :]
            dk_ref[rows, :] = (dk * cos_ref[rows, :] - partner(dk) * sin_ref[rows, :]).astype(BF16)
            dv_ref[rows, :] = dv_acc[rows, :].astype(BF16)


def attention_cost(tree_len, width, products):
    pairs = tree_len * tree_len // 2
    heads = width // HEAD_DIM
    return pl.CostEstimate(
        flops=products * 2 * pairs * 128 * heads * 2,
        bytes_accessed=tree_len * width * 24,
        transcendentals=pairs * heads,
    )


def attention_forward(qkv, cosine, sine, seg_keys, seg_queries, width):
    tree_len = qkv.shape[0]
    gw = min(2 * HEAD_DIM, width)
    groups, heads = width // gw, gw // HEAD_DIM
    row_block = pl.BlockSpec((BQ, gw), lambda g, i: (i, g))
    table = pl.BlockSpec((tree_len, gw), lambda g, i: (0, 0))
    full = pl.BlockSpec((tree_len, gw), lambda g, i: (0, g))
    act = jax.ShapeDtypeStruct((tree_len, width), BF16)
    if width % 128 == 0:
        queries, keys, values, step = qkv, qkv, qkv, groups
    else:
        queries, keys, values = jnp.split(qkv, 3, axis=1)
        step = 0
    return pl.pallas_call(
        functools.partial(fwd_kernel, heads),
        grid=(groups, tree_len // BQ),
        in_specs=[
            row_block,
            pl.BlockSpec((tree_len, gw), lambda g, i: (0, step + g)),
            pl.BlockSpec((tree_len, gw), lambda g, i: (0, 2 * step + g)),
            table,
            table,
            pl.BlockSpec((1, tree_len), lambda g, i: (0, 0)),
            pl.BlockSpec((BQ, 2), lambda g, i: (i, 0)),
        ],
        out_specs=[row_block, pl.BlockSpec((1, BQ, heads), lambda g, i: (g, i, 0)), row_block, full, full],
        out_shape=[act, jax.ShapeDtypeStruct((groups, tree_len, heads), F32), act, act, act],
        scratch_shapes=[
            pltpu.VMEM((heads, BQ, 1), F32),
            pltpu.VMEM((heads, BQ, 1), F32),
            pltpu.VMEM((heads, BQ, gw), F32),
        ],
        compiler_params=pltpu.CompilerParams(vmem_limit_bytes=56 << 20),
        cost_estimate=attention_cost(tree_len, width, 2),
        name="tree_attention_forward",
    )(queries, keys, values, cosine, sine, seg_keys, seg_queries)


def attention_backward(q, k, v, out, grad, lse, cosine, sine, seg_keys, seg_queries):
    tree_len, width = q.shape
    gw = min(2 * HEAD_DIM, width)
    groups, heads = width // gw, gw // HEAD_DIM
    row_block = pl.BlockSpec((BQ, gw), lambda g, i: (i, g))
    table = pl.BlockSpec((tree_len, gw), lambda g, i: (0, 0))
    full = pl.BlockSpec((tree_len, gw), lambda g, i: (0, g))
    act = jax.ShapeDtypeStruct((tree_len, width), BF16)
    return pl.pallas_call(
        functools.partial(bwd_kernel, heads),
        grid=(groups, tree_len // BQ),
        in_specs=[
            row_block, full, full, row_block, row_block,
            pl.BlockSpec((1, BQ, heads), lambda g, i: (g, i, 0)),
            table, table,
            pl.BlockSpec((1, tree_len), lambda g, i: (0, 0)),
            pl.BlockSpec((BQ, 2), lambda g, i: (i, 0)),
        ],
        out_specs=[row_block, full, full],
        out_shape=[act, act, act],
        scratch_shapes=[
            pltpu.VMEM((heads, BQ, gw), F32),
            pltpu.VMEM((tree_len, gw), F32),
            pltpu.VMEM((tree_len, gw), F32),
        ],
        compiler_params=pltpu.CompilerParams(vmem_limit_bytes=56 << 20),
        cost_estimate=attention_cost(tree_len, width, 5),
        name="tree_attention_backward",
    )(q, k, v, out, grad, lse, cosine, sine, seg_keys, seg_queries)


def gather_rows(rows):
    return lax.all_gather(rows, GROUP, axis=0, tiled=True)


def scatter_rows(rows):
    return lax.psum_scatter(rows.astype(BF16), GROUP, scatter_dimension=0, tiled=True)


def line_gather(own):
    size = lax.axis_size("fsdp")
    me = lax.axis_index("fsdp")
    ups = [(i, i + 1) for i in range(size - 1)]
    downs = [(i + 1, i) for i in range(size - 1)]
    rows = own.shape[0]
    from_below, from_above = [own], [own]
    for _ in range(size - 1):
        from_below.append(lax.ppermute(from_below[-1], "fsdp", ups))
        from_above.append(lax.ppermute(from_above[-1], "fsdp", downs))
    whole = jnp.zeros((size * rows,) + own.shape[1:], own.dtype)
    whole = lax.dynamic_update_slice_in_dim(whole, own, me * rows, 0)
    for k in range(1, size):
        piece = jnp.where(me >= k, from_below[k], from_above[size - k])
        whole = lax.dynamic_update_slice_in_dim(whole, piece, ((me - k) % size) * rows, 0)
    return whole


def line_scatter(blocks):
    size = lax.axis_size("fsdp")
    me = lax.axis_index("fsdp")
    ups = [(i, i + 1) for i in range(size - 1)]
    downs = [(i + 1, i) for i in range(size - 1)]
    rows = blocks.shape[0] // size

    def block(offset):
        return lax.dynamic_slice_in_dim(blocks, ((me + offset) % size) * rows, rows, 0)

    up, down = block(size - 1), block(-(size - 1))
    for k in range(size - 2, 0, -1):
        up = lax.ppermute(up, "fsdp", ups)
        down = lax.ppermute(down, "fsdp", downs)
        up = (block(k).astype(F32) + up.astype(F32)).astype(BF16)
        down = (block(-k).astype(F32) + down.astype(F32)).astype(BF16)
    up = lax.ppermute(up, "fsdp", ups)
    down = lax.ppermute(down, "fsdp", downs)
    return (block(0).astype(F32) + up.astype(F32) + down.astype(F32)).astype(BF16)


def swap_columns(part, count):
    size = lax.axis_size("ctx")
    rows, columns = part.shape[0] // size, part.shape[1] // count
    got = lax.all_to_all(part.reshape(size, rows, count, columns), "ctx", split_axis=0, concat_axis=0)
    got = got.reshape(size, rows, count, columns)
    return [got[:, :, c].transpose(1, 0, 2).reshape(rows, size * columns).astype(F32) for c in range(count)]


def normalize(rows):
    norm_inv = lax.rsqrt(jnp.mean(rows * rows, axis=1, keepdims=True) + EPSILON)
    return (rows * norm_inv, norm_inv)


def norm_backward(grad_rows, scaled, norm_inv, gain):
    weighted = grad_rows * gain[None, :]
    inner = jnp.mean(weighted * scaled, axis=1, keepdims=True)
    return norm_inv * (weighted - scaled * inner)


def body(
    tokens_in,
    attn_gain,
    query_weight,
    key_weight,
    value_weight,
    output_weight,
    mlp_gain,
    gate_weight,
    up_weight,
    down_weight,
    seg_lengths,
    leaf_parent,
    cotangent,
):
    ctx = lax.axis_index("ctx")
    parts = lax.axis_size("ctx")
    tree_len = tokens_in.shape[0] * parts * lax.axis_size("tensor")
    width = query_weight.shape[1] // parts
    units = gate_weight.shape[1] // parts

    def mine(weight, columns):
        return lax.dynamic_slice_in_dim(weight, ctx * columns, columns, 1)

    x_rows = tokens_in.astype(F32)
    attn_scaled, attn_inv = normalize(x_rows)
    attn_in = gather_rows((attn_scaled * attn_gain[None, :]).astype(BF16))
    w_attn = line_gather(
        jnp.concatenate([mine(w, width) for w in (query_weight, key_weight, value_weight, output_weight)], axis=1)
    )
    w_gate = line_gather(mine(gate_weight, units))
    w_up = line_gather(mine(up_weight, units))
    w_down = line_gather(mine(down_weight, units))
    w_qkv, w_out = w_attn[:, : 3 * width], w_attn[:, 3 * width :]

    segment, parent, depth = tree_tables(seg_lengths[0], leaf_parent[0], tree_len)
    cosine, sine = rope_tables(depth, min(2 * HEAD_DIM, width))
    seg_keys = segment[None, :]
    seg_queries = jnp.stack([segment, parent], axis=1)

    qkv = jnp.dot(attn_in, w_qkv, preferred_element_type=F32)
    attn_out, lse, query_rows, key_rows, value_rows = attention_forward(
        qkv, cosine, sine, seg_keys, seg_queries, width
    )
    mid_rows = x_rows + scatter_rows(dot_t(attn_out, w_out)).astype(F32)
    mlp_scaled, mlp_inv = normalize(mid_rows)
    mlp_in = gather_rows((mlp_scaled * mlp_gain[None, :]).astype(BF16))
    cot_all = gather_rows(cotangent)

    gate = jnp.dot(mlp_in, w_gate, preferred_element_type=F32)
    up_proj = jnp.dot(mlp_in, w_up, preferred_element_type=F32)
    sigmoid_gate = jax.nn.sigmoid(gate)
    hidden = (gate * sigmoid_gate * up_proj).astype(BF16)
    hidden_grad = jnp.dot(cot_all, w_down, preferred_element_type=F32)
    gate_rows_grad = (
        hidden_grad * up_proj * sigmoid_gate * (1.0 + gate * (1.0 - sigmoid_gate))
    ).astype(BF16)
    up_rows_grad = (hidden_grad * gate * sigmoid_gate).astype(BF16)

    mlp_in_grad = scatter_rows(dot_t(gate_rows_grad, w_gate) + dot_t(up_rows_grad, w_up)).astype(F32)
    mlp_back = norm_backward(mlp_in_grad, mlp_scaled, mlp_inv, mlp_gain)
    mlp_gain_part = jnp.sum(mlp_in_grad * mlp_scaled, axis=0)
    mid_grad = cotangent.astype(F32) + mlp_back
    mid_all = gather_rows(mid_grad.astype(BF16))

    gate_grad = line_scatter(dot_tn(mlp_in, gate_rows_grad).astype(BF16))
    up_grad = line_scatter(dot_tn(mlp_in, up_rows_grad).astype(BF16))
    down_grad = line_scatter(dot_tn(cot_all, hidden).astype(BF16))
    block_out = (mid_rows + scatter_rows(dot_t(hidden, w_down)).astype(F32)).astype(BF16)

    out_heads_grad = jnp.dot(mid_all, w_out, preferred_element_type=F32).astype(BF16)
    output_grad = dot_tn(mid_all, attn_out)
    query_pre_grad, key_pre_grad, value_pre_grad = attention_backward(
        query_rows, key_rows, value_rows, attn_out, out_heads_grad, lse, cosine, sine, seg_keys, seg_queries
    )
    pre_grad = jnp.concatenate([query_pre_grad, key_pre_grad, value_pre_grad], axis=1)
    attn_in_grad = scatter_rows(dot_t(pre_grad, w_qkv)).astype(F32)
    qkv_grad = dot_tn(attn_in, pre_grad)
    attn_gain_part = jnp.sum(qkv_grad * w_qkv.astype(F32), axis=1) / attn_gain
    gain_grads = lax.psum_scatter(
        jnp.stack([attn_gain_part, mlp_gain_part]), ("fsdp", "ctx", "tensor"), scatter_dimension=1, tiled=True
    )
    attn_grad = line_scatter(jnp.concatenate([qkv_grad, output_grad], axis=1).astype(BF16))
    query_out, key_out, value_out, output_out = swap_columns(attn_grad, 4)
    (gate_out,) = swap_columns(gate_grad, 1)
    (up_out,) = swap_columns(up_grad, 1)
    (down_out,) = swap_columns(down_grad, 1)

    attn_back = norm_backward(attn_in_grad, attn_scaled, attn_inv, attn_gain)
    input_grad = (mid_grad + attn_back).astype(BF16)
    return (
        block_out,
        input_grad,
        gain_grads[0],
        query_out,
        key_out,
        value_out,
        output_out,
        gain_grads[1],
        gate_out,
        up_out,
        down_out,
    )


def solution(mesh):
    rows = P(("fsdp", "ctx", "tensor"), None)
    weight = P("fsdp", "tensor")
    gain = P(("fsdp", "ctx", "tensor"))
    grad = P(("fsdp", "ctx"), "tensor")
    in_specs = (
        rows, P(), weight, weight, weight, weight, P(), weight, weight, weight, P("fsdp", None), P("fsdp", None), rows,
    )
    out_specs = (rows, rows, gain, grad, grad, grad, grad, gain, grad, grad, grad)
    return jax.shard_map(body, mesh=mesh, in_specs=in_specs, out_specs=out_specs, check_vma=False)
```

```python
import functools

import jax
import jax.numpy as jnp
from jax import lax
from jax.experimental import pallas as pl
from jax.experimental.pallas import tpu as pltpu
from jax.sharding import PartitionSpec as P

HEAD_DIM = 64
TRUNK = 2176
MOST_SEG = 128
ROPE_BASE = 130000.0
EPSILON = 1e-05
NEG_LARGE = -1e30
SCALE = HEAD_DIM ** (-0.5)

BQ = 512
BK = 512
GROUP = ("ctx", "tensor")

F32 = jnp.float32
BF16 = jnp.bfloat16


def pick_table(onehot, table):
    return jnp.sum(jnp.where(onehot, table[None, :], 0), axis=1)


def tree_tables(lengths_row, parent_row, tree_len):
    branches = lengths_row.shape[0] - parent_row.shape[0]
    ends = TRUNK + jnp.cumsum(lengths_row)
    starts = ends - lengths_row
    matches = parent_row[:, None] - 1 == jnp.arange(branches, dtype=jnp.int32)[None, :]
    parent_len = jnp.sum(jnp.where(matches, lengths_row[None, :branches], 0), axis=1)
    zero_one = jnp.zeros((1,), jnp.int32)
    seg_start = jnp.concatenate([zero_one, starts])
    seg_base = jnp.concatenate(
        [zero_one, jnp.full((branches,), TRUNK, jnp.int32), TRUNK + parent_len]
    )
    seg_parent = jnp.concatenate([zero_one, jnp.zeros((branches,), jnp.int32), parent_row])
    positions = jnp.arange(tree_len, dtype=jnp.int32)
    above = jnp.sum((ends[None, :] <= positions[:, None]).astype(jnp.int32), axis=1)
    segment = (positions >= TRUNK).astype(jnp.int32) + above
    onehot = segment[:, None] == jnp.arange(seg_start.shape[0], dtype=jnp.int32)[None, :]
    depth = positions - pick_table(onehot, seg_start) + pick_table(onehot, seg_base)
    parent = pick_table(onehot, seg_parent)
    return (segment, parent, depth)


def rope_tables(depth, width):
    half = HEAD_DIM // 2
    lane = jnp.arange(width, dtype=jnp.int32)
    freqs = jnp.power(ROPE_BASE, -(2.0 * (lane % half).astype(F32)) / HEAD_DIM)
    angles = depth.astype(F32)[:, None] * freqs[None, :]
    sign = jnp.where(lane % HEAD_DIM < half, -1.0, 1.0)
    return jnp.cos(angles), jnp.sin(angles) * sign[None, :]


def partner(x):
    half = HEAD_DIM // 2
    width = x.shape[1]
    if width == HEAD_DIM:
        return jnp.concatenate([x[:, half:], x[:, :half]], axis=1)
    lane = lax.broadcasted_iota(jnp.int32, x.shape, 1)
    ahead = pltpu.roll(x, width - half, 1)
    behind = pltpu.roll(x, half, 1)
    return jnp.where(lane % HEAD_DIM < half, ahead, behind)


def head_mask(shape, head):
    lane = lax.broadcasted_iota(jnp.int32, shape, 1)
    return lane // HEAD_DIM == head


def dot_t(a, b):
    return lax.dot_general(a, b, (((1,), (1,)), ((), ())), preferred_element_type=F32)


def dot_n(a, b):
    return lax.dot_general(a, b, (((1,), (0,)), ((), ())), preferred_element_type=F32)


def dot_tn(a, b):
    return lax.dot_general(a, b, (((0,), (0,)), ((), ())), preferred_element_type=F32)


def key_plan(i, tile):
    base = TRUNK // BK * BK
    branch_end = TRUNK + 4 * MOST_SEG
    first_tree = base // BQ
    mixed_end = -(-(branch_end + MOST_SEG) // BQ)
    chunks = jnp.minimum(i * BQ, base) // BK

    @pl.when(i < first_tree)
    def _():
        @pl.loop(0, chunks)
        def _(j):
            start = pl.multiple_of(j * BK, BK)
            tile(start, BK, 0, start)

    @pl.when(i >= first_tree)
    def _():
        tile(0, base, 0, 0)

    @pl.when(i < first_tree)
    def _():
        start = pl.multiple_of(chunks * BK, BK)
        tile(start, BK, 1, start)

    for block in range(first_tree, mixed_end):

        @pl.when(i == block)
        def _(block=block):
            tile(base, (block + 1) * BQ - base, 2, base)

    @pl.when(i >= mixed_end)
    def _():
        tile(base, branch_end - base, 3, base)
        tile(pl.multiple_of(i * BQ - MOST_SEG, MOST_SEG), BQ + MOST_SEG, 4, branch_end)


def most_keys():
    return TRUNK + 4 * MOST_SEG + BQ + MOST_SEG


def seen_mask(kind, q_at, k_at, seg_q, par_q, seg_k):
    if kind == 3:
        return (seg_k == 0) | (seg_k == par_q)
    causal = k_at <= q_at
    if kind == 1:
        return causal
    if kind == 4:
        return causal & (seg_k == seg_q)
    return causal & ((seg_k == 0) | (seg_k == seg_q) | (seg_k == par_q))


def fwd_kernel(
    heads, q_ref, k_ref, v_ref, cos_ref, sin_ref, segk_ref, segq_ref,
    o_ref, lse_ref, qr_ref, kr_ref, vr_ref, kt_ref, va_ref, s_ref, m_ref, acc_ref,
):
    i = pl.program_id(1)
    wide = 2 * HEAD_DIM

    @pl.when(i == 0)
    def _():
        @pl.loop(0, k_ref.shape[0] // BK)
        def _(j):
            rows = pl.ds(pl.multiple_of(j * BK, BK), BK)
            k = k_ref[rows, :]
            k = (k * cos_ref[rows, :] + partner(k) * sin_ref[rows, :]).astype(BF16)
            kr_ref[rows, :] = k
            kt_ref[:, rows] = jnp.transpose(k)
            v = v_ref[rows, :].astype(BF16)
            vr_ref[rows, :] = v
            if heads == 1:
                va_ref[0, rows, :] = jnp.concatenate([v, jnp.ones_like(v)], axis=1)
            else:
                for h in range(heads):
                    va_ref[h, rows, :] = jnp.where(head_mask(v.shape, h), v, jnp.ones_like(v))

    rows = pl.ds(pl.multiple_of(i * BQ, BQ), BQ)
    q = q_ref[...]
    q = (q * cos_ref[rows, :] + partner(q) * sin_ref[rows, :]).astype(BF16)
    qr_ref[...] = q
    q = q * jnp.asarray(SCALE, BF16)
    q_heads = [jnp.where(head_mask(q.shape, h), q, jnp.zeros_like(q)) for h in range(heads)]
    m_ref[...] = jnp.full_like(m_ref, NEG_LARGE)
    acc_ref[...] = jnp.zeros_like(acc_ref)

    def score_tile(start, width, kind, place):
        keys = pl.ds(start, width)
        k = kt_ref[:, keys]
        seen = None
        if kind != 0:
            shape = (BQ, width)
            seen = seen_mask(
                kind,
                lax.broadcasted_iota(jnp.int32, shape, 0) + i * BQ,
                lax.broadcasted_iota(jnp.int32, shape, 1) + start,
                segq_ref[:, 0:1], segq_ref[:, 1:2], segk_ref[:, keys],
            )
        for h in range(heads):
            s = dot_n(q_heads[h], k)
            if seen is not None:
                s = jnp.where(seen, s, NEG_LARGE)
            s_ref[h, :, pl.ds(place, width)] = s
            largest = m_ref[h]
            for c in range(width // 128):
                largest = jnp.maximum(largest, s[:, c * 128 : (c + 1) * 128])
            m_ref[h] = largest

    key_plan(i, score_tile)
    for h in range(heads):
        m_ref[h] = jnp.broadcast_to(jnp.max(m_ref[h], axis=1, keepdims=True), (BQ, 128))

    def value_tile(start, width, kind, place):
        keys = pl.ds(start, width)
        for h in range(heads):
            m = m_ref[h]
            parts = [
                jnp.exp(s_ref[h, :, pl.ds(place + c * 128, 128)] - m).astype(BF16) for c in range(width // 128)
            ]
            acc_ref[h] += dot_n(jnp.concatenate(parts, axis=1), va_ref[h, keys, :])

    key_plan(i, value_tile)
    out, lse = None, None
    for h in range(heads):
        acc = acc_ref[h]
        part = acc / pltpu.roll(acc, HEAD_DIM, 1)
        stat = m_ref[h] + jnp.log(jnp.broadcast_to(acc[:, (1 - h) * HEAD_DIM : (1 - h) * HEAD_DIM + 1], (BQ, wide)))
        mask = head_mask((BQ, wide), h)
        out = part if h == 0 else jnp.where(mask, part, out)
        lse = stat if h == 0 else jnp.where(mask, stat, lse)
    o_ref[...] = out[:, : heads * HEAD_DIM].astype(BF16)
    turned = jnp.transpose(lse)
    for h in range(heads):
        lse_ref[0, h : h + 1, :] = turned[h * HEAD_DIM : h * HEAD_DIM + 1, :]


def bwd_kernel(
    heads, q_ref, k_ref, v_ref, o_ref, do_ref, lse_ref, cos_ref, sin_ref, segk_ref, segq_ref,
    dq_ref, dk_ref, dv_ref, dq_acc, dk_acc, dv_acc,
):
    i = pl.program_id(1)

    @pl.when(i == 0)
    def _():
        dk_acc[...] = jnp.zeros_like(dk_acc)
        dv_acc[...] = jnp.zeros_like(dv_acc)

    q = q_ref[...]
    scaled = q * jnp.asarray(SCALE, BF16)
    do = do_ref[...]
    product = jnp.transpose(do.astype(F32) * o_ref[...].astype(F32))
    zero = jnp.zeros_like(q)
    masks = [head_mask(q.shape, h) for h in range(heads)]
    q_heads = [jnp.where(m, scaled, zero) for m in masks]
    do_heads = [jnp.where(m, do, zero) for m in masks]
    deltas = [
        jnp.sum(product[h * HEAD_DIM : (h + 1) * HEAD_DIM, :], axis=0, keepdims=True) for h in range(heads)
    ]
    lses = [lse_ref[0, h : h + 1, :] for h in range(heads)]
    q_turned = [jnp.transpose(x) for x in q_heads]
    do_turned = [jnp.transpose(x) for x in do_heads]
    q_stack = jnp.concatenate(q_heads, axis=0)
    do_stack = jnp.concatenate(do_heads, axis=0)
    dq_acc[...] = jnp.zeros_like(dq_acc)

    def tile(start, width, kind, place):
        keys = pl.ds(start, width)
        k = k_ref[keys, :]
        v = v_ref[keys, :]
        seen = None
        if kind != 0:
            shape = (width, BQ)
            seen = seen_mask(
                kind,
                lax.broadcasted_iota(jnp.int32, shape, 1) + i * BQ,
                lax.broadcasted_iota(jnp.int32, shape, 0) + start,
                segq_ref[0:1, :], segq_ref[1:2, :], segk_ref[keys, :],
            )
        probs, grads, k_heads = [], [], []
        for h in range(heads):
            s = dot_n(k, q_turned[h])
            p = jnp.exp(s - lses[h])
            if seen is not None:
                p = jnp.where(seen, p, 0.0)
            dp = dot_n(v, do_turned[h])
            probs.append(p.astype(BF16))
            grads.append((p * (dp - deltas[h])).astype(BF16))
            k_heads.append(jnp.where(head_mask(k.shape, h), k, jnp.zeros_like(k)))
        grad_row = jnp.concatenate(grads, axis=1)
        dv_acc[keys, :] += dot_n(jnp.concatenate(probs, axis=1), do_stack)
        dk_acc[keys, :] += dot_n(grad_row, q_stack)
        dq_acc[...] += dot_tn(jnp.concatenate(grads, axis=0), jnp.concatenate(k_heads, axis=0))

    key_plan(i, tile)
    dq = dq_acc[...] * SCALE
    rows = pl.ds(pl.multiple_of(i * BQ, BQ), BQ)
    dq_ref[...] = (dq * cos_ref[rows, :] - partner(dq) * sin_ref[rows, :]).astype(BF16)

    @pl.when(i == pl.num_programs(1) - 1)
    def _():
        @pl.loop(0, dk_acc.shape[0] // BK)
        def _(j):
            rows = pl.ds(pl.multiple_of(j * BK, BK), BK)
            dk = dk_acc[rows, :]
            dk_ref[rows, :] = (dk * cos_ref[rows, :] - partner(dk) * sin_ref[rows, :]).astype(BF16)
            dv_ref[rows, :] = dv_acc[rows, :].astype(BF16)


def small_cost():
    return pl.CostEstimate(flops=1 << 20, bytes_accessed=1 << 20, transcendentals=0)


def attention_forward(qkv, cosine, sine, seg_keys, seg_queries, width):
    tree_len = qkv.shape[0]
    gw = min(2 * HEAD_DIM, width)
    groups, heads = width // gw, gw // HEAD_DIM
    row_block = pl.BlockSpec((BQ, gw), lambda g, i: (i, g))
    table = pl.BlockSpec((tree_len, gw), lambda g, i: (0, 0))
    full = pl.BlockSpec((tree_len, gw), lambda g, i: (0, g))
    act = jax.ShapeDtypeStruct((tree_len, width), BF16)
    if width % 128 == 0:
        queries, keys, values, step = qkv, qkv, qkv, groups
    else:
        queries, keys, values = jnp.split(qkv, 3, axis=1)
        step = 0
    return pl.pallas_call(
        functools.partial(fwd_kernel, heads),
        grid=(groups, tree_len // BQ),
        in_specs=[
            row_block,
            pl.BlockSpec((tree_len, gw), lambda g, i: (0, step + g)),
            pl.BlockSpec((tree_len, gw), lambda g, i: (0, 2 * step + g)),
            table,
            table,
            pl.BlockSpec((1, tree_len), lambda g, i: (0, 0)),
            pl.BlockSpec((BQ, 2), lambda g, i: (i, 0)),
        ],
        out_specs=[row_block, pl.BlockSpec((1, heads, BQ), lambda g, i: (g, 0, i)), row_block, full, full],
        out_shape=[act, jax.ShapeDtypeStruct((groups, heads, tree_len), F32), act, act, act],
        scratch_shapes=[
            pltpu.VMEM((gw, tree_len), BF16),
            pltpu.VMEM((heads, tree_len, 128), BF16),
            pltpu.VMEM((heads, BQ, most_keys()), F32),
            pltpu.VMEM((heads, BQ, 128), F32),
            pltpu.VMEM((heads, BQ, 128), F32),
        ],
        compiler_params=pltpu.CompilerParams(vmem_limit_bytes=56 << 20),
        cost_estimate=small_cost(),
        name="tree_attention_forward",
    )(queries, keys, values, cosine, sine, seg_keys, seg_queries)


def attention_backward(q, k, v, out, grad, lse, cosine, sine, seg_keys, seg_queries):
    tree_len, width = q.shape
    gw = min(2 * HEAD_DIM, width)
    groups, heads = width // gw, gw // HEAD_DIM
    row_block = pl.BlockSpec((BQ, gw), lambda g, i: (i, g))
    table = pl.BlockSpec((tree_len, gw), lambda g, i: (0, 0))
    full = pl.BlockSpec((tree_len, gw), lambda g, i: (0, g))
    act = jax.ShapeDtypeStruct((tree_len, width), BF16)
    return pl.pallas_call(
        functools.partial(bwd_kernel, heads),
        grid=(groups, tree_len // BQ),
        in_specs=[
            row_block, full, full, row_block, row_block,
            pl.BlockSpec((1, heads, BQ), lambda g, i: (g, 0, i)),
            table, table,
            pl.BlockSpec((tree_len, 1), lambda g, i: (0, 0)),
            pl.BlockSpec((2, BQ), lambda g, i: (0, i)),
        ],
        out_specs=[row_block, full, full],
        out_shape=[act, act, act],
        scratch_shapes=[
            pltpu.VMEM((BQ, gw), F32),
            pltpu.VMEM((tree_len, gw), F32),
            pltpu.VMEM((tree_len, gw), F32),
        ],
        compiler_params=pltpu.CompilerParams(vmem_limit_bytes=56 << 20),
        cost_estimate=small_cost(),
        name="tree_attention_backward",
    )(q, k, v, out, grad, lse, cosine, sine, seg_keys.T, seg_queries.T)


MESH = pl.DeviceIdType.MESH


def plane_place():
    ctx, row = lax.axis_index("ctx"), lax.axis_index("tensor")
    x, core = ctx // 2, ctx % 2
    return x, core, row


def plane_neighbours(x, core, row):
    over_x = {"ctx": (1 - x) * 2 + core}
    over_core = {"ctx": x * 2 + 1 - core}
    over_row = {"tensor": 1 - row}
    return over_x, over_row, over_core


def enter_plane(neighbours):
    barrier = pltpu.get_barrier_semaphore()
    for device in neighbours:
        pl.semaphore_signal(barrier, inc=1, device_id=device, device_id_type=MESH)
    pl.semaphore_wait(barrier, 3)


def gather_kernel(own_ref, all_ref, local_sem, send_sem, recv_sem):
    x, core, row = plane_place()
    over_x, over_row, over_core = plane_neighbours(x, core, row)
    rows = own_ref.shape[0]
    half = rows // 2

    def place(far_x, far_row, part):
        bx = x + far_x - 2 * far_x * x
        by = row + far_row - 2 * far_row * row
        return pl.ds(pl.multiple_of(((bx * 2 + core) * 2 + by) * rows + part * half, half), half)

    enter_plane((over_x, over_row, over_core))
    copies = {}

    def send(slot, source, target, device):
        copies[slot] = pltpu.make_async_remote_copy(
            src_ref=source, dst_ref=all_ref.at[target], send_sem=send_sem.at[slot], recv_sem=recv_sem.at[slot],
            device_id=device, device_id_type=MESH,
        )
        copies[slot].start()

    mine = [own_ref.at[pl.ds(part * half, half)] for part in range(2)]
    own = [place(0, 0, part) for part in range(2)]
    send(0, mine[0], own[0], over_row)
    send(3, mine[1], own[1], over_x)
    send(1, mine[1], own[1], over_row)
    send(4, mine[0], own[0], over_x)
    send(6, mine[0], own[0], over_core)
    send(7, mine[1], own[1], over_core)
    local = [pltpu.make_async_copy(mine[part], all_ref.at[own[part]], local_sem.at[part]) for part in range(2)]
    for copy in local:
        copy.start()

    def forward(got, target, hops):
        copies[got].wait_recv()
        for slot, device in hops:
            send(slot, all_ref.at[target], target, device)

    forward(0, place(0, 1, 0), ((5, over_x), (8, over_core)))
    forward(3, place(1, 0, 1), ((2, over_row), (9, over_core)))
    forward(1, place(0, 1, 1), ((10, over_core),))
    forward(4, place(1, 0, 0), ((11, over_core),))
    forward(5, place(1, 1, 0), ((12, over_core),))
    forward(2, place(1, 1, 1), ((13, over_core),))
    for slot in range(6, 14):
        copies[slot].wait_recv()
    for slot in range(14):
        copies[slot].wait_send()
    for copy in local:
        copy.wait()


def plane_gather(rows):
    count, width = rows.shape
    return pl.pallas_call(
        gather_kernel,
        in_specs=[pl.BlockSpec(memory_space=pl.ANY)],
        out_specs=pl.BlockSpec(memory_space=pl.ANY),
        out_shape=jax.ShapeDtypeStruct((8 * count, width), rows.dtype),
        scratch_shapes=[
            pltpu.SemaphoreType.DMA((2,)),
            pltpu.SemaphoreType.DMA((14,)),
            pltpu.SemaphoreType.DMA((14,)),
        ],
        compiler_params=pltpu.CompilerParams(collective_id=0, has_side_effects=True),
        cost_estimate=small_cost(),
        name="plane_gather",
    )(rows)


PIECES = ((1, 1, 0), (1, 1, 1), (1, 0, 0), (0, 1, 1), (0, 1, 0), (1, 0, 1), (0, 0, 0), (0, 0, 1))
COLS = 512


def scatter_kernel(rows, parts, *refs):
    a_refs, (w_ref, out_ref, core_out, core_in, sums, first_in, next_out, next_in, sems) = refs[:parts], refs[parts:]
    x, core, row = plane_place()
    over_x, over_row, over_core = plane_neighbours(x, core, row)
    half = rows // 2
    width = out_ref.shape[1]
    chunks = width // COLS

    def place(piece, on_core):
        far_x, far_row, part = PIECES[piece]
        bx = x + far_x - 2 * far_x * x
        by = row + far_row - 2 * far_row * row
        return pl.ds(pl.multiple_of(((bx * 2 + on_core) * 2 + by) * rows + part * half, half), half)

    enter_plane((over_x, over_row, over_core))

    def columns(j):
        return pl.ds(pl.multiple_of(j * COLS, COLS), COLS)

    def partial(piece, on_core, j):
        taken, total = place(piece, on_core), None
        for p, a_ref in enumerate(a_refs):
            depth = a_ref.shape[1]
            term = dot_t(a_ref[taken, :], w_ref[columns(j), p * depth : (p + 1) * depth])
            total = term if p == 0 else total + term
        return total

    def remote(source, target, slot, device):
        return pltpu.make_async_remote_copy(
            src_ref=source, dst_ref=target, send_sem=sems.at[0, slot], recv_sem=sems.at[1, slot],
            device_id=device, device_id_type=MESH,
        )

    core_copies, first_copies, next_copies = [], [], []

    def for_partner(piece):
        @pl.loop(0, chunks)
        def _(j):
            core_out[piece, :, columns(j)] = partial(piece, 1 - core, j).astype(BF16)

        copy = remote(core_out.at[piece], core_in.at[piece], piece, over_core)
        copy.start()
        core_copies.append(copy)

    def for_self(piece):
        core_copies[piece].wait_recv()

        @pl.loop(0, chunks)
        def _(j):
            total = partial(piece, core, j) + core_in[piece, :, columns(j)].astype(F32)
            sums[piece, :, columns(j)] = total.astype(BF16)

        if piece < 4:
            copy = remote(sums.at[piece], first_in.at[piece], 8 + piece, over_x if piece % 2 == 0 else over_row)
            copy.start()
            first_copies.append(copy)

    for_partner(0)
    for piece in range(8):
        if piece < 7:
            for_partner(piece + 1)
        for_self(piece)
    for part in range(2):
        first_copies[part].wait_recv()

        @pl.loop(0, chunks)
        def _(j):
            total = sums[4 + part, :, columns(j)].astype(F32) + first_in[part, :, columns(j)].astype(F32)
            next_out[part, :, columns(j)] = total.astype(BF16)

        copy = remote(next_out.at[part], next_in.at[part], 12 + part, over_row if part == 0 else over_x)
        copy.start()
        next_copies.append(copy)
    for part in range(2):
        first_copies[2 + part].wait_recv()
        next_copies[part].wait_recv()

        @pl.loop(0, chunks)
        def _(j):
            total = sums[6 + part, :, columns(j)].astype(F32) + first_in[2 + part, :, columns(j)].astype(F32)
            out_ref[pl.ds(part * half, half), columns(j)] = total + next_in[part, :, columns(j)].astype(F32)

    for copy in core_copies + first_copies + next_copies:
        copy.wait_send()


def plane_scatter(parts, w, collective_id):
    count = parts[0].shape[0]
    width = w.shape[0]
    rows = count // 8
    half = rows // 2
    return pl.pallas_call(
        functools.partial(scatter_kernel, rows, len(parts)),
        in_specs=[pl.BlockSpec(memory_space=pltpu.VMEM)] * (len(parts) + 1),
        out_specs=pl.BlockSpec(memory_space=pltpu.VMEM),
        out_shape=jax.ShapeDtypeStruct((rows, width), F32),
        scratch_shapes=[
            pltpu.VMEM((8, half, width), BF16),
            pltpu.VMEM((8, half, width), BF16),
            pltpu.VMEM((8, half, width), BF16),
            pltpu.VMEM((4, half, width), BF16),
            pltpu.VMEM((2, half, width), BF16),
            pltpu.VMEM((2, half, width), BF16),
            pltpu.SemaphoreType.DMA((2, 14)),
        ],
        compiler_params=pltpu.CompilerParams(
            collective_id=collective_id, has_side_effects=True, vmem_limit_bytes=60 << 20
        ),
        cost_estimate=small_cost(),
        name="plane_scatter",
    )(*parts, w)


def is_plane():
    return lax.axis_size("ctx") == 4 and lax.axis_size("tensor") == 2


def gather_rows(rows):
    return lax.all_gather(rows, GROUP, axis=0, tiled=True)


def scatter_rows(rows):
    return lax.psum_scatter(rows.astype(BF16), GROUP, scatter_dimension=0, tiled=True).astype(F32)


def gather_now(rows):
    return plane_gather(rows) if is_plane() else gather_rows(rows)


def product_scatter(parts, w, collective_id):
    if is_plane():
        return plane_scatter(parts, w, collective_id)
    return scatter_rows(dot_t(jnp.concatenate(parts, axis=1), w))


def gather_weight(own):
    return lax.all_gather(own, "fsdp", axis=0, tiled=True)


def scatter_weight(grad):
    return lax.psum_scatter(grad.astype(BF16), "fsdp", scatter_dimension=0, tiled=True)


def swap_columns(part, count):
    size = lax.axis_size("ctx")
    rows, columns = part.shape[0] // size, part.shape[1] // count
    got = lax.all_to_all(part.reshape(size, rows, count * columns), "ctx", split_axis=0, concat_axis=0)
    return [
        jnp.concatenate([got[j, :, c * columns : (c + 1) * columns] for j in range(size)], axis=1).astype(F32)
        for c in range(count)
    ]


def normalize(rows):
    norm_inv = lax.rsqrt(jnp.mean(rows * rows, axis=1, keepdims=True) + EPSILON)
    return (rows * norm_inv, norm_inv)


def norm_backward(grad_rows, scaled, norm_inv, gain):
    weighted = grad_rows * gain[None, :]
    inner = jnp.mean(weighted * scaled, axis=1, keepdims=True)
    return norm_inv * (weighted - scaled * inner)


def body(
    tokens_in,
    attn_gain,
    query_weight,
    key_weight,
    value_weight,
    output_weight,
    mlp_gain,
    gate_weight,
    up_weight,
    down_weight,
    seg_lengths,
    leaf_parent,
    cotangent,
):
    ctx = lax.axis_index("ctx")
    parts = lax.axis_size("ctx")
    tree_len = tokens_in.shape[0] * parts * lax.axis_size("tensor")
    width = query_weight.shape[1] // parts
    units = gate_weight.shape[1] // parts

    def mine(weight, columns):
        return lax.dynamic_slice_in_dim(weight, ctx * columns, columns, 1)

    x_rows = tokens_in.astype(F32)
    attn_scaled, attn_inv = normalize(x_rows)
    w_attn = gather_weight(
        jnp.concatenate([mine(w, width) for w in (query_weight, key_weight, value_weight, output_weight)], axis=1)
    )
    w_gate = gather_weight(mine(gate_weight, units))
    w_up = gather_weight(mine(up_weight, units))
    cot_all = gather_rows(cotangent)
    w_down = gather_weight(mine(down_weight, units))
    attn_in = gather_now((attn_scaled * attn_gain[None, :]).astype(BF16))
    w_qkv, w_out = w_attn[:, : 3 * width], w_attn[:, 3 * width :]

    segment, parent, depth = tree_tables(seg_lengths[0], leaf_parent[0], tree_len)
    cosine, sine = rope_tables(depth, min(2 * HEAD_DIM, width))
    seg_keys = segment[None, :]
    seg_queries = jnp.stack([segment, parent], axis=1)

    qkv = jnp.dot(attn_in, w_qkv, preferred_element_type=F32)
    attn_out, lse, query_rows, key_rows, value_rows = attention_forward(
        qkv, cosine, sine, seg_keys, seg_queries, width
    )
    mid_rows = x_rows + product_scatter([attn_out], w_out, 1)
    mlp_scaled, mlp_inv = normalize(mid_rows)
    mlp_in = gather_now((mlp_scaled * mlp_gain[None, :]).astype(BF16))

    gate = jnp.dot(mlp_in, w_gate, preferred_element_type=F32)
    up_proj = jnp.dot(mlp_in, w_up, preferred_element_type=F32)
    sigmoid_gate = jax.nn.sigmoid(gate)
    hidden = (gate * sigmoid_gate * up_proj).astype(BF16)
    down_rows, cot_all = lax.optimization_barrier((dot_t(hidden, w_down).astype(BF16), cot_all))
    down_rows = scatter_rows(down_rows)
    hidden_grad = jnp.dot(cot_all, w_down, preferred_element_type=F32)
    gate_rows_grad = (
        hidden_grad * up_proj * sigmoid_gate * (1.0 + gate * (1.0 - sigmoid_gate))
    ).astype(BF16)
    up_rows_grad = (hidden_grad * gate * sigmoid_gate).astype(BF16)

    mlp_in_grad = scatter_rows(dot_t(gate_rows_grad, w_gate) + dot_t(up_rows_grad, w_up))
    gate_part = dot_tn(mlp_in, gate_rows_grad).astype(BF16)
    up_part = dot_tn(mlp_in, up_rows_grad).astype(BF16)
    down_part = dot_tn(cot_all, hidden).astype(BF16)
    mlp_in_grad, gate_part, up_part, down_part, down_rows = lax.optimization_barrier(
        (mlp_in_grad, gate_part, up_part, down_part, down_rows)
    )
    block_out = (mid_rows + down_rows).astype(BF16)
    mlp_back = norm_backward(mlp_in_grad, mlp_scaled, mlp_inv, mlp_gain)
    mlp_gain_part = jnp.sum(mlp_in_grad * mlp_scaled, axis=0)
    mid_grad = cotangent.astype(F32) + mlp_back
    mid_all = gather_now(mid_grad.astype(BF16))

    gate_grad = scatter_weight(gate_part)
    up_grad = scatter_weight(up_part)
    down_grad = scatter_weight(down_part)

    out_heads_grad = jnp.dot(mid_all, w_out, preferred_element_type=F32).astype(BF16)
    output_grad = dot_tn(mid_all, attn_out)
    pre_grads = attention_backward(
        query_rows, key_rows, value_rows, attn_out, out_heads_grad, lse, cosine, sine, seg_keys, seg_queries
    )
    pre_grads, gate_grad, up_grad, down_grad = lax.optimization_barrier((pre_grads, gate_grad, up_grad, down_grad))
    qkv_grad = jnp.concatenate([dot_tn(attn_in, grad) for grad in pre_grads], axis=1)
    attn_gain_part = jnp.sum(qkv_grad * w_qkv.astype(F32), axis=1) / attn_gain
    attn_part = jnp.concatenate([qkv_grad, output_grad], axis=1).astype(BF16)
    pre_grads, attn_part = lax.optimization_barrier((pre_grads, attn_part))
    attn_in_grad = product_scatter(pre_grads, w_qkv, 2)
    gain_grads = lax.psum_scatter(
        jnp.stack([attn_gain_part, mlp_gain_part]), ("fsdp", "ctx", "tensor"), scatter_dimension=1, tiled=True
    )
    attn_grad = scatter_weight(attn_part)
    (gate_out,) = swap_columns(gate_grad, 1)
    (up_out,) = swap_columns(up_grad, 1)
    (down_out,) = swap_columns(down_grad, 1)
    query_out, key_out, value_out, output_out = swap_columns(attn_grad, 4)

    attn_back = norm_backward(attn_in_grad, attn_scaled, attn_inv, attn_gain)
    input_grad = (mid_grad + attn_back).astype(BF16)
    return (
        block_out,
        input_grad,
        gain_grads[0],
        query_out,
        key_out,
        value_out,
        output_out,
        gain_grads[1],
        gate_out,
        up_out,
        down_out,
    )


def solution(mesh):
    rows = P(("fsdp", "ctx", "tensor"), None)
    weight = P("fsdp", "tensor")
    gain = P(("fsdp", "ctx", "tensor"))
    grad = P(("fsdp", "ctx"), "tensor")
    in_specs = (
        rows, P(), weight, weight, weight, weight, P(), weight, weight, weight, P("fsdp", None), P("fsdp", None), rows,
    )
    out_specs = (rows, rows, gain, grad, grad, grad, grad, gain, grad, grad, grad)
    return jax.shard_map(body, mesh=mesh, in_specs=in_specs, out_specs=out_specs, check_vma=False)
```

```python
import functools

import jax
import jax.numpy as jnp
from jax import lax
from jax.experimental import pallas as pl
from jax.experimental.pallas import tpu as pltpu
from jax.sharding import PartitionSpec as P

HEAD_DIM = 64
TRUNK = 2176
MOST_SEG = 128
ROPE_BASE = 130000.0
EPSILON = 1e-05
NEG_LARGE = -1e30
SCALE = HEAD_DIM ** (-0.5)

BQ = 512
BK = 512
GROUP = ("ctx", "tensor")

F32 = jnp.float32
BF16 = jnp.bfloat16


def pick_table(onehot, table):
    return jnp.sum(jnp.where(onehot, table[None, :], 0), axis=1)


def tree_tables(lengths_row, parent_row, tree_len):
    branches = lengths_row.shape[0] - parent_row.shape[0]
    ends = TRUNK + jnp.cumsum(lengths_row)
    starts = ends - lengths_row
    matches = parent_row[:, None] - 1 == jnp.arange(branches, dtype=jnp.int32)[None, :]
    parent_len = jnp.sum(jnp.where(matches, lengths_row[None, :branches], 0), axis=1)
    zero_one = jnp.zeros((1,), jnp.int32)
    seg_start = jnp.concatenate([zero_one, starts])
    seg_base = jnp.concatenate(
        [zero_one, jnp.full((branches,), TRUNK, jnp.int32), TRUNK + parent_len]
    )
    seg_parent = jnp.concatenate([zero_one, jnp.zeros((branches,), jnp.int32), parent_row])
    positions = jnp.arange(tree_len, dtype=jnp.int32)
    above = jnp.sum((ends[None, :] <= positions[:, None]).astype(jnp.int32), axis=1)
    segment = (positions >= TRUNK).astype(jnp.int32) + above
    onehot = segment[:, None] == jnp.arange(seg_start.shape[0], dtype=jnp.int32)[None, :]
    depth = positions - pick_table(onehot, seg_start) + pick_table(onehot, seg_base)
    parent = pick_table(onehot, seg_parent)
    return (segment, parent, depth)


def rope_tables(depth, width):
    half = HEAD_DIM // 2
    lane = jnp.arange(width, dtype=jnp.int32)
    freqs = jnp.power(ROPE_BASE, -(2.0 * (lane % half).astype(F32)) / HEAD_DIM)
    angles = depth.astype(F32)[:, None] * freqs[None, :]
    sign = jnp.where(lane % HEAD_DIM < half, -1.0, 1.0)
    return jnp.cos(angles), jnp.sin(angles) * sign[None, :]


def partner(x):
    half = HEAD_DIM // 2
    width = x.shape[1]
    if width == HEAD_DIM:
        return jnp.concatenate([x[:, half:], x[:, :half]], axis=1)
    lane = lax.broadcasted_iota(jnp.int32, x.shape, 1)
    ahead = pltpu.roll(x, width - half, 1)
    behind = pltpu.roll(x, half, 1)
    return jnp.where(lane % HEAD_DIM < half, ahead, behind)


def head_mask(shape, head):
    lane = lax.broadcasted_iota(jnp.int32, shape, 1)
    return lane // HEAD_DIM == head


def dot_t(a, b):
    return lax.dot_general(a, b, (((1,), (1,)), ((), ())), preferred_element_type=F32)


def dot_n(a, b):
    return lax.dot_general(a, b, (((1,), (0,)), ((), ())), preferred_element_type=F32)


def dot_tn(a, b):
    return lax.dot_general(a, b, (((0,), (0,)), ((), ())), preferred_element_type=F32)


def key_plan(i, tile):
    base = TRUNK // BK * BK
    branch_end = TRUNK + 4 * MOST_SEG
    first_tree = base // BQ
    mixed_end = -(-(branch_end + MOST_SEG) // BQ)
    chunks = jnp.minimum(i * BQ, base) // BK

    @pl.when(i < first_tree)
    def _():
        @pl.loop(0, chunks)
        def _(j):
            start = pl.multiple_of(j * BK, BK)
            tile(start, BK, 0, start)

    @pl.when(i >= first_tree)
    def _():
        tile(0, base, 0, 0)

    @pl.when(i < first_tree)
    def _():
        start = pl.multiple_of(chunks * BK, BK)
        tile(start, BK, 1, start)

    for block in range(first_tree, mixed_end):

        @pl.when(i == block)
        def _(block=block):
            tile(base, (block + 1) * BQ - base, 2, base)

    @pl.when(i >= mixed_end)
    def _():
        tile(base, branch_end - base, 3, base)
        tile(pl.multiple_of(i * BQ - MOST_SEG, MOST_SEG), BQ + MOST_SEG, 4, branch_end)


def most_keys():
    return TRUNK + 4 * MOST_SEG + BQ + MOST_SEG


def seen_mask(kind, q_at, k_at, seg_q, par_q, seg_k):
    if kind == 3:
        return (seg_k == 0) | (seg_k == par_q)
    causal = k_at <= q_at
    if kind == 1:
        return causal
    if kind == 4:
        return causal & (seg_k == seg_q)
    return causal & ((seg_k == 0) | (seg_k == seg_q) | (seg_k == par_q))


def fwd_kernel(
    heads, q_ref, k_ref, v_ref, cos_ref, sin_ref, segk_ref, segq_ref,
    o_ref, lse_ref, qr_ref, kr_ref, vr_ref, kt_ref, va_ref, s_ref, m_ref, acc_ref,
):
    i = pl.program_id(1)
    wide = 2 * HEAD_DIM

    @pl.when(i == 0)
    def _():
        @pl.loop(0, k_ref.shape[0] // BK)
        def _(j):
            rows = pl.ds(pl.multiple_of(j * BK, BK), BK)
            k = k_ref[rows, :]
            k = (k * cos_ref[rows, :] + partner(k) * sin_ref[rows, :]).astype(BF16)
            kr_ref[rows, :] = k
            kt_ref[:, rows] = jnp.transpose(k)
            v = v_ref[rows, :].astype(BF16)
            vr_ref[rows, :] = v
            if heads == 1:
                va_ref[0, rows, :] = jnp.concatenate([v, jnp.ones_like(v)], axis=1)
            else:
                for h in range(heads):
                    va_ref[h, rows, :] = jnp.where(head_mask(v.shape, h), v, jnp.ones_like(v))

    rows = pl.ds(pl.multiple_of(i * BQ, BQ), BQ)
    q = q_ref[...]
    q = (q * cos_ref[rows, :] + partner(q) * sin_ref[rows, :]).astype(BF16)
    qr_ref[...] = q
    q = q * jnp.asarray(SCALE, BF16)
    q_heads = [jnp.where(head_mask(q.shape, h), q, jnp.zeros_like(q)) for h in range(heads)]
    m_ref[...] = jnp.full_like(m_ref, NEG_LARGE)
    acc_ref[...] = jnp.zeros_like(acc_ref)

    def score_tile(start, width, kind, place):
        keys = pl.ds(start, width)
        k = kt_ref[:, keys]
        seen = None
        if kind != 0:
            shape = (BQ, width)
            seen = seen_mask(
                kind,
                lax.broadcasted_iota(jnp.int32, shape, 0) + i * BQ,
                lax.broadcasted_iota(jnp.int32, shape, 1) + start,
                segq_ref[:, 0:1], segq_ref[:, 1:2], segk_ref[:, keys],
            )
        for h in range(heads):
            s = dot_n(q_heads[h], k)
            if seen is not None:
                s = jnp.where(seen, s, NEG_LARGE)
            s_ref[h, :, pl.ds(place, width)] = s
            largest = m_ref[h]
            for c in range(width // 128):
                largest = jnp.maximum(largest, s[:, c * 128 : (c + 1) * 128])
            m_ref[h] = largest

    key_plan(i, score_tile)
    for h in range(heads):
        m_ref[h] = jnp.broadcast_to(jnp.max(m_ref[h], axis=1, keepdims=True), (BQ, 128))

    def value_tile(start, width, kind, place):
        keys = pl.ds(start, width)
        for h in range(heads):
            m = m_ref[h]
            parts = [
                jnp.exp(s_ref[h, :, pl.ds(place + c * 128, 128)] - m).astype(BF16) for c in range(width // 128)
            ]
            acc_ref[h] += dot_n(jnp.concatenate(parts, axis=1), va_ref[h, keys, :])

    key_plan(i, value_tile)
    out, lse = None, None
    for h in range(heads):
        acc = acc_ref[h]
        part = acc / pltpu.roll(acc, HEAD_DIM, 1)
        stat = m_ref[h] + jnp.log(jnp.broadcast_to(acc[:, (1 - h) * HEAD_DIM : (1 - h) * HEAD_DIM + 1], (BQ, wide)))
        mask = head_mask((BQ, wide), h)
        out = part if h == 0 else jnp.where(mask, part, out)
        lse = stat if h == 0 else jnp.where(mask, stat, lse)
    o_ref[...] = out[:, : heads * HEAD_DIM].astype(BF16)
    turned = jnp.transpose(lse)
    for h in range(heads):
        lse_ref[0, h : h + 1, :] = turned[h * HEAD_DIM : h * HEAD_DIM + 1, :]


def bwd_kernel(
    heads, q_ref, k_ref, v_ref, o_ref, do_ref, lse_ref, cos_ref, sin_ref, segk_ref, segq_ref,
    dq_ref, dk_ref, dv_ref, dq_acc, dk_acc, dv_acc,
):
    i = pl.program_id(1)

    @pl.when(i == 0)
    def _():
        dk_acc[...] = jnp.zeros_like(dk_acc)
        dv_acc[...] = jnp.zeros_like(dv_acc)

    q = q_ref[...]
    scaled = q * jnp.asarray(SCALE, BF16)
    do = do_ref[...]
    product = jnp.transpose(do.astype(F32) * o_ref[...].astype(F32))
    zero = jnp.zeros_like(q)
    masks = [head_mask(q.shape, h) for h in range(heads)]
    q_heads = [jnp.where(m, scaled, zero) for m in masks]
    do_heads = [jnp.where(m, do, zero) for m in masks]
    deltas = [
        jnp.sum(product[h * HEAD_DIM : (h + 1) * HEAD_DIM, :], axis=0, keepdims=True) for h in range(heads)
    ]
    lses = [lse_ref[0, h : h + 1, :] for h in range(heads)]
    q_turned = [jnp.transpose(x) for x in q_heads]
    do_turned = [jnp.transpose(x) for x in do_heads]
    q_stack = jnp.concatenate(q_heads, axis=0)
    do_stack = jnp.concatenate(do_heads, axis=0)
    dq_acc[...] = jnp.zeros_like(dq_acc)

    def tile(start, width, kind, place):
        keys = pl.ds(start, width)
        k = k_ref[keys, :]
        v = v_ref[keys, :]
        seen = None
        if kind != 0:
            shape = (width, BQ)
            seen = seen_mask(
                kind,
                lax.broadcasted_iota(jnp.int32, shape, 1) + i * BQ,
                lax.broadcasted_iota(jnp.int32, shape, 0) + start,
                segq_ref[0:1, :], segq_ref[1:2, :], segk_ref[keys, :],
            )
        probs, grads, k_heads = [], [], []
        for h in range(heads):
            s = dot_n(k, q_turned[h])
            p = jnp.exp(s - lses[h])
            if seen is not None:
                p = jnp.where(seen, p, 0.0)
            dp = dot_n(v, do_turned[h])
            probs.append(p.astype(BF16))
            grads.append((p * (dp - deltas[h])).astype(BF16))
            k_heads.append(jnp.where(head_mask(k.shape, h), k, jnp.zeros_like(k)))
        grad_row = jnp.concatenate(grads, axis=1)
        dv_acc[keys, :] += dot_n(jnp.concatenate(probs, axis=1), do_stack)
        dk_acc[keys, :] += dot_n(grad_row, q_stack)
        dq_acc[...] += dot_tn(jnp.concatenate(grads, axis=0), jnp.concatenate(k_heads, axis=0))

    key_plan(i, tile)
    dq = dq_acc[...] * SCALE
    rows = pl.ds(pl.multiple_of(i * BQ, BQ), BQ)
    dq_ref[...] = (dq * cos_ref[rows, :] - partner(dq) * sin_ref[rows, :]).astype(BF16)

    @pl.when(i == pl.num_programs(1) - 1)
    def _():
        @pl.loop(0, dk_acc.shape[0] // BK)
        def _(j):
            rows = pl.ds(pl.multiple_of(j * BK, BK), BK)
            dk = dk_acc[rows, :]
            dk_ref[rows, :] = (dk * cos_ref[rows, :] - partner(dk) * sin_ref[rows, :]).astype(BF16)
            dv_ref[rows, :] = dv_acc[rows, :].astype(BF16)


def small_cost():
    return pl.CostEstimate(flops=1 << 20, bytes_accessed=1 << 20, transcendentals=0)


def attention_forward(qkv, cosine, sine, seg_keys, seg_queries, width):
    tree_len = qkv.shape[0]
    gw = min(2 * HEAD_DIM, width)
    groups, heads = width // gw, gw // HEAD_DIM
    row_block = pl.BlockSpec((BQ, gw), lambda g, i: (i, g))
    table = pl.BlockSpec((tree_len, gw), lambda g, i: (0, 0))
    full = pl.BlockSpec((tree_len, gw), lambda g, i: (0, g))
    act = jax.ShapeDtypeStruct((tree_len, width), BF16)
    if width % 128 == 0:
        queries, keys, values, step = qkv, qkv, qkv, groups
    else:
        queries, keys, values = jnp.split(qkv, 3, axis=1)
        step = 0
    return pl.pallas_call(
        functools.partial(fwd_kernel, heads),
        grid=(groups, tree_len // BQ),
        in_specs=[
            row_block,
            pl.BlockSpec((tree_len, gw), lambda g, i: (0, step + g)),
            pl.BlockSpec((tree_len, gw), lambda g, i: (0, 2 * step + g)),
            table,
            table,
            pl.BlockSpec((1, tree_len), lambda g, i: (0, 0)),
            pl.BlockSpec((BQ, 2), lambda g, i: (i, 0)),
        ],
        out_specs=[row_block, pl.BlockSpec((1, heads, BQ), lambda g, i: (g, 0, i)), row_block, full, full],
        out_shape=[act, jax.ShapeDtypeStruct((groups, heads, tree_len), F32), act, act, act],
        scratch_shapes=[
            pltpu.VMEM((gw, tree_len), BF16),
            pltpu.VMEM((heads, tree_len, 128), BF16),
            pltpu.VMEM((heads, BQ, most_keys()), F32),
            pltpu.VMEM((heads, BQ, 128), F32),
            pltpu.VMEM((heads, BQ, 128), F32),
        ],
        compiler_params=pltpu.CompilerParams(vmem_limit_bytes=56 << 20),
        cost_estimate=small_cost(),
        name="tree_attention_forward",
    )(queries, keys, values, cosine, sine, seg_keys, seg_queries)


def attention_backward(q, k, v, out, grad, lse, cosine, sine, seg_keys, seg_queries):
    tree_len, width = q.shape
    gw = min(2 * HEAD_DIM, width)
    groups, heads = width // gw, gw // HEAD_DIM
    row_block = pl.BlockSpec((BQ, gw), lambda g, i: (i, g))
    table = pl.BlockSpec((tree_len, gw), lambda g, i: (0, 0))
    full = pl.BlockSpec((tree_len, gw), lambda g, i: (0, g))
    act = jax.ShapeDtypeStruct((tree_len, width), BF16)
    return pl.pallas_call(
        functools.partial(bwd_kernel, heads),
        grid=(groups, tree_len // BQ),
        in_specs=[
            row_block, full, full, row_block, row_block,
            pl.BlockSpec((1, heads, BQ), lambda g, i: (g, 0, i)),
            table, table,
            pl.BlockSpec((tree_len, 1), lambda g, i: (0, 0)),
            pl.BlockSpec((2, BQ), lambda g, i: (0, i)),
        ],
        out_specs=[row_block, full, full],
        out_shape=[act, act, act],
        scratch_shapes=[
            pltpu.VMEM((BQ, gw), F32),
            pltpu.VMEM((tree_len, gw), F32),
            pltpu.VMEM((tree_len, gw), F32),
        ],
        compiler_params=pltpu.CompilerParams(vmem_limit_bytes=56 << 20),
        cost_estimate=small_cost(),
        name="tree_attention_backward",
    )(q, k, v, out, grad, lse, cosine, sine, seg_keys.T, seg_queries.T)


MESH = pl.DeviceIdType.MESH


def plane_place():
    ctx, row = lax.axis_index("ctx"), lax.axis_index("tensor")
    x, core = ctx // 2, ctx % 2
    return x, core, row


def plane_neighbours(x, core, row):
    over_x = {"ctx": (1 - x) * 2 + core}
    over_core = {"ctx": x * 2 + 1 - core}
    over_row = {"tensor": 1 - row}
    return over_x, over_row, over_core


def enter_plane(neighbours):
    barrier = pltpu.get_barrier_semaphore()
    for device in neighbours:
        pl.semaphore_signal(barrier, inc=1, device_id=device, device_id_type=MESH)
    pl.semaphore_wait(barrier, 3)


def gather_kernel(own_ref, all_ref, local_sem, send_sem, recv_sem):
    x, core, row = plane_place()
    over_x, over_row, over_core = plane_neighbours(x, core, row)
    rows = own_ref.shape[0]
    half = rows // 2

    def place(far_x, far_row, part):
        bx = x + far_x - 2 * far_x * x
        by = row + far_row - 2 * far_row * row
        return pl.ds(pl.multiple_of(((bx * 2 + core) * 2 + by) * rows + part * half, half), half)

    enter_plane((over_x, over_row, over_core))
    copies = {}

    def send(slot, source, target, device):
        copies[slot] = pltpu.make_async_remote_copy(
            src_ref=source, dst_ref=all_ref.at[target], send_sem=send_sem.at[slot], recv_sem=recv_sem.at[slot],
            device_id=device, device_id_type=MESH,
        )
        copies[slot].start()

    mine = [own_ref.at[pl.ds(part * half, half)] for part in range(2)]
    own = [place(0, 0, part) for part in range(2)]
    send(0, mine[0], own[0], over_row)
    send(3, mine[1], own[1], over_x)
    send(1, mine[1], own[1], over_row)
    send(4, mine[0], own[0], over_x)
    send(6, mine[0], own[0], over_core)
    send(7, mine[1], own[1], over_core)
    local = [pltpu.make_async_copy(mine[part], all_ref.at[own[part]], local_sem.at[part]) for part in range(2)]
    for copy in local:
        copy.start()

    def forward(got, target, hops):
        copies[got].wait_recv()
        for slot, device in hops:
            send(slot, all_ref.at[target], target, device)

    forward(0, place(0, 1, 0), ((5, over_x), (8, over_core)))
    forward(3, place(1, 0, 1), ((2, over_row), (9, over_core)))
    forward(1, place(0, 1, 1), ((10, over_core),))
    forward(4, place(1, 0, 0), ((11, over_core),))
    forward(5, place(1, 1, 0), ((12, over_core),))
    forward(2, place(1, 1, 1), ((13, over_core),))
    for slot in range(6, 14):
        copies[slot].wait_recv()
    for slot in range(14):
        copies[slot].wait_send()
    for copy in local:
        copy.wait()


def plane_gather(rows):
    count, width = rows.shape
    return pl.pallas_call(
        gather_kernel,
        in_specs=[pl.BlockSpec(memory_space=pl.ANY)],
        out_specs=pl.BlockSpec(memory_space=pl.ANY),
        out_shape=jax.ShapeDtypeStruct((8 * count, width), rows.dtype),
        scratch_shapes=[
            pltpu.SemaphoreType.DMA((2,)),
            pltpu.SemaphoreType.DMA((14,)),
            pltpu.SemaphoreType.DMA((14,)),
        ],
        compiler_params=pltpu.CompilerParams(collective_id=0, has_side_effects=True),
        cost_estimate=small_cost(),
        name="plane_gather",
    )(rows)


PIECES = ((1, 1, 0), (1, 1, 1), (1, 0, 0), (0, 1, 1), (0, 1, 0), (1, 0, 1), (0, 0, 0), (0, 0, 1))
COLS = 512


def scatter_kernel(rows, parts, *refs):
    a_refs, w_refs = refs[:parts], refs[parts : 2 * parts]
    (out_ref, core_out, core_in, first_in, next_in, sems), rest = refs[2 * parts : 2 * parts + 6], refs[2 * parts + 6 :]
    a_bufs, a_sems = rest[:parts], rest[parts]
    x, core, row = plane_place()
    over_x, over_row, over_core = plane_neighbours(x, core, row)
    half = rows // 2
    width = out_ref.shape[1]
    chunks = width // COLS

    def place(piece, on_core):
        far_x, far_row, part = PIECES[piece]
        bx = x + far_x - 2 * far_x * x
        by = row + far_row - 2 * far_row * row
        return pl.ds(pl.multiple_of(((bx * 2 + on_core) * 2 + by) * rows + part * half, half), half)

    def columns(j):
        return pl.ds(pl.multiple_of(j * COLS, COLS), COLS)

    steps = [(0, True)]
    for piece in range(8):
        steps += [(piece + 1, True)] * (piece < 7) + [(piece, False)]

    def load(step):
        piece, partner_half = steps[step]
        taken = place(piece, 1 - core if partner_half else core)
        return [
            pltpu.make_async_copy(a_ref.at[taken], a_buf.at[step % 2], a_sems.at[step % 2, p])
            for p, (a_ref, a_buf) in enumerate(zip(a_refs, a_bufs))
        ]

    loads = {0: load(0)}
    for copy in loads[0]:
        copy.start()
    enter_plane((over_x, over_row, over_core))

    def partial(slot, j):
        total = None
        for a_buf, w_ref in zip(a_bufs, w_refs):
            term = dot_t(a_buf[slot], w_ref[columns(j), :])
            total = term if total is None else total + term
        return total

    def remote(source, target, slot, device):
        return pltpu.make_async_remote_copy(
            src_ref=source, dst_ref=target, send_sem=sems.at[0, slot], recv_sem=sems.at[1, slot],
            device_id=device, device_id_type=MESH,
        )

    core_copies, first_copies, next_copies = [], [], []
    for step, (piece, partner_half) in enumerate(steps):
        for copy in loads[step]:
            copy.wait()
        if step + 1 < len(steps):
            loads[step + 1] = load(step + 1)
            for copy in loads[step + 1]:
                copy.start()
        if partner_half:

            @pl.loop(0, chunks)
            def _(j, step=step, piece=piece):
                core_out[piece, :, columns(j)] = partial(step % 2, j).astype(BF16)

            core_copies.append(remote(core_out.at[piece], core_in.at[piece], piece, over_core))
            core_copies[-1].start()
            continue
        core_copies[piece].wait_recv()

        @pl.loop(0, chunks)
        def _(j, step=step, piece=piece):
            total = partial(step % 2, j) + core_in[piece, :, columns(j)].astype(F32)
            core_in[piece, :, columns(j)] = total.astype(BF16)

        if piece < 4:
            first_copies.append(
                remote(core_in.at[piece], first_in.at[piece], 8 + piece, over_x if piece % 2 == 0 else over_row)
            )
            first_copies[-1].start()
    for part in range(2):
        first_copies[part].wait_recv()

        @pl.loop(0, chunks)
        def _(j, part=part):
            total = core_in[4 + part, :, columns(j)].astype(F32) + first_in[part, :, columns(j)].astype(F32)
            core_in[4 + part, :, columns(j)] = total.astype(BF16)

        next_copies.append(remote(core_in.at[4 + part], next_in.at[part], 12 + part, over_row if part == 0 else over_x))
        next_copies[-1].start()
    for part in range(2):
        first_copies[2 + part].wait_recv()
        next_copies[part].wait_recv()

        @pl.loop(0, chunks)
        def _(j, part=part):
            total = core_in[6 + part, :, columns(j)].astype(F32) + first_in[2 + part, :, columns(j)].astype(F32)
            out_ref[pl.ds(part * half, half), columns(j)] = total + next_in[part, :, columns(j)].astype(F32)

    for copy in core_copies + first_copies + next_copies:
        copy.wait_send()


def plane_scatter(parts, weights, collective_id):
    count = parts[0].shape[0]
    width = weights[0].shape[0]
    rows = count // 8
    half = rows // 2
    vmem = pl.BlockSpec(memory_space=pltpu.VMEM)
    return pl.pallas_call(
        functools.partial(scatter_kernel, rows, len(parts)),
        in_specs=[pl.BlockSpec(memory_space=pl.ANY)] * len(parts) + [vmem] * len(parts),
        out_specs=vmem,
        out_shape=jax.ShapeDtypeStruct((rows, width), F32),
        scratch_shapes=[
            pltpu.VMEM((8, half, width), BF16),
            pltpu.VMEM((8, half, width), BF16),
            pltpu.VMEM((4, half, width), BF16),
            pltpu.VMEM((2, half, width), BF16),
            pltpu.SemaphoreType.DMA((2, 14)),
        ]
        + [pltpu.VMEM((2, half, a.shape[1]), BF16) for a in parts]
        + [pltpu.SemaphoreType.DMA((2, len(parts)))],
        compiler_params=pltpu.CompilerParams(
            collective_id=collective_id, has_side_effects=True, vmem_limit_bytes=52 << 20
        ),
        cost_estimate=small_cost(),
        name="plane_scatter",
    )(*parts, *weights)


def is_plane():
    return lax.axis_size("ctx") == 4 and lax.axis_size("tensor") == 2


def gather_rows(rows):
    return lax.all_gather(rows, GROUP, axis=0, tiled=True)


def scatter_rows(rows):
    return lax.psum_scatter(rows.astype(BF16), GROUP, scatter_dimension=0, tiled=True).astype(F32)


def gather_now(rows):
    return plane_gather(rows) if is_plane() else gather_rows(rows)


def product_scatter(parts, weights, collective_id):
    if is_plane():
        return plane_scatter(parts, weights, collective_id)
    return scatter_rows(dot_t(jnp.concatenate(parts, axis=1), jnp.concatenate(weights, axis=1)))


def gather_weight(own):
    return lax.all_gather(own, "fsdp", axis=0, tiled=True)


def scatter_weight(grad):
    return lax.psum_scatter(grad.astype(BF16), "fsdp", scatter_dimension=0, tiled=True)


def swap_columns(part, count):
    size = lax.axis_size("ctx")
    rows, columns = part.shape[0] // size, part.shape[1] // count
    got = lax.all_to_all(part.reshape(size, rows, count * columns), "ctx", split_axis=0, concat_axis=0)
    return [
        jnp.concatenate([got[j, :, c * columns : (c + 1) * columns] for j in range(size)], axis=1).astype(F32)
        for c in range(count)
    ]


def normalize(rows):
    norm_inv = lax.rsqrt(jnp.mean(rows * rows, axis=1, keepdims=True) + EPSILON)
    return (rows * norm_inv, norm_inv)


def norm_backward(grad_rows, scaled, norm_inv, gain):
    weighted = grad_rows * gain[None, :]
    inner = jnp.mean(weighted * scaled, axis=1, keepdims=True)
    return norm_inv * (weighted - scaled * inner)


def body(
    tokens_in,
    attn_gain,
    query_weight,
    key_weight,
    value_weight,
    output_weight,
    mlp_gain,
    gate_weight,
    up_weight,
    down_weight,
    seg_lengths,
    leaf_parent,
    cotangent,
):
    ctx = lax.axis_index("ctx")
    parts = lax.axis_size("ctx")
    tree_len = tokens_in.shape[0] * parts * lax.axis_size("tensor")
    width = query_weight.shape[1] // parts
    units = gate_weight.shape[1] // parts

    def mine(weight, columns):
        return lax.dynamic_slice_in_dim(weight, ctx * columns, columns, 1)

    x_rows = tokens_in.astype(F32)
    attn_scaled, attn_inv = normalize(x_rows)
    w_attn = gather_weight(
        jnp.concatenate([mine(w, width) for w in (query_weight, key_weight, value_weight, output_weight)], axis=1)
    )
    cot_all = gather_rows(cotangent)
    w_gate = gather_weight(mine(gate_weight, units))
    w_up = gather_weight(mine(up_weight, units))
    w_down = gather_weight(mine(down_weight, units))
    attn_in = gather_now((attn_scaled * attn_gain[None, :]).astype(BF16))
    w_qkv, w_out = w_attn[:, : 3 * width], w_attn[:, 3 * width :]

    attn_in, lengths_row, parent_row = lax.optimization_barrier((attn_in, seg_lengths[0], leaf_parent[0]))
    segment, parent, depth = tree_tables(lengths_row, parent_row, tree_len)
    cosine, sine = rope_tables(depth, min(2 * HEAD_DIM, width))
    seg_keys = segment[None, :]
    seg_queries = jnp.stack([segment, parent], axis=1)

    qkv = jnp.dot(attn_in, w_qkv, preferred_element_type=F32)
    attn_out, lse, query_rows, key_rows, value_rows = attention_forward(
        qkv, cosine, sine, seg_keys, seg_queries, width
    )
    mid_rows = x_rows + product_scatter([attn_out], [w_out], 1)
    mlp_scaled, mlp_inv = normalize(mid_rows)
    mlp_own, cot_all = lax.optimization_barrier(((mlp_scaled * mlp_gain[None, :]).astype(BF16), cot_all))
    mlp_in = gather_now(mlp_own)

    gate = jnp.dot(mlp_in, w_gate, preferred_element_type=F32)
    up_proj = jnp.dot(mlp_in, w_up, preferred_element_type=F32)
    sigmoid_gate = jax.nn.sigmoid(gate)
    hidden = (gate * sigmoid_gate * up_proj).astype(BF16)
    down_rows, cot_all = lax.optimization_barrier((dot_t(hidden, w_down).astype(BF16), cot_all))
    down_rows = scatter_rows(down_rows)
    hidden_grad = jnp.dot(cot_all, w_down, preferred_element_type=F32)
    gate_rows_grad = (
        hidden_grad * up_proj * sigmoid_gate * (1.0 + gate * (1.0 - sigmoid_gate))
    ).astype(BF16)
    up_rows_grad = (hidden_grad * gate * sigmoid_gate).astype(BF16)

    mlp_in_grad = product_scatter([gate_rows_grad, up_rows_grad], [w_gate, w_up], 3)
    mlp_back = norm_backward(mlp_in_grad, mlp_scaled, mlp_inv, mlp_gain)
    mlp_gain_part = jnp.sum(mlp_in_grad * mlp_scaled, axis=0)
    mid_grad = cotangent.astype(F32) + mlp_back
    mid_low, mlp_in, cot_all, down_rows = lax.optimization_barrier(
        (mid_grad.astype(BF16), mlp_in, cot_all, down_rows)
    )
    block_out = (mid_rows + down_rows).astype(BF16)
    mid_all = gather_rows(mid_low)
    gate_part = dot_tn(mlp_in, gate_rows_grad).astype(BF16)
    up_part = dot_tn(mlp_in, up_rows_grad).astype(BF16)
    down_part = dot_tn(cot_all, hidden).astype(BF16)
    mid_all, gate_part, up_part, down_part = lax.optimization_barrier((mid_all, gate_part, up_part, down_part))
    gate_grad = scatter_weight(gate_part)
    up_grad = scatter_weight(up_part)
    down_grad = scatter_weight(down_part)

    out_heads_grad = jnp.dot(mid_all, w_out, preferred_element_type=F32).astype(BF16)
    output_grad = dot_tn(mid_all, attn_out)
    pre_grads = attention_backward(
        query_rows, key_rows, value_rows, attn_out, out_heads_grad, lse, cosine, sine, seg_keys, seg_queries
    )
    pre_grads, gate_grad, up_grad = lax.optimization_barrier((pre_grads, gate_grad, up_grad))
    qkv_grad = jnp.concatenate([dot_tn(attn_in, grad) for grad in pre_grads], axis=1)
    attn_gain_part = jnp.sum(qkv_grad * w_qkv.astype(F32), axis=1) / attn_gain
    attn_part = jnp.concatenate([qkv_grad, output_grad], axis=1).astype(BF16)
    pre_grads, attn_part = lax.optimization_barrier((pre_grads, attn_part))
    attn_in_grad = product_scatter(
        pre_grads, [w_attn[:, j * width : (j + 1) * width] for j in range(3)], 2
    )
    devices = lax.axis_size(("fsdp", "ctx", "tensor"))
    gain_parts = [part.reshape(devices, -1) for part in (attn_gain_part, mlp_gain_part)]
    gain_grads = lax.psum_scatter(
        jnp.concatenate(gain_parts, axis=1), ("fsdp", "ctx", "tensor"), scatter_dimension=0, tiled=True
    ).reshape(2, -1)
    attn_grad = scatter_weight(attn_part)
    gate_out, up_out, down_out = swap_columns(jnp.concatenate([gate_grad, up_grad, down_grad], axis=1), 3)
    query_out, key_out, value_out, output_out = swap_columns(attn_grad, 4)

    attn_back = norm_backward(attn_in_grad, attn_scaled, attn_inv, attn_gain)
    input_grad = (mid_grad + attn_back).astype(BF16)
    return (
        block_out,
        input_grad,
        gain_grads[0],
        query_out,
        key_out,
        value_out,
        output_out,
        gain_grads[1],
        gate_out,
        up_out,
        down_out,
    )


def solution(mesh):
    rows = P(("fsdp", "ctx", "tensor"), None)
    weight = P("fsdp", "tensor")
    gain = P(("fsdp", "ctx", "tensor"))
    grad = P(("fsdp", "ctx"), "tensor")
    in_specs = (
        rows, P(), weight, weight, weight, weight, P(), weight, weight, weight, P("fsdp", None), P("fsdp", None), rows,
    )
    out_specs = (rows, rows, gain, grad, grad, grad, grad, gain, grad, grad, grad)
    return jax.shard_map(body, mesh=mesh, in_specs=in_specs, out_specs=out_specs, check_vma=False)
```

```python
import functools

import jax
import jax.numpy as jnp
from jax import lax
from jax.experimental import pallas as pl
from jax.experimental.pallas import tpu as pltpu
from jax.sharding import PartitionSpec as P

HEAD_DIM = 64
TRUNK = 2176
MOST_SEG = 128
ROPE_BASE = 130000.0
EPSILON = 1e-05
NEG_LARGE = -1e30
SCALE = HEAD_DIM ** (-0.5)

BQ = 512
BK = 512
GROUP = ("ctx", "tensor")

F32 = jnp.float32
BF16 = jnp.bfloat16


def pick_table(onehot, table):
    return jnp.sum(jnp.where(onehot, table[None, :], 0), axis=1)


def tree_tables(lengths_row, parent_row, tree_len):
    branches = lengths_row.shape[0] - parent_row.shape[0]
    ends = TRUNK + jnp.cumsum(lengths_row)
    starts = ends - lengths_row
    matches = parent_row[:, None] - 1 == jnp.arange(branches, dtype=jnp.int32)[None, :]
    parent_len = jnp.sum(jnp.where(matches, lengths_row[None, :branches], 0), axis=1)
    zero_one = jnp.zeros((1,), jnp.int32)
    seg_start = jnp.concatenate([zero_one, starts])
    seg_base = jnp.concatenate(
        [zero_one, jnp.full((branches,), TRUNK, jnp.int32), TRUNK + parent_len]
    )
    seg_parent = jnp.concatenate([zero_one, jnp.zeros((branches,), jnp.int32), parent_row])
    positions = jnp.arange(tree_len, dtype=jnp.int32)
    above = jnp.sum((ends[None, :] <= positions[:, None]).astype(jnp.int32), axis=1)
    segment = (positions >= TRUNK).astype(jnp.int32) + above
    onehot = segment[:, None] == jnp.arange(seg_start.shape[0], dtype=jnp.int32)[None, :]
    depth = positions - pick_table(onehot, seg_start) + pick_table(onehot, seg_base)
    parent = pick_table(onehot, seg_parent)
    return (segment, parent, depth)


def rope_tables(depth, width):
    half = HEAD_DIM // 2
    lane = jnp.arange(width, dtype=jnp.int32)
    freqs = jnp.power(ROPE_BASE, -(2.0 * (lane % half).astype(F32)) / HEAD_DIM)
    angles = depth.astype(F32)[:, None] * freqs[None, :]
    sign = jnp.where(lane % HEAD_DIM < half, -1.0, 1.0)
    return jnp.cos(angles), jnp.sin(angles) * sign[None, :]


def partner(x):
    half = HEAD_DIM // 2
    width = x.shape[1]
    if width == HEAD_DIM:
        return jnp.concatenate([x[:, half:], x[:, :half]], axis=1)
    lane = lax.broadcasted_iota(jnp.int32, x.shape, 1)
    ahead = pltpu.roll(x, width - half, 1)
    behind = pltpu.roll(x, half, 1)
    return jnp.where(lane % HEAD_DIM < half, ahead, behind)


def head_mask(shape, head):
    lane = lax.broadcasted_iota(jnp.int32, shape, 1)
    return lane // HEAD_DIM == head


def dot_t(a, b):
    return lax.dot_general(a, b, (((1,), (1,)), ((), ())), preferred_element_type=F32)


def dot_n(a, b):
    return lax.dot_general(a, b, (((1,), (0,)), ((), ())), preferred_element_type=F32)


def dot_tn(a, b):
    return lax.dot_general(a, b, (((0,), (0,)), ((), ())), preferred_element_type=F32)


def key_plan(i, tile):
    base = TRUNK // BK * BK
    branch_end = TRUNK + 4 * MOST_SEG
    first_tree = base // BQ
    mixed_end = -(-(branch_end + MOST_SEG) // BQ)
    chunks = jnp.minimum(i * BQ, base) // BK

    @pl.when(i < first_tree)
    def _():
        @pl.loop(0, chunks)
        def _(j):
            start = pl.multiple_of(j * BK, BK)
            tile(start, BK, 0, start)

    @pl.when(i >= first_tree)
    def _():
        tile(0, base, 0, 0)

    @pl.when(i < first_tree)
    def _():
        start = pl.multiple_of(chunks * BK, BK)
        tile(start, BK, 1, start)

    for block in range(first_tree, mixed_end):

        @pl.when(i == block)
        def _(block=block):
            tile(base, (block + 1) * BQ - base, 2, base)

    @pl.when(i >= mixed_end)
    def _():
        tile(base, branch_end - base, 3, base)
        tile(pl.multiple_of(i * BQ - MOST_SEG, MOST_SEG), BQ + MOST_SEG, 4, branch_end)


def most_keys():
    return TRUNK + 4 * MOST_SEG + BQ + MOST_SEG


def seen_mask(kind, q_at, k_at, seg_q, par_q, seg_k):
    if kind == 3:
        return (seg_k == 0) | (seg_k == par_q)
    causal = k_at <= q_at
    if kind == 1:
        return causal
    if kind == 4:
        return causal & (seg_k == seg_q)
    return causal & ((seg_k == 0) | (seg_k == seg_q) | (seg_k == par_q))


def fwd_kernel(
    heads, q_ref, k_ref, v_ref, cos_ref, sin_ref, segk_ref, segq_ref,
    o_ref, lse_ref, qr_ref, kr_ref, vr_ref, kt_ref, va_ref, s_ref, m_ref, acc_ref,
):
    i = pl.program_id(1)
    wide = 2 * HEAD_DIM

    @pl.when(i == 0)
    def _():
        @pl.loop(0, k_ref.shape[0] // BK)
        def _(j):
            rows = pl.ds(pl.multiple_of(j * BK, BK), BK)
            k = k_ref[rows, :]
            k = (k * cos_ref[rows, :] + partner(k) * sin_ref[rows, :]).astype(BF16)
            kr_ref[rows, :] = k
            kt_ref[:, rows] = jnp.transpose(k)
            v = v_ref[rows, :].astype(BF16)
            vr_ref[rows, :] = v
            if heads == 1:
                va_ref[0, rows, :] = jnp.concatenate([v, jnp.ones_like(v)], axis=1)
            else:
                for h in range(heads):
                    va_ref[h, rows, :] = jnp.where(head_mask(v.shape, h), v, jnp.ones_like(v))

    rows = pl.ds(pl.multiple_of(i * BQ, BQ), BQ)
    q = q_ref[...]
    q = (q * cos_ref[rows, :] + partner(q) * sin_ref[rows, :]).astype(BF16)
    qr_ref[...] = q
    q = q * jnp.asarray(SCALE, BF16)
    q_heads = [jnp.where(head_mask(q.shape, h), q, jnp.zeros_like(q)) for h in range(heads)]
    m_ref[...] = jnp.full_like(m_ref, NEG_LARGE)
    acc_ref[...] = jnp.zeros_like(acc_ref)

    def score_tile(start, width, kind, place):
        keys = pl.ds(start, width)
        k = kt_ref[:, keys]
        seen = None
        if kind != 0:
            shape = (BQ, width)
            seen = seen_mask(
                kind,
                lax.broadcasted_iota(jnp.int32, shape, 0) + i * BQ,
                lax.broadcasted_iota(jnp.int32, shape, 1) + start,
                segq_ref[:, 0:1], segq_ref[:, 1:2], segk_ref[:, keys],
            )
        for h in range(heads):
            s = dot_n(q_heads[h], k)
            if seen is not None:
                s = jnp.where(seen, s, NEG_LARGE)
            s_ref[h, :, pl.ds(place, width)] = s
            largest = m_ref[h]
            for c in range(width // 128):
                largest = jnp.maximum(largest, s[:, c * 128 : (c + 1) * 128])
            m_ref[h] = largest

    key_plan(i, score_tile)
    for h in range(heads):
        m_ref[h] = jnp.broadcast_to(jnp.max(m_ref[h], axis=1, keepdims=True), (BQ, 128))

    def value_tile(start, width, kind, place):
        keys = pl.ds(start, width)
        for h in range(heads):
            m = m_ref[h]
            parts = [
                jnp.exp(s_ref[h, :, pl.ds(place + c * 128, 128)] - m).astype(BF16) for c in range(width // 128)
            ]
            acc_ref[h] += dot_n(jnp.concatenate(parts, axis=1), va_ref[h, keys, :])

    key_plan(i, value_tile)
    out, lse = None, None
    for h in range(heads):
        acc = acc_ref[h]
        part = acc / pltpu.roll(acc, HEAD_DIM, 1)
        stat = m_ref[h] + jnp.log(jnp.broadcast_to(acc[:, (1 - h) * HEAD_DIM : (1 - h) * HEAD_DIM + 1], (BQ, wide)))
        mask = head_mask((BQ, wide), h)
        out = part if h == 0 else jnp.where(mask, part, out)
        lse = stat if h == 0 else jnp.where(mask, stat, lse)
    o_ref[...] = out[:, : heads * HEAD_DIM].astype(BF16)
    turned = jnp.transpose(lse)
    for h in range(heads):
        lse_ref[0, h : h + 1, :] = turned[h * HEAD_DIM : h * HEAD_DIM + 1, :]


def bwd_kernel(
    heads, q_ref, k_ref, v_ref, o_ref, do_ref, lse_ref, cos_ref, sin_ref, segk_ref, segq_ref,
    dq_ref, dk_ref, dv_ref, dq_acc, dk_acc, dv_acc,
):
    i = pl.program_id(1)

    @pl.when(i == 0)
    def _():
        dk_acc[...] = jnp.zeros_like(dk_acc)
        dv_acc[...] = jnp.zeros_like(dv_acc)

    q = q_ref[...]
    scaled = q * jnp.asarray(SCALE, BF16)
    do = do_ref[...]
    product = jnp.transpose(do.astype(F32) * o_ref[...].astype(F32))
    zero = jnp.zeros_like(q)
    masks = [head_mask(q.shape, h) for h in range(heads)]
    q_heads = [jnp.where(m, scaled, zero) for m in masks]
    do_heads = [jnp.where(m, do, zero) for m in masks]
    deltas = [
        jnp.sum(product[h * HEAD_DIM : (h + 1) * HEAD_DIM, :], axis=0, keepdims=True) for h in range(heads)
    ]
    lses = [lse_ref[0, h : h + 1, :] for h in range(heads)]
    q_turned = [jnp.transpose(x) for x in q_heads]
    do_turned = [jnp.transpose(x) for x in do_heads]
    q_stack = jnp.concatenate(q_heads, axis=0)
    do_stack = jnp.concatenate(do_heads, axis=0)
    dq_acc[...] = jnp.zeros_like(dq_acc)

    def tile(start, width, kind, place):
        keys = pl.ds(start, width)
        k = k_ref[keys, :]
        v = v_ref[keys, :]
        seen = None
        if kind != 0:
            shape = (width, BQ)
            seen = seen_mask(
                kind,
                lax.broadcasted_iota(jnp.int32, shape, 1) + i * BQ,
                lax.broadcasted_iota(jnp.int32, shape, 0) + start,
                segq_ref[0:1, :], segq_ref[1:2, :], segk_ref[keys, :],
            )
        probs, grads, k_heads = [], [], []
        for h in range(heads):
            s = dot_n(k, q_turned[h])
            p = jnp.exp(s - lses[h])
            if seen is not None:
                p = jnp.where(seen, p, 0.0)
            dp = dot_n(v, do_turned[h])
            probs.append(p.astype(BF16))
            grads.append((p * (dp - deltas[h])).astype(BF16))
            k_heads.append(jnp.where(head_mask(k.shape, h), k, jnp.zeros_like(k)))
        grad_row = jnp.concatenate(grads, axis=1)
        dv_acc[keys, :] += dot_n(jnp.concatenate(probs, axis=1), do_stack)
        dk_acc[keys, :] += dot_n(grad_row, q_stack)
        dq_acc[...] += dot_tn(jnp.concatenate(grads, axis=0), jnp.concatenate(k_heads, axis=0))

    key_plan(i, tile)
    dq = dq_acc[...] * SCALE
    rows = pl.ds(pl.multiple_of(i * BQ, BQ), BQ)
    dq_ref[...] = (dq * cos_ref[rows, :] - partner(dq) * sin_ref[rows, :]).astype(BF16)

    @pl.when(i == pl.num_programs(1) - 1)
    def _():
        @pl.loop(0, dk_acc.shape[0] // BK)
        def _(j):
            rows = pl.ds(pl.multiple_of(j * BK, BK), BK)
            dk = dk_acc[rows, :]
            dk_ref[rows, :] = (dk * cos_ref[rows, :] - partner(dk) * sin_ref[rows, :]).astype(BF16)
            dv_ref[rows, :] = dv_acc[rows, :].astype(BF16)


def small_cost():
    return pl.CostEstimate(flops=1 << 20, bytes_accessed=1 << 20, transcendentals=0)


def attention_forward(qkv, cosine, sine, seg_keys, seg_queries, width):
    tree_len = qkv.shape[0]
    gw = min(2 * HEAD_DIM, width)
    groups, heads = width // gw, gw // HEAD_DIM
    row_block = pl.BlockSpec((BQ, gw), lambda g, i: (i, g))
    table = pl.BlockSpec((tree_len, gw), lambda g, i: (0, 0))
    full = pl.BlockSpec((tree_len, gw), lambda g, i: (0, g))
    act = jax.ShapeDtypeStruct((tree_len, width), BF16)
    if width % 128 == 0:
        queries, keys, values, step = qkv, qkv, qkv, groups
    else:
        queries, keys, values = jnp.split(qkv, 3, axis=1)
        step = 0
    return pl.pallas_call(
        functools.partial(fwd_kernel, heads),
        grid=(groups, tree_len // BQ),
        in_specs=[
            row_block,
            pl.BlockSpec((tree_len, gw), lambda g, i: (0, step + g)),
            pl.BlockSpec((tree_len, gw), lambda g, i: (0, 2 * step + g)),
            table,
            table,
            pl.BlockSpec((1, tree_len), lambda g, i: (0, 0)),
            pl.BlockSpec((BQ, 2), lambda g, i: (i, 0)),
        ],
        out_specs=[row_block, pl.BlockSpec((1, heads, BQ), lambda g, i: (g, 0, i)), row_block, full, full],
        out_shape=[act, jax.ShapeDtypeStruct((groups, heads, tree_len), F32), act, act, act],
        scratch_shapes=[
            pltpu.VMEM((gw, tree_len), BF16),
            pltpu.VMEM((heads, tree_len, 128), BF16),
            pltpu.VMEM((heads, BQ, most_keys()), F32),
            pltpu.VMEM((heads, BQ, 128), F32),
            pltpu.VMEM((heads, BQ, 128), F32),
        ],
        compiler_params=pltpu.CompilerParams(vmem_limit_bytes=56 << 20),
        cost_estimate=small_cost(),
        name="tree_attention_forward",
    )(queries, keys, values, cosine, sine, seg_keys, seg_queries)


def attention_backward(q, k, v, out, grad, lse, cosine, sine, seg_keys, seg_queries):
    tree_len, width = q.shape
    gw = min(2 * HEAD_DIM, width)
    groups, heads = width // gw, gw // HEAD_DIM
    row_block = pl.BlockSpec((BQ, gw), lambda g, i: (i, g))
    table = pl.BlockSpec((tree_len, gw), lambda g, i: (0, 0))
    full = pl.BlockSpec((tree_len, gw), lambda g, i: (0, g))
    act = jax.ShapeDtypeStruct((tree_len, width), BF16)
    return pl.pallas_call(
        functools.partial(bwd_kernel, heads),
        grid=(groups, tree_len // BQ),
        in_specs=[
            row_block, full, full, row_block, row_block,
            pl.BlockSpec((1, heads, BQ), lambda g, i: (g, 0, i)),
            table, table,
            pl.BlockSpec((tree_len, 1), lambda g, i: (0, 0)),
            pl.BlockSpec((2, BQ), lambda g, i: (0, i)),
        ],
        out_specs=[row_block, full, full],
        out_shape=[act, act, act],
        scratch_shapes=[
            pltpu.VMEM((BQ, gw), F32),
            pltpu.VMEM((tree_len, gw), F32),
            pltpu.VMEM((tree_len, gw), F32),
        ],
        compiler_params=pltpu.CompilerParams(vmem_limit_bytes=56 << 20),
        cost_estimate=small_cost(),
        name="tree_attention_backward",
    )(q, k, v, out, grad, lse, cosine, sine, seg_keys.T, seg_queries.T)


MESH = pl.DeviceIdType.MESH


def plane_place():
    ctx, row = lax.axis_index("ctx"), lax.axis_index("tensor")
    x, core = ctx // 2, ctx % 2
    return x, core, row


def plane_neighbours(x, core, row):
    over_x = {"ctx": (1 - x) * 2 + core}
    over_core = {"ctx": x * 2 + 1 - core}
    over_row = {"tensor": 1 - row}
    return over_x, over_row, over_core


def enter_plane(neighbours):
    barrier = pltpu.get_barrier_semaphore()
    for device in neighbours:
        pl.semaphore_signal(barrier, inc=1, device_id=device, device_id_type=MESH)
    pl.semaphore_wait(barrier, 3)


TOKENS_AT_ONCE = 2048
LEFT_AT_ONCE = 512
STEP = 512


def product_buffers(columns):
    return [
        pltpu.VMEM((2, TOKENS_AT_ONCE, LEFT_AT_ONCE), BF16),
        pltpu.VMEM((2 * TOKENS_AT_ONCE, columns), BF16),
        pltpu.VMEM((LEFT_AT_ONCE, columns), F32),
        pltpu.VMEM((LEFT_AT_ONCE, columns), BF16),
        pltpu.SemaphoreType.DMA((4,)),
    ]


def token_product(left_ref, right_ref, out_ref, left_buf, right_buf, total, out_buf, sems):
    tokens = left_ref.shape[0]
    parts, groups = tokens // TOKENS_AT_ONCE, left_ref.shape[1] // LEFT_AT_ONCE

    def load(step):
        group, part = step // parts, step % parts
        source = left_ref.at[
            pl.ds(part * TOKENS_AT_ONCE, TOKENS_AT_ONCE), pl.ds(group * LEFT_AT_ONCE, LEFT_AT_ONCE)
        ]
        return pltpu.make_async_copy(source, left_buf.at[step % 2], sems.at[step % 2])

    def store(group):
        return pltpu.make_async_copy(out_buf, out_ref.at[pl.ds(group * LEFT_AT_ONCE, LEFT_AT_ONCE)], sems.at[3])

    whole = pltpu.make_async_copy(right_ref, right_buf, sems.at[2])
    whole.start()
    load(0).start()
    whole.wait()
    for group in range(groups):
        for part in range(parts):
            step = group * parts + part
            load(step).wait()
            if step + 1 < groups * parts:
                load(step + 1).start()
            if part == 0:
                total[...] = jnp.zeros_like(total)

            @pl.loop(0, TOKENS_AT_ONCE // STEP)
            def _(j, step=step, part=part):
                left = left_buf[step % 2, pl.ds(pl.multiple_of(j * STEP, STEP), STEP), :]
                right = right_buf[pl.ds(pl.multiple_of(part * TOKENS_AT_ONCE + j * STEP, STEP), STEP), :]
                total[...] += dot_tn(left, right)

        if group > 0:
            store(group - 1).wait()
        out_buf[...] = total[...].astype(BF16)
        store(group).start()
        yield
    store(groups - 1).wait()


def finish(product):
    for _ in product:
        pass


def gather_kernel(*refs):
    if len(refs) == 5:
        own_ref, all_ref, local_sem, send_sem, recv_sem = refs
        product = iter(())
    else:
        own_ref, left_ref, right_ref, all_ref, out_ref, local_sem, send_sem, recv_sem = refs[:8]
        product = token_product(left_ref, right_ref, out_ref, *refs[8:])
    x, core, row = plane_place()
    over_x, over_row, over_core = plane_neighbours(x, core, row)
    rows = own_ref.shape[0]
    half = rows // 2

    def place(far_x, far_row, part):
        bx = x + far_x - 2 * far_x * x
        by = row + far_row - 2 * far_row * row
        return pl.ds(pl.multiple_of(((bx * 2 + core) * 2 + by) * rows + part * half, half), half)

    enter_plane((over_x, over_row, over_core))
    copies = {}

    def send(slot, source, target, device):
        copies[slot] = pltpu.make_async_remote_copy(
            src_ref=source, dst_ref=all_ref.at[target], send_sem=send_sem.at[slot], recv_sem=recv_sem.at[slot],
            device_id=device, device_id_type=MESH,
        )
        copies[slot].start()

    mine = [own_ref.at[pl.ds(part * half, half)] for part in range(2)]
    own = [place(0, 0, part) for part in range(2)]
    send(0, mine[0], own[0], over_row)
    send(3, mine[1], own[1], over_x)
    send(1, mine[1], own[1], over_row)
    send(4, mine[0], own[0], over_x)
    send(6, mine[0], own[0], over_core)
    send(7, mine[1], own[1], over_core)
    local = [pltpu.make_async_copy(mine[part], all_ref.at[own[part]], local_sem.at[part]) for part in range(2)]
    for copy in local:
        copy.start()

    def forward(got, target, hops):
        copies[got].wait_recv()
        for slot, device in hops:
            send(slot, all_ref.at[target], target, device)

    for _ in range(3):
        next(product, None)
    forward(0, place(0, 1, 0), ((5, over_x), (8, over_core)))
    forward(3, place(1, 0, 1), ((2, over_row), (9, over_core)))
    finish(product)
    forward(1, place(0, 1, 1), ((10, over_core),))
    forward(4, place(1, 0, 0), ((11, over_core),))
    forward(5, place(1, 1, 0), ((12, over_core),))
    forward(2, place(1, 1, 1), ((13, over_core),))
    for slot in range(6, 14):
        copies[slot].wait_recv()
    for slot in range(14):
        copies[slot].wait_send()
    for copy in local:
        copy.wait()


def plane_gather(rows, left=None, right=None):
    count, width = rows.shape
    hbm = pl.BlockSpec(memory_space=pl.ANY)
    scratch = [pltpu.SemaphoreType.DMA((2,)), pltpu.SemaphoreType.DMA((14,)), pltpu.SemaphoreType.DMA((14,))]
    inputs, outputs = [rows], [jax.ShapeDtypeStruct((8 * count, width), rows.dtype)]
    if left is not None:
        inputs += [left, right]
        outputs += [jax.ShapeDtypeStruct((left.shape[1], right.shape[1]), BF16)]
        scratch += product_buffers(right.shape[1])
    result = pl.pallas_call(
        gather_kernel,
        in_specs=[hbm] * len(inputs),
        out_specs=[hbm] * len(outputs),
        out_shape=outputs,
        scratch_shapes=scratch,
        compiler_params=pltpu.CompilerParams(
            collective_id=0 if left is None else 4,
            has_side_effects=True,
            vmem_limit_bytes=None if left is None else 48 << 20,
        ),
        cost_estimate=small_cost(),
        name="plane_gather",
    )(*inputs)
    return result[0] if left is None else result


PIECES = ((1, 1, 0), (1, 1, 1), (1, 0, 0), (0, 1, 1), (0, 1, 0), (1, 0, 1), (0, 0, 0), (0, 0, 1))
COLS = 512


def scatter_kernel(rows, parts, jobs, *refs):
    def take(count):
        nonlocal refs
        taken, refs = refs[:count], refs[count:]
        return taken

    a_refs, w_refs, lefts, rights = take(parts), take(parts), take(jobs), take(jobs)
    (out_ref,), products = take(1), take(jobs)
    core_out, core_in, first_in, next_in, sems = take(5)
    a_bufs, (a_sems,), buffers = take(parts), take(1), refs

    def work(job):
        if job < jobs:
            finish(token_product(lefts[job], rights[job], products[job], *buffers))

    x, core, row = plane_place()
    over_x, over_row, over_core = plane_neighbours(x, core, row)
    half = rows // 2
    width = out_ref.shape[1]
    chunks = width // COLS

    def place(piece, on_core):
        far_x, far_row, part = PIECES[piece]
        bx = x + far_x - 2 * far_x * x
        by = row + far_row - 2 * far_row * row
        return pl.ds(pl.multiple_of(((bx * 2 + on_core) * 2 + by) * rows + part * half, half), half)

    def columns(j):
        return pl.ds(pl.multiple_of(j * COLS, COLS), COLS)

    steps = [(0, True)]
    for piece in range(8):
        steps += [(piece + 1, True)] * (piece < 7) + [(piece, False)]

    def load(step):
        piece, partner_half = steps[step]
        taken = place(piece, 1 - core if partner_half else core)
        return [
            pltpu.make_async_copy(a_ref.at[taken], a_buf.at[step % 2], a_sems.at[step % 2, p])
            for p, (a_ref, a_buf) in enumerate(zip(a_refs, a_bufs))
        ]

    loads = {0: load(0)}
    for copy in loads[0]:
        copy.start()
    enter_plane((over_x, over_row, over_core))

    def partial(slot, j):
        total = None
        for a_buf, w_ref in zip(a_bufs, w_refs):
            term = dot_t(a_buf[slot], w_ref[columns(j), :])
            total = term if total is None else total + term
        return total

    def remote(source, target, slot, device):
        return pltpu.make_async_remote_copy(
            src_ref=source, dst_ref=target, send_sem=sems.at[0, slot], recv_sem=sems.at[1, slot],
            device_id=device, device_id_type=MESH,
        )

    core_copies, first_copies, next_copies = [], [], []
    for step, (piece, partner_half) in enumerate(steps):
        for copy in loads[step]:
            copy.wait()
        if step + 1 < len(steps):
            loads[step + 1] = load(step + 1)
            for copy in loads[step + 1]:
                copy.start()
        if partner_half:

            @pl.loop(0, chunks)
            def _(j, step=step, piece=piece):
                core_out[piece, :, columns(j)] = partial(step % 2, j).astype(BF16)

            core_copies.append(remote(core_out.at[piece], core_in.at[piece], piece, over_core))
            core_copies[-1].start()
            continue
        core_copies[piece].wait_recv()

        @pl.loop(0, chunks)
        def _(j, step=step, piece=piece):
            total = partial(step % 2, j) + core_in[piece, :, columns(j)].astype(F32)
            core_in[piece, :, columns(j)] = total.astype(BF16)

        if piece < 4:
            first_copies.append(
                remote(core_in.at[piece], first_in.at[piece], 8 + piece, over_x if piece % 2 == 0 else over_row)
            )
            first_copies[-1].start()
    work(0)
    for part in range(2):
        first_copies[part].wait_recv()

        @pl.loop(0, chunks)
        def _(j, part=part):
            total = core_in[4 + part, :, columns(j)].astype(F32) + first_in[part, :, columns(j)].astype(F32)
            core_in[4 + part, :, columns(j)] = total.astype(BF16)

        next_copies.append(remote(core_in.at[4 + part], next_in.at[part], 12 + part, over_row if part == 0 else over_x))
        next_copies[-1].start()
    work(1)
    for part in range(2):
        first_copies[2 + part].wait_recv()
        next_copies[part].wait_recv()

        @pl.loop(0, chunks)
        def _(j, part=part):
            total = core_in[6 + part, :, columns(j)].astype(F32) + first_in[2 + part, :, columns(j)].astype(F32)
            out_ref[pl.ds(part * half, half), columns(j)] = total + next_in[part, :, columns(j)].astype(F32)

    for copy in core_copies + first_copies + next_copies:
        copy.wait_send()


def plane_scatter(parts, weights, collective_id, jobs=()):
    count = parts[0].shape[0]
    width = weights[0].shape[0]
    rows = count // 8
    half = rows // 2
    vmem, hbm = pl.BlockSpec(memory_space=pltpu.VMEM), pl.BlockSpec(memory_space=pl.ANY)
    lefts, rights = [left for left, _ in jobs], [right for _, right in jobs]
    return pl.pallas_call(
        functools.partial(scatter_kernel, rows, len(parts), len(jobs)),
        in_specs=[hbm] * len(parts) + [vmem] * len(parts) + [hbm] * (2 * len(jobs)),
        out_specs=[vmem] + [hbm] * len(jobs),
        out_shape=[jax.ShapeDtypeStruct((rows, width), F32)]
        + [jax.ShapeDtypeStruct((left.shape[1], right.shape[1]), BF16) for left, right in jobs],
        scratch_shapes=[
            pltpu.VMEM((8, half, width), BF16),
            pltpu.VMEM((8, half, width), BF16),
            pltpu.VMEM((4, half, width), BF16),
            pltpu.VMEM((2, half, width), BF16),
            pltpu.SemaphoreType.DMA((2, 14)),
        ]
        + [pltpu.VMEM((2, half, a.shape[1]), BF16) for a in parts]
        + [pltpu.SemaphoreType.DMA((2, len(parts)))]
        + (product_buffers(rights[0].shape[1]) if jobs else []),
        compiler_params=pltpu.CompilerParams(
            collective_id=collective_id, has_side_effects=True, vmem_limit_bytes=(58 if jobs else 52) << 20
        ),
        cost_estimate=small_cost(),
        name="plane_scatter",
    )(*parts, *weights, *lefts, *rights)


def is_plane():
    return lax.axis_size("ctx") == 4 and lax.axis_size("tensor") == 2


def gather_rows(rows):
    return lax.all_gather(rows, GROUP, axis=0, tiled=True)


def scatter_rows(rows):
    return lax.psum_scatter(rows.astype(BF16), GROUP, scatter_dimension=0, tiled=True).astype(F32)


def gather_now(rows):
    return plane_gather(rows) if is_plane() else gather_rows(rows)


def gather_with_product(rows, left, right):
    if is_plane():
        return plane_gather(rows, left, right)
    return gather_rows(rows), dot_tn(left, right).astype(BF16)


def product_scatter(parts, weights, collective_id, jobs=()):
    if is_plane():
        return plane_scatter(parts, weights, collective_id, jobs)
    rows = scatter_rows(dot_t(jnp.concatenate(parts, axis=1), jnp.concatenate(weights, axis=1)))
    return [rows] + [dot_tn(left, right).astype(BF16) for left, right in jobs]


def gather_weight(own):
    return lax.all_gather(own, "fsdp", axis=0, tiled=True)


def scatter_weight(grad):
    return lax.psum_scatter(grad.astype(BF16), "fsdp", scatter_dimension=0, tiled=True)


def swap_columns(part, count):
    size = lax.axis_size("ctx")
    rows, columns = part.shape[0] // size, part.shape[1] // count
    got = lax.all_to_all(part.reshape(size, rows, count * columns), "ctx", split_axis=0, concat_axis=0)
    return [
        jnp.concatenate([got[j, :, c * columns : (c + 1) * columns] for j in range(size)], axis=1).astype(F32)
        for c in range(count)
    ]


def normalize(rows):
    norm_inv = lax.rsqrt(jnp.mean(rows * rows, axis=1, keepdims=True) + EPSILON)
    return (rows * norm_inv, norm_inv)


def norm_backward(grad_rows, scaled, norm_inv, gain):
    weighted = grad_rows * gain[None, :]
    inner = jnp.mean(weighted * scaled, axis=1, keepdims=True)
    return norm_inv * (weighted - scaled * inner)


def body(
    tokens_in,
    attn_gain,
    query_weight,
    key_weight,
    value_weight,
    output_weight,
    mlp_gain,
    gate_weight,
    up_weight,
    down_weight,
    seg_lengths,
    leaf_parent,
    cotangent,
):
    ctx = lax.axis_index("ctx")
    parts = lax.axis_size("ctx")
    tree_len = tokens_in.shape[0] * parts * lax.axis_size("tensor")
    width = query_weight.shape[1] // parts
    units = gate_weight.shape[1] // parts

    def mine(weight, columns):
        return lax.dynamic_slice_in_dim(weight, ctx * columns, columns, 1)

    x_rows = tokens_in.astype(F32)
    attn_scaled, attn_inv = normalize(x_rows)
    w_attn = gather_weight(
        jnp.concatenate([mine(w, width) for w in (query_weight, key_weight, value_weight, output_weight)], axis=1)
    )
    cot_all = gather_rows(cotangent)
    w_gate = gather_weight(mine(gate_weight, units))
    w_up = gather_weight(mine(up_weight, units))
    w_down = gather_weight(mine(down_weight, units))
    attn_in = gather_now((attn_scaled * attn_gain[None, :]).astype(BF16))
    w_qkv, w_out = w_attn[:, : 3 * width], w_attn[:, 3 * width :]

    attn_in, lengths_row, parent_row = lax.optimization_barrier((attn_in, seg_lengths[0], leaf_parent[0]))
    segment, parent, depth = tree_tables(lengths_row, parent_row, tree_len)
    cosine, sine = rope_tables(depth, min(2 * HEAD_DIM, width))
    seg_keys = segment[None, :]
    seg_queries = jnp.stack([segment, parent], axis=1)

    qkv = jnp.dot(attn_in, w_qkv, preferred_element_type=F32)
    attn_out, lse, query_rows, key_rows, value_rows = attention_forward(
        qkv, cosine, sine, seg_keys, seg_queries, width
    )
    mid_rows = x_rows + product_scatter([attn_out], [w_out], 1)[0]
    mlp_scaled, mlp_inv = normalize(mid_rows)
    mlp_own, cot_all = lax.optimization_barrier(((mlp_scaled * mlp_gain[None, :]).astype(BF16), cot_all))
    mlp_in = gather_now(mlp_own)

    gate = jnp.dot(mlp_in, w_gate, preferred_element_type=F32)
    up_proj = jnp.dot(mlp_in, w_up, preferred_element_type=F32)
    sigmoid_gate = jax.nn.sigmoid(gate)
    hidden = (gate * sigmoid_gate * up_proj).astype(BF16)
    down_rows, cot_all = lax.optimization_barrier((dot_t(hidden, w_down).astype(BF16), cot_all))
    down_rows = scatter_rows(down_rows)
    hidden_grad = jnp.dot(cot_all, w_down, preferred_element_type=F32)
    gate_rows_grad = (
        hidden_grad * up_proj * sigmoid_gate * (1.0 + gate * (1.0 - sigmoid_gate))
    ).astype(BF16)
    up_rows_grad = (hidden_grad * gate * sigmoid_gate).astype(BF16)

    mlp_in_grad, down_part, up_part = product_scatter(
        [gate_rows_grad, up_rows_grad], [w_gate, w_up], 3, [(cot_all, hidden), (mlp_in, up_rows_grad)]
    )
    down_grad = scatter_weight(down_part)
    up_grad = scatter_weight(up_part)
    mid_grad = cotangent.astype(F32) + norm_backward(mlp_in_grad, mlp_scaled, mlp_inv, mlp_gain)
    mid_low, down_rows = lax.optimization_barrier((mid_grad.astype(BF16), down_rows))
    block_out = (mid_rows + down_rows).astype(BF16)
    mid_all, gate_part = gather_with_product(mid_low, mlp_in, gate_rows_grad)
    gate_grad = scatter_weight(gate_part)

    out_heads_grad = jnp.dot(mid_all, w_out, preferred_element_type=F32).astype(BF16)
    output_grad = dot_tn(mid_all, attn_out).astype(BF16)
    pre_grads = attention_backward(
        query_rows, key_rows, value_rows, attn_out, out_heads_grad, lse, cosine, sine, seg_keys, seg_queries
    )
    pre_grads, gate_grad, up_grad, down_grad = lax.optimization_barrier((pre_grads, gate_grad, up_grad, down_grad))
    attn_part = jnp.concatenate([dot_tn(attn_in, grad).astype(BF16) for grad in pre_grads] + [output_grad], axis=1)
    attn_grad = scatter_weight(attn_part)
    pre_grads, attn_part = lax.optimization_barrier((pre_grads, attn_part))
    (attn_in_grad,) = product_scatter(pre_grads, [w_attn[:, j * width : (j + 1) * width] for j in range(3)], 2)
    attn_in_grad, attn_grad = lax.optimization_barrier((attn_in_grad, attn_grad))
    gate_out, up_out, down_out = swap_columns(jnp.concatenate([gate_grad, up_grad, down_grad], axis=1), 3)
    query_out, key_out, value_out, output_out = swap_columns(attn_grad, 4)

    def gain_part(pairs, gain):
        held = query_out.shape[0]
        total = sum(
            jnp.sum(lax.dynamic_slice_in_dim(weight, ctx * held, held, 0).astype(F32) * grad, axis=1)
            for weight, grad in pairs
        )
        first = (lax.axis_index("fsdp") * parts + ctx) * held
        return total / lax.dynamic_slice_in_dim(gain, first, held, 0)

    sums = jnp.stack(
        [
            gain_part([(query_weight, query_out), (key_weight, key_out), (value_weight, value_out)], attn_gain),
            gain_part([(gate_weight, gate_out), (up_weight, up_out)], mlp_gain),
        ]
    )
    row, others = lax.axis_index("tensor"), lax.axis_size("tensor")
    kept = sums.shape[1] // others
    if others == 2:
        got = lax.ppermute(lax.dynamic_slice_in_dim(sums, (1 - row) * kept, kept, 1), "tensor", [(0, 1), (1, 0)])
        gain_grads = lax.dynamic_slice_in_dim(sums, row * kept, kept, 1) + got
    else:
        gain_grads = lax.dynamic_slice_in_dim(lax.psum(sums, "tensor"), row * kept, kept, 1)

    attn_back = norm_backward(attn_in_grad, attn_scaled, attn_inv, attn_gain)
    input_grad = (mid_grad + attn_back).astype(BF16)
    return (
        block_out,
        input_grad,
        gain_grads[0],
        query_out,
        key_out,
        value_out,
        output_out,
        gain_grads[1],
        gate_out,
        up_out,
        down_out,
    )


def solution(mesh):
    rows = P(("fsdp", "ctx", "tensor"), None)
    weight = P("fsdp", "tensor")
    gain = P(("fsdp", "ctx", "tensor"))
    grad = P(("fsdp", "ctx"), "tensor")
    in_specs = (
        rows, P(), weight, weight, weight, weight, P(), weight, weight, weight, P("fsdp", None), P("fsdp", None), rows,
    )
    out_specs = (rows, rows, gain, grad, grad, grad, grad, gain, grad, grad, grad)
    return jax.shard_map(body, mesh=mesh, in_specs=in_specs, out_specs=out_specs, check_vma=False)
```

```python
import functools

import jax
import jax.numpy as jnp
from jax import lax
from jax.experimental import pallas as pl
from jax.experimental.pallas import tpu as pltpu
from jax.sharding import PartitionSpec as P

HEAD_DIM = 64
TRUNK = 2176
MOST_SEG = 128
ROPE_BASE = 130000.0
EPSILON = 1e-05
NEG_LARGE = -1e30
SCALE = HEAD_DIM ** (-0.5)

BQ = 512
BK = 512
GROUP = ("ctx", "tensor")

F32 = jnp.float32
BF16 = jnp.bfloat16


def pick_table(onehot, table):
    return jnp.sum(jnp.where(onehot, table[None, :], 0), axis=1)


def tree_tables(lengths_row, parent_row, tree_len):
    branches = lengths_row.shape[0] - parent_row.shape[0]
    ends = TRUNK + jnp.cumsum(lengths_row)
    starts = ends - lengths_row
    matches = parent_row[:, None] - 1 == jnp.arange(branches, dtype=jnp.int32)[None, :]
    parent_len = jnp.sum(jnp.where(matches, lengths_row[None, :branches], 0), axis=1)
    zero_one = jnp.zeros((1,), jnp.int32)
    seg_start = jnp.concatenate([zero_one, starts])
    seg_base = jnp.concatenate(
        [zero_one, jnp.full((branches,), TRUNK, jnp.int32), TRUNK + parent_len]
    )
    seg_parent = jnp.concatenate([zero_one, jnp.zeros((branches,), jnp.int32), parent_row])
    positions = jnp.arange(tree_len, dtype=jnp.int32)
    above = jnp.sum((ends[None, :] <= positions[:, None]).astype(jnp.int32), axis=1)
    segment = (positions >= TRUNK).astype(jnp.int32) + above
    onehot = segment[:, None] == jnp.arange(seg_start.shape[0], dtype=jnp.int32)[None, :]
    depth = positions - pick_table(onehot, seg_start) + pick_table(onehot, seg_base)
    parent = pick_table(onehot, seg_parent)
    return (segment, parent, depth)


def rope_tables(depth, width):
    half = HEAD_DIM // 2
    lane = jnp.arange(width, dtype=jnp.int32)
    freqs = jnp.power(ROPE_BASE, -(2.0 * (lane % half).astype(F32)) / HEAD_DIM)
    angles = depth.astype(F32)[:, None] * freqs[None, :]
    sign = jnp.where(lane % HEAD_DIM < half, -1.0, 1.0)
    return jnp.cos(angles), jnp.sin(angles) * sign[None, :]


MESH = pl.DeviceIdType.MESH


def plane_place():
    ctx, row = lax.axis_index("ctx"), lax.axis_index("tensor")
    x, core = ctx // 2, ctx % 2
    return x, core, row


def plane_neighbours(x, core, row):
    over_x = {"ctx": (1 - x) * 2 + core}
    over_core = {"ctx": x * 2 + 1 - core}
    over_row = {"tensor": 1 - row}
    return over_x, over_row, over_core


def enter_plane(neighbours):
    barrier = pltpu.get_barrier_semaphore()
    for device in neighbours:
        pl.semaphore_signal(barrier, inc=1, device_id=device, device_id_type=MESH)
    pl.semaphore_wait(barrier, 3)


PIECES = ((1, 1, 0), (1, 1, 1), (1, 0, 0), (0, 1, 1), (0, 1, 0), (1, 0, 1), (0, 0, 0), (0, 0, 1))
COLS = 512


class PlaneGather:
    def __init__(self, own_ref, all_ref, local_sem, send_sem, recv_sem):
        self.own_ref, self.all_ref, self.sems = own_ref, all_ref, (local_sem, send_sem, recv_sem)
        self.x, self.core, self.row = plane_place()
        self.devices = plane_neighbours(self.x, self.core, self.row)
        self.rows = own_ref.shape[0]

    def place(self, far_x, far_row, part):
        bx = self.x + far_x - 2 * far_x * self.x
        by = self.row + far_row - 2 * far_row * self.row
        half = self.rows // 2
        return pl.ds(pl.multiple_of(((bx * 2 + self.core) * 2 + by) * self.rows + part * half, half), half)

    def copy(self, slot):
        far_x, far_row, part, device = (
            (0, 0, 0, 1), (0, 0, 1, 1), (1, 0, 1, 1), (0, 0, 1, 0), (0, 0, 0, 0), (0, 1, 0, 0), (0, 0, 0, 2),
            (0, 0, 1, 2), (0, 1, 0, 2), (1, 0, 1, 2), (0, 1, 1, 2), (1, 0, 0, 2), (1, 1, 0, 2), (1, 1, 1, 2),
        )[slot]
        half = self.rows // 2
        target = self.place(far_x, far_row, part)
        own = far_x == 0 and far_row == 0
        source = self.own_ref.at[pl.ds(part * half, half)] if own else self.all_ref.at[target]
        return pltpu.make_async_remote_copy(
            src_ref=source, dst_ref=self.all_ref.at[target], send_sem=self.sems[1].at[slot],
            recv_sem=self.sems[2].at[slot], device_id=self.devices[device], device_id_type=MESH,
        )

    def local(self, part):
        half = self.rows // 2
        return pltpu.make_async_copy(
            self.own_ref.at[pl.ds(part * half, half)], self.all_ref.at[self.place(0, 0, part)], self.sems[0].at[part]
        )

    def start(self):
        enter_plane(self.devices)
        for slot in (0, 3, 1, 4, 6, 7):
            self.copy(slot).start()
        for part in range(2):
            self.local(part).start()

    def forward(self, got, slots):
        self.copy(got).wait_recv()
        for slot in slots:
            self.copy(slot).start()

    def first(self):
        self.forward(0, (5, 8))
        self.forward(3, (2, 9))

    def second(self):
        self.forward(1, (10,))
        self.forward(4, (11,))

    def finish(self):
        self.forward(5, (12,))
        self.forward(2, (13,))
        for slot in range(6, 14):
            self.copy(slot).wait_recv()
        for slot in range(14):
            self.copy(slot).wait_send()
        for part in range(2):
            self.local(part).wait()


def gather_sems():
    return [pltpu.SemaphoreType.DMA((2,)), pltpu.SemaphoreType.DMA((14,)), pltpu.SemaphoreType.DMA((14,))]


class PlaneScatter:
    def __init__(self, part_ref, out_ref, core_in, first_in, next_in, own, total, sems, own_sems):
        self.part_ref, self.out_ref, self.core_in, self.first_in, self.next_in = part_ref, out_ref, core_in, first_in, next_in
        self.own, self.total, self.sems, self.own_sems = own, total, sems, own_sems
        self.x, self.core, self.row = plane_place()
        self.devices = plane_neighbours(self.x, self.core, self.row)
        self.rows = part_ref.shape[0] // 8

    def place(self, piece, on_core):
        far_x, far_row, part = PIECES[piece]
        bx = self.x + far_x - 2 * far_x * self.x
        by = self.row + far_row - 2 * far_row * self.row
        half = self.rows // 2
        return pl.ds(pl.multiple_of(((bx * 2 + on_core) * 2 + by) * self.rows + part * half, half), half)

    def copy(self, slot):
        if slot < 8:
            source, target, device = self.part_ref.at[self.place(slot, 1 - self.core)], self.core_in.at[slot], 2
        elif slot < 12:
            source, target, device = self.core_in.at[slot - 8], self.first_in.at[slot - 8], slot % 2
        else:
            source, target, device = self.core_in.at[slot - 8], self.next_in.at[slot - 12], 1 - slot % 2
        return pltpu.make_async_remote_copy(
            src_ref=source, dst_ref=target, send_sem=self.sems.at[0, slot], recv_sem=self.sems.at[1, slot],
            device_id=self.devices[device], device_id_type=MESH,
        )

    def load(self, piece):
        return pltpu.make_async_copy(
            self.part_ref.at[self.place(piece, self.core)], self.own.at[piece % 4], self.own_sems.at[piece % 4]
        )

    def add(self, target, where, *others):
        @pl.loop(0, target.shape[-1] // COLS)
        def _(j):
            columns = pl.ds(pl.multiple_of(j * COLS, COLS), COLS)
            total = sum(ref[slot, :, columns].astype(F32) for ref, slot in others)
            target[where, :, columns] = total.astype(target.dtype)

    def start(self):
        enter_plane(self.devices)
        for slot in range(8):
            self.copy(slot).start()
        for piece in range(4):
            self.load(piece).start()

    def first(self):
        for piece in range(4):
            self.load(piece).wait()
            self.copy(piece).wait_recv()
            self.add(self.core_in, piece, (self.own, piece), (self.core_in, piece))
            self.copy(8 + piece).start()
        for piece in range(4, 8):
            self.load(piece).start()

    def second(self):
        for piece in range(4, 8):
            self.load(piece).wait()
            self.copy(piece).wait_recv()
            self.add(self.core_in, piece, (self.own, piece - 4), (self.core_in, piece))

    def third(self):
        for part in range(2):
            self.copy(8 + part).wait_recv()
            self.add(self.core_in, 4 + part, (self.core_in, 4 + part), (self.first_in, part))
            self.copy(12 + part).start()

    def finish(self):
        half = self.rows // 2
        for part in range(2):
            self.copy(10 + part).wait_recv()
            self.copy(12 + part).wait_recv()
            self.add(self.total, part, (self.core_in, 6 + part), (self.first_in, 2 + part), (self.next_in, part))
        stores = [
            pltpu.make_async_copy(
                self.total.at[part], self.out_ref.at[pl.ds(part * half, half)], self.own_sems.at[part]
            )
            for part in range(2)
        ]
        for store in stores:
            store.start()
        for slot in range(14):
            self.copy(slot).wait_send()
        for store in stores:
            store.wait()


def scatter_scratch(rows, width):
    half = rows // 2
    return [
        pltpu.VMEM((8, half, width), BF16),
        pltpu.VMEM((4, half, width), BF16),
        pltpu.VMEM((2, half, width), BF16),
        pltpu.VMEM((4, half, width), BF16),
        pltpu.VMEM((2, half, width), BF16),
        pltpu.SemaphoreType.DMA((2, 14)),
        pltpu.SemaphoreType.DMA((4,)),
    ]


def at_step(step, total, places):
    for place, phase in places:

        @pl.when(step == place)
        def _(phase=phase):
            phase()


def partner(x):
    half = HEAD_DIM // 2
    width = x.shape[1]
    if width == HEAD_DIM:
        return jnp.concatenate([x[:, half:], x[:, :half]], axis=1)
    lane = lax.broadcasted_iota(jnp.int32, x.shape, 1)
    ahead = pltpu.roll(x, width - half, 1)
    behind = pltpu.roll(x, half, 1)
    return jnp.where(lane % HEAD_DIM < half, ahead, behind)


def head_mask(shape, head):
    lane = lax.broadcasted_iota(jnp.int32, shape, 1)
    return lane // HEAD_DIM == head


def dot_t(a, b):
    return lax.dot_general(a, b, (((1,), (1,)), ((), ())), preferred_element_type=F32)


def dot_n(a, b):
    return lax.dot_general(a, b, (((1,), (0,)), ((), ())), preferred_element_type=F32)


def dot_tn(a, b):
    return lax.dot_general(a, b, (((0,), (0,)), ((), ())), preferred_element_type=F32)


def key_plan(i, tile):
    base = TRUNK // BK * BK
    branch_end = TRUNK + 4 * MOST_SEG
    first_tree = base // BQ
    mixed_end = -(-(branch_end + MOST_SEG) // BQ)
    chunks = jnp.minimum(i * BQ, base) // BK

    @pl.when(i < first_tree)
    def _():
        @pl.loop(0, chunks)
        def _(j):
            start = pl.multiple_of(j * BK, BK)
            tile(start, BK, 0, start)

    @pl.when(i >= first_tree)
    def _():
        tile(0, base, 0, 0)

    @pl.when(i < first_tree)
    def _():
        start = pl.multiple_of(chunks * BK, BK)
        tile(start, BK, 1, start)

    for block in range(first_tree, mixed_end):

        @pl.when(i == block)
        def _(block=block):
            tile(base, (block + 1) * BQ - base, 2, base)

    @pl.when(i >= mixed_end)
    def _():
        tile(base, branch_end - base, 3, base)
        tile(pl.multiple_of(i * BQ - MOST_SEG, MOST_SEG), BQ + MOST_SEG, 4, branch_end)


def most_keys():
    return TRUNK + 4 * MOST_SEG + BQ + MOST_SEG


def seen_mask(kind, q_at, k_at, seg_q, par_q, seg_k):
    if kind == 3:
        return (seg_k == 0) | (seg_k == par_q)
    causal = k_at <= q_at
    if kind == 1:
        return causal
    if kind == 4:
        return causal & (seg_k == seg_q)
    return causal & ((seg_k == 0) | (seg_k == seg_q) | (seg_k == par_q))


def fwd_kernel(heads, hosts, *refs):
    if not hosts:
        return fwd_work(heads, *refs)
    gather = PlaneGather(refs[7], refs[13], *refs[-3:])
    step, total = pl.program_id(0) * pl.num_programs(1) + pl.program_id(1), 16
    at_step(step, total, ((0, gather.start), (6, gather.first), (12, gather.second)))
    fwd_work(heads, *refs[:7], *refs[8:13], *refs[14:-3])
    at_step(step, total, ((total - 1, gather.finish),))


def fwd_work(
    heads, q_ref, k_ref, v_ref, cos_ref, sin_ref, segk_ref, segq_ref,
    o_ref, lse_ref, qr_ref, kr_ref, vr_ref, kt_ref, va_ref, s_ref, m_ref, acc_ref,
):
    i = pl.program_id(1)
    wide = 2 * HEAD_DIM

    @pl.when(i == 0)
    def _():
        @pl.loop(0, k_ref.shape[0] // BK)
        def _(j):
            rows = pl.ds(pl.multiple_of(j * BK, BK), BK)
            k = k_ref[rows, :]
            k = (k * cos_ref[rows, :] + partner(k) * sin_ref[rows, :]).astype(BF16)
            kr_ref[rows, :] = k
            kt_ref[:, rows] = jnp.transpose(k)
            v = v_ref[rows, :].astype(BF16)
            vr_ref[rows, :] = v
            if heads == 1:
                va_ref[0, rows, :] = jnp.concatenate([v, jnp.ones_like(v)], axis=1)
            else:
                for h in range(heads):
                    va_ref[h, rows, :] = jnp.where(head_mask(v.shape, h), v, jnp.ones_like(v))

    rows = pl.ds(pl.multiple_of(i * BQ, BQ), BQ)
    q = q_ref[...]
    q = (q * cos_ref[rows, :] + partner(q) * sin_ref[rows, :]).astype(BF16)
    qr_ref[...] = q
    q = q * jnp.asarray(SCALE, BF16)
    q_heads = [jnp.where(head_mask(q.shape, h), q, jnp.zeros_like(q)) for h in range(heads)]
    m_ref[...] = jnp.full_like(m_ref, NEG_LARGE)
    acc_ref[...] = jnp.zeros_like(acc_ref)

    def score_tile(start, width, kind, place):
        keys = pl.ds(start, width)
        k = kt_ref[:, keys]
        seen = None
        if kind != 0:
            shape = (BQ, width)
            seen = seen_mask(
                kind,
                lax.broadcasted_iota(jnp.int32, shape, 0) + i * BQ,
                lax.broadcasted_iota(jnp.int32, shape, 1) + start,
                segq_ref[:, 0:1], segq_ref[:, 1:2], segk_ref[:, keys],
            )
        for h in range(heads):
            s = dot_n(q_heads[h], k)
            if seen is not None:
                s = jnp.where(seen, s, NEG_LARGE)
            s_ref[h, :, pl.ds(place, width)] = s
            largest = m_ref[h]
            for c in range(width // 128):
                largest = jnp.maximum(largest, s[:, c * 128 : (c + 1) * 128])
            m_ref[h] = largest

    key_plan(i, score_tile)
    for h in range(heads):
        m_ref[h] = jnp.broadcast_to(jnp.max(m_ref[h], axis=1, keepdims=True), (BQ, 128))

    def value_tile(start, width, kind, place):
        keys = pl.ds(start, width)
        for h in range(heads):
            m = m_ref[h]
            parts = [
                jnp.exp(s_ref[h, :, pl.ds(place + c * 128, 128)] - m).astype(BF16) for c in range(width // 128)
            ]
            acc_ref[h] += dot_n(jnp.concatenate(parts, axis=1), va_ref[h, keys, :])

    key_plan(i, value_tile)
    out, lse = None, None
    for h in range(heads):
        acc = acc_ref[h]
        part = acc / pltpu.roll(acc, HEAD_DIM, 1)
        stat = m_ref[h] + jnp.log(jnp.broadcast_to(acc[:, (1 - h) * HEAD_DIM : (1 - h) * HEAD_DIM + 1], (BQ, wide)))
        mask = head_mask((BQ, wide), h)
        out = part if h == 0 else jnp.where(mask, part, out)
        lse = stat if h == 0 else jnp.where(mask, stat, lse)
    o_ref[...] = out[:, : heads * HEAD_DIM].astype(BF16)
    turned = jnp.transpose(lse)
    for h in range(heads):
        lse_ref[0, h : h + 1, :] = turned[h * HEAD_DIM : h * HEAD_DIM + 1, :]


def bwd_kernel(heads, hosts, *refs):
    if not hosts:
        return bwd_work(heads, *refs)
    scatter = PlaneScatter(refs[10], refs[14], *refs[-7:])
    step, total = pl.program_id(0) * pl.num_programs(1) + pl.program_id(1), 16
    at_step(
        step, total, ((0, scatter.start), (3, scatter.first), (5, scatter.second), (7, scatter.third))
    )
    bwd_work(heads, *refs[:10], *refs[11:14], *refs[15:-7])
    at_step(step, total, ((total - 1, scatter.finish),))


def bwd_work(
    heads, q_ref, k_ref, v_ref, o_ref, do_ref, lse_ref, cos_ref, sin_ref, segk_ref, segq_ref,
    dq_ref, dk_ref, dv_ref, dq_acc, dk_acc, dv_acc,
):
    i = pl.program_id(1)

    @pl.when(i == 0)
    def _():
        dk_acc[...] = jnp.zeros_like(dk_acc)
        dv_acc[...] = jnp.zeros_like(dv_acc)

    q = q_ref[...]
    scaled = q * jnp.asarray(SCALE, BF16)
    do = do_ref[...]
    product = jnp.transpose(do.astype(F32) * o_ref[...].astype(F32))
    zero = jnp.zeros_like(q)
    masks = [head_mask(q.shape, h) for h in range(heads)]
    q_heads = [jnp.where(m, scaled, zero) for m in masks]
    do_heads = [jnp.where(m, do, zero) for m in masks]
    deltas = [
        jnp.sum(product[h * HEAD_DIM : (h + 1) * HEAD_DIM, :], axis=0, keepdims=True) for h in range(heads)
    ]
    lses = [lse_ref[0, h : h + 1, :] for h in range(heads)]
    q_turned = [jnp.transpose(x) for x in q_heads]
    do_turned = [jnp.transpose(x) for x in do_heads]
    q_stack = jnp.concatenate(q_heads, axis=0)
    do_stack = jnp.concatenate(do_heads, axis=0)
    dq_acc[...] = jnp.zeros_like(dq_acc)

    def tile(start, width, kind, place):
        keys = pl.ds(start, width)
        k = k_ref[keys, :]
        v = v_ref[keys, :]
        seen = None
        if kind != 0:
            shape = (width, BQ)
            seen = seen_mask(
                kind,
                lax.broadcasted_iota(jnp.int32, shape, 1) + i * BQ,
                lax.broadcasted_iota(jnp.int32, shape, 0) + start,
                segq_ref[0:1, :], segq_ref[1:2, :], segk_ref[keys, :],
            )
        probs, grads, k_heads = [], [], []
        for h in range(heads):
            s = dot_n(k, q_turned[h])
            p = jnp.exp(s - lses[h])
            if seen is not None:
                p = jnp.where(seen, p, 0.0)
            dp = dot_n(v, do_turned[h])
            probs.append(p.astype(BF16))
            grads.append((p * (dp - deltas[h])).astype(BF16))
            k_heads.append(jnp.where(head_mask(k.shape, h), k, jnp.zeros_like(k)))
        grad_row = jnp.concatenate(grads, axis=1)
        dv_acc[keys, :] += dot_n(jnp.concatenate(probs, axis=1), do_stack)
        dk_acc[keys, :] += dot_n(grad_row, q_stack)
        dq_acc[...] += dot_tn(jnp.concatenate(grads, axis=0), jnp.concatenate(k_heads, axis=0))

    key_plan(i, tile)
    dq = dq_acc[...] * SCALE
    rows = pl.ds(pl.multiple_of(i * BQ, BQ), BQ)
    dq_ref[...] = (dq * cos_ref[rows, :] - partner(dq) * sin_ref[rows, :]).astype(BF16)

    @pl.when(i == pl.num_programs(1) - 1)
    def _():
        @pl.loop(0, dk_acc.shape[0] // BK)
        def _(j):
            rows = pl.ds(pl.multiple_of(j * BK, BK), BK)
            dk = dk_acc[rows, :]
            dk_ref[rows, :] = (dk * cos_ref[rows, :] - partner(dk) * sin_ref[rows, :]).astype(BF16)
            dv_ref[rows, :] = dv_acc[rows, :].astype(BF16)


def small_cost():
    return pl.CostEstimate(flops=1 << 20, bytes_accessed=1 << 20, transcendentals=0)


def attention_forward(qkv, cosine, sine, seg_keys, seg_queries, width, hosted=None):
    tree_len = qkv.shape[0]
    gw = min(2 * HEAD_DIM, width)
    groups, heads = width // gw, gw // HEAD_DIM
    row_block = pl.BlockSpec((BQ, gw), lambda g, i: (i, g))
    table = pl.BlockSpec((tree_len, gw), lambda g, i: (0, 0))
    full = pl.BlockSpec((tree_len, gw), lambda g, i: (0, g))
    act = jax.ShapeDtypeStruct((tree_len, width), BF16)
    if width % 128 == 0:
        queries, keys, values, step = qkv, qkv, qkv, groups
    else:
        queries, keys, values = jnp.split(qkv, 3, axis=1)
        step = 0
    hosts = hosted is not None
    hbm = pl.BlockSpec(memory_space=pl.ANY)
    return pl.pallas_call(
        functools.partial(fwd_kernel, heads, hosts),
        grid=(groups, tree_len // BQ),
        in_specs=[
            row_block,
            pl.BlockSpec((tree_len, gw), lambda g, i: (0, step + g)),
            pl.BlockSpec((tree_len, gw), lambda g, i: (0, 2 * step + g)),
            table,
            table,
            pl.BlockSpec((1, tree_len), lambda g, i: (0, 0)),
            pl.BlockSpec((BQ, 2), lambda g, i: (i, 0)),
        ]
        + [hbm] * hosts,
        out_specs=[row_block, pl.BlockSpec((1, heads, BQ), lambda g, i: (g, 0, i)), row_block, full, full] + [hbm] * hosts,
        out_shape=[act, jax.ShapeDtypeStruct((groups, heads, tree_len), F32), act, act, act]
        + ([jax.ShapeDtypeStruct((8 * hosted.shape[0], hosted.shape[1]), BF16)] if hosts else []),
        scratch_shapes=[
            pltpu.VMEM((gw, tree_len), BF16),
            pltpu.VMEM((heads, tree_len, 128), BF16),
            pltpu.VMEM((heads, BQ, most_keys()), F32),
            pltpu.VMEM((heads, BQ, 128), F32),
            pltpu.VMEM((heads, BQ, 128), F32),
        ]
        + (gather_sems() if hosts else []),
        compiler_params=pltpu.CompilerParams(
            vmem_limit_bytes=56 << 20, collective_id=6 if hosts else None, has_side_effects=hosts
        ),
        cost_estimate=small_cost(),
        name="tree_attention_forward",
    )(queries, keys, values, cosine, sine, seg_keys, seg_queries, *([hosted] if hosts else []))


def attention_backward(q, k, v, out, grad, lse, cosine, sine, seg_keys, seg_queries, hosted=None):
    tree_len, width = q.shape
    gw = min(2 * HEAD_DIM, width)
    groups, heads = width // gw, gw // HEAD_DIM
    row_block = pl.BlockSpec((BQ, gw), lambda g, i: (i, g))
    table = pl.BlockSpec((tree_len, gw), lambda g, i: (0, 0))
    full = pl.BlockSpec((tree_len, gw), lambda g, i: (0, g))
    act = jax.ShapeDtypeStruct((tree_len, width), BF16)
    hosts = hosted is not None
    hbm = pl.BlockSpec(memory_space=pl.ANY)
    return pl.pallas_call(
        functools.partial(bwd_kernel, heads, hosts),
        grid=(groups, tree_len // BQ),
        in_specs=[
            row_block, full, full, row_block, row_block,
            pl.BlockSpec((1, heads, BQ), lambda g, i: (g, 0, i)),
            table, table,
            pl.BlockSpec((tree_len, 1), lambda g, i: (0, 0)),
            pl.BlockSpec((2, BQ), lambda g, i: (0, i)),
        ]
        + [hbm] * hosts,
        out_specs=[row_block, full, full] + [hbm] * hosts,
        out_shape=[act, act, act]
        + ([jax.ShapeDtypeStruct((hosted.shape[0] // 8, hosted.shape[1]), BF16)] if hosts else []),
        scratch_shapes=[
            pltpu.VMEM((BQ, gw), F32),
            pltpu.VMEM((tree_len, gw), F32),
            pltpu.VMEM((tree_len, gw), F32),
        ]
        + (scatter_scratch(hosted.shape[0] // 8, hosted.shape[1]) if hosts else []),
        compiler_params=pltpu.CompilerParams(
            vmem_limit_bytes=60 << 20, collective_id=7 if hosts else None, has_side_effects=hosts
        ),
        cost_estimate=small_cost(),
        name="tree_attention_backward",
    )(q, k, v, out, grad, lse, cosine, sine, seg_keys.T, seg_queries.T, *([hosted] if hosts else []))


TOKENS_AT_ONCE = 2048
LEFT_AT_ONCE = 512
STEP = 512


def product_buffers(columns):
    return [
        pltpu.VMEM((2, TOKENS_AT_ONCE, LEFT_AT_ONCE), BF16),
        pltpu.VMEM((2 * TOKENS_AT_ONCE, columns), BF16),
        pltpu.VMEM((LEFT_AT_ONCE, columns), F32),
        pltpu.VMEM((LEFT_AT_ONCE, columns), BF16),
        pltpu.SemaphoreType.DMA((4,)),
    ]


def token_product(left_ref, right_ref, out_ref, left_buf, right_buf, total, out_buf, sems):
    tokens = left_ref.shape[0]
    parts, groups = tokens // TOKENS_AT_ONCE, left_ref.shape[1] // LEFT_AT_ONCE

    def load(step):
        group, part = step // parts, step % parts
        source = left_ref.at[
            pl.ds(part * TOKENS_AT_ONCE, TOKENS_AT_ONCE), pl.ds(group * LEFT_AT_ONCE, LEFT_AT_ONCE)
        ]
        return pltpu.make_async_copy(source, left_buf.at[step % 2], sems.at[step % 2])

    def store(group):
        return pltpu.make_async_copy(out_buf, out_ref.at[pl.ds(group * LEFT_AT_ONCE, LEFT_AT_ONCE)], sems.at[3])

    whole = pltpu.make_async_copy(right_ref, right_buf, sems.at[2])
    whole.start()
    load(0).start()
    whole.wait()
    for group in range(groups):
        for part in range(parts):
            step = group * parts + part
            load(step).wait()
            if step + 1 < groups * parts:
                load(step + 1).start()
            if part == 0:
                total[...] = jnp.zeros_like(total)

            @pl.loop(0, TOKENS_AT_ONCE // STEP)
            def _(j, step=step, part=part):
                left = left_buf[step % 2, pl.ds(pl.multiple_of(j * STEP, STEP), STEP), :]
                right = right_buf[pl.ds(pl.multiple_of(part * TOKENS_AT_ONCE + j * STEP, STEP), STEP), :]
                total[...] += dot_tn(left, right)

        if group > 0:
            store(group - 1).wait()
        out_buf[...] = total[...].astype(BF16)
        store(group).start()
        yield
    store(groups - 1).wait()


def finish(product):
    for _ in product:
        pass


def row_product(left_ref, right_ref, out_ref, left_buf, right_buf, out_buf, sems):
    groups = left_ref.shape[0] // LEFT_AT_ONCE

    def rows(group):
        return pl.ds(group * LEFT_AT_ONCE, LEFT_AT_ONCE)

    def load(group):
        return pltpu.make_async_copy(left_ref.at[rows(group)], left_buf.at[group % 2], sems.at[group % 2])

    def store(group):
        return pltpu.make_async_copy(out_buf.at[group % 2], out_ref.at[rows(group)], sems.at[3 + group % 2])

    whole = pltpu.make_async_copy(right_ref, right_buf, sems.at[2])
    whole.start()
    load(0).start()
    whole.wait()
    for group in range(groups):
        load(group).wait()
        if group + 1 < groups:
            load(group + 1).start()
        if group > 1:
            store(group - 2).wait()

        @pl.loop(0, right_ref.shape[1] // STEP)
        def _(j, group=group):
            columns = pl.ds(pl.multiple_of(j * STEP, STEP), STEP)
            out_buf[group % 2, :, columns] = dot_n(left_buf[group % 2], right_buf[:, columns]).astype(BF16)

        store(group).start()
        yield
    for group in range(max(0, groups - 2), groups):
        store(group).wait()


def row_product_buffers(depth, columns):
    return [
        pltpu.VMEM((2, LEFT_AT_ONCE, depth), BF16),
        pltpu.VMEM((depth, columns), BF16),
        pltpu.VMEM((2, LEFT_AT_ONCE, columns), BF16),
        pltpu.SemaphoreType.DMA((5,)),
    ]


def gather_kernel(kind, jobs, *refs):
    own_ref, lefts, rights = refs[0], refs[1 : 1 + jobs], refs[1 + jobs : 1 + 2 * jobs]
    all_ref, outs, refs = refs[1 + 2 * jobs], refs[2 + 2 * jobs : 2 + 3 * jobs], refs[2 + 3 * jobs :]
    gather, buffers = PlaneGather(own_ref, all_ref, *refs[:3]), refs[3:]

    def work():
        for job in range(jobs):
            yield from kind(lefts[job], rights[job], outs[job], *buffers)

    work = work()

    def some(count):
        for _ in range(count):
            next(work, None)

    gather.start()
    some(4)
    gather.first()
    some(4)
    gather.second()
    finish(work)
    gather.finish()


def plane_gather(rows, kind=None, jobs=(), buffers=(), shape=()):
    count, width = rows.shape
    hbm = pl.BlockSpec(memory_space=pl.ANY)
    outputs = [jax.ShapeDtypeStruct((8 * count, width), rows.dtype)] + [jax.ShapeDtypeStruct(shape, BF16)] * len(jobs)
    return pl.pallas_call(
        functools.partial(gather_kernel, kind, len(jobs)),
        in_specs=[hbm] * (1 + 2 * len(jobs)),
        out_specs=[hbm] * len(outputs),
        out_shape=outputs,
        scratch_shapes=gather_sems() + list(buffers),
        compiler_params=pltpu.CompilerParams(
            collective_id=0 if kind is None else 4 if kind is token_product else 5,
            has_side_effects=True,
            vmem_limit_bytes=None if kind is None else 48 << 20,
        ),
        cost_estimate=small_cost(),
        name="plane_gather",
    )(rows, *[left for left, _ in jobs], *[right for _, right in jobs])


def scatter_kernel(rows, parts, jobs, *refs):
    def take(count):
        nonlocal refs
        taken, refs = refs[:count], refs[count:]
        return taken

    a_refs, w_refs, lefts, rights = take(parts), take(parts), take(jobs), take(jobs)
    (out_ref,), products = take(1), take(jobs)
    core_out, core_in, first_in, next_in, sems = take(5)
    a_bufs, (a_sems,), buffers = take(parts), take(1), refs

    def work(job):
        if job < jobs:
            finish(token_product(lefts[job], rights[job], products[job], *buffers))

    x, core, row = plane_place()
    over_x, over_row, over_core = plane_neighbours(x, core, row)
    half = rows // 2
    width = out_ref.shape[1]
    chunks = width // COLS

    def place(piece, on_core):
        far_x, far_row, part = PIECES[piece]
        bx = x + far_x - 2 * far_x * x
        by = row + far_row - 2 * far_row * row
        return pl.ds(pl.multiple_of(((bx * 2 + on_core) * 2 + by) * rows + part * half, half), half)

    def columns(j):
        return pl.ds(pl.multiple_of(j * COLS, COLS), COLS)

    steps = [(0, True)]
    for piece in range(8):
        steps += [(piece + 1, True)] * (piece < 7) + [(piece, False)]

    def load(step):
        piece, partner_half = steps[step]
        taken = place(piece, 1 - core if partner_half else core)
        return [
            pltpu.make_async_copy(a_ref.at[taken], a_buf.at[step % 2], a_sems.at[step % 2, p])
            for p, (a_ref, a_buf) in enumerate(zip(a_refs, a_bufs))
        ]

    loads = {0: load(0)}
    for copy in loads[0]:
        copy.start()
    enter_plane((over_x, over_row, over_core))

    def partial(slot, j):
        total = None
        for a_buf, w_ref in zip(a_bufs, w_refs):
            term = dot_t(a_buf[slot], w_ref[columns(j), :])
            total = term if total is None else total + term
        return total

    def remote(source, target, slot, device):
        return pltpu.make_async_remote_copy(
            src_ref=source, dst_ref=target, send_sem=sems.at[0, slot], recv_sem=sems.at[1, slot],
            device_id=device, device_id_type=MESH,
        )

    core_copies, first_copies, next_copies = [], [], []
    for step, (piece, partner_half) in enumerate(steps):
        for copy in loads[step]:
            copy.wait()
        if step + 1 < len(steps):
            loads[step + 1] = load(step + 1)
            for copy in loads[step + 1]:
                copy.start()
        if partner_half:

            @pl.loop(0, chunks)
            def _(j, step=step, piece=piece):
                core_out[piece, :, columns(j)] = partial(step % 2, j).astype(BF16)

            core_copies.append(remote(core_out.at[piece], core_in.at[piece], piece, over_core))
            core_copies[-1].start()
            continue
        core_copies[piece].wait_recv()

        @pl.loop(0, chunks)
        def _(j, step=step, piece=piece):
            total = partial(step % 2, j) + core_in[piece, :, columns(j)].astype(F32)
            core_in[piece, :, columns(j)] = total.astype(BF16)

        if piece < 4:
            first_copies.append(
                remote(core_in.at[piece], first_in.at[piece], 8 + piece, over_x if piece % 2 == 0 else over_row)
            )
            first_copies[-1].start()
    work(0)
    for part in range(2):
        first_copies[part].wait_recv()

        @pl.loop(0, chunks)
        def _(j, part=part):
            total = core_in[4 + part, :, columns(j)].astype(F32) + first_in[part, :, columns(j)].astype(F32)
            core_in[4 + part, :, columns(j)] = total.astype(BF16)

        next_copies.append(remote(core_in.at[4 + part], next_in.at[part], 12 + part, over_row if part == 0 else over_x))
        next_copies[-1].start()
    work(1)
    for part in range(2):
        first_copies[2 + part].wait_recv()
        next_copies[part].wait_recv()

        @pl.loop(0, chunks)
        def _(j, part=part):
            total = core_in[6 + part, :, columns(j)].astype(F32) + first_in[2 + part, :, columns(j)].astype(F32)
            out_ref[pl.ds(part * half, half), columns(j)] = total + next_in[part, :, columns(j)].astype(F32)

    for copy in core_copies + first_copies + next_copies:
        copy.wait_send()


def plane_scatter(parts, weights, collective_id, jobs=()):
    count = parts[0].shape[0]
    width = weights[0].shape[0]
    rows = count // 8
    half = rows // 2
    vmem, hbm = pl.BlockSpec(memory_space=pltpu.VMEM), pl.BlockSpec(memory_space=pl.ANY)
    lefts, rights = [left for left, _ in jobs], [right for _, right in jobs]
    return pl.pallas_call(
        functools.partial(scatter_kernel, rows, len(parts), len(jobs)),
        in_specs=[hbm] * len(parts) + [vmem] * len(parts) + [hbm] * (2 * len(jobs)),
        out_specs=[vmem] + [hbm] * len(jobs),
        out_shape=[jax.ShapeDtypeStruct((rows, width), F32)]
        + [jax.ShapeDtypeStruct((left.shape[1], right.shape[1]), BF16) for left, right in jobs],
        scratch_shapes=[
            pltpu.VMEM((8, half, width), BF16),
            pltpu.VMEM((8, half, width), BF16),
            pltpu.VMEM((4, half, width), BF16),
            pltpu.VMEM((2, half, width), BF16),
            pltpu.SemaphoreType.DMA((2, 14)),
        ]
        + [pltpu.VMEM((2, half, a.shape[1]), BF16) for a in parts]
        + [pltpu.SemaphoreType.DMA((2, len(parts)))]
        + (product_buffers(rights[0].shape[1]) if jobs else []),
        compiler_params=pltpu.CompilerParams(
            collective_id=collective_id, has_side_effects=True, vmem_limit_bytes=(58 if jobs else 52) << 20
        ),
        cost_estimate=small_cost(),
        name="plane_scatter",
    )(*parts, *weights, *lefts, *rights)


def is_plane():
    return lax.axis_size("ctx") == 4 and lax.axis_size("tensor") == 2


def gather_rows(rows):
    return lax.all_gather(rows, GROUP, axis=0, tiled=True)


def scatter_rows(rows):
    return lax.psum_scatter(rows.astype(BF16), GROUP, scatter_dimension=0, tiled=True).astype(F32)


def gather_now(rows):
    return plane_gather(rows)[0] if is_plane() else gather_rows(rows)


def gather_with_token_products(rows, jobs):
    if is_plane():
        columns = jobs[0][1].shape[1]
        return plane_gather(rows, token_product, jobs, product_buffers(columns), (jobs[0][0].shape[1], columns))
    return [gather_rows(rows)] + [dot_tn(left, right).astype(BF16) for left, right in jobs]


def gather_with_row_product(rows, left, right):
    if is_plane():
        shape = (left.shape[0], right.shape[1])
        return plane_gather(rows, row_product, [(left, right)], row_product_buffers(*right.shape), shape)
    return gather_rows(rows), dot_n(left, right).astype(BF16)


def product_scatter(parts, weights, collective_id, jobs=()):
    if is_plane():
        return plane_scatter(parts, weights, collective_id, jobs)
    rows = scatter_rows(dot_t(jnp.concatenate(parts, axis=1), jnp.concatenate(weights, axis=1)))
    return [rows] + [dot_tn(left, right).astype(BF16) for left, right in jobs]


def gather_weight(own):
    return lax.all_gather(own, "fsdp", axis=0, tiled=True)


def scatter_weight(grad):
    return lax.psum_scatter(grad.astype(BF16), "fsdp", scatter_dimension=0, tiled=True)


def swap_columns(part, count):
    size = lax.axis_size("ctx")
    rows, columns = part.shape[0] // size, part.shape[1] // count
    got = lax.all_to_all(part.reshape(size, rows, count * columns), "ctx", split_axis=0, concat_axis=0)
    return [
        jnp.concatenate([got[j, :, c * columns : (c + 1) * columns] for j in range(size)], axis=1).astype(F32)
        for c in range(count)
    ]


def normalize(rows):
    norm_inv = lax.rsqrt(jnp.mean(rows * rows, axis=1, keepdims=True) + EPSILON)
    return (rows * norm_inv, norm_inv)


def norm_backward(grad_rows, scaled, norm_inv, gain):
    weighted = grad_rows * gain[None, :]
    inner = jnp.mean(weighted * scaled, axis=1, keepdims=True)
    return norm_inv * (weighted - scaled * inner)


def body(
    tokens_in,
    attn_gain,
    query_weight,
    key_weight,
    value_weight,
    output_weight,
    mlp_gain,
    gate_weight,
    up_weight,
    down_weight,
    seg_lengths,
    leaf_parent,
    cotangent,
):
    ctx = lax.axis_index("ctx")
    parts = lax.axis_size("ctx")
    tree_len = tokens_in.shape[0] * parts * lax.axis_size("tensor")
    width = query_weight.shape[1] // parts
    units = gate_weight.shape[1] // parts

    def mine(weight, columns):
        return lax.dynamic_slice_in_dim(weight, ctx * columns, columns, 1)

    x_rows = tokens_in.astype(F32)
    attn_scaled, attn_inv = normalize(x_rows)
    w_attn = gather_weight(
        jnp.concatenate([mine(w, width) for w in (query_weight, key_weight, value_weight, output_weight)], axis=1)
    )
    w_gate = gather_weight(mine(gate_weight, units))
    w_down = gather_weight(mine(down_weight, units))
    w_up = gather_weight(mine(up_weight, units))
    attn_in = gather_now((attn_scaled * attn_gain[None, :]).astype(BF16))
    w_qkv, w_out = w_attn[:, : 3 * width], w_attn[:, 3 * width :]

    attn_in, lengths_row, parent_row = lax.optimization_barrier((attn_in, seg_lengths[0], leaf_parent[0]))
    segment, parent, depth = tree_tables(lengths_row, parent_row, tree_len)
    cosine, sine = rope_tables(depth, min(2 * HEAD_DIM, width))
    seg_keys = segment[None, :]
    seg_queries = jnp.stack([segment, parent], axis=1)

    qkv = jnp.dot(attn_in, w_qkv, preferred_element_type=F32)
    if is_plane():
        attn_out, lse, query_rows, key_rows, value_rows, cot_all = attention_forward(
            qkv, cosine, sine, seg_keys, seg_queries, width, cotangent
        )
    else:
        attn_out, lse, query_rows, key_rows, value_rows = attention_forward(
            qkv, cosine, sine, seg_keys, seg_queries, width
        )
        cot_all = gather_rows(cotangent)
    mid_rows = x_rows + product_scatter([attn_out], [w_out], 1)[0]
    mlp_scaled, mlp_inv = normalize(mid_rows)
    mlp_own = (mlp_scaled * mlp_gain[None, :]).astype(BF16)
    mlp_in, hidden_grad = gather_with_row_product(mlp_own, cot_all, w_down)

    gate = jnp.dot(mlp_in, w_gate, preferred_element_type=F32)
    up_proj = jnp.dot(mlp_in, w_up, preferred_element_type=F32)
    sigmoid_gate = jax.nn.sigmoid(gate)
    hidden = (gate * sigmoid_gate * up_proj).astype(BF16)
    hidden_grad = hidden_grad.astype(F32)
    gate_rows_grad = (
        hidden_grad * up_proj * sigmoid_gate * (1.0 + gate * (1.0 - sigmoid_gate))
    ).astype(BF16)
    up_rows_grad = (hidden_grad * gate * sigmoid_gate).astype(BF16)

    mlp_in_grad, down_part = product_scatter(
        [gate_rows_grad, up_rows_grad], [w_gate, w_up], 3, [(cot_all, hidden)]
    )
    down_grad = scatter_weight(down_part)
    mid_grad = cotangent.astype(F32) + norm_backward(mlp_in_grad, mlp_scaled, mlp_inv, mlp_gain)
    mid_all, up_part, gate_part = gather_with_token_products(
        mid_grad.astype(BF16), [(mlp_in, up_rows_grad), (mlp_in, gate_rows_grad)]
    )
    up_grad = scatter_weight(up_part)
    gate_grad = scatter_weight(gate_part)

    out_heads_grad = jnp.dot(mid_all, w_out, preferred_element_type=F32).astype(BF16)
    output_grad = dot_tn(mid_all, attn_out).astype(BF16)
    out_heads_grad, down_grad = lax.optimization_barrier((out_heads_grad, down_grad))
    down_rows = dot_t(hidden, w_down).astype(BF16)
    if is_plane():
        *pre_grads, down_rows = attention_backward(
            query_rows, key_rows, value_rows, attn_out, out_heads_grad, lse, cosine, sine, seg_keys, seg_queries, down_rows
        )
    else:
        pre_grads = attention_backward(
            query_rows, key_rows, value_rows, attn_out, out_heads_grad, lse, cosine, sine, seg_keys, seg_queries
        )
        down_rows = scatter_rows(down_rows)
    block_out = (mid_rows + down_rows.astype(F32)).astype(BF16)
    pre_grads, up_grad = lax.optimization_barrier((pre_grads, up_grad))
    attn_part = jnp.concatenate([dot_tn(attn_in, grad).astype(BF16) for grad in pre_grads] + [output_grad], axis=1)
    pre_grads, attn_part, gate_grad = lax.optimization_barrier((pre_grads, attn_part, gate_grad))
    attn_grad = scatter_weight(attn_part)
    (attn_in_grad,) = product_scatter(pre_grads, [w_attn[:, j * width : (j + 1) * width] for j in range(3)], 2)
    attn_in_grad, attn_grad = lax.optimization_barrier((attn_in_grad, attn_grad))
    gate_out, up_out, down_out = swap_columns(jnp.concatenate([gate_grad, up_grad, down_grad], axis=1), 3)
    query_out, key_out, value_out, output_out = swap_columns(attn_grad, 4)

    def gain_part(pairs, gain):
        held = query_out.shape[0]
        total = sum(
            jnp.sum(lax.dynamic_slice_in_dim(weight, ctx * held, held, 0).astype(F32) * grad, axis=1)
            for weight, grad in pairs
        )
        first = (lax.axis_index("fsdp") * parts + ctx) * held
        return total / lax.dynamic_slice_in_dim(gain, first, held, 0)

    sums = jnp.stack(
        [
            gain_part([(query_weight, query_out), (key_weight, key_out), (value_weight, value_out)], attn_gain),
            gain_part([(gate_weight, gate_out), (up_weight, up_out)], mlp_gain),
        ]
    )
    row, others = lax.axis_index("tensor"), lax.axis_size("tensor")
    kept = sums.shape[1] // others
    if others == 2:
        got = lax.ppermute(lax.dynamic_slice_in_dim(sums, (1 - row) * kept, kept, 1), "tensor", [(0, 1), (1, 0)])
        gain_grads = lax.dynamic_slice_in_dim(sums, row * kept, kept, 1) + got
    else:
        gain_grads = lax.dynamic_slice_in_dim(lax.psum(sums, "tensor"), row * kept, kept, 1)

    attn_back = norm_backward(attn_in_grad, attn_scaled, attn_inv, attn_gain)
    input_grad = (mid_grad + attn_back).astype(BF16)
    return (
        block_out,
        input_grad,
        gain_grads[0],
        query_out,
        key_out,
        value_out,
        output_out,
        gain_grads[1],
        gate_out,
        up_out,
        down_out,
    )


def solution(mesh):
    rows = P(("fsdp", "ctx", "tensor"), None)
    weight = P("fsdp", "tensor")
    gain = P(("fsdp", "ctx", "tensor"))
    grad = P(("fsdp", "ctx"), "tensor")
    in_specs = (
        rows, P(), weight, weight, weight, weight, P(), weight, weight, weight, P("fsdp", None), P("fsdp", None), rows,
    )
    out_specs = (rows, rows, gain, grad, grad, grad, grad, gain, grad, grad, grad)
    return jax.shard_map(body, mesh=mesh, in_specs=in_specs, out_specs=out_specs, check_vma=False)
```

```python
import functools

import jax
import jax.numpy as jnp
import numpy as np
from jax import lax
from jax.experimental import pallas as pl
from jax.experimental.pallas import tpu as pltpu
from jax.sharding import PartitionSpec as P

HEAD_DIM = 64
TRUNK = 2176
MOST_SEG = 128
ROPE_BASE = 130000.0
EPSILON = 1e-05
NEG_LARGE = -1e30
SCALE = HEAD_DIM ** (-0.5)

BQ = 512
BK = 512
GROUP = ("ctx", "tensor")

F32 = jnp.float32
BF16 = jnp.bfloat16


def pick_table(onehot, table):
    return jnp.sum(jnp.where(onehot, table[None, :], 0), axis=1)


def tree_tables(lengths_row, parent_row, tree_len):
    branches = lengths_row.shape[0] - parent_row.shape[0]
    ends = TRUNK + jnp.cumsum(lengths_row)
    starts = ends - lengths_row
    matches = parent_row[:, None] - 1 == jnp.arange(branches, dtype=jnp.int32)[None, :]
    parent_len = jnp.sum(jnp.where(matches, lengths_row[None, :branches], 0), axis=1)
    zero_one = jnp.zeros((1,), jnp.int32)
    seg_start = jnp.concatenate([zero_one, starts])
    seg_base = jnp.concatenate(
        [zero_one, jnp.full((branches,), TRUNK, jnp.int32), TRUNK + parent_len]
    )
    seg_parent = jnp.concatenate([zero_one, jnp.zeros((branches,), jnp.int32), parent_row])
    positions = jnp.arange(tree_len, dtype=jnp.int32)
    above = jnp.sum((ends[None, :] <= positions[:, None]).astype(jnp.int32), axis=1)
    segment = (positions >= TRUNK).astype(jnp.int32) + above
    onehot = segment[:, None] == jnp.arange(seg_start.shape[0], dtype=jnp.int32)[None, :]
    depth = positions - pick_table(onehot, seg_start) + pick_table(onehot, seg_base)
    parent = pick_table(onehot, seg_parent)
    return (segment, parent, depth)


def rope_freqs(width):
    half = HEAD_DIM // 2
    powers = -2.0 * (np.arange(width) % half) / HEAD_DIM
    return np.power(ROPE_BASE, powers).astype(np.float32)[None, :]


def rope_tables(depth, width):
    angles = depth.astype(F32)[:, None] * rope_freqs(width)
    sign = np.where(np.arange(width) % HEAD_DIM < HEAD_DIM // 2, -1.0, 1.0).astype(np.float32)
    return jnp.cos(angles), jnp.sin(angles) * sign[None, :]


def lay_out(segment, parent):
    both = jnp.stack([segment, parent])
    return jnp.pad(both, ((0, 6), (0, 0))), jnp.pad(both.T, ((0, 0), (0, 126)))


TABLE_ROWS = 512
TABLE_STEP = 64


def tables_at(positions, lengths, parents):
    leaves = parents.shape[1]
    branches = lengths.shape[1] - leaves
    zero = jnp.zeros_like(positions)
    segment = jnp.where(positions >= TRUNK, 1, 0)
    parent, depth = zero, positions
    end = jnp.full((1, 1), TRUNK, jnp.int32)
    starts = []
    for s in range(branches + leaves):
        start, end = end, end + lengths[:, s : s + 1]
        inside = (positions >= start) & (positions < end)
        base, above = jnp.full((1, 1), TRUNK, jnp.int32), jnp.zeros((1, 1), jnp.int32)
        if s >= branches:
            above = parents[:, s - branches : s - branches + 1]
            for b in range(branches):
                base = base + jnp.where(above == b + 1, lengths[:, b : b + 1], 0)
        segment = segment + jnp.where(positions >= end, 1, 0)
        parent = jnp.where(inside, above, parent)
        depth = jnp.where(inside, positions - start + base, depth)
    return segment, parent, depth


def sine_cosine(x):
    turns = jnp.floor(x * np.float32(2.0 / np.pi) + 0.5)
    r = x - turns * np.float32(1.5703125)
    r = r - turns * np.float32(4.837512969970703125e-4)
    r = r - turns * np.float32(7.549789954891882e-8)
    z = r * r
    sine = ((np.float32(-1.9515295891e-4) * z + np.float32(8.3321608736e-3)) * z - np.float32(1.6666654611e-1)) * z * r + r
    cosine = (
        (np.float32(2.443315711809948e-5) * z - np.float32(1.388731625493765e-3)) * z + np.float32(4.166664568298827e-2)
    ) * z * z - np.float32(0.5) * z + np.float32(1.0)
    quarter = turns.astype(jnp.int32) & 3
    odd = (quarter & 1) == 1
    first, second = jnp.where(odd, cosine, sine), jnp.where(odd, sine, cosine)
    return jnp.where(quarter >= 2, -first, first), jnp.where((quarter == 1) | (quarter == 2), -second, second)


def table_work(lengths, parents, freqs, rows_ref, cols_ref, cos_ref, sin_ref, cols_buf, cos_buf, sin_buf, sems):
    tokens = cos_ref.shape[0]
    shape = (8, tokens)
    segment, parent, _ = tables_at(lax.broadcasted_iota(jnp.int32, shape, 1), lengths, parents)
    line = lax.broadcasted_iota(jnp.int32, shape, 0)
    rows_ref[...] = jnp.where(line == 0, segment, jnp.where(line == 1, parent, 0))
    copies = []
    for chunk in range(tokens // TABLE_ROWS):
        rows = pl.ds(chunk * TABLE_ROWS, TABLE_ROWS)

        @pl.loop(0, TABLE_ROWS // TABLE_STEP)
        def _(j, chunk=chunk):
            first = pl.multiple_of(chunk * TABLE_ROWS + j * TABLE_STEP, TABLE_STEP)
            taken = pl.ds(first, TABLE_STEP)
            shape = (TABLE_STEP, 128)
            lane = lax.broadcasted_iota(jnp.int32, shape, 1)
            segment, parent, depth = tables_at(lax.broadcasted_iota(jnp.int32, shape, 0) + first, lengths, parents)
            cols_buf[taken, :] = jnp.where(lane == 0, segment, jnp.where(lane == 1, parent, 0))
            sine, cosine = sine_cosine(depth.astype(F32) * freqs[...])
            cos_buf[taken, :] = cosine
            sin_buf[taken, :] = jnp.where(lane % HEAD_DIM < HEAD_DIM // 2, -sine, sine)

        for kind, (source, target) in enumerate(((cols_buf, cols_ref), (cos_buf, cos_ref), (sin_buf, sin_ref))):
            copies.append(pltpu.make_async_copy(source.at[rows], target.at[rows], sems.at[kind, chunk]))
            copies[-1].start()
        yield
    for copy in copies:
        copy.wait()


MESH = pl.DeviceIdType.MESH


def plane_place():
    ctx, row = lax.axis_index("ctx"), lax.axis_index("tensor")
    x, core = ctx // 2, ctx % 2
    return x, core, row


def plane_neighbours(x, core, row):
    over_x = {"ctx": (1 - x) * 2 + core}
    over_core = {"ctx": x * 2 + 1 - core}
    over_row = {"tensor": 1 - row}
    return over_x, over_row, over_core


def enter_plane(neighbours):
    barrier = pltpu.get_barrier_semaphore()
    for device in neighbours:
        pl.semaphore_signal(barrier, inc=1, device_id=device, device_id_type=MESH)
    pl.semaphore_wait(barrier, 3)


PIECES = ((1, 1, 0), (1, 1, 1), (1, 0, 0), (0, 1, 1), (0, 1, 0), (1, 0, 1), (0, 0, 0), (0, 0, 1))
COLS = 512


class PlaneGather:
    def __init__(self, own_ref, all_ref, local_sem, send_sem, recv_sem):
        self.own_ref, self.all_ref, self.sems = own_ref, all_ref, (local_sem, send_sem, recv_sem)
        self.x, self.core, self.row = plane_place()
        self.devices = plane_neighbours(self.x, self.core, self.row)
        self.rows = own_ref.shape[0]

    def place(self, far_x, far_row, part):
        bx = self.x + far_x - 2 * far_x * self.x
        by = self.row + far_row - 2 * far_row * self.row
        half = self.rows // 2
        return pl.ds(pl.multiple_of(((bx * 2 + self.core) * 2 + by) * self.rows + part * half, half), half)

    def copy(self, slot):
        far_x, far_row, part, device = (
            (0, 0, 0, 1), (0, 0, 1, 1), (1, 0, 1, 1), (0, 0, 1, 0), (0, 0, 0, 0), (0, 1, 0, 0), (0, 0, 0, 2),
            (0, 0, 1, 2), (0, 1, 0, 2), (1, 0, 1, 2), (0, 1, 1, 2), (1, 0, 0, 2), (1, 1, 0, 2), (1, 1, 1, 2),
        )[slot]
        half = self.rows // 2
        target = self.place(far_x, far_row, part)
        own = far_x == 0 and far_row == 0
        source = self.own_ref.at[pl.ds(part * half, half)] if own else self.all_ref.at[target]
        return pltpu.make_async_remote_copy(
            src_ref=source, dst_ref=self.all_ref.at[target], send_sem=self.sems[1].at[slot],
            recv_sem=self.sems[2].at[slot], device_id=self.devices[device], device_id_type=MESH,
        )

    def local(self, part):
        half = self.rows // 2
        return pltpu.make_async_copy(
            self.own_ref.at[pl.ds(part * half, half)], self.all_ref.at[self.place(0, 0, part)], self.sems[0].at[part]
        )

    def start(self):
        enter_plane(self.devices)
        for slot in (0, 3, 1, 4, 6, 7):
            self.copy(slot).start()
        for part in range(2):
            self.local(part).start()

    def forward(self, got, slots):
        self.copy(got).wait_recv()
        for slot in slots:
            self.copy(slot).start()

    def first(self):
        self.forward(0, (5, 8))
        self.forward(3, (2, 9))

    def second(self):
        self.forward(1, (10,))
        self.forward(4, (11,))

    def finish(self):
        self.forward(5, (12,))
        self.forward(2, (13,))
        for slot in range(6, 14):
            self.copy(slot).wait_recv()
        for slot in range(14):
            self.copy(slot).wait_send()
        for part in range(2):
            self.local(part).wait()


def gather_sems():
    return [pltpu.SemaphoreType.DMA((2,)), pltpu.SemaphoreType.DMA((14,)), pltpu.SemaphoreType.DMA((14,))]


class PlaneScatter:
    def __init__(self, part_ref, out_ref, core_in, first_in, next_in, own, total, sems, own_sems):
        self.part_ref, self.out_ref, self.core_in, self.first_in, self.next_in = part_ref, out_ref, core_in, first_in, next_in
        self.own, self.total, self.sems, self.own_sems = own, total, sems, own_sems
        self.x, self.core, self.row = plane_place()
        self.devices = plane_neighbours(self.x, self.core, self.row)
        self.rows = part_ref.shape[0] // 8

    def place(self, piece, on_core):
        far_x, far_row, part = PIECES[piece]
        bx = self.x + far_x - 2 * far_x * self.x
        by = self.row + far_row - 2 * far_row * self.row
        half = self.rows // 2
        return pl.ds(pl.multiple_of(((bx * 2 + on_core) * 2 + by) * self.rows + part * half, half), half)

    def copy(self, slot):
        if slot < 8:
            source, target, device = self.part_ref.at[self.place(slot, 1 - self.core)], self.core_in.at[slot], 2
        elif slot < 12:
            source, target, device = self.core_in.at[slot - 8], self.first_in.at[slot - 8], slot % 2
        else:
            source, target, device = self.core_in.at[slot - 8], self.next_in.at[slot - 12], 1 - slot % 2
        return pltpu.make_async_remote_copy(
            src_ref=source, dst_ref=target, send_sem=self.sems.at[0, slot], recv_sem=self.sems.at[1, slot],
            device_id=self.devices[device], device_id_type=MESH,
        )

    def load(self, piece):
        return pltpu.make_async_copy(
            self.part_ref.at[self.place(piece, self.core)], self.own.at[piece % 4], self.own_sems.at[piece % 4]
        )

    def add(self, target, where, *others):
        @pl.loop(0, target.shape[-1] // COLS)
        def _(j):
            columns = pl.ds(pl.multiple_of(j * COLS, COLS), COLS)
            total = sum(ref[slot, :, columns].astype(F32) for ref, slot in others)
            target[where, :, columns] = total.astype(target.dtype)

    def start(self):
        enter_plane(self.devices)
        for slot in range(8):
            self.copy(slot).start()
        for piece in range(4):
            self.load(piece).start()

    def first(self):
        for piece in range(4):
            self.load(piece).wait()
            self.copy(piece).wait_recv()
            self.add(self.core_in, piece, (self.own, piece), (self.core_in, piece))
            self.copy(8 + piece).start()
        for piece in range(4, 8):
            self.load(piece).start()

    def second(self):
        for piece in range(4, 8):
            self.load(piece).wait()
            self.copy(piece).wait_recv()
            self.add(self.core_in, piece, (self.own, piece - 4), (self.core_in, piece))

    def third(self):
        for part in range(2):
            self.copy(8 + part).wait_recv()
            self.add(self.core_in, 4 + part, (self.core_in, 4 + part), (self.first_in, part))
            self.copy(12 + part).start()

    def finish(self):
        half = self.rows // 2
        for part in range(2):
            self.copy(10 + part).wait_recv()
            self.copy(12 + part).wait_recv()
            self.add(self.total, part, (self.core_in, 6 + part), (self.first_in, 2 + part), (self.next_in, part))
        stores = [
            pltpu.make_async_copy(
                self.total.at[part], self.out_ref.at[pl.ds(part * half, half)], self.own_sems.at[part]
            )
            for part in range(2)
        ]
        for store in stores:
            store.start()
        for slot in range(14):
            self.copy(slot).wait_send()
        for store in stores:
            store.wait()


def scatter_scratch(rows, width):
    half = rows // 2
    return [
        pltpu.VMEM((8, half, width), BF16),
        pltpu.VMEM((4, half, width), BF16),
        pltpu.VMEM((2, half, width), BF16),
        pltpu.VMEM((4, half, width), BF16),
        pltpu.VMEM((2, half, width), BF16),
        pltpu.SemaphoreType.DMA((2, 14)),
        pltpu.SemaphoreType.DMA((4,)),
    ]


def at_step(step, total, places):
    for place, phase in places:

        @pl.when(step == place)
        def _(phase=phase):
            phase()


def partner(x):
    half = HEAD_DIM // 2
    width = x.shape[1]
    if width == HEAD_DIM:
        return jnp.concatenate([x[:, half:], x[:, :half]], axis=1)
    lane = lax.broadcasted_iota(jnp.int32, x.shape, 1)
    ahead = pltpu.roll(x, width - half, 1)
    behind = pltpu.roll(x, half, 1)
    return jnp.where(lane % HEAD_DIM < half, ahead, behind)


def head_mask(shape, head):
    lane = lax.broadcasted_iota(jnp.int32, shape, 1)
    return lane // HEAD_DIM == head


def dot_t(a, b):
    return lax.dot_general(a, b, (((1,), (1,)), ((), ())), preferred_element_type=F32)


def dot_n(a, b):
    return lax.dot_general(a, b, (((1,), (0,)), ((), ())), preferred_element_type=F32)


def dot_tn(a, b):
    return lax.dot_general(a, b, (((0,), (0,)), ((), ())), preferred_element_type=F32)


def key_plan(i, tile):
    base = TRUNK // BK * BK
    branch_end = TRUNK + 4 * MOST_SEG
    first_tree = base // BQ
    mixed_end = -(-(branch_end + MOST_SEG) // BQ)
    chunks = jnp.minimum(i * BQ, base) // BK

    @pl.when(i < first_tree)
    def _():
        @pl.loop(0, chunks)
        def _(j):
            start = pl.multiple_of(j * BK, BK)
            tile(start, BK, 0, start)

    @pl.when(i >= first_tree)
    def _():
        tile(0, base, 0, 0)

    @pl.when(i < first_tree)
    def _():
        start = pl.multiple_of(chunks * BK, BK)
        tile(start, BK, 1, start)

    for block in range(first_tree, mixed_end):

        @pl.when(i == block)
        def _(block=block):
            tile(base, (block + 1) * BQ - base, 2, base)

    @pl.when(i >= mixed_end)
    def _():
        tile(base, branch_end - base, 3, base)
        tile(pl.multiple_of(i * BQ - MOST_SEG, MOST_SEG), BQ + MOST_SEG, 4, branch_end)


def most_keys():
    return TRUNK + 4 * MOST_SEG + BQ + MOST_SEG


def seen_mask(kind, q_at, k_at, seg_q, par_q, seg_k):
    if kind == 3:
        return (seg_k == 0) | (seg_k == par_q)
    causal = k_at <= q_at
    if kind == 1:
        return causal
    if kind == 4:
        return causal & (seg_k == seg_q)
    return causal & ((seg_k == 0) | (seg_k == seg_q) | (seg_k == par_q))


def fwd_kernel(heads, hosts, *refs):
    if not hosts:
        return fwd_work(heads, *refs)
    gather = PlaneGather(refs[7], refs[13], *refs[-3:])
    step, total = pl.program_id(0) * pl.num_programs(1) + pl.program_id(1), 16
    at_step(step, total, ((0, gather.start), (6, gather.first), (12, gather.second)))
    fwd_work(heads, *refs[:7], *refs[8:13], *refs[14:-3])
    at_step(step, total, ((total - 1, gather.finish),))


def fwd_work(
    heads, q_ref, k_ref, v_ref, cos_ref, sin_ref, rows_ref, cols_ref,
    o_ref, lse_ref, qr_ref, kr_ref, vr_ref, kt_ref, va_ref, s_ref, m_ref, acc_ref,
):
    i = pl.program_id(1)
    wide = 2 * HEAD_DIM

    @pl.when(i == 0)
    def _():
        @pl.loop(0, k_ref.shape[0] // BK)
        def _(j):
            rows = pl.ds(pl.multiple_of(j * BK, BK), BK)
            k = k_ref[rows, :]
            k = (k * cos_ref[rows, :] + partner(k) * sin_ref[rows, :]).astype(BF16)
            kr_ref[rows, :] = k
            kt_ref[:, rows] = jnp.transpose(k)
            v = v_ref[rows, :].astype(BF16)
            vr_ref[rows, :] = v
            if heads == 1:
                va_ref[0, rows, :] = jnp.concatenate([v, jnp.ones_like(v)], axis=1)
            else:
                for h in range(heads):
                    va_ref[h, rows, :] = jnp.where(head_mask(v.shape, h), v, jnp.ones_like(v))

    rows = pl.ds(pl.multiple_of(i * BQ, BQ), BQ)
    q = q_ref[...]
    q = (q * cos_ref[rows, :] + partner(q) * sin_ref[rows, :]).astype(BF16)
    qr_ref[...] = q
    q = q * jnp.asarray(SCALE, BF16)
    q_heads = [jnp.where(head_mask(q.shape, h), q, jnp.zeros_like(q)) for h in range(heads)]
    m_ref[...] = jnp.full_like(m_ref, NEG_LARGE)
    acc_ref[...] = jnp.zeros_like(acc_ref)

    def score_tile(start, width, kind, place):
        keys = pl.ds(start, width)
        k = kt_ref[:, keys]
        seen = None
        if kind != 0:
            shape = (BQ, width)
            seen = seen_mask(
                kind,
                lax.broadcasted_iota(jnp.int32, shape, 0) + i * BQ,
                lax.broadcasted_iota(jnp.int32, shape, 1) + start,
                cols_ref[:, 0:1], cols_ref[:, 1:2], rows_ref[0:1, keys],
            )
        for h in range(heads):
            s = dot_n(q_heads[h], k)
            if seen is not None:
                s = jnp.where(seen, s, NEG_LARGE)
            s_ref[h, :, pl.ds(place, width)] = s
            largest = m_ref[h]
            for c in range(width // 128):
                largest = jnp.maximum(largest, s[:, c * 128 : (c + 1) * 128])
            m_ref[h] = largest

    key_plan(i, score_tile)
    for h in range(heads):
        m_ref[h] = jnp.broadcast_to(jnp.max(m_ref[h], axis=1, keepdims=True), (BQ, 128))

    def value_tile(start, width, kind, place):
        keys = pl.ds(start, width)
        for h in range(heads):
            m = m_ref[h]
            parts = [
                jnp.exp(s_ref[h, :, pl.ds(place + c * 128, 128)] - m).astype(BF16) for c in range(width // 128)
            ]
            acc_ref[h] += dot_n(jnp.concatenate(parts, axis=1), va_ref[h, keys, :])

    key_plan(i, value_tile)
    out, lse = None, None
    for h in range(heads):
        acc = acc_ref[h]
        part = acc / pltpu.roll(acc, HEAD_DIM, 1)
        stat = m_ref[h] + jnp.log(jnp.broadcast_to(acc[:, (1 - h) * HEAD_DIM : (1 - h) * HEAD_DIM + 1], (BQ, wide)))
        mask = head_mask((BQ, wide), h)
        out = part if h == 0 else jnp.where(mask, part, out)
        lse = stat if h == 0 else jnp.where(mask, stat, lse)
    o_ref[...] = out[:, : heads * HEAD_DIM].astype(BF16)
    turned = jnp.transpose(lse)
    for h in range(heads):
        lse_ref[0, h : h + 1, :] = turned[h * HEAD_DIM : h * HEAD_DIM + 1, :]


def bwd_kernel(heads, hosts, *refs):
    if not hosts:
        return bwd_work(heads, *refs)
    scatter = PlaneScatter(refs[10], refs[14], *refs[-7:])
    step, total = pl.program_id(0) * pl.num_programs(1) + pl.program_id(1), 16
    at_step(
        step, total, ((0, scatter.start), (3, scatter.first), (5, scatter.second), (7, scatter.third))
    )
    bwd_work(heads, *refs[:10], *refs[11:14], *refs[15:-7])
    at_step(step, total, ((total - 1, scatter.finish),))


def bwd_work(
    heads, q_ref, k_ref, v_ref, o_ref, do_ref, lse_ref, cos_ref, sin_ref, rows_ref, cols_ref,
    dq_ref, dk_ref, dv_ref, dq_acc, dk_acc, dv_acc,
):
    i = pl.program_id(1)

    @pl.when(i == 0)
    def _():
        dk_acc[...] = jnp.zeros_like(dk_acc)
        dv_acc[...] = jnp.zeros_like(dv_acc)

    q = q_ref[...]
    scaled = q * jnp.asarray(SCALE, BF16)
    do = do_ref[...]
    product = jnp.transpose(do.astype(F32) * o_ref[...].astype(F32))
    zero = jnp.zeros_like(q)
    masks = [head_mask(q.shape, h) for h in range(heads)]
    q_heads = [jnp.where(m, scaled, zero) for m in masks]
    do_heads = [jnp.where(m, do, zero) for m in masks]
    deltas = [
        jnp.sum(product[h * HEAD_DIM : (h + 1) * HEAD_DIM, :], axis=0, keepdims=True) for h in range(heads)
    ]
    lses = [lse_ref[0, h : h + 1, :] for h in range(heads)]
    q_turned = [jnp.transpose(x) for x in q_heads]
    do_turned = [jnp.transpose(x) for x in do_heads]
    q_stack = jnp.concatenate(q_heads, axis=0)
    do_stack = jnp.concatenate(do_heads, axis=0)
    dq_acc[...] = jnp.zeros_like(dq_acc)

    def tile(start, width, kind, place):
        keys = pl.ds(start, width)
        k = k_ref[keys, :]
        v = v_ref[keys, :]
        seen = None
        if kind != 0:
            shape = (width, BQ)
            seen = seen_mask(
                kind,
                lax.broadcasted_iota(jnp.int32, shape, 1) + i * BQ,
                lax.broadcasted_iota(jnp.int32, shape, 0) + start,
                rows_ref[0:1, :], rows_ref[1:2, :], cols_ref[keys, 0:1],
            )
        probs, grads, k_heads = [], [], []
        for h in range(heads):
            s = dot_n(k, q_turned[h])
            p = jnp.exp(s - lses[h])
            if seen is not None:
                p = jnp.where(seen, p, 0.0)
            dp = dot_n(v, do_turned[h])
            probs.append(p.astype(BF16))
            grads.append((p * (dp - deltas[h])).astype(BF16))
            k_heads.append(jnp.where(head_mask(k.shape, h), k, jnp.zeros_like(k)))
        grad_row = jnp.concatenate(grads, axis=1)
        dv_acc[keys, :] += dot_n(jnp.concatenate(probs, axis=1), do_stack)
        dk_acc[keys, :] += dot_n(grad_row, q_stack)
        dq_acc[...] += dot_tn(jnp.concatenate(grads, axis=0), jnp.concatenate(k_heads, axis=0))

    key_plan(i, tile)
    dq = dq_acc[...] * SCALE
    rows = pl.ds(pl.multiple_of(i * BQ, BQ), BQ)
    dq_ref[...] = (dq * cos_ref[rows, :] - partner(dq) * sin_ref[rows, :]).astype(BF16)

    @pl.when(i == pl.num_programs(1) - 1)
    def _():
        @pl.loop(0, dk_acc.shape[0] // BK)
        def _(j):
            rows = pl.ds(pl.multiple_of(j * BK, BK), BK)
            dk = dk_acc[rows, :]
            dk_ref[rows, :] = (dk * cos_ref[rows, :] - partner(dk) * sin_ref[rows, :]).astype(BF16)
            dv_ref[rows, :] = dv_acc[rows, :].astype(BF16)


def small_cost():
    return pl.CostEstimate(flops=1 << 20, bytes_accessed=1 << 20, transcendentals=0)


def attention_forward(qkv, cosine, sine, rows_table, cols_table, width, hosted=None):
    tree_len = qkv.shape[0]
    gw = min(2 * HEAD_DIM, width)
    groups, heads = width // gw, gw // HEAD_DIM
    row_block = pl.BlockSpec((BQ, gw), lambda g, i: (i, g))
    table = pl.BlockSpec((tree_len, gw), lambda g, i: (0, 0))
    full = pl.BlockSpec((tree_len, gw), lambda g, i: (0, g))
    act = jax.ShapeDtypeStruct((tree_len, width), BF16)
    if width % 128 == 0:
        queries, keys, values, step = qkv, qkv, qkv, groups
    else:
        queries, keys, values = jnp.split(qkv, 3, axis=1)
        step = 0
    hosts = hosted is not None
    hbm = pl.BlockSpec(memory_space=pl.ANY)
    return pl.pallas_call(
        functools.partial(fwd_kernel, heads, hosts),
        grid=(groups, tree_len // BQ),
        in_specs=[
            row_block,
            pl.BlockSpec((tree_len, gw), lambda g, i: (0, step + g)),
            pl.BlockSpec((tree_len, gw), lambda g, i: (0, 2 * step + g)),
            table,
            table,
            pl.BlockSpec((8, tree_len), lambda g, i: (0, 0)),
            pl.BlockSpec((BQ, 128), lambda g, i: (i, 0)),
        ]
        + [hbm] * hosts,
        out_specs=[row_block, pl.BlockSpec((1, heads, BQ), lambda g, i: (g, 0, i)), row_block, full, full] + [hbm] * hosts,
        out_shape=[act, jax.ShapeDtypeStruct((groups, heads, tree_len), F32), act, act, act]
        + ([jax.ShapeDtypeStruct((8 * hosted.shape[0], hosted.shape[1]), BF16)] if hosts else []),
        scratch_shapes=[
            pltpu.VMEM((gw, tree_len), BF16),
            pltpu.VMEM((heads, tree_len, 128), BF16),
            pltpu.VMEM((heads, BQ, most_keys()), F32),
            pltpu.VMEM((heads, BQ, 128), F32),
            pltpu.VMEM((heads, BQ, 128), F32),
        ]
        + (gather_sems() if hosts else []),
        compiler_params=pltpu.CompilerParams(
            vmem_limit_bytes=56 << 20, collective_id=6 if hosts else None, has_side_effects=hosts
        ),
        cost_estimate=small_cost(),
        name="tree_attention_forward",
    )(queries, keys, values, cosine, sine, rows_table, cols_table, *([hosted] if hosts else []))


def attention_backward(q, k, v, out, grad, lse, cosine, sine, rows_table, cols_table, hosted=None):
    tree_len, width = q.shape
    gw = min(2 * HEAD_DIM, width)
    groups, heads = width // gw, gw // HEAD_DIM
    row_block = pl.BlockSpec((BQ, gw), lambda g, i: (i, g))
    table = pl.BlockSpec((tree_len, gw), lambda g, i: (0, 0))
    full = pl.BlockSpec((tree_len, gw), lambda g, i: (0, g))
    act = jax.ShapeDtypeStruct((tree_len, width), BF16)
    hosts = hosted is not None
    hbm = pl.BlockSpec(memory_space=pl.ANY)
    return pl.pallas_call(
        functools.partial(bwd_kernel, heads, hosts),
        grid=(groups, tree_len // BQ),
        in_specs=[
            row_block, full, full, row_block, row_block,
            pl.BlockSpec((1, heads, BQ), lambda g, i: (g, 0, i)),
            table, table,
            pl.BlockSpec((8, BQ), lambda g, i: (0, i)),
            pl.BlockSpec((tree_len, 128), lambda g, i: (0, 0)),
        ]
        + [hbm] * hosts,
        out_specs=[row_block, full, full] + [hbm] * hosts,
        out_shape=[act, act, act]
        + ([jax.ShapeDtypeStruct((hosted.shape[0] // 8, hosted.shape[1]), BF16)] if hosts else []),
        scratch_shapes=[
            pltpu.VMEM((BQ, gw), F32),
            pltpu.VMEM((tree_len, gw), F32),
            pltpu.VMEM((tree_len, gw), F32),
        ]
        + (scatter_scratch(hosted.shape[0] // 8, hosted.shape[1]) if hosts else []),
        compiler_params=pltpu.CompilerParams(
            vmem_limit_bytes=60 << 20, collective_id=7 if hosts else None, has_side_effects=hosts
        ),
        cost_estimate=small_cost(),
        name="tree_attention_backward",
    )(q, k, v, out, grad, lse, cosine, sine, rows_table, cols_table, *([hosted] if hosts else []))


TOKENS_AT_ONCE = 2048
LEFT_AT_ONCE = 512
STEP = 512


def product_buffers(columns):
    return [
        pltpu.VMEM((2, TOKENS_AT_ONCE, LEFT_AT_ONCE), BF16),
        pltpu.VMEM((2 * TOKENS_AT_ONCE, columns), BF16),
        pltpu.VMEM((LEFT_AT_ONCE, columns), F32),
        pltpu.VMEM((LEFT_AT_ONCE, columns), BF16),
        pltpu.SemaphoreType.DMA((4,)),
    ]


def token_product(left_ref, right_ref, out_ref, left_buf, right_buf, total, out_buf, sems):
    tokens = left_ref.shape[0]
    parts, groups = tokens // TOKENS_AT_ONCE, left_ref.shape[1] // LEFT_AT_ONCE

    def load(step):
        group, part = step // parts, step % parts
        source = left_ref.at[
            pl.ds(part * TOKENS_AT_ONCE, TOKENS_AT_ONCE), pl.ds(group * LEFT_AT_ONCE, LEFT_AT_ONCE)
        ]
        return pltpu.make_async_copy(source, left_buf.at[step % 2], sems.at[step % 2])

    def store(group):
        return pltpu.make_async_copy(out_buf, out_ref.at[pl.ds(group * LEFT_AT_ONCE, LEFT_AT_ONCE)], sems.at[3])

    whole = pltpu.make_async_copy(right_ref, right_buf, sems.at[2])
    whole.start()
    load(0).start()
    whole.wait()
    for group in range(groups):
        for part in range(parts):
            step = group * parts + part
            load(step).wait()
            if step + 1 < groups * parts:
                load(step + 1).start()
            if part == 0:
                total[...] = jnp.zeros_like(total)

            @pl.loop(0, TOKENS_AT_ONCE // STEP)
            def _(j, step=step, part=part):
                left = left_buf[step % 2, pl.ds(pl.multiple_of(j * STEP, STEP), STEP), :]
                right = right_buf[pl.ds(pl.multiple_of(part * TOKENS_AT_ONCE + j * STEP, STEP), STEP), :]
                total[...] += dot_tn(left, right)

        if group > 0:
            store(group - 1).wait()
        out_buf[...] = total[...].astype(BF16)
        store(group).start()
        yield
    store(groups - 1).wait()


def finish(product):
    for _ in product:
        pass


def row_product(turned, left_ref, right_ref, out_ref, left_buf, right_buf, out_buf, sems):
    groups = left_ref.shape[0] // LEFT_AT_ONCE

    def rows(group):
        return pl.ds(group * LEFT_AT_ONCE, LEFT_AT_ONCE)

    def load(group):
        return pltpu.make_async_copy(left_ref.at[rows(group)], left_buf.at[group % 2], sems.at[group % 2])

    def store(group):
        return pltpu.make_async_copy(out_buf.at[group % 2], out_ref.at[rows(group)], sems.at[3 + group % 2])

    whole = pltpu.make_async_copy(right_ref, right_buf, sems.at[2])
    whole.start()
    load(0).start()
    whole.wait()
    for group in range(groups):
        load(group).wait()
        if group + 1 < groups:
            load(group + 1).start()
        if group > 1:
            store(group - 2).wait()

        @pl.loop(0, out_ref.shape[1] // STEP)
        def _(j, group=group):
            columns = pl.ds(pl.multiple_of(j * STEP, STEP), STEP)
            if turned:
                part = dot_t(left_buf[group % 2], right_buf[columns, :])
            else:
                part = dot_n(left_buf[group % 2], right_buf[:, columns])
            out_buf[group % 2, :, columns] = part.astype(BF16)

        store(group).start()
        yield
    for group in range(max(0, groups - 2), groups):
        store(group).wait()


def row_product_buffers(right, turned):
    return [
        pltpu.VMEM((2, LEFT_AT_ONCE, right.shape[1 if turned else 0]), BF16),
        pltpu.VMEM(right.shape, BF16),
        pltpu.VMEM((2, LEFT_AT_ONCE, right.shape[0 if turned else 1]), BF16),
        pltpu.SemaphoreType.DMA((5,)),
    ]


def gather_kernel(works, counts, paces, *refs):
    def take(count):
        nonlocal refs
        taken, refs = refs[:count], refs[count:]
        return taken

    (own_ref,) = take(1)
    inputs = [take(count[0]) for count in counts]
    (all_ref,) = take(1)
    outputs = [take(count[1]) for count in counts]
    gather = PlaneGather(own_ref, all_ref, *take(3))
    buffers, held = [], {}
    for work, count in zip(works, counts):
        if work not in held:
            held[work] = take(count[2])
        buffers.append(held[work])

    def all_work():
        for work, given, wanted, room in zip(works, inputs, outputs, buffers):
            yield from work(*given, *wanted, *room)

    going = all_work()

    def some(count):
        for _ in range(count):
            next(going, None)

    gather.start()
    some(paces[0])
    gather.first()
    some(paces[1])
    gather.second()
    finish(going)
    gather.finish()


def plane_gather(rows, collective_id=0, jobs=(), paces=(0, 0)):
    count, width = rows.shape
    hbm = pl.BlockSpec(memory_space=pl.ANY)
    scratch, held = gather_sems(), set()
    for work, _, _, _, _, buffers in jobs:
        if work not in held:
            held.add(work)
            scratch += buffers
    return pl.pallas_call(
        functools.partial(
            gather_kernel,
            [job[0] for job in jobs],
            [(len(job[1]), len(job[3]), len(job[5])) for job in jobs],
            paces,
        ),
        in_specs=[hbm] + [spec for job in jobs for spec in job[2]],
        out_specs=[hbm] + [spec for job in jobs for spec in job[4]],
        out_shape=[jax.ShapeDtypeStruct((8 * count, width), rows.dtype)] + [out for job in jobs for out in job[3]],
        scratch_shapes=scratch,
        compiler_params=pltpu.CompilerParams(
            collective_id=collective_id, has_side_effects=True, vmem_limit_bytes=(48 << 20) if jobs else None
        ),
        cost_estimate=small_cost(),
        name="plane_gather",
    )(rows, *[value for job in jobs for value in job[1]])


HBM = pl.BlockSpec(memory_space=pl.ANY)
VMEM = pl.BlockSpec(memory_space=pltpu.VMEM)
ROWS_TURNED = functools.partial(row_product, True)
ROWS_STRAIGHT = functools.partial(row_product, False)


def token_job(left, right):
    out = jax.ShapeDtypeStruct((left.shape[1], right.shape[1]), BF16)
    return token_product, [left, right], [HBM] * 2, [out], [HBM], product_buffers(right.shape[1])


def row_job(left, right, turned):
    out = jax.ShapeDtypeStruct((left.shape[0], right.shape[0 if turned else 1]), BF16)
    work = ROWS_TURNED if turned else ROWS_STRAIGHT
    return work, [left, right], [HBM] * 2, [out], [HBM], row_product_buffers(right, turned)


def table_job(lengths, parents, tokens):
    outs = [jax.ShapeDtypeStruct((8, tokens), jnp.int32), jax.ShapeDtypeStruct((tokens, 128), jnp.int32)]
    outs += [jax.ShapeDtypeStruct((tokens, 128), F32)] * 2
    room = [pltpu.VMEM(out.shape, out.dtype) for out in outs[1:]]
    room += [pltpu.SemaphoreType.DMA((3, tokens // TABLE_ROWS))]
    return table_work, [lengths, parents, rope_freqs(128)], [VMEM] * 3, outs, [VMEM, HBM, HBM, HBM], room


def scatter_kernel(rows, parts, jobs, *refs):
    def take(count):
        nonlocal refs
        taken, refs = refs[:count], refs[count:]
        return taken

    a_refs, w_refs, lefts, rights = take(parts), take(parts), take(jobs), take(jobs)
    (out_ref,), products = take(1), take(jobs)
    core_out, core_in, first_in, next_in, sems = take(5)
    a_bufs, (a_sems,), buffers = take(parts), take(1), refs

    def work(job):
        if job < jobs:
            finish(token_product(lefts[job], rights[job], products[job], *buffers))

    x, core, row = plane_place()
    over_x, over_row, over_core = plane_neighbours(x, core, row)
    half = rows // 2
    width = out_ref.shape[1]
    chunks = width // COLS

    def place(piece, on_core):
        far_x, far_row, part = PIECES[piece]
        bx = x + far_x - 2 * far_x * x
        by = row + far_row - 2 * far_row * row
        return pl.ds(pl.multiple_of(((bx * 2 + on_core) * 2 + by) * rows + part * half, half), half)

    def columns(j):
        return pl.ds(pl.multiple_of(j * COLS, COLS), COLS)

    steps = [(0, True)]
    for piece in range(8):
        steps += [(piece + 1, True)] * (piece < 7) + [(piece, False)]

    def load(step):
        piece, partner_half = steps[step]
        taken = place(piece, 1 - core if partner_half else core)
        return [
            pltpu.make_async_copy(a_ref.at[taken], a_buf.at[step % 2], a_sems.at[step % 2, p])
            for p, (a_ref, a_buf) in enumerate(zip(a_refs, a_bufs))
        ]

    loads = {0: load(0)}
    for copy in loads[0]:
        copy.start()
    enter_plane((over_x, over_row, over_core))

    def partial(slot, j):
        total = None
        for a_buf, w_ref in zip(a_bufs, w_refs):
            term = dot_t(a_buf[slot], w_ref[columns(j), :])
            total = term if total is None else total + term
        return total

    def remote(source, target, slot, device):
        return pltpu.make_async_remote_copy(
            src_ref=source, dst_ref=target, send_sem=sems.at[0, slot], recv_sem=sems.at[1, slot],
            device_id=device, device_id_type=MESH,
        )

    core_copies, first_copies, next_copies = [], [], []
    for step, (piece, partner_half) in enumerate(steps):
        for copy in loads[step]:
            copy.wait()
        if step + 1 < len(steps):
            loads[step + 1] = load(step + 1)
            for copy in loads[step + 1]:
                copy.start()
        if partner_half:

            @pl.loop(0, chunks)
            def _(j, step=step, piece=piece):
                core_out[piece, :, columns(j)] = partial(step % 2, j).astype(BF16)

            core_copies.append(remote(core_out.at[piece], core_in.at[piece], piece, over_core))
            core_copies[-1].start()
            continue
        core_copies[piece].wait_recv()

        @pl.loop(0, chunks)
        def _(j, step=step, piece=piece):
            total = partial(step % 2, j) + core_in[piece, :, columns(j)].astype(F32)
            core_in[piece, :, columns(j)] = total.astype(BF16)

        if piece < 4:
            first_copies.append(
                remote(core_in.at[piece], first_in.at[piece], 8 + piece, over_x if piece % 2 == 0 else over_row)
            )
            first_copies[-1].start()
    for part in range(2):
        first_copies[part].wait_recv()

        @pl.loop(0, chunks)
        def _(j, part=part):
            total = core_in[4 + part, :, columns(j)].astype(F32) + first_in[part, :, columns(j)].astype(F32)
            core_in[4 + part, :, columns(j)] = total.astype(BF16)

        next_copies.append(remote(core_in.at[4 + part], next_in.at[part], 12 + part, over_row if part == 0 else over_x))
        next_copies[-1].start()
    for job in range(jobs):
        work(job)
    for part in range(2):
        first_copies[2 + part].wait_recv()
        next_copies[part].wait_recv()

        @pl.loop(0, chunks)
        def _(j, part=part):
            total = core_in[6 + part, :, columns(j)].astype(F32) + first_in[2 + part, :, columns(j)].astype(F32)
            out_ref[pl.ds(part * half, half), columns(j)] = total + next_in[part, :, columns(j)].astype(F32)

    for copy in core_copies + first_copies + next_copies:
        copy.wait_send()


def plane_scatter(parts, weights, collective_id, jobs=()):
    count = parts[0].shape[0]
    width = weights[0].shape[0]
    rows = count // 8
    half = rows // 2
    vmem, hbm = pl.BlockSpec(memory_space=pltpu.VMEM), pl.BlockSpec(memory_space=pl.ANY)
    lefts, rights = [left for left, _ in jobs], [right for _, right in jobs]
    return pl.pallas_call(
        functools.partial(scatter_kernel, rows, len(parts), len(jobs)),
        in_specs=[hbm] * len(parts) + [vmem] * len(parts) + [hbm] * (2 * len(jobs)),
        out_specs=[vmem] + [hbm] * len(jobs),
        out_shape=[jax.ShapeDtypeStruct((rows, width), F32)]
        + [jax.ShapeDtypeStruct((left.shape[1], right.shape[1]), BF16) for left, right in jobs],
        scratch_shapes=[
            pltpu.VMEM((8, half, width), BF16),
            pltpu.VMEM((8, half, width), BF16),
            pltpu.VMEM((4, half, width), BF16),
            pltpu.VMEM((2, half, width), BF16),
            pltpu.SemaphoreType.DMA((2, 14)),
        ]
        + [pltpu.VMEM((2, half, a.shape[1]), BF16) for a in parts]
        + [pltpu.SemaphoreType.DMA((2, len(parts)))]
        + (product_buffers(rights[0].shape[1]) if jobs else []),
        compiler_params=pltpu.CompilerParams(
            collective_id=collective_id, has_side_effects=True, vmem_limit_bytes=(58 if jobs else 52) << 20
        ),
        cost_estimate=small_cost(),
        name="plane_scatter",
    )(*parts, *weights, *lefts, *rights)


def is_plane():
    return lax.axis_size("ctx") == 4 and lax.axis_size("tensor") == 2


def gather_rows(rows):
    return lax.all_gather(rows, GROUP, axis=0, tiled=True)


def scatter_rows(rows):
    return lax.psum_scatter(rows.astype(BF16), GROUP, scatter_dimension=0, tiled=True).astype(F32)


def gather_now(rows):
    return plane_gather(rows)[0] if is_plane() else gather_rows(rows)


def gather_with_tables(rows, lengths, parents, tokens, width):
    if is_plane():
        return plane_gather(rows, 8, [table_job(lengths, parents, tokens)], (4, 4))
    segment, parent, depth = tree_tables(lengths[0], parents[0], tokens)
    return [gather_rows(rows), *lay_out(segment, parent), *rope_tables(depth, width)]


def gather_with_products(rows, collective_id, token_pairs, row_pairs):
    if is_plane():
        jobs = [token_job(*pair) for pair in token_pairs] + [row_job(*pair) for pair in row_pairs]
        return plane_gather(rows, collective_id, jobs, (4, 4))
    return (
        [gather_rows(rows)]
        + [dot_tn(left, right).astype(BF16) for left, right in token_pairs]
        + [(dot_t if turned else dot_n)(left, right).astype(BF16) for left, right, turned in row_pairs]
    )


def product_scatter(parts, weights, collective_id, jobs=()):
    if is_plane():
        return plane_scatter(parts, weights, collective_id, jobs)
    rows = scatter_rows(dot_t(jnp.concatenate(parts, axis=1), jnp.concatenate(weights, axis=1)))
    return [rows] + [dot_tn(left, right).astype(BF16) for left, right in jobs]


def gather_weight(own):
    return lax.all_gather(own, "fsdp", axis=0, tiled=True)


def scatter_weight(grad):
    return lax.psum_scatter(grad.astype(BF16), "fsdp", scatter_dimension=0, tiled=True)


def swap_rows(part):
    size = lax.axis_size("ctx")
    return lax.all_to_all(part.reshape(size, part.shape[0] // size, -1), "ctx", split_axis=0, concat_axis=0)


def lay_side_by_side(got, count):
    columns = got.shape[2] // count
    return [
        jnp.concatenate([got[j, :, c * columns : (c + 1) * columns] for j in range(got.shape[0])], axis=1).astype(F32)
        for c in range(count)
    ]


def normalize(rows):
    norm_inv = lax.rsqrt(jnp.mean(rows * rows, axis=1, keepdims=True) + EPSILON)
    return (rows * norm_inv, norm_inv)


def norm_backward(grad_rows, scaled, norm_inv, gain):
    weighted = grad_rows * gain[None, :]
    inner = jnp.mean(weighted * scaled, axis=1, keepdims=True)
    return norm_inv * (weighted - scaled * inner)


def body(
    tokens_in,
    attn_gain,
    query_weight,
    key_weight,
    value_weight,
    output_weight,
    mlp_gain,
    gate_weight,
    up_weight,
    down_weight,
    seg_lengths,
    leaf_parent,
    cotangent,
):
    ctx = lax.axis_index("ctx")
    parts = lax.axis_size("ctx")
    tree_len = tokens_in.shape[0] * parts * lax.axis_size("tensor")
    width = query_weight.shape[1] // parts
    units = gate_weight.shape[1] // parts

    def mine(weight, columns):
        return lax.dynamic_slice_in_dim(weight, ctx * columns, columns, 1)

    x_rows = tokens_in.astype(F32)
    attn_scaled, attn_inv = normalize(x_rows)
    w_attn = gather_weight(
        jnp.concatenate([mine(w, width) for w in (query_weight, key_weight, value_weight, output_weight)], axis=1)
    )
    w_gate = gather_weight(mine(gate_weight, units))
    w_down = gather_weight(mine(down_weight, units))
    w_up = gather_weight(mine(up_weight, units))
    attn_in, rows_table, cols_table, cosine, sine = gather_with_tables(
        (attn_scaled * attn_gain[None, :]).astype(BF16), seg_lengths, leaf_parent, tree_len, min(2 * HEAD_DIM, width)
    )
    w_qkv, w_out = w_attn[:, : 3 * width], w_attn[:, 3 * width :]

    qkv = jnp.dot(attn_in, w_qkv, preferred_element_type=F32)
    if is_plane():
        attn_out, lse, query_rows, key_rows, value_rows, cot_all = attention_forward(
            qkv, cosine, sine, rows_table, cols_table, width, cotangent
        )
    else:
        attn_out, lse, query_rows, key_rows, value_rows = attention_forward(
            qkv, cosine, sine, rows_table, cols_table, width
        )
        cot_all = gather_rows(cotangent)
    mid_rows = x_rows + product_scatter([attn_out], [w_out], 1)[0]
    mlp_scaled, mlp_inv = normalize(mid_rows)
    mlp_own = (mlp_scaled * mlp_gain[None, :]).astype(BF16)
    mlp_in, hidden_grad = gather_with_products(mlp_own, 5, [], [(cot_all, w_down, False)])

    gate = jnp.dot(mlp_in, w_gate, preferred_element_type=F32)
    up_proj = jnp.dot(mlp_in, w_up, preferred_element_type=F32)
    sigmoid_gate = jax.nn.sigmoid(gate)
    hidden = (gate * sigmoid_gate * up_proj).astype(BF16)
    hidden_grad = hidden_grad.astype(F32)
    gate_rows_grad = (
        hidden_grad * up_proj * sigmoid_gate * (1.0 + gate * (1.0 - sigmoid_gate))
    ).astype(BF16)
    up_rows_grad = (hidden_grad * gate * sigmoid_gate).astype(BF16)

    mlp_in_grad, down_part = product_scatter(
        [gate_rows_grad, up_rows_grad], [w_gate, w_up], 3, [(cot_all, hidden)]
    )
    down_grad = scatter_weight(down_part)
    mid_grad = cotangent.astype(F32) + norm_backward(mlp_in_grad, mlp_scaled, mlp_inv, mlp_gain)
    mid_all, up_part, gate_part, down_rows = gather_with_products(
        mid_grad.astype(BF16), 4, [(mlp_in, up_rows_grad), (mlp_in, gate_rows_grad)], [(hidden, w_down, True)]
    )
    up_grad = scatter_weight(up_part)
    gate_grad = scatter_weight(gate_part)

    out_heads_grad = jnp.dot(mid_all, w_out, preferred_element_type=F32).astype(BF16)
    output_grad = dot_tn(mid_all, attn_out).astype(BF16)
    out_heads_grad, down_grad = lax.optimization_barrier((out_heads_grad, down_grad))
    if is_plane():
        *pre_grads, down_rows = attention_backward(
            query_rows, key_rows, value_rows, attn_out, out_heads_grad, lse, cosine, sine, rows_table, cols_table, down_rows
        )
    else:
        pre_grads = attention_backward(
            query_rows, key_rows, value_rows, attn_out, out_heads_grad, lse, cosine, sine, rows_table, cols_table
        )
        down_rows = scatter_rows(down_rows)
    block_out = (mid_rows + down_rows.astype(F32)).astype(BF16)
    pre_grads, up_grad, gate_grad = lax.optimization_barrier((pre_grads, up_grad, gate_grad))
    swapped = swap_rows(jnp.concatenate([gate_grad, up_grad, down_grad], axis=1))
    attn_part = jnp.concatenate([dot_tn(attn_in, grad).astype(BF16) for grad in pre_grads] + [output_grad], axis=1)
    pre_grads, attn_part, swapped = lax.optimization_barrier((pre_grads, attn_part, swapped))
    attn_grad = scatter_weight(attn_part)
    (attn_in_grad,) = product_scatter(pre_grads, [w_attn[:, j * width : (j + 1) * width] for j in range(3)], 2)
    attn_in_grad, attn_grad = lax.optimization_barrier((attn_in_grad, attn_grad))
    gate_out, up_out, down_out = lay_side_by_side(swapped, 3)
    query_out, key_out, value_out, output_out = lay_side_by_side(swap_rows(attn_grad), 4)

    def gain_part(pairs, gain):
        held = query_out.shape[0]
        total = sum(
            jnp.sum(lax.dynamic_slice_in_dim(weight, ctx * held, held, 0).astype(F32) * grad, axis=1)
            for weight, grad in pairs
        )
        first = (lax.axis_index("fsdp") * parts + ctx) * held
        return total / lax.dynamic_slice_in_dim(gain, first, held, 0)

    sums = jnp.stack(
        [
            gain_part([(query_weight, query_out), (key_weight, key_out), (value_weight, value_out)], attn_gain),
            gain_part([(gate_weight, gate_out), (up_weight, up_out)], mlp_gain),
        ]
    )
    row, others = lax.axis_index("tensor"), lax.axis_size("tensor")
    kept = sums.shape[1] // others
    if others == 2:
        got = lax.ppermute(lax.dynamic_slice_in_dim(sums, (1 - row) * kept, kept, 1), "tensor", [(0, 1), (1, 0)])
        gain_grads = lax.dynamic_slice_in_dim(sums, row * kept, kept, 1) + got
    else:
        gain_grads = lax.dynamic_slice_in_dim(lax.psum(sums, "tensor"), row * kept, kept, 1)

    attn_back = norm_backward(attn_in_grad, attn_scaled, attn_inv, attn_gain)
    input_grad = (mid_grad + attn_back).astype(BF16)
    return (
        block_out,
        input_grad,
        gain_grads[0],
        query_out,
        key_out,
        value_out,
        output_out,
        gain_grads[1],
        gate_out,
        up_out,
        down_out,
    )


def solution(mesh):
    rows = P(("fsdp", "ctx", "tensor"), None)
    weight = P("fsdp", "tensor")
    gain = P(("fsdp", "ctx", "tensor"))
    grad = P(("fsdp", "ctx"), "tensor")
    in_specs = (
        rows, P(), weight, weight, weight, weight, P(), weight, weight, weight, P("fsdp", None), P("fsdp", None), rows,
    )
    out_specs = (rows, rows, gain, grad, grad, grad, grad, gain, grad, grad, grad)
    return jax.shard_map(body, mesh=mesh, in_specs=in_specs, out_specs=out_specs, check_vma=False)
```

```python
import functools

import jax
import jax.numpy as jnp
import numpy as np
from jax import lax
from jax.experimental import pallas as pl
from jax.experimental.pallas import tpu as pltpu
from jax.sharding import PartitionSpec as P

HEAD_DIM = 64
TRUNK = 2176
MOST_SEG = 128
ROPE_BASE = 130000.0
EPSILON = 1e-05
NEG_LARGE = -1e30
SCALE = HEAD_DIM ** (-0.5)

BQ = 512
BK = 512
GROUP = ("ctx", "tensor")

F32 = jnp.float32
BF16 = jnp.bfloat16


def pick_table(onehot, table):
    return jnp.sum(jnp.where(onehot, table[None, :], 0), axis=1)


def tree_tables(lengths_row, parent_row, tree_len):
    branches = lengths_row.shape[0] - parent_row.shape[0]
    ends = TRUNK + jnp.cumsum(lengths_row)
    starts = ends - lengths_row
    matches = parent_row[:, None] - 1 == jnp.arange(branches, dtype=jnp.int32)[None, :]
    parent_len = jnp.sum(jnp.where(matches, lengths_row[None, :branches], 0), axis=1)
    zero_one = jnp.zeros((1,), jnp.int32)
    seg_start = jnp.concatenate([zero_one, starts])
    seg_base = jnp.concatenate(
        [zero_one, jnp.full((branches,), TRUNK, jnp.int32), TRUNK + parent_len]
    )
    seg_parent = jnp.concatenate([zero_one, jnp.zeros((branches,), jnp.int32), parent_row])
    positions = jnp.arange(tree_len, dtype=jnp.int32)
    above = jnp.sum((ends[None, :] <= positions[:, None]).astype(jnp.int32), axis=1)
    segment = (positions >= TRUNK).astype(jnp.int32) + above
    onehot = segment[:, None] == jnp.arange(seg_start.shape[0], dtype=jnp.int32)[None, :]
    depth = positions - pick_table(onehot, seg_start) + pick_table(onehot, seg_base)
    parent = pick_table(onehot, seg_parent)
    return (segment, parent, depth)


def rope_freqs(width):
    half = HEAD_DIM // 2
    powers = -2.0 * (np.arange(width) % half) / HEAD_DIM
    return np.power(ROPE_BASE, powers).astype(np.float32)[None, :]


def rope_tables(depth, width):
    angles = depth.astype(F32)[:, None] * rope_freqs(width)
    sign = np.where(np.arange(width) % HEAD_DIM < HEAD_DIM // 2, -1.0, 1.0).astype(np.float32)
    return jnp.cos(angles), jnp.sin(angles) * sign[None, :]


def lay_out(segment, parent):
    both = jnp.stack([segment, parent])
    return jnp.pad(both, ((0, 6), (0, 0))), jnp.pad(both.T, ((0, 0), (0, 126)))


TABLE_ROWS = 512
TABLE_STEP = 64


def tables_at(positions, lengths, parents):
    leaves = parents.shape[1]
    branches = lengths.shape[1] - leaves
    zero = jnp.zeros_like(positions)
    segment = jnp.where(positions >= TRUNK, 1, 0)
    parent, depth = zero, positions
    end = jnp.full((1, 1), TRUNK, jnp.int32)
    starts = []
    for s in range(branches + leaves):
        start, end = end, end + lengths[:, s : s + 1]
        inside = (positions >= start) & (positions < end)
        base, above = jnp.full((1, 1), TRUNK, jnp.int32), jnp.zeros((1, 1), jnp.int32)
        if s >= branches:
            above = parents[:, s - branches : s - branches + 1]
            for b in range(branches):
                base = base + jnp.where(above == b + 1, lengths[:, b : b + 1], 0)
        segment = segment + jnp.where(positions >= end, 1, 0)
        parent = jnp.where(inside, above, parent)
        depth = jnp.where(inside, positions - start + base, depth)
    return segment, parent, depth


def sine_cosine(x):
    turns = jnp.floor(x * np.float32(2.0 / np.pi) + 0.5)
    r = x - turns * np.float32(1.5703125)
    r = r - turns * np.float32(4.837512969970703125e-4)
    r = r - turns * np.float32(7.549789954891882e-8)
    z = r * r
    sine = ((np.float32(-1.9515295891e-4) * z + np.float32(8.3321608736e-3)) * z - np.float32(1.6666654611e-1)) * z * r + r
    cosine = (
        (np.float32(2.443315711809948e-5) * z - np.float32(1.388731625493765e-3)) * z + np.float32(4.166664568298827e-2)
    ) * z * z - np.float32(0.5) * z + np.float32(1.0)
    quarter = turns.astype(jnp.int32) & 3
    odd = (quarter & 1) == 1
    first, second = jnp.where(odd, cosine, sine), jnp.where(odd, sine, cosine)
    return jnp.where(quarter >= 2, -first, first), jnp.where((quarter == 1) | (quarter == 2), -second, second)


def table_work(lengths, parents, freqs, rows_ref, cols_ref, cos_ref, sin_ref, cols_buf, cos_buf, sin_buf, sems):
    yield
    tokens = cos_ref.shape[0]
    shape = (8, tokens)
    segment, parent, _ = tables_at(lax.broadcasted_iota(jnp.int32, shape, 1), lengths, parents)
    line = lax.broadcasted_iota(jnp.int32, shape, 0)
    rows_ref[...] = jnp.where(line == 0, segment, jnp.where(line == 1, parent, 0))
    copies = []
    for chunk in range(tokens // TABLE_ROWS):
        rows = pl.ds(chunk * TABLE_ROWS, TABLE_ROWS)

        @pl.loop(0, TABLE_ROWS // TABLE_STEP)
        def _(j, chunk=chunk):
            first = pl.multiple_of(chunk * TABLE_ROWS + j * TABLE_STEP, TABLE_STEP)
            taken = pl.ds(first, TABLE_STEP)
            shape = (TABLE_STEP, 128)
            lane = lax.broadcasted_iota(jnp.int32, shape, 1)
            segment, parent, depth = tables_at(lax.broadcasted_iota(jnp.int32, shape, 0) + first, lengths, parents)
            cols_buf[taken, :] = jnp.where(lane == 0, segment, jnp.where(lane == 1, parent, 0))
            sine, cosine = sine_cosine(depth.astype(F32) * freqs[...])
            cos_buf[taken, :] = cosine
            sin_buf[taken, :] = jnp.where(lane % HEAD_DIM < HEAD_DIM // 2, -sine, sine)

        for kind, (source, target) in enumerate(((cols_buf, cols_ref), (cos_buf, cos_ref), (sin_buf, sin_ref))):
            copies.append(pltpu.make_async_copy(source.at[rows], target.at[rows], sems.at[kind, chunk]))
            copies[-1].start()
        yield
    for copy in copies:
        copy.wait()


MESH = pl.DeviceIdType.MESH


def plane_place():
    ctx, row = lax.axis_index("ctx"), lax.axis_index("tensor")
    x, core = ctx // 2, ctx % 2
    return x, core, row


def plane_neighbours(x, core, row):
    over_x = {"ctx": (1 - x) * 2 + core}
    over_core = {"ctx": x * 2 + 1 - core}
    over_row = {"tensor": 1 - row}
    return over_x, over_row, over_core


def enter_plane(neighbours):
    barrier = pltpu.get_barrier_semaphore()
    for device in neighbours:
        pl.semaphore_signal(barrier, inc=1, device_id=device, device_id_type=MESH)
    pl.semaphore_wait(barrier, 3)


PIECES = ((1, 1, 0), (1, 1, 1), (1, 0, 0), (0, 1, 1), (0, 1, 0), (1, 0, 1), (0, 0, 0), (0, 0, 1))
COLS = 512


class PlaneGather:
    def __init__(self, own_ref, all_ref, local_sem, send_sem, recv_sem):
        self.own_ref, self.all_ref, self.sems = own_ref, all_ref, (local_sem, send_sem, recv_sem)
        self.x, self.core, self.row = plane_place()
        self.devices = plane_neighbours(self.x, self.core, self.row)
        self.rows = own_ref.shape[0]

    def place(self, far_x, far_row, part):
        bx = self.x + far_x - 2 * far_x * self.x
        by = self.row + far_row - 2 * far_row * self.row
        half = self.rows // 2
        return pl.ds(pl.multiple_of(((bx * 2 + self.core) * 2 + by) * self.rows + part * half, half), half)

    def copy(self, slot):
        far_x, far_row, part, device = (
            (0, 0, 0, 1), (0, 0, 1, 1), (1, 0, 1, 1), (0, 0, 1, 0), (0, 0, 0, 0), (0, 1, 0, 0), (0, 0, 0, 2),
            (0, 0, 1, 2), (0, 1, 0, 2), (1, 0, 1, 2), (0, 1, 1, 2), (1, 0, 0, 2), (1, 1, 0, 2), (1, 1, 1, 2),
        )[slot]
        half = self.rows // 2
        target = self.place(far_x, far_row, part)
        own = far_x == 0 and far_row == 0
        source = self.own_ref.at[pl.ds(part * half, half)] if own else self.all_ref.at[target]
        return pltpu.make_async_remote_copy(
            src_ref=source, dst_ref=self.all_ref.at[target], send_sem=self.sems[1].at[slot],
            recv_sem=self.sems[2].at[slot], device_id=self.devices[device], device_id_type=MESH,
        )

    def local(self, part):
        half = self.rows // 2
        return pltpu.make_async_copy(
            self.own_ref.at[pl.ds(part * half, half)], self.all_ref.at[self.place(0, 0, part)], self.sems[0].at[part]
        )

    def start(self):
        enter_plane(self.devices)
        for slot in (0, 3, 1, 4, 6, 7):
            self.copy(slot).start()
        for part in range(2):
            self.local(part).start()

    def forward(self, got, slots):
        self.copy(got).wait_recv()
        for slot in slots:
            self.copy(slot).start()

    def first(self):
        self.forward(0, (5, 8))
        self.forward(3, (2, 9))

    def second(self):
        self.forward(1, (10,))
        self.forward(4, (11,))

    def finish(self):
        self.forward(5, (12,))
        self.forward(2, (13,))
        for slot in range(6, 14):
            self.copy(slot).wait_recv()
        for slot in range(14):
            self.copy(slot).wait_send()
        for part in range(2):
            self.local(part).wait()


def gather_sems():
    return [pltpu.SemaphoreType.DMA((2,)), pltpu.SemaphoreType.DMA((14,)), pltpu.SemaphoreType.DMA((14,))]


class PlaneScatter:
    def __init__(self, part_ref, out_ref, core_in, first_in, next_in, own, total, sems, own_sems):
        self.part_ref, self.out_ref, self.core_in, self.first_in, self.next_in = part_ref, out_ref, core_in, first_in, next_in
        self.own, self.total, self.sems, self.own_sems = own, total, sems, own_sems
        self.x, self.core, self.row = plane_place()
        self.devices = plane_neighbours(self.x, self.core, self.row)
        self.rows = part_ref.shape[0] // 8

    def place(self, piece, on_core):
        far_x, far_row, part = PIECES[piece]
        bx = self.x + far_x - 2 * far_x * self.x
        by = self.row + far_row - 2 * far_row * self.row
        half = self.rows // 2
        return pl.ds(pl.multiple_of(((bx * 2 + on_core) * 2 + by) * self.rows + part * half, half), half)

    def copy(self, slot):
        if slot < 8:
            source, target, device = self.part_ref.at[self.place(slot, 1 - self.core)], self.core_in.at[slot], 2
        elif slot < 12:
            source, target, device = self.core_in.at[slot - 8], self.first_in.at[slot - 8], slot % 2
        else:
            source, target, device = self.core_in.at[slot - 8], self.next_in.at[slot - 12], 1 - slot % 2
        return pltpu.make_async_remote_copy(
            src_ref=source, dst_ref=target, send_sem=self.sems.at[0, slot], recv_sem=self.sems.at[1, slot],
            device_id=self.devices[device], device_id_type=MESH,
        )

    def load(self, piece):
        return pltpu.make_async_copy(
            self.part_ref.at[self.place(piece, self.core)], self.own.at[piece % 4], self.own_sems.at[piece % 4]
        )

    def add(self, target, where, *others):
        @pl.loop(0, target.shape[-1] // COLS)
        def _(j):
            columns = pl.ds(pl.multiple_of(j * COLS, COLS), COLS)
            total = sum(ref[slot, :, columns].astype(F32) for ref, slot in others)
            target[where, :, columns] = total.astype(target.dtype)

    def start(self):
        enter_plane(self.devices)
        for slot in range(8):
            self.copy(slot).start()
        for piece in range(4):
            self.load(piece).start()

    def first(self):
        for piece in range(4):
            self.load(piece).wait()
            self.copy(piece).wait_recv()
            self.add(self.core_in, piece, (self.own, piece), (self.core_in, piece))
            self.copy(8 + piece).start()
        for piece in range(4, 8):
            self.load(piece).start()

    def second(self):
        for piece in range(4, 8):
            self.load(piece).wait()
            self.copy(piece).wait_recv()
            self.add(self.core_in, piece, (self.own, piece - 4), (self.core_in, piece))

    def third(self):
        for part in range(2):
            self.copy(8 + part).wait_recv()
            self.add(self.core_in, 4 + part, (self.core_in, 4 + part), (self.first_in, part))
            self.copy(12 + part).start()

    def finish(self):
        half = self.rows // 2
        for part in range(2):
            self.copy(10 + part).wait_recv()
            self.copy(12 + part).wait_recv()
            self.add(self.total, part, (self.core_in, 6 + part), (self.first_in, 2 + part), (self.next_in, part))
        stores = [
            pltpu.make_async_copy(
                self.total.at[part], self.out_ref.at[pl.ds(part * half, half)], self.own_sems.at[part]
            )
            for part in range(2)
        ]
        for store in stores:
            store.start()
        for slot in range(14):
            self.copy(slot).wait_send()
        for store in stores:
            store.wait()


def scatter_scratch(rows, width):
    half = rows // 2
    return [
        pltpu.VMEM((8, half, width), BF16),
        pltpu.VMEM((4, half, width), BF16),
        pltpu.VMEM((2, half, width), BF16),
        pltpu.VMEM((4, half, width), BF16),
        pltpu.VMEM((2, half, width), BF16),
        pltpu.SemaphoreType.DMA((2, 14)),
        pltpu.SemaphoreType.DMA((4,)),
    ]


def at_step(step, total, places):
    for place, phase in places:

        @pl.when(step == place)
        def _(phase=phase):
            phase()


def partner(x):
    half = HEAD_DIM // 2
    width = x.shape[1]
    if width == HEAD_DIM:
        return jnp.concatenate([x[:, half:], x[:, :half]], axis=1)
    lane = lax.broadcasted_iota(jnp.int32, x.shape, 1)
    ahead = pltpu.roll(x, width - half, 1)
    behind = pltpu.roll(x, half, 1)
    return jnp.where(lane % HEAD_DIM < half, ahead, behind)


def head_mask(shape, head):
    lane = lax.broadcasted_iota(jnp.int32, shape, 1)
    return lane // HEAD_DIM == head


def dot_t(a, b):
    return lax.dot_general(a, b, (((1,), (1,)), ((), ())), preferred_element_type=F32)


def dot_n(a, b):
    return lax.dot_general(a, b, (((1,), (0,)), ((), ())), preferred_element_type=F32)


def dot_tn(a, b):
    return lax.dot_general(a, b, (((0,), (0,)), ((), ())), preferred_element_type=F32)


def key_plan(i, tile):
    base = TRUNK // BK * BK
    branch_end = TRUNK + 4 * MOST_SEG
    first_tree = base // BQ
    mixed_end = -(-(branch_end + MOST_SEG) // BQ)
    chunks = jnp.minimum(i * BQ, base) // BK

    @pl.when(i < first_tree)
    def _():
        @pl.loop(0, chunks)
        def _(j):
            start = pl.multiple_of(j * BK, BK)
            tile(start, BK, 0, start)

    @pl.when(i >= first_tree)
    def _():
        tile(0, base, 0, 0)

    @pl.when(i < first_tree)
    def _():
        start = pl.multiple_of(chunks * BK, BK)
        tile(start, BK, 1, start)

    for block in range(first_tree, mixed_end):

        @pl.when(i == block)
        def _(block=block):
            tile(base, (block + 1) * BQ - base, 2, base)

    @pl.when(i >= mixed_end)
    def _():
        tile(base, branch_end - base, 3, base)
        tile(pl.multiple_of(i * BQ - MOST_SEG, MOST_SEG), BQ + MOST_SEG, 4, branch_end)


def most_keys():
    return TRUNK + 4 * MOST_SEG + BQ + MOST_SEG


def seen_mask(kind, q_at, k_at, seg_q, par_q, seg_k):
    if kind == 3:
        return (seg_k == 0) | (seg_k == par_q)
    causal = k_at <= q_at
    if kind == 1:
        return causal
    if kind == 4:
        return causal & (seg_k == seg_q)
    return causal & ((seg_k == 0) | (seg_k == seg_q) | (seg_k == par_q))


def fwd_kernel(heads, hosts, *refs):
    if not hosts:
        return fwd_work(heads, *refs)
    gather = PlaneGather(refs[7], refs[13], *refs[-3:])
    step, total = pl.program_id(0) * pl.num_programs(1) + pl.program_id(1), 16
    at_step(step, total, ((0, gather.start), (6, gather.first), (12, gather.second)))
    fwd_work(heads, *refs[:7], *refs[8:13], *refs[14:-3])
    at_step(step, total, ((total - 1, gather.finish),))


def fwd_work(
    heads, q_ref, k_ref, v_ref, cos_ref, sin_ref, rows_ref, cols_ref,
    o_ref, lse_ref, qr_ref, kr_ref, vr_ref, kt_ref, va_ref, s_ref, m_ref, acc_ref,
):
    i = pl.program_id(1)
    wide = 2 * HEAD_DIM

    @pl.when(i == 0)
    def _():
        @pl.loop(0, k_ref.shape[0] // BK)
        def _(j):
            rows = pl.ds(pl.multiple_of(j * BK, BK), BK)
            k = k_ref[rows, :]
            k = (k * cos_ref[rows, :] + partner(k) * sin_ref[rows, :]).astype(BF16)
            kr_ref[rows, :] = k
            kt_ref[:, rows] = jnp.transpose(k)
            v = v_ref[rows, :].astype(BF16)
            vr_ref[rows, :] = v
            if heads == 1:
                va_ref[0, rows, :] = jnp.concatenate([v, jnp.ones_like(v)], axis=1)
            else:
                for h in range(heads):
                    va_ref[h, rows, :] = jnp.where(head_mask(v.shape, h), v, jnp.ones_like(v))

    rows = pl.ds(pl.multiple_of(i * BQ, BQ), BQ)
    q = q_ref[...]
    q = (q * cos_ref[rows, :] + partner(q) * sin_ref[rows, :]).astype(BF16)
    qr_ref[...] = q
    q = q * jnp.asarray(SCALE, BF16)
    q_heads = [jnp.where(head_mask(q.shape, h), q, jnp.zeros_like(q)) for h in range(heads)]
    m_ref[...] = jnp.full_like(m_ref, NEG_LARGE)
    acc_ref[...] = jnp.zeros_like(acc_ref)

    def score_tile(start, width, kind, place):
        keys = pl.ds(start, width)
        k = kt_ref[:, keys]
        seen = None
        if kind != 0:
            shape = (BQ, width)
            seen = seen_mask(
                kind,
                lax.broadcasted_iota(jnp.int32, shape, 0) + i * BQ,
                lax.broadcasted_iota(jnp.int32, shape, 1) + start,
                cols_ref[:, 0:1], cols_ref[:, 1:2], rows_ref[0:1, keys],
            )
        for h in range(heads):
            s = dot_n(q_heads[h], k)
            if seen is not None:
                s = jnp.where(seen, s, NEG_LARGE)
            s_ref[h, :, pl.ds(place, width)] = s
            largest = m_ref[h]
            for c in range(width // 128):
                largest = jnp.maximum(largest, s[:, c * 128 : (c + 1) * 128])
            m_ref[h] = largest

    key_plan(i, score_tile)
    for h in range(heads):
        m_ref[h] = jnp.broadcast_to(jnp.max(m_ref[h], axis=1, keepdims=True), (BQ, 128))

    def value_tile(start, width, kind, place):
        keys = pl.ds(start, width)
        for h in range(heads):
            m = m_ref[h]
            parts = [
                jnp.exp(s_ref[h, :, pl.ds(place + c * 128, 128)] - m).astype(BF16) for c in range(width // 128)
            ]
            acc_ref[h] += dot_n(jnp.concatenate(parts, axis=1), va_ref[h, keys, :])

    key_plan(i, value_tile)
    out, lse = None, None
    for h in range(heads):
        acc = acc_ref[h]
        part = acc / pltpu.roll(acc, HEAD_DIM, 1)
        stat = m_ref[h] + jnp.log(jnp.broadcast_to(acc[:, (1 - h) * HEAD_DIM : (1 - h) * HEAD_DIM + 1], (BQ, wide)))
        mask = head_mask((BQ, wide), h)
        out = part if h == 0 else jnp.where(mask, part, out)
        lse = stat if h == 0 else jnp.where(mask, stat, lse)
    o_ref[...] = out[:, : heads * HEAD_DIM].astype(BF16)
    turned = jnp.transpose(lse)
    for h in range(heads):
        lse_ref[0, h : h + 1, :] = turned[h * HEAD_DIM : h * HEAD_DIM + 1, :]


def bwd_kernel(heads, hosts, *refs):
    if not hosts:
        return bwd_work(heads, *refs)
    scatter = PlaneScatter(refs[10], refs[12], *refs[-7:])
    step, total = pl.program_id(0) * pl.num_programs(1) + pl.program_id(1), 16
    at_step(
        step, total, ((0, scatter.start), (3, scatter.first), (5, scatter.second), (7, scatter.third))
    )
    bwd_work(heads, *refs[:10], *refs[13:-7], together=refs[11])
    at_step(step, total, ((total - 1, scatter.finish),))


def bwd_work(
    heads, q_ref, k_ref, v_ref, o_ref, do_ref, lse_ref, cos_ref, sin_ref, rows_ref, cols_ref,
    *refs, together=None,
):
    if together is None:
        dq_ref, dk_ref, dv_ref, dq_acc, dk_acc, dv_acc = refs
    else:
        dq_acc, dk_acc, dv_acc, dq_ref, dk_ref, dv_ref, out_sems = refs
    i = pl.program_id(1)

    def store(kind, source, rows):
        groups, width = pl.num_programs(0), source.shape[1]
        columns = pl.ds(pl.multiple_of((kind * groups + pl.program_id(0)) * width, width), width)
        return pltpu.make_async_copy(source, together.at[rows, columns], out_sems.at[kind])

    @pl.when(i == 0)
    def _():
        dk_acc[...] = jnp.zeros_like(dk_acc)
        dv_acc[...] = jnp.zeros_like(dv_acc)

    q = q_ref[...]
    scaled = q * jnp.asarray(SCALE, BF16)
    do = do_ref[...]
    product = jnp.transpose(do.astype(F32) * o_ref[...].astype(F32))
    zero = jnp.zeros_like(q)
    masks = [head_mask(q.shape, h) for h in range(heads)]
    q_heads = [jnp.where(m, scaled, zero) for m in masks]
    do_heads = [jnp.where(m, do, zero) for m in masks]
    deltas = [
        jnp.sum(product[h * HEAD_DIM : (h + 1) * HEAD_DIM, :], axis=0, keepdims=True) for h in range(heads)
    ]
    lses = [lse_ref[0, h : h + 1, :] for h in range(heads)]
    q_turned = [jnp.transpose(x) for x in q_heads]
    do_turned = [jnp.transpose(x) for x in do_heads]
    q_stack = jnp.concatenate(q_heads, axis=0)
    do_stack = jnp.concatenate(do_heads, axis=0)
    dq_acc[...] = jnp.zeros_like(dq_acc)

    def tile(start, width, kind, place):
        keys = pl.ds(start, width)
        k = k_ref[keys, :]
        v = v_ref[keys, :]
        seen = None
        if kind != 0:
            shape = (width, BQ)
            seen = seen_mask(
                kind,
                lax.broadcasted_iota(jnp.int32, shape, 1) + i * BQ,
                lax.broadcasted_iota(jnp.int32, shape, 0) + start,
                rows_ref[0:1, :], rows_ref[1:2, :], cols_ref[keys, 0:1],
            )
        probs, grads, k_heads = [], [], []
        for h in range(heads):
            s = dot_n(k, q_turned[h])
            p = jnp.exp(s - lses[h])
            if seen is not None:
                p = jnp.where(seen, p, 0.0)
            dp = dot_n(v, do_turned[h])
            probs.append(p.astype(BF16))
            grads.append((p * (dp - deltas[h])).astype(BF16))
            k_heads.append(jnp.where(head_mask(k.shape, h), k, jnp.zeros_like(k)))
        grad_row = jnp.concatenate(grads, axis=1)
        dv_acc[keys, :] += dot_n(jnp.concatenate(probs, axis=1), do_stack)
        dk_acc[keys, :] += dot_n(grad_row, q_stack)
        dq_acc[...] += dot_tn(jnp.concatenate(grads, axis=0), jnp.concatenate(k_heads, axis=0))

    key_plan(i, tile)
    dq = dq_acc[...] * SCALE
    rows = pl.ds(pl.multiple_of(i * BQ, BQ), BQ)
    dq = (dq * cos_ref[rows, :] - partner(dq) * sin_ref[rows, :]).astype(BF16)
    dq_ref[...] = dq
    if together is not None:
        copy = store(0, dq_ref, rows)
        copy.start()
        copy.wait()

    @pl.when(i == pl.num_programs(1) - 1)
    def _():
        @pl.loop(0, dk_acc.shape[0] // BK)
        def _(j):
            rows = pl.ds(pl.multiple_of(j * BK, BK), BK)
            dk = dk_acc[rows, :]
            dk_ref[rows, :] = (dk * cos_ref[rows, :] - partner(dk) * sin_ref[rows, :]).astype(BF16)
            dv_ref[rows, :] = dv_acc[rows, :].astype(BF16)

        if together is not None:
            every = pl.ds(0, dk_acc.shape[0])
            copies = [store(1, dk_ref, every), store(2, dv_ref, every)]
            for copy in copies:
                copy.start()
            for copy in copies:
                copy.wait()


def small_cost():
    return pl.CostEstimate(flops=1 << 20, bytes_accessed=1 << 20, transcendentals=0)


def attention_forward(qkv, cosine, sine, rows_table, cols_table, width, hosted=None):
    tree_len = qkv.shape[0]
    gw = min(2 * HEAD_DIM, width)
    groups, heads = width // gw, gw // HEAD_DIM
    row_block = pl.BlockSpec((BQ, gw), lambda g, i: (i, g))
    table = pl.BlockSpec((tree_len, gw), lambda g, i: (0, 0))
    full = pl.BlockSpec((tree_len, gw), lambda g, i: (0, g))
    act = jax.ShapeDtypeStruct((tree_len, width), BF16)
    if width % 128 == 0:
        queries, keys, values, step = qkv, qkv, qkv, groups
    else:
        queries, keys, values = jnp.split(qkv, 3, axis=1)
        step = 0
    hosts = hosted is not None
    hbm = pl.BlockSpec(memory_space=pl.ANY)
    return pl.pallas_call(
        functools.partial(fwd_kernel, heads, hosts),
        grid=(groups, tree_len // BQ),
        in_specs=[
            row_block,
            pl.BlockSpec((tree_len, gw), lambda g, i: (0, step + g)),
            pl.BlockSpec((tree_len, gw), lambda g, i: (0, 2 * step + g)),
            table,
            table,
            pl.BlockSpec((8, tree_len), lambda g, i: (0, 0)),
            pl.BlockSpec((BQ, 128), lambda g, i: (i, 0)),
        ]
        + [hbm] * hosts,
        out_specs=[row_block, pl.BlockSpec((1, heads, BQ), lambda g, i: (g, 0, i)), row_block, full, full] + [hbm] * hosts,
        out_shape=[act, jax.ShapeDtypeStruct((groups, heads, tree_len), F32), act, act, act]
        + ([jax.ShapeDtypeStruct((8 * hosted.shape[0], hosted.shape[1]), BF16)] if hosts else []),
        scratch_shapes=[
            pltpu.VMEM((gw, tree_len), BF16),
            pltpu.VMEM((heads, tree_len, 128), BF16),
            pltpu.VMEM((heads, BQ, most_keys()), F32),
            pltpu.VMEM((heads, BQ, 128), F32),
            pltpu.VMEM((heads, BQ, 128), F32),
        ]
        + (gather_sems() if hosts else []),
        compiler_params=pltpu.CompilerParams(
            vmem_limit_bytes=56 << 20, collective_id=6 if hosts else None, has_side_effects=hosts
        ),
        cost_estimate=small_cost(),
        name="tree_attention_forward",
    )(queries, keys, values, cosine, sine, rows_table, cols_table, *([hosted] if hosts else []))


def attention_backward(q, k, v, out, grad, lse, cosine, sine, rows_table, cols_table, hosted=None):
    tree_len, width = q.shape
    gw = min(2 * HEAD_DIM, width)
    groups, heads = width // gw, gw // HEAD_DIM
    row_block = pl.BlockSpec((BQ, gw), lambda g, i: (i, g))
    table = pl.BlockSpec((tree_len, gw), lambda g, i: (0, 0))
    full = pl.BlockSpec((tree_len, gw), lambda g, i: (0, g))
    act = jax.ShapeDtypeStruct((tree_len, width), BF16)
    hosts = hosted is not None
    hbm = pl.BlockSpec(memory_space=pl.ANY)
    return pl.pallas_call(
        functools.partial(bwd_kernel, heads, hosts),
        grid=(groups, tree_len // BQ),
        in_specs=[
            row_block, full, full, row_block, row_block,
            pl.BlockSpec((1, heads, BQ), lambda g, i: (g, 0, i)),
            table, table,
            pl.BlockSpec((8, BQ), lambda g, i: (0, i)),
            pl.BlockSpec((tree_len, 128), lambda g, i: (0, 0)),
        ]
        + [hbm] * hosts,
        out_specs=[hbm] * 2 if hosts else [row_block, full, full],
        out_shape=[
            jax.ShapeDtypeStruct((tree_len, 3 * width), BF16),
            jax.ShapeDtypeStruct((hosted.shape[0] // 8, hosted.shape[1]), BF16),
        ]
        if hosts
        else [act, act, act],
        scratch_shapes=[
            pltpu.VMEM((BQ, gw), F32),
            pltpu.VMEM((tree_len, gw), F32),
            pltpu.VMEM((tree_len, gw), F32),
        ]
        + (
            [pltpu.VMEM((rows, gw), BF16) for rows in (BQ, tree_len, tree_len)]
            + [pltpu.SemaphoreType.DMA((3,))]
            + scatter_scratch(hosted.shape[0] // 8, hosted.shape[1])
            if hosts
            else []
        ),
        compiler_params=pltpu.CompilerParams(
            vmem_limit_bytes=60 << 20, collective_id=7 if hosts else None, has_side_effects=hosts
        ),
        cost_estimate=small_cost(),
        name="tree_attention_backward",
    )(q, k, v, out, grad, lse, cosine, sine, rows_table, cols_table, *([hosted] if hosts else []))


TOKENS_AT_ONCE = 2048
LEFT_AT_ONCE = 512
STEP = 512


def product_buffers(columns):
    return [
        pltpu.VMEM((2, TOKENS_AT_ONCE, LEFT_AT_ONCE), BF16),
        pltpu.VMEM((2 * TOKENS_AT_ONCE, columns), BF16),
        pltpu.VMEM((LEFT_AT_ONCE, columns), F32),
        pltpu.VMEM((LEFT_AT_ONCE, columns), BF16),
        pltpu.SemaphoreType.DMA((4,)),
    ]


def token_product(left_ref, right_ref, out_ref, left_buf, right_buf, total, out_buf, sems):
    tokens = left_ref.shape[0]
    parts, groups = tokens // TOKENS_AT_ONCE, left_ref.shape[1] // LEFT_AT_ONCE

    def load(step):
        group, part = step // parts, step % parts
        source = left_ref.at[
            pl.ds(part * TOKENS_AT_ONCE, TOKENS_AT_ONCE), pl.ds(group * LEFT_AT_ONCE, LEFT_AT_ONCE)
        ]
        return pltpu.make_async_copy(source, left_buf.at[step % 2], sems.at[step % 2])

    def store(group):
        return pltpu.make_async_copy(out_buf, out_ref.at[pl.ds(group * LEFT_AT_ONCE, LEFT_AT_ONCE)], sems.at[3])

    whole = pltpu.make_async_copy(right_ref, right_buf, sems.at[2])
    whole.start()
    load(0).start()
    yield
    whole.wait()
    for group in range(groups):
        for part in range(parts):
            step = group * parts + part
            load(step).wait()
            if step + 1 < groups * parts:
                load(step + 1).start()
            if part == 0:
                total[...] = jnp.zeros_like(total)

            @pl.loop(0, TOKENS_AT_ONCE // STEP)
            def _(j, step=step, part=part):
                left = left_buf[step % 2, pl.ds(pl.multiple_of(j * STEP, STEP), STEP), :]
                right = right_buf[pl.ds(pl.multiple_of(part * TOKENS_AT_ONCE + j * STEP, STEP), STEP), :]
                total[...] += dot_tn(left, right)

        if group > 0:
            store(group - 1).wait()
        out_buf[...] = total[...].astype(BF16)
        store(group).start()
        yield
    store(groups - 1).wait()


def finish(product):
    for _ in product:
        pass


def pair_product(left_ref, first_ref, second_ref, out_first, out_second, left_buf, right_buf, total, out_buf, sems):
    tokens, columns = first_ref.shape
    parts, groups = tokens // TOKENS_AT_ONCE, left_ref.shape[1] // LEFT_AT_ONCE
    sides = [pl.ds(0, columns), pl.ds(columns, columns)]

    def load(step):
        group, part = step // parts, step % parts
        source = left_ref.at[
            pl.ds(part * TOKENS_AT_ONCE, TOKENS_AT_ONCE), pl.ds(group * LEFT_AT_ONCE, LEFT_AT_ONCE)
        ]
        return pltpu.make_async_copy(source, left_buf.at[step % 2], sems.at[step % 2])

    def stores(group):
        rows = pl.ds(group * LEFT_AT_ONCE, LEFT_AT_ONCE)
        return [
            pltpu.make_async_copy(out_buf.at[:, side], out_ref.at[rows], sems.at[4 + n])
            for n, (side, out_ref) in enumerate(zip(sides, (out_first, out_second)))
        ]

    wholes = [
        pltpu.make_async_copy(ref, right_buf.at[:, side], sems.at[2 + n])
        for n, (side, ref) in enumerate(zip(sides, (first_ref, second_ref)))
    ]
    load(0).start()
    for copy in wholes:
        copy.start()
    yield
    for copy in wholes:
        copy.wait()
    for group in range(groups):
        for part in range(parts):
            step = group * parts + part
            load(step).wait()
            if step + 1 < groups * parts:
                load(step + 1).start()
            if part == 0:
                total[...] = jnp.zeros_like(total)

            @pl.loop(0, TOKENS_AT_ONCE // STEP)
            def _(j, step=step, part=part):
                left = left_buf[step % 2, pl.ds(pl.multiple_of(j * STEP, STEP), STEP), :]
                right = right_buf[pl.ds(pl.multiple_of(part * TOKENS_AT_ONCE + j * STEP, STEP), STEP), :]
                total[...] += dot_tn(left, right)

        if group > 0:
            for copy in stores(group - 1):
                copy.wait()
        out_buf[...] = total[...].astype(BF16)
        for copy in stores(group):
            copy.start()
        yield
    for copy in stores(groups - 1):
        copy.wait()


def cut_columns(*refs):
    count = (len(refs) - 1) // 2
    sources, targets, sems = refs[:count], refs[count:-1], refs[-1]
    copies = []
    for n, (source, target) in enumerate(zip(sources, targets)):
        columns = target.shape[1]
        taken = pl.ds(pl.multiple_of(lax.axis_index("ctx") * columns, columns), columns)
        copies.append(pltpu.make_async_copy(source.at[:, taken], target, sems.at[n]))
        copies[-1].start()
    yield
    for copy in copies:
        copy.wait()


def row_product(turned, left_ref, right_ref, out_ref, left_buf, right_buf, out_buf, sems):
    groups = left_ref.shape[0] // LEFT_AT_ONCE

    def rows(group):
        return pl.ds(group * LEFT_AT_ONCE, LEFT_AT_ONCE)

    def load(group):
        return pltpu.make_async_copy(left_ref.at[rows(group)], left_buf.at[group % 2], sems.at[group % 2])

    def store(group):
        return pltpu.make_async_copy(out_buf.at[group % 2], out_ref.at[rows(group)], sems.at[3 + group % 2])

    whole = pltpu.make_async_copy(right_ref, right_buf, sems.at[2])
    whole.start()
    load(0).start()
    yield
    whole.wait()
    for group in range(groups):
        load(group).wait()
        if group + 1 < groups:
            load(group + 1).start()
        if group > 1:
            store(group - 2).wait()

        @pl.loop(0, out_ref.shape[1] // STEP)
        def _(j, group=group):
            columns = pl.ds(pl.multiple_of(j * STEP, STEP), STEP)
            if turned:
                part = dot_t(left_buf[group % 2], right_buf[columns, :])
            else:
                part = dot_n(left_buf[group % 2], right_buf[:, columns])
            out_buf[group % 2, :, columns] = part.astype(BF16)

        store(group).start()
        yield
    for group in range(max(0, groups - 2), groups):
        store(group).wait()


def row_product_buffers(right, turned):
    return [
        pltpu.VMEM((2, LEFT_AT_ONCE, right.shape[1 if turned else 0]), BF16),
        pltpu.VMEM(right.shape, BF16),
        pltpu.VMEM((2, LEFT_AT_ONCE, right.shape[0 if turned else 1]), BF16),
        pltpu.SemaphoreType.DMA((5,)),
    ]


def gather_kernel(works, counts, paces, *refs):
    def take(count):
        nonlocal refs
        taken, refs = refs[:count], refs[count:]
        return taken

    (own_ref,) = take(1)
    inputs = [take(count[0]) for count in counts]
    (all_ref,) = take(1)
    outputs = [take(count[1]) for count in counts]
    gather = PlaneGather(own_ref, all_ref, *take(3))
    buffers, held = [], {}
    for work, count in zip(works, counts):
        if work not in held:
            held[work] = take(count[2])
        buffers.append(held[work])

    def all_work():
        started = [work(*given, *wanted, *room) for work, given, wanted, room in zip(works, inputs, outputs, buffers)]
        for one in started:
            next(one)
        for one in started:
            yield from one

    going = all_work()

    def some(count):
        for _ in range(count):
            next(going, None)

    gather.start()
    some(paces[0])
    gather.first()
    some(paces[1])
    gather.second()
    finish(going)
    gather.finish()


def plane_gather(rows, collective_id=0, jobs=(), paces=(0, 0)):
    count, width = rows.shape
    hbm = pl.BlockSpec(memory_space=pl.ANY)
    scratch, held = gather_sems(), set()
    for work, _, _, _, _, buffers in jobs:
        if work not in held:
            held.add(work)
            scratch += buffers
    return pl.pallas_call(
        functools.partial(
            gather_kernel,
            [job[0] for job in jobs],
            [(len(job[1]), len(job[3]), len(job[5])) for job in jobs],
            paces,
        ),
        in_specs=[hbm] + [spec for job in jobs for spec in job[2]],
        out_specs=[hbm] + [spec for job in jobs for spec in job[4]],
        out_shape=[jax.ShapeDtypeStruct((8 * count, width), rows.dtype)] + [out for job in jobs for out in job[3]],
        scratch_shapes=scratch,
        compiler_params=pltpu.CompilerParams(
            collective_id=collective_id, has_side_effects=True, vmem_limit_bytes=(48 << 20) if jobs else None
        ),
        cost_estimate=small_cost(),
        name="plane_gather",
    )(rows, *[value for job in jobs for value in job[1]])


HBM = pl.BlockSpec(memory_space=pl.ANY)
VMEM = pl.BlockSpec(memory_space=pltpu.VMEM)
ROWS_TURNED = functools.partial(row_product, True)
ROWS_STRAIGHT = functools.partial(row_product, False)


def token_job(left, right):
    out = jax.ShapeDtypeStruct((left.shape[1], right.shape[1]), BF16)
    return token_product, [left, right], [HBM] * 2, [out], [HBM], product_buffers(right.shape[1])


def pair_job(left, first, second):
    columns = first.shape[1]
    out = jax.ShapeDtypeStruct((left.shape[1], columns), BF16)
    room = [
        pltpu.VMEM((2, TOKENS_AT_ONCE, LEFT_AT_ONCE), BF16),
        pltpu.VMEM((left.shape[0], 2 * columns), BF16),
        pltpu.VMEM((LEFT_AT_ONCE, 2 * columns), F32),
        pltpu.VMEM((LEFT_AT_ONCE, 2 * columns), BF16),
        pltpu.SemaphoreType.DMA((6,)),
    ]
    return pair_product, [left, first, second], [HBM] * 3, [out] * 2, [HBM] * 2, room


def cut_job(weights, parts):
    outs = [jax.ShapeDtypeStruct((w.shape[0], w.shape[1] // parts), w.dtype) for w in weights]
    return cut_columns, list(weights), [HBM] * len(weights), outs, [HBM] * len(weights), [pltpu.SemaphoreType.DMA((len(weights),))]


def row_job(left, right, turned):
    out = jax.ShapeDtypeStruct((left.shape[0], right.shape[0 if turned else 1]), BF16)
    work = ROWS_TURNED if turned else ROWS_STRAIGHT
    return work, [left, right], [HBM] * 2, [out], [HBM], row_product_buffers(right, turned)


def table_job(lengths, parents, tokens):
    outs = [jax.ShapeDtypeStruct((8, tokens), jnp.int32), jax.ShapeDtypeStruct((tokens, 128), jnp.int32)]
    outs += [jax.ShapeDtypeStruct((tokens, 128), F32)] * 2
    room = [pltpu.VMEM(out.shape, out.dtype) for out in outs[1:]]
    room += [pltpu.SemaphoreType.DMA((3, tokens // TABLE_ROWS))]
    return table_work, [lengths, parents, rope_freqs(128)], [VMEM] * 3, outs, [VMEM, HBM, HBM, HBM], room


def scatter_kernel(rows, parts, jobs, *refs):
    def take(count):
        nonlocal refs
        taken, refs = refs[:count], refs[count:]
        return taken

    a_refs, w_refs, lefts, rights = take(parts), take(parts), take(jobs), take(jobs)
    (out_ref,), products = take(1), take(jobs)
    core_out, core_in, first_in, next_in, sems = take(5)
    a_bufs, (a_sems,), buffers = take(parts), take(1), refs

    def work(job):
        if job < jobs:
            finish(token_product(lefts[job], rights[job], products[job], *buffers))

    x, core, row = plane_place()
    over_x, over_row, over_core = plane_neighbours(x, core, row)
    half = rows // 2
    width = out_ref.shape[1]
    chunks = width // COLS

    def place(piece, on_core):
        far_x, far_row, part = PIECES[piece]
        bx = x + far_x - 2 * far_x * x
        by = row + far_row - 2 * far_row * row
        return pl.ds(pl.multiple_of(((bx * 2 + on_core) * 2 + by) * rows + part * half, half), half)

    def columns(j):
        return pl.ds(pl.multiple_of(j * COLS, COLS), COLS)

    steps = [(0, True)]
    for piece in range(8):
        steps += [(piece + 1, True)] * (piece < 7) + [(piece, False)]

    def load(step):
        piece, partner_half = steps[step]
        taken = place(piece, 1 - core if partner_half else core)
        return [
            pltpu.make_async_copy(a_ref.at[taken], a_buf.at[step % 2], a_sems.at[step % 2, p])
            for p, (a_ref, a_buf) in enumerate(zip(a_refs, a_bufs))
        ]

    loads = {0: load(0)}
    for copy in loads[0]:
        copy.start()
    enter_plane((over_x, over_row, over_core))

    def partial(slot, j):
        total = None
        for a_buf, w_ref in zip(a_bufs, w_refs):
            term = dot_t(a_buf[slot], w_ref[columns(j), :])
            total = term if total is None else total + term
        return total

    def remote(source, target, slot, device):
        return pltpu.make_async_remote_copy(
            src_ref=source, dst_ref=target, send_sem=sems.at[0, slot], recv_sem=sems.at[1, slot],
            device_id=device, device_id_type=MESH,
        )

    core_copies, first_copies, next_copies = [], [], []
    for step, (piece, partner_half) in enumerate(steps):
        for copy in loads[step]:
            copy.wait()
        if step + 1 < len(steps):
            loads[step + 1] = load(step + 1)
            for copy in loads[step + 1]:
                copy.start()
        if partner_half:

            @pl.loop(0, chunks)
            def _(j, step=step, piece=piece):
                core_out[piece, :, columns(j)] = partial(step % 2, j).astype(BF16)

            core_copies.append(remote(core_out.at[piece], core_in.at[piece], piece, over_core))
            core_copies[-1].start()
            continue
        core_copies[piece].wait_recv()

        @pl.loop(0, chunks)
        def _(j, step=step, piece=piece):
            total = partial(step % 2, j) + core_in[piece, :, columns(j)].astype(F32)
            core_in[piece, :, columns(j)] = total.astype(BF16)

        if piece < 4:
            first_copies.append(
                remote(core_in.at[piece], first_in.at[piece], 8 + piece, over_x if piece % 2 == 0 else over_row)
            )
            first_copies[-1].start()
    for part in range(2):
        first_copies[part].wait_recv()

        @pl.loop(0, chunks)
        def _(j, part=part):
            total = core_in[4 + part, :, columns(j)].astype(F32) + first_in[part, :, columns(j)].astype(F32)
            core_in[4 + part, :, columns(j)] = total.astype(BF16)

        next_copies.append(remote(core_in.at[4 + part], next_in.at[part], 12 + part, over_row if part == 0 else over_x))
        next_copies[-1].start()
    for job in range(jobs):
        work(job)
    for part in range(2):
        first_copies[2 + part].wait_recv()
        next_copies[part].wait_recv()

        @pl.loop(0, chunks)
        def _(j, part=part):
            total = core_in[6 + part, :, columns(j)].astype(F32) + first_in[2 + part, :, columns(j)].astype(F32)
            out_ref[pl.ds(part * half, half), columns(j)] = total + next_in[part, :, columns(j)].astype(F32)

    for copy in core_copies + first_copies + next_copies:
        copy.wait_send()


def plane_scatter(parts, weights, collective_id, jobs=()):
    count = parts[0].shape[0]
    width = weights[0].shape[0]
    rows = count // 8
    half = rows // 2
    vmem, hbm = pl.BlockSpec(memory_space=pltpu.VMEM), pl.BlockSpec(memory_space=pl.ANY)
    lefts, rights = [left for left, _ in jobs], [right for _, right in jobs]
    return pl.pallas_call(
        functools.partial(scatter_kernel, rows, len(parts), len(jobs)),
        in_specs=[hbm] * len(parts) + [vmem] * len(parts) + [hbm] * (2 * len(jobs)),
        out_specs=[vmem] + [hbm] * len(jobs),
        out_shape=[jax.ShapeDtypeStruct((rows, width), F32)]
        + [jax.ShapeDtypeStruct((left.shape[1], right.shape[1]), BF16) for left, right in jobs],
        scratch_shapes=[
            pltpu.VMEM((8, half, width), BF16),
            pltpu.VMEM((8, half, width), BF16),
            pltpu.VMEM((4, half, width), BF16),
            pltpu.VMEM((2, half, width), BF16),
            pltpu.SemaphoreType.DMA((2, 14)),
        ]
        + [pltpu.VMEM((2, half, a.shape[1]), BF16) for a in parts]
        + [pltpu.SemaphoreType.DMA((2, len(parts)))]
        + (product_buffers(rights[0].shape[1]) if jobs else []),
        compiler_params=pltpu.CompilerParams(
            collective_id=collective_id, has_side_effects=True, vmem_limit_bytes=(58 if jobs else 52) << 20
        ),
        cost_estimate=small_cost(),
        name="plane_scatter",
    )(*parts, *weights, *lefts, *rights)


def gated_kernel(x_ref, grad_ref, gate_ref, up_ref, hidden_ref, gate_grad_ref, up_grad_ref):
    columns = gate_ref.shape[1]
    step = min(256, columns)
    together = min(2, columns // step)

    @pl.loop(0, columns // (step * together))
    def _(j):
        for part in range(together):
            taken = pl.ds(pl.multiple_of((j * together + part) * step, step), step)
            gate = dot_n(x_ref[...], gate_ref[:, taken])
            up = dot_n(x_ref[...], up_ref[:, taken])
            grad = grad_ref[:, taken].astype(F32)
            sigmoid = jax.nn.sigmoid(gate)
            silu = gate * sigmoid
            hidden_ref[:, taken] = (silu * up).astype(BF16)
            gate_grad_ref[:, taken] = (grad * up * sigmoid * (1.0 + gate * (1.0 - sigmoid))).astype(BF16)
            up_grad_ref[:, taken] = (grad * silu).astype(BF16)


def gated_rows(x, hidden_grad, w_gate, w_up):
    tokens, depth = x.shape
    columns = w_gate.shape[1]
    block = 512
    rows = pl.BlockSpec((block, columns), lambda i: (i, 0))
    weight = pl.BlockSpec((depth, columns), lambda i: (0, 0), pipeline_mode=pl.Buffered(1))
    out = jax.ShapeDtypeStruct((tokens, columns), BF16)
    return pl.pallas_call(
        gated_kernel,
        grid=(tokens // block,),
        in_specs=[pl.BlockSpec((block, depth), lambda i: (i, 0)), rows, weight, weight],
        out_specs=[rows] * 3,
        out_shape=[out] * 3,
        compiler_params=pltpu.CompilerParams(vmem_limit_bytes=48 << 20),
        cost_estimate=small_cost(),
        name="gated_rows",
    )(x, hidden_grad, w_gate, w_up)


def is_plane():
    return lax.axis_size("ctx") == 4 and lax.axis_size("tensor") == 2


def gather_rows(rows):
    return lax.all_gather(rows, GROUP, axis=0, tiled=True)


def scatter_rows(rows):
    return lax.psum_scatter(rows.astype(BF16), GROUP, scatter_dimension=0, tiled=True).astype(F32)


def gather_now(rows):
    return plane_gather(rows)[0] if is_plane() else gather_rows(rows)


def cut(weight):
    columns = weight.shape[1] // lax.axis_size("ctx")
    return lax.dynamic_slice_in_dim(weight, lax.axis_index("ctx") * columns, columns, 1)


def gather_with_tables(rows, lengths, parents, tokens, width, weights):
    if is_plane():
        jobs = [cut_job(weights, lax.axis_size("ctx")), table_job(lengths, parents, tokens)]
        got = plane_gather(rows, 8, jobs, (4, 4))
        return got[:1] + got[1 + len(weights) :], got[1 : 1 + len(weights)]
    segment, parent, depth = tree_tables(lengths[0], parents[0], tokens)
    return [gather_rows(rows), *lay_out(segment, parent), *rope_tables(depth, width)], [cut(w) for w in weights]


def gather_with_product(rows, left, right):
    if is_plane():
        return plane_gather(rows, 5, [row_job(left, right, False)], (4, 4))
    return gather_rows(rows), dot_n(left, right).astype(BF16)


def gather_with_three(rows, left, right, shared, first, second):
    if is_plane():
        return plane_gather(rows, 4, [row_job(left, right, True), pair_job(shared, first, second)], (8, 3))
    products = dot_t(left, right), dot_tn(shared, first), dot_tn(shared, second)
    return [gather_rows(rows)] + [product.astype(BF16) for product in products]


def product_scatter(parts, weights, collective_id, jobs=()):
    if is_plane():
        return plane_scatter(parts, weights, collective_id, jobs)
    rows = scatter_rows(dot_t(jnp.concatenate(parts, axis=1), jnp.concatenate(weights, axis=1)))
    return [rows] + [dot_tn(left, right).astype(BF16) for left, right in jobs]


def gather_weight(own):
    return lax.all_gather(own, "fsdp", axis=0, tiled=True)


def scatter_weight(grad):
    return lax.psum_scatter(grad.astype(BF16), "fsdp", scatter_dimension=0, tiled=True)


def swap_rows(part):
    size = lax.axis_size("ctx")
    return lax.all_to_all(part.reshape(size, part.shape[0] // size, -1), "ctx", split_axis=0, concat_axis=0)


def lay_side_by_side(got, count):
    columns = got.shape[2] // count
    return [
        jnp.concatenate([got[j, :, c * columns : (c + 1) * columns] for j in range(got.shape[0])], axis=1).astype(F32)
        for c in range(count)
    ]


def normalize(rows):
    norm_inv = lax.rsqrt(jnp.mean(rows * rows, axis=1, keepdims=True) + EPSILON)
    return (rows * norm_inv, norm_inv)


def norm_backward(grad_rows, scaled, norm_inv, gain):
    weighted = grad_rows * gain[None, :]
    inner = jnp.mean(weighted * scaled, axis=1, keepdims=True)
    return norm_inv * (weighted - scaled * inner)


def body(
    tokens_in,
    attn_gain,
    query_weight,
    key_weight,
    value_weight,
    output_weight,
    mlp_gain,
    gate_weight,
    up_weight,
    down_weight,
    seg_lengths,
    leaf_parent,
    cotangent,
):
    ctx = lax.axis_index("ctx")
    parts = lax.axis_size("ctx")
    tree_len = tokens_in.shape[0] * parts * lax.axis_size("tensor")
    width = query_weight.shape[1] // parts
    units = gate_weight.shape[1] // parts

    def mine(weight, columns):
        return lax.dynamic_slice_in_dim(weight, ctx * columns, columns, 1)

    x_rows = tokens_in.astype(F32)
    attn_scaled, attn_inv = normalize(x_rows)
    w_attn = gather_weight(
        jnp.concatenate([mine(w, width) for w in (query_weight, key_weight, value_weight, output_weight)], axis=1)
    )
    (attn_in, rows_table, cols_table, cosine, sine), cuts = gather_with_tables(
        (attn_scaled * attn_gain[None, :]).astype(BF16),
        seg_lengths,
        leaf_parent,
        tree_len,
        min(2 * HEAD_DIM, width),
        [gate_weight, down_weight, up_weight],
    )
    w_gate, w_down, w_up = [gather_weight(own) for own in cuts]
    w_qkv, w_out = w_attn[:, : 3 * width], w_attn[:, 3 * width :]

    qkv = jnp.dot(attn_in, w_qkv, preferred_element_type=F32)
    if is_plane():
        attn_out, lse, query_rows, key_rows, value_rows, cot_all = attention_forward(
            qkv, cosine, sine, rows_table, cols_table, width, cotangent
        )
    else:
        attn_out, lse, query_rows, key_rows, value_rows = attention_forward(
            qkv, cosine, sine, rows_table, cols_table, width
        )
        cot_all = gather_rows(cotangent)
    mid_rows = x_rows + product_scatter([attn_out], [w_out], 1)[0]
    mlp_scaled, mlp_inv = normalize(mid_rows)
    mlp_own = (mlp_scaled * mlp_gain[None, :]).astype(BF16)
    mlp_in, hidden_grad = gather_with_product(mlp_own, cot_all, w_down)
    hidden, gate_rows_grad, up_rows_grad = gated_rows(mlp_in, hidden_grad, w_gate, w_up)

    mlp_in_grad, down_part = product_scatter(
        [gate_rows_grad, up_rows_grad], [w_gate, w_up], 3, [(cot_all, hidden)]
    )
    down_grad = scatter_weight(down_part)
    mid_grad = cotangent.astype(F32) + norm_backward(mlp_in_grad, mlp_scaled, mlp_inv, mlp_gain)
    mid_all, down_rows, up_part, gate_part = gather_with_three(
        mid_grad.astype(BF16), hidden, w_down, mlp_in, up_rows_grad, gate_rows_grad
    )
    up_grad = scatter_weight(up_part)
    gate_grad = scatter_weight(gate_part)

    out_heads_grad = jnp.dot(mid_all, w_out, preferred_element_type=F32).astype(BF16)
    output_grad = dot_tn(mid_all, attn_out).astype(BF16)
    out_heads_grad, down_grad = lax.optimization_barrier((out_heads_grad, down_grad))
    if is_plane():
        pre_grads, down_rows = attention_backward(
            query_rows, key_rows, value_rows, attn_out, out_heads_grad, lse, cosine, sine, rows_table, cols_table, down_rows
        )
    else:
        pre_grads = attention_backward(
            query_rows, key_rows, value_rows, attn_out, out_heads_grad, lse, cosine, sine, rows_table, cols_table
        )
        pre_grads = jnp.concatenate(pre_grads, axis=1)
        down_rows = scatter_rows(down_rows)
    block_out = (mid_rows + down_rows.astype(F32)).astype(BF16)
    pre_grads, up_grad, gate_grad = lax.optimization_barrier((pre_grads, up_grad, gate_grad))
    swapped = swap_rows(jnp.concatenate([gate_grad, up_grad, down_grad], axis=1))
    attn_part = jnp.concatenate([dot_tn(attn_in, pre_grads).astype(BF16), output_grad], axis=1)
    pre_grads, attn_part, swapped = lax.optimization_barrier((pre_grads, attn_part, swapped))
    attn_grad = scatter_weight(attn_part)
    (attn_in_grad,) = product_scatter([pre_grads], [w_qkv], 2)
    attn_in_grad, attn_grad = lax.optimization_barrier((attn_in_grad, attn_grad))
    gate_out, up_out, down_out = lay_side_by_side(swapped, 3)
    query_out, key_out, value_out, output_out = lay_side_by_side(swap_rows(attn_grad), 4)

    def gain_part(pairs, gain):
        held = query_out.shape[0]
        total = sum(
            jnp.sum(lax.dynamic_slice_in_dim(weight, ctx * held, held, 0).astype(F32) * grad, axis=1)
            for weight, grad in pairs
        )
        first = (lax.axis_index("fsdp") * parts + ctx) * held
        return total / lax.dynamic_slice_in_dim(gain, first, held, 0)

    sums = jnp.stack(
        [
            gain_part([(query_weight, query_out), (key_weight, key_out), (value_weight, value_out)], attn_gain),
            gain_part([(gate_weight, gate_out), (up_weight, up_out)], mlp_gain),
        ]
    )
    row, others = lax.axis_index("tensor"), lax.axis_size("tensor")
    kept = sums.shape[1] // others
    if others == 2:
        got = lax.ppermute(lax.dynamic_slice_in_dim(sums, (1 - row) * kept, kept, 1), "tensor", [(0, 1), (1, 0)])
        gain_grads = lax.dynamic_slice_in_dim(sums, row * kept, kept, 1) + got
    else:
        gain_grads = lax.dynamic_slice_in_dim(lax.psum(sums, "tensor"), row * kept, kept, 1)

    attn_back = norm_backward(attn_in_grad, attn_scaled, attn_inv, attn_gain)
    input_grad = (mid_grad + attn_back).astype(BF16)
    return (
        block_out,
        input_grad,
        gain_grads[0],
        query_out,
        key_out,
        value_out,
        output_out,
        gain_grads[1],
        gate_out,
        up_out,
        down_out,
    )


def solution(mesh):
    rows = P(("fsdp", "ctx", "tensor"), None)
    weight = P("fsdp", "tensor")
    gain = P(("fsdp", "ctx", "tensor"))
    grad = P(("fsdp", "ctx"), "tensor")
    in_specs = (
        rows, P(), weight, weight, weight, weight, P(), weight, weight, weight, P("fsdp", None), P("fsdp", None), rows,
    )
    out_specs = (rows, rows, gain, grad, grad, grad, grad, gain, grad, grad, grad)
    return jax.shard_map(body, mesh=mesh, in_specs=in_specs, out_specs=out_specs, check_vma=False)
```

```python
import functools

import jax
import jax.numpy as jnp
import numpy as np
from jax import lax
from jax.experimental import pallas as pl
from jax.experimental.pallas import tpu as pltpu
from jax.sharding import PartitionSpec as P

HEAD_DIM = 64
TRUNK = 2176
MOST_SEG = 128
ROPE_BASE = 130000.0
EPSILON = 1e-05
NEG_LARGE = -1e30
SCALE = HEAD_DIM ** (-0.5)

BQ = 512
BK = 512
GROUP = ("ctx", "tensor")

F32 = jnp.float32
BF16 = jnp.bfloat16


def pick_table(onehot, table):
    return jnp.sum(jnp.where(onehot, table[None, :], 0), axis=1)


def tree_tables(lengths_row, parent_row, tree_len):
    branches = lengths_row.shape[0] - parent_row.shape[0]
    ends = TRUNK + jnp.cumsum(lengths_row)
    starts = ends - lengths_row
    matches = parent_row[:, None] - 1 == jnp.arange(branches, dtype=jnp.int32)[None, :]
    parent_len = jnp.sum(jnp.where(matches, lengths_row[None, :branches], 0), axis=1)
    zero_one = jnp.zeros((1,), jnp.int32)
    seg_start = jnp.concatenate([zero_one, starts])
    seg_base = jnp.concatenate(
        [zero_one, jnp.full((branches,), TRUNK, jnp.int32), TRUNK + parent_len]
    )
    seg_parent = jnp.concatenate([zero_one, jnp.zeros((branches,), jnp.int32), parent_row])
    positions = jnp.arange(tree_len, dtype=jnp.int32)
    above = jnp.sum((ends[None, :] <= positions[:, None]).astype(jnp.int32), axis=1)
    segment = (positions >= TRUNK).astype(jnp.int32) + above
    onehot = segment[:, None] == jnp.arange(seg_start.shape[0], dtype=jnp.int32)[None, :]
    depth = positions - pick_table(onehot, seg_start) + pick_table(onehot, seg_base)
    parent = pick_table(onehot, seg_parent)
    return (segment, parent, depth)


def rope_freqs(width):
    half = HEAD_DIM // 2
    powers = -2.0 * (np.arange(width) % half) / HEAD_DIM
    return np.power(ROPE_BASE, powers).astype(np.float32)[None, :]


def rope_tables(depth, width):
    angles = depth.astype(F32)[:, None] * rope_freqs(width)
    sign = np.where(np.arange(width) % HEAD_DIM < HEAD_DIM // 2, -1.0, 1.0).astype(np.float32)
    return jnp.cos(angles), jnp.sin(angles) * sign[None, :]


def lay_out(segment, parent):
    both = jnp.stack([segment, parent])
    return jnp.pad(both, ((0, 6), (0, 0))), jnp.pad(both.T, ((0, 0), (0, 126)))


TABLE_ROWS = 512
TABLE_STEP = 64


def tables_at(positions, lengths, parents):
    leaves = parents.shape[1]
    branches = lengths.shape[1] - leaves
    zero = jnp.zeros_like(positions)
    segment = jnp.where(positions >= TRUNK, 1, 0)
    parent, depth = zero, positions
    end = jnp.full((1, 1), TRUNK, jnp.int32)
    starts = []
    for s in range(branches + leaves):
        start, end = end, end + lengths[:, s : s + 1]
        inside = (positions >= start) & (positions < end)
        base, above = jnp.full((1, 1), TRUNK, jnp.int32), jnp.zeros((1, 1), jnp.int32)
        if s >= branches:
            above = parents[:, s - branches : s - branches + 1]
            for b in range(branches):
                base = base + jnp.where(above == b + 1, lengths[:, b : b + 1], 0)
        segment = segment + jnp.where(positions >= end, 1, 0)
        parent = jnp.where(inside, above, parent)
        depth = jnp.where(inside, positions - start + base, depth)
    return segment, parent, depth


def sine_cosine(x):
    turns = jnp.floor(x * np.float32(2.0 / np.pi) + 0.5)
    r = x - turns * np.float32(1.5703125)
    r = r - turns * np.float32(4.837512969970703125e-4)
    r = r - turns * np.float32(7.549789954891882e-8)
    z = r * r
    sine = ((np.float32(-1.9515295891e-4) * z + np.float32(8.3321608736e-3)) * z - np.float32(1.6666654611e-1)) * z * r + r
    cosine = (
        (np.float32(2.443315711809948e-5) * z - np.float32(1.388731625493765e-3)) * z + np.float32(4.166664568298827e-2)
    ) * z * z - np.float32(0.5) * z + np.float32(1.0)
    quarter = turns.astype(jnp.int32) & 3
    odd = (quarter & 1) == 1
    first, second = jnp.where(odd, cosine, sine), jnp.where(odd, sine, cosine)
    return jnp.where(quarter >= 2, -first, first), jnp.where((quarter == 1) | (quarter == 2), -second, second)


def table_work(lengths, parents, freqs, rows_ref, cols_ref, cos_ref, sin_ref, cols_buf, cos_buf, sin_buf, sems):
    yield
    tokens = cos_ref.shape[0]
    shape = (8, tokens)
    segment, parent, _ = tables_at(lax.broadcasted_iota(jnp.int32, shape, 1), lengths, parents)
    line = lax.broadcasted_iota(jnp.int32, shape, 0)
    rows_ref[...] = jnp.where(line == 0, segment, jnp.where(line == 1, parent, 0))
    copies = []
    for chunk in range(tokens // TABLE_ROWS):
        rows = pl.ds(chunk * TABLE_ROWS, TABLE_ROWS)

        @pl.loop(0, TABLE_ROWS // TABLE_STEP)
        def _(j, chunk=chunk):
            first = pl.multiple_of(chunk * TABLE_ROWS + j * TABLE_STEP, TABLE_STEP)
            taken = pl.ds(first, TABLE_STEP)
            shape = (TABLE_STEP, 128)
            lane = lax.broadcasted_iota(jnp.int32, shape, 1)
            segment, parent, depth = tables_at(lax.broadcasted_iota(jnp.int32, shape, 0) + first, lengths, parents)
            cols_buf[taken, :] = jnp.where(lane == 0, segment, jnp.where(lane == 1, parent, 0))
            sine, cosine = sine_cosine(depth.astype(F32) * freqs[...])
            cos_buf[taken, :] = cosine
            sin_buf[taken, :] = jnp.where(lane % HEAD_DIM < HEAD_DIM // 2, -sine, sine)

        for kind, (source, target) in enumerate(((cols_buf, cols_ref), (cos_buf, cos_ref), (sin_buf, sin_ref))):
            copies.append(pltpu.make_async_copy(source.at[rows], target.at[rows], sems.at[kind, chunk]))
            copies[-1].start()
        yield
    for copy in copies:
        copy.wait()


MESH = pl.DeviceIdType.MESH


def plane_place():
    ctx, row = lax.axis_index("ctx"), lax.axis_index("tensor")
    x, core = ctx // 2, ctx % 2
    return x, core, row


def plane_neighbours(x, core, row):
    over_x = {"ctx": (1 - x) * 2 + core}
    over_core = {"ctx": x * 2 + 1 - core}
    over_row = {"tensor": 1 - row}
    return over_x, over_row, over_core


def enter_plane(neighbours):
    barrier = pltpu.get_barrier_semaphore()
    for device in neighbours:
        pl.semaphore_signal(barrier, inc=1, device_id=device, device_id_type=MESH)
    pl.semaphore_wait(barrier, 3)


PIECES = ((1, 1, 0), (1, 1, 1), (1, 0, 0), (0, 1, 1), (0, 1, 0), (1, 0, 1), (0, 0, 0), (0, 0, 1))
COLS = 512


class PlaneGather:
    def __init__(self, own_ref, all_ref, local_sem, send_sem, recv_sem):
        self.own_ref, self.all_ref, self.sems = own_ref, all_ref, (local_sem, send_sem, recv_sem)
        self.x, self.core, self.row = plane_place()
        self.devices = plane_neighbours(self.x, self.core, self.row)
        self.rows = own_ref.shape[0]

    def place(self, far_x, far_row, part):
        bx = self.x + far_x - 2 * far_x * self.x
        by = self.row + far_row - 2 * far_row * self.row
        half = self.rows // 2
        return pl.ds(pl.multiple_of(((bx * 2 + self.core) * 2 + by) * self.rows + part * half, half), half)

    def copy(self, slot):
        far_x, far_row, part, device = (
            (0, 0, 0, 1), (0, 0, 1, 1), (1, 0, 1, 1), (0, 0, 1, 0), (0, 0, 0, 0), (0, 1, 0, 0), (0, 0, 0, 2),
            (0, 0, 1, 2), (0, 1, 0, 2), (1, 0, 1, 2), (0, 1, 1, 2), (1, 0, 0, 2), (1, 1, 0, 2), (1, 1, 1, 2),
        )[slot]
        half = self.rows // 2
        target = self.place(far_x, far_row, part)
        own = far_x == 0 and far_row == 0
        source = self.own_ref.at[pl.ds(part * half, half)] if own else self.all_ref.at[target]
        return pltpu.make_async_remote_copy(
            src_ref=source, dst_ref=self.all_ref.at[target], send_sem=self.sems[1].at[slot],
            recv_sem=self.sems[2].at[slot], device_id=self.devices[device], device_id_type=MESH,
        )

    def local(self, part):
        half = self.rows // 2
        return pltpu.make_async_copy(
            self.own_ref.at[pl.ds(part * half, half)], self.all_ref.at[self.place(0, 0, part)], self.sems[0].at[part]
        )

    def start(self):
        enter_plane(self.devices)
        for slot in (0, 3, 1, 4, 6, 7):
            self.copy(slot).start()
        for part in range(2):
            self.local(part).start()

    def forward(self, got, slots):
        self.copy(got).wait_recv()
        for slot in slots:
            self.copy(slot).start()

    def first(self):
        self.forward(0, (5, 8))
        self.forward(3, (2, 9))

    def second(self):
        self.forward(1, (10,))
        self.forward(4, (11,))

    def finish(self):
        self.forward(5, (12,))
        self.forward(2, (13,))
        for slot in range(6, 14):
            self.copy(slot).wait_recv()
        for slot in range(14):
            self.copy(slot).wait_send()
        for part in range(2):
            self.local(part).wait()


def gather_sems():
    return [pltpu.SemaphoreType.DMA((2,)), pltpu.SemaphoreType.DMA((14,)), pltpu.SemaphoreType.DMA((14,))]


class PlaneScatter:
    def __init__(self, part_ref, out_ref, core_in, first_in, next_in, own, total, sems, own_sems):
        self.part_ref, self.out_ref, self.core_in, self.first_in, self.next_in = part_ref, out_ref, core_in, first_in, next_in
        self.own, self.total, self.sems, self.own_sems = own, total, sems, own_sems
        self.x, self.core, self.row = plane_place()
        self.devices = plane_neighbours(self.x, self.core, self.row)
        self.rows = part_ref.shape[0] // 8

    def place(self, piece, on_core):
        far_x, far_row, part = PIECES[piece]
        bx = self.x + far_x - 2 * far_x * self.x
        by = self.row + far_row - 2 * far_row * self.row
        half = self.rows // 2
        return pl.ds(pl.multiple_of(((bx * 2 + on_core) * 2 + by) * self.rows + part * half, half), half)

    def copy(self, slot):
        if slot < 8:
            source, target, device = self.part_ref.at[self.place(slot, 1 - self.core)], self.core_in.at[slot], 2
        elif slot < 12:
            source, target, device = self.core_in.at[slot - 8], self.first_in.at[slot - 8], slot % 2
        else:
            source, target, device = self.core_in.at[slot - 8], self.next_in.at[slot - 12], 1 - slot % 2
        return pltpu.make_async_remote_copy(
            src_ref=source, dst_ref=target, send_sem=self.sems.at[0, slot], recv_sem=self.sems.at[1, slot],
            device_id=self.devices[device], device_id_type=MESH,
        )

    def load(self, piece):
        return pltpu.make_async_copy(
            self.part_ref.at[self.place(piece, self.core)], self.own.at[piece % 4], self.own_sems.at[piece % 4]
        )

    def add(self, target, where, *others):
        @pl.loop(0, target.shape[-1] // COLS)
        def _(j):
            columns = pl.ds(pl.multiple_of(j * COLS, COLS), COLS)
            total = sum(ref[slot, :, columns].astype(F32) for ref, slot in others)
            target[where, :, columns] = total.astype(target.dtype)

    def start(self):
        enter_plane(self.devices)
        for slot in range(8):
            self.copy(slot).start()
        for piece in range(4):
            self.load(piece).start()

    def first(self):
        for piece in range(4):
            self.load(piece).wait()
            self.copy(piece).wait_recv()
            self.add(self.core_in, piece, (self.own, piece), (self.core_in, piece))
            self.copy(8 + piece).start()
        for piece in range(4, 8):
            self.load(piece).start()

    def second(self):
        for piece in range(4, 8):
            self.load(piece).wait()
            self.copy(piece).wait_recv()
            self.add(self.core_in, piece, (self.own, piece - 4), (self.core_in, piece))

    def third(self):
        for part in range(2):
            self.copy(8 + part).wait_recv()
            self.add(self.core_in, 4 + part, (self.core_in, 4 + part), (self.first_in, part))
            self.copy(12 + part).start()

    def finish(self):
        half = self.rows // 2
        for part in range(2):
            self.copy(10 + part).wait_recv()
            self.copy(12 + part).wait_recv()
            self.add(self.total, part, (self.core_in, 6 + part), (self.first_in, 2 + part), (self.next_in, part))
        stores = [
            pltpu.make_async_copy(
                self.total.at[part], self.out_ref.at[pl.ds(part * half, half)], self.own_sems.at[part]
            )
            for part in range(2)
        ]
        for store in stores:
            store.start()
        for slot in range(14):
            self.copy(slot).wait_send()
        for store in stores:
            store.wait()


def scatter_scratch(rows, width):
    half = rows // 2
    return [
        pltpu.VMEM((8, half, width), BF16),
        pltpu.VMEM((4, half, width), BF16),
        pltpu.VMEM((2, half, width), BF16),
        pltpu.VMEM((4, half, width), BF16),
        pltpu.VMEM((2, half, width), BF16),
        pltpu.SemaphoreType.DMA((2, 14)),
        pltpu.SemaphoreType.DMA((4,)),
    ]


def at_step(step, total, places):
    for place, phase in places:

        @pl.when(step == place)
        def _(phase=phase):
            phase()


def partner(x):
    half = HEAD_DIM // 2
    width = x.shape[1]
    if width == HEAD_DIM:
        return jnp.concatenate([x[:, half:], x[:, :half]], axis=1)
    lane = lax.broadcasted_iota(jnp.int32, x.shape, 1)
    ahead = pltpu.roll(x, width - half, 1)
    behind = pltpu.roll(x, half, 1)
    return jnp.where(lane % HEAD_DIM < half, ahead, behind)


def head_mask(shape, head):
    lane = lax.broadcasted_iota(jnp.int32, shape, 1)
    return lane // HEAD_DIM == head


def dot_t(a, b):
    return lax.dot_general(a, b, (((1,), (1,)), ((), ())), preferred_element_type=F32)


def dot_n(a, b):
    return lax.dot_general(a, b, (((1,), (0,)), ((), ())), preferred_element_type=F32)


def dot_tn(a, b):
    return lax.dot_general(a, b, (((0,), (0,)), ((), ())), preferred_element_type=F32)


def key_plan(i, tile):
    base = TRUNK // BK * BK
    branch_end = TRUNK + 4 * MOST_SEG
    first_tree = base // BQ
    mixed_end = -(-(branch_end + MOST_SEG) // BQ)
    chunks = jnp.minimum(i * BQ, base) // BK

    @pl.when(i < first_tree)
    def _():
        @pl.loop(0, chunks)
        def _(j):
            start = pl.multiple_of(j * BK, BK)
            tile(start, BK, 0, start)

    @pl.when(i >= first_tree)
    def _():
        tile(0, base, 0, 0)

    @pl.when(i < first_tree)
    def _():
        start = pl.multiple_of(chunks * BK, BK)
        tile(start, BK, 1, start)

    for block in range(first_tree, mixed_end):

        @pl.when(i == block)
        def _(block=block):
            tile(base, (block + 1) * BQ - base, 2, base)

    @pl.when(i >= mixed_end)
    def _():
        tile(base, branch_end - base, 3, base)
        tile(pl.multiple_of(i * BQ - MOST_SEG, MOST_SEG), BQ + MOST_SEG, 4, branch_end)


def most_keys():
    return TRUNK + 4 * MOST_SEG + BQ + MOST_SEG


def seen_mask(kind, q_at, k_at, seg_q, par_q, seg_k):
    if kind == 3:
        return (seg_k == 0) | (seg_k == par_q)
    causal = k_at <= q_at
    if kind == 1:
        return causal
    if kind == 4:
        return causal & (seg_k == seg_q)
    return causal & ((seg_k == 0) | (seg_k == seg_q) | (seg_k == par_q))


def fwd_kernel(heads, hosts, *refs):
    if not hosts:
        return fwd_work(heads, *refs)
    gather = PlaneGather(refs[7], refs[13], *refs[-3:])
    step, total = pl.program_id(0) * pl.num_programs(1) + pl.program_id(1), 16
    at_step(step, total, ((0, gather.start), (6, gather.first), (12, gather.second)))
    fwd_work(heads, *refs[:7], *refs[8:13], *refs[14:-3])
    at_step(step, total, ((total - 1, gather.finish),))


def fwd_work(
    heads, q_ref, k_ref, v_ref, cos_ref, sin_ref, rows_ref, cols_ref,
    o_ref, lse_ref, qr_ref, kr_ref, vr_ref, kt_ref, va_ref, s_ref, m_ref, acc_ref,
):
    i = pl.program_id(1)
    wide = 2 * HEAD_DIM

    @pl.when(i == 0)
    def _():
        @pl.loop(0, k_ref.shape[0] // BK)
        def _(j):
            rows = pl.ds(pl.multiple_of(j * BK, BK), BK)
            k = k_ref[rows, :]
            k = (k * cos_ref[rows, :] + partner(k) * sin_ref[rows, :]).astype(BF16)
            kr_ref[rows, :] = k
            kt_ref[:, rows] = jnp.transpose(k)
            v = v_ref[rows, :].astype(BF16)
            vr_ref[rows, :] = v
            if heads == 1:
                va_ref[0, rows, :] = jnp.concatenate([v, jnp.ones_like(v)], axis=1)
            else:
                for h in range(heads):
                    va_ref[h, rows, :] = jnp.where(head_mask(v.shape, h), v, jnp.ones_like(v))

    rows = pl.ds(pl.multiple_of(i * BQ, BQ), BQ)
    q = q_ref[...]
    q = (q * cos_ref[rows, :] + partner(q) * sin_ref[rows, :]).astype(BF16)
    qr_ref[...] = q
    q = q * jnp.asarray(SCALE, BF16)
    q_heads = [jnp.where(head_mask(q.shape, h), q, jnp.zeros_like(q)) for h in range(heads)]
    m_ref[...] = jnp.full_like(m_ref, NEG_LARGE)
    acc_ref[...] = jnp.zeros_like(acc_ref)

    def score_tile(start, width, kind, place):
        keys = pl.ds(start, width)
        k = kt_ref[:, keys]
        seen = None
        if kind != 0:
            shape = (BQ, width)
            seen = seen_mask(
                kind,
                lax.broadcasted_iota(jnp.int32, shape, 0) + i * BQ,
                lax.broadcasted_iota(jnp.int32, shape, 1) + start,
                cols_ref[:, 0:1], cols_ref[:, 1:2], rows_ref[0:1, keys],
            )
        for h in range(heads):
            s = dot_n(q_heads[h], k)
            if seen is not None:
                s = jnp.where(seen, s, NEG_LARGE)
            s_ref[h, :, pl.ds(place, width)] = s
            largest = m_ref[h]
            for c in range(width // 128):
                largest = jnp.maximum(largest, s[:, c * 128 : (c + 1) * 128])
            m_ref[h] = largest

    key_plan(i, score_tile)
    for h in range(heads):
        m_ref[h] = jnp.broadcast_to(jnp.max(m_ref[h], axis=1, keepdims=True), (BQ, 128))

    def value_tile(start, width, kind, place):
        keys = pl.ds(start, width)
        for h in range(heads):
            m = m_ref[h]
            parts = [
                jnp.exp(s_ref[h, :, pl.ds(place + c * 128, 128)] - m).astype(BF16) for c in range(width // 128)
            ]
            acc_ref[h] += dot_n(jnp.concatenate(parts, axis=1), va_ref[h, keys, :])

    key_plan(i, value_tile)
    out, lse = None, None
    for h in range(heads):
        acc = acc_ref[h]
        part = acc / pltpu.roll(acc, HEAD_DIM, 1)
        stat = m_ref[h] + jnp.log(jnp.broadcast_to(acc[:, (1 - h) * HEAD_DIM : (1 - h) * HEAD_DIM + 1], (BQ, wide)))
        mask = head_mask((BQ, wide), h)
        out = part if h == 0 else jnp.where(mask, part, out)
        lse = stat if h == 0 else jnp.where(mask, stat, lse)
    o_ref[...] = out[:, : heads * HEAD_DIM].astype(BF16)
    turned = jnp.transpose(lse)
    for h in range(heads):
        lse_ref[0, h : h + 1, :] = turned[h * HEAD_DIM : h * HEAD_DIM + 1, :]


def bwd_kernel(heads, hosts, *refs):
    if not hosts:
        return bwd_work(heads, *refs)
    scatter = PlaneScatter(refs[10], refs[12], *refs[-7:])
    step, total = pl.program_id(0) * pl.num_programs(1) + pl.program_id(1), 16
    at_step(
        step, total, ((0, scatter.start), (3, scatter.first), (5, scatter.second), (7, scatter.third))
    )
    bwd_work(heads, *refs[:10], *refs[13:-7], together=refs[11])
    at_step(step, total, ((total - 1, scatter.finish),))


def bwd_work(
    heads, q_ref, k_ref, v_ref, o_ref, do_ref, lse_ref, cos_ref, sin_ref, rows_ref, cols_ref,
    *refs, together=None,
):
    if together is None:
        dq_ref, dk_ref, dv_ref, dq_acc, dk_acc, dv_acc = refs
    else:
        dq_acc, dk_acc, dv_acc, dq_ref, dk_ref, dv_ref, out_sems = refs
    i = pl.program_id(1)

    def store(kind, source, rows, sem):
        groups, width = pl.num_programs(0), source.shape[1]
        columns = pl.ds(pl.multiple_of((kind * groups + pl.program_id(0)) * width, width), width)
        return pltpu.make_async_copy(source, together.at[rows, columns], out_sems.at[sem])

    @pl.when(i == 0)
    def _():
        dk_acc[...] = jnp.zeros_like(dk_acc)
        dv_acc[...] = jnp.zeros_like(dv_acc)

    q = q_ref[...]
    scaled = q * jnp.asarray(SCALE, BF16)
    do = do_ref[...]
    product = jnp.transpose(do.astype(F32) * o_ref[...].astype(F32))
    zero = jnp.zeros_like(q)
    masks = [head_mask(q.shape, h) for h in range(heads)]
    q_heads = [jnp.where(m, scaled, zero) for m in masks]
    do_heads = [jnp.where(m, do, zero) for m in masks]
    deltas = [
        jnp.sum(product[h * HEAD_DIM : (h + 1) * HEAD_DIM, :], axis=0, keepdims=True) for h in range(heads)
    ]
    lses = [lse_ref[0, h : h + 1, :] for h in range(heads)]
    q_turned = [jnp.transpose(x) for x in q_heads]
    do_turned = [jnp.transpose(x) for x in do_heads]
    q_stack = jnp.concatenate(q_heads, axis=0)
    do_stack = jnp.concatenate(do_heads, axis=0)
    dq_acc[...] = jnp.zeros_like(dq_acc)

    def tile(start, width, kind, place):
        keys = pl.ds(start, width)
        k = k_ref[keys, :]
        v = v_ref[keys, :]
        seen = None
        if kind != 0:
            shape = (width, BQ)
            seen = seen_mask(
                kind,
                lax.broadcasted_iota(jnp.int32, shape, 1) + i * BQ,
                lax.broadcasted_iota(jnp.int32, shape, 0) + start,
                rows_ref[0:1, :], rows_ref[1:2, :], cols_ref[keys, 0:1],
            )
        probs, grads, k_heads = [], [], []
        for h in range(heads):
            s = dot_n(k, q_turned[h])
            p = jnp.exp(s - lses[h])
            if seen is not None:
                p = jnp.where(seen, p, 0.0)
            dp = dot_n(v, do_turned[h])
            probs.append(p.astype(BF16))
            grads.append((p * (dp - deltas[h])).astype(BF16))
            k_heads.append(jnp.where(head_mask(k.shape, h), k, jnp.zeros_like(k)))
        grad_row = jnp.concatenate(grads, axis=1)
        dv_acc[keys, :] += dot_n(jnp.concatenate(probs, axis=1), do_stack)
        dk_acc[keys, :] += dot_n(grad_row, q_stack)
        dq_acc[...] += dot_tn(jnp.concatenate(grads, axis=0), jnp.concatenate(k_heads, axis=0))

    key_plan(i, tile)
    dq = dq_acc[...] * SCALE
    rows = pl.ds(pl.multiple_of(i * BQ, BQ), BQ)
    dq = (dq * cos_ref[rows, :] - partner(dq) * sin_ref[rows, :]).astype(BF16)
    if together is None:
        dq_ref[...] = dq
    else:
        step, last = pl.program_id(0) * pl.num_programs(1) + i, pl.num_programs(0) * pl.num_programs(1) - 1
        for slot in range(2):

            @pl.when(step % 2 == slot)
            def _(slot=slot):
                @pl.when(step >= 2)
                def _():
                    store(0, dq_ref.at[slot], rows, slot).wait()

                dq_ref[slot] = dq
                store(0, dq_ref.at[slot], rows, slot).start()

        @pl.when(step == last)
        def _():
            for slot in range(2):
                store(0, dq_ref.at[slot], rows, slot).wait()

    @pl.when(i == pl.num_programs(1) - 1)
    def _():
        @pl.loop(0, dk_acc.shape[0] // BK)
        def _(j):
            rows = pl.ds(pl.multiple_of(j * BK, BK), BK)
            dk = dk_acc[rows, :]
            dk_ref[rows, :] = (dk * cos_ref[rows, :] - partner(dk) * sin_ref[rows, :]).astype(BF16)
            dv_ref[rows, :] = dv_acc[rows, :].astype(BF16)

        if together is not None:
            every = pl.ds(0, dk_acc.shape[0])
            copies = [store(1, dk_ref, every, 2), store(2, dv_ref, every, 3)]
            for copy in copies:
                copy.start()
            for copy in copies:
                copy.wait()


def small_cost():
    return pl.CostEstimate(flops=1 << 20, bytes_accessed=1 << 20, transcendentals=0)


def attention_forward(qkv, cosine, sine, rows_table, cols_table, width, hosted=None):
    tree_len = qkv.shape[0]
    gw = min(2 * HEAD_DIM, width)
    groups, heads = width // gw, gw // HEAD_DIM
    row_block = pl.BlockSpec((BQ, gw), lambda g, i: (i, g))
    table = pl.BlockSpec((tree_len, gw), lambda g, i: (0, 0))
    full = pl.BlockSpec((tree_len, gw), lambda g, i: (0, g))
    act = jax.ShapeDtypeStruct((tree_len, width), BF16)
    if width % 128 == 0:
        queries, keys, values, step = qkv, qkv, qkv, groups
    else:
        queries, keys, values = jnp.split(qkv, 3, axis=1)
        step = 0
    hosts = hosted is not None
    hbm = pl.BlockSpec(memory_space=pl.ANY)
    return pl.pallas_call(
        functools.partial(fwd_kernel, heads, hosts),
        grid=(groups, tree_len // BQ),
        in_specs=[
            row_block,
            pl.BlockSpec((tree_len, gw), lambda g, i: (0, step + g)),
            pl.BlockSpec((tree_len, gw), lambda g, i: (0, 2 * step + g)),
            table,
            table,
            pl.BlockSpec((8, tree_len), lambda g, i: (0, 0)),
            pl.BlockSpec((BQ, 128), lambda g, i: (i, 0)),
        ]
        + [hbm] * hosts,
        out_specs=[row_block, pl.BlockSpec((1, heads, BQ), lambda g, i: (g, 0, i)), row_block, full, full] + [hbm] * hosts,
        out_shape=[act, jax.ShapeDtypeStruct((groups, heads, tree_len), F32), act, act, act]
        + ([jax.ShapeDtypeStruct((8 * hosted.shape[0], hosted.shape[1]), BF16)] if hosts else []),
        scratch_shapes=[
            pltpu.VMEM((gw, tree_len), BF16),
            pltpu.VMEM((heads, tree_len, 128), BF16),
            pltpu.VMEM((heads, BQ, most_keys()), F32),
            pltpu.VMEM((heads, BQ, 128), F32),
            pltpu.VMEM((heads, BQ, 128), F32),
        ]
        + (gather_sems() if hosts else []),
        compiler_params=pltpu.CompilerParams(
            vmem_limit_bytes=56 << 20, collective_id=6 if hosts else None, has_side_effects=hosts
        ),
        cost_estimate=small_cost(),
        name="tree_attention_forward",
    )(queries, keys, values, cosine, sine, rows_table, cols_table, *([hosted] if hosts else []))


def attention_backward(q, k, v, out, grad, lse, cosine, sine, rows_table, cols_table, hosted=None):
    tree_len, width = q.shape
    gw = min(2 * HEAD_DIM, width)
    groups, heads = width // gw, gw // HEAD_DIM
    row_block = pl.BlockSpec((BQ, gw), lambda g, i: (i, g))
    table = pl.BlockSpec((tree_len, gw), lambda g, i: (0, 0))
    full = pl.BlockSpec((tree_len, gw), lambda g, i: (0, g))
    act = jax.ShapeDtypeStruct((tree_len, width), BF16)
    hosts = hosted is not None
    hbm = pl.BlockSpec(memory_space=pl.ANY)
    return pl.pallas_call(
        functools.partial(bwd_kernel, heads, hosts),
        grid=(groups, tree_len // BQ),
        in_specs=[
            row_block, full, full, row_block, row_block,
            pl.BlockSpec((1, heads, BQ), lambda g, i: (g, 0, i)),
            table, table,
            pl.BlockSpec((8, BQ), lambda g, i: (0, i)),
            pl.BlockSpec((tree_len, 128), lambda g, i: (0, 0)),
        ]
        + [hbm] * hosts,
        out_specs=[hbm] * 2 if hosts else [row_block, full, full],
        out_shape=[
            jax.ShapeDtypeStruct((tree_len, 3 * width), BF16),
            jax.ShapeDtypeStruct((hosted.shape[0] // 8, hosted.shape[1]), BF16),
        ]
        if hosts
        else [act, act, act],
        scratch_shapes=[
            pltpu.VMEM((BQ, gw), F32),
            pltpu.VMEM((tree_len, gw), F32),
            pltpu.VMEM((tree_len, gw), F32),
        ]
        + (
            [pltpu.VMEM(shape, BF16) for shape in ((2, BQ, gw), (tree_len, gw), (tree_len, gw))]
            + [pltpu.SemaphoreType.DMA((4,))]
            + scatter_scratch(hosted.shape[0] // 8, hosted.shape[1])
            if hosts
            else []
        ),
        compiler_params=pltpu.CompilerParams(
            vmem_limit_bytes=60 << 20, collective_id=7 if hosts else None, has_side_effects=hosts
        ),
        cost_estimate=small_cost(),
        name="tree_attention_backward",
    )(q, k, v, out, grad, lse, cosine, sine, rows_table, cols_table, *([hosted] if hosts else []))


TOKENS_AT_ONCE = 2048
LEFT_AT_ONCE = 512
STEP = 512


def product_buffers(columns):
    return [
        pltpu.VMEM((2, TOKENS_AT_ONCE, LEFT_AT_ONCE), BF16),
        pltpu.VMEM((2 * TOKENS_AT_ONCE, columns), BF16),
        pltpu.VMEM((LEFT_AT_ONCE, columns), F32),
        pltpu.VMEM((LEFT_AT_ONCE, columns), BF16),
        pltpu.SemaphoreType.DMA((4,)),
    ]


def token_product(left_ref, right_ref, out_ref, left_buf, right_buf, total, out_buf, sems):
    tokens = left_ref.shape[0]
    parts, groups = tokens // TOKENS_AT_ONCE, left_ref.shape[1] // LEFT_AT_ONCE

    def load(step):
        group, part = step // parts, step % parts
        source = left_ref.at[
            pl.ds(part * TOKENS_AT_ONCE, TOKENS_AT_ONCE), pl.ds(group * LEFT_AT_ONCE, LEFT_AT_ONCE)
        ]
        return pltpu.make_async_copy(source, left_buf.at[step % 2], sems.at[step % 2])

    def store(group):
        return pltpu.make_async_copy(out_buf, out_ref.at[pl.ds(group * LEFT_AT_ONCE, LEFT_AT_ONCE)], sems.at[3])

    whole = pltpu.make_async_copy(right_ref, right_buf, sems.at[2])
    whole.start()
    load(0).start()
    yield
    whole.wait()
    for group in range(groups):
        for part in range(parts):
            step = group * parts + part
            load(step).wait()
            if step + 1 < groups * parts:
                load(step + 1).start()
            if part == 0:
                total[...] = jnp.zeros_like(total)

            @pl.loop(0, TOKENS_AT_ONCE // STEP)
            def _(j, step=step, part=part):
                left = left_buf[step % 2, pl.ds(pl.multiple_of(j * STEP, STEP), STEP), :]
                right = right_buf[pl.ds(pl.multiple_of(part * TOKENS_AT_ONCE + j * STEP, STEP), STEP), :]
                total[...] += dot_tn(left, right)

        if group > 0:
            store(group - 1).wait()
        out_buf[...] = total[...].astype(BF16)
        store(group).start()
        yield
    store(groups - 1).wait()


def finish(product):
    for _ in product:
        pass


def pair_product(left_ref, first_ref, second_ref, out_first, out_second, left_buf, right_buf, total, out_buf, sems):
    tokens, columns = first_ref.shape
    parts, groups = tokens // TOKENS_AT_ONCE, left_ref.shape[1] // LEFT_AT_ONCE
    sides = [pl.ds(0, columns), pl.ds(columns, columns)]

    def load(step):
        group, part = step // parts, step % parts
        source = left_ref.at[
            pl.ds(part * TOKENS_AT_ONCE, TOKENS_AT_ONCE), pl.ds(group * LEFT_AT_ONCE, LEFT_AT_ONCE)
        ]
        return pltpu.make_async_copy(source, left_buf.at[step % 2], sems.at[step % 2])

    def stores(group):
        rows = pl.ds(group * LEFT_AT_ONCE, LEFT_AT_ONCE)
        return [
            pltpu.make_async_copy(out_buf.at[:, side], out_ref.at[rows], sems.at[4 + n])
            for n, (side, out_ref) in enumerate(zip(sides, (out_first, out_second)))
        ]

    wholes = [
        pltpu.make_async_copy(ref, right_buf.at[:, side], sems.at[2 + n])
        for n, (side, ref) in enumerate(zip(sides, (first_ref, second_ref)))
    ]
    load(0).start()
    for copy in wholes:
        copy.start()
    yield
    for copy in wholes:
        copy.wait()
    for group in range(groups):
        for part in range(parts):
            step = group * parts + part
            load(step).wait()
            if step + 1 < groups * parts:
                load(step + 1).start()
            if part == 0:
                total[...] = jnp.zeros_like(total)

            @pl.loop(0, TOKENS_AT_ONCE // STEP)
            def _(j, step=step, part=part):
                left = left_buf[step % 2, pl.ds(pl.multiple_of(j * STEP, STEP), STEP), :]
                right = right_buf[pl.ds(pl.multiple_of(part * TOKENS_AT_ONCE + j * STEP, STEP), STEP), :]
                total[...] += dot_tn(left, right)

        if group > 0:
            for copy in stores(group - 1):
                copy.wait()
        out_buf[...] = total[...].astype(BF16)
        for copy in stores(group):
            copy.start()
        yield
    for copy in stores(groups - 1):
        copy.wait()


def cut_columns(*refs):
    count = (len(refs) - 2) // 2
    sources, targets, (room, sems) = refs[:count], refs[count : 2 * count], refs[2 * count :]

    def inward(n):
        columns = targets[n].shape[1]
        taken = pl.ds(pl.multiple_of(lax.axis_index("ctx") * columns, columns), columns)
        return pltpu.make_async_copy(sources[n].at[:, taken], room.at[n], sems.at[0, n])

    def outward(n):
        return pltpu.make_async_copy(room.at[n], targets[n], sems.at[1, n])

    for n in range(count):
        inward(n).start()
    yield
    for n in range(count):
        inward(n).wait()
        outward(n).start()
    yield
    for n in range(count):
        outward(n).wait()


def row_product(turned, left_ref, right_ref, out_ref, left_buf, right_buf, out_buf, sems):
    groups = left_ref.shape[0] // LEFT_AT_ONCE

    def rows(group):
        return pl.ds(group * LEFT_AT_ONCE, LEFT_AT_ONCE)

    def load(group):
        return pltpu.make_async_copy(left_ref.at[rows(group)], left_buf.at[group % 2], sems.at[group % 2])

    def store(group):
        return pltpu.make_async_copy(out_buf.at[group % 2], out_ref.at[rows(group)], sems.at[3 + group % 2])

    whole = pltpu.make_async_copy(right_ref, right_buf, sems.at[2])
    whole.start()
    load(0).start()
    yield
    whole.wait()
    for group in range(groups):
        load(group).wait()
        if group + 1 < groups:
            load(group + 1).start()
        if group > 1:
            store(group - 2).wait()

        @pl.loop(0, out_ref.shape[1] // STEP)
        def _(j, group=group):
            columns = pl.ds(pl.multiple_of(j * STEP, STEP), STEP)
            if turned:
                part = dot_t(left_buf[group % 2], right_buf[columns, :])
            else:
                part = dot_n(left_buf[group % 2], right_buf[:, columns])
            out_buf[group % 2, :, columns] = part.astype(BF16)

        store(group).start()
        yield
    for group in range(max(0, groups - 2), groups):
        store(group).wait()


def row_product_buffers(right, turned):
    return [
        pltpu.VMEM((2, LEFT_AT_ONCE, right.shape[1 if turned else 0]), BF16),
        pltpu.VMEM(right.shape, BF16),
        pltpu.VMEM((2, LEFT_AT_ONCE, right.shape[0 if turned else 1]), BF16),
        pltpu.SemaphoreType.DMA((5,)),
    ]


def gather_kernel(works, counts, paces, *refs):
    def take(count):
        nonlocal refs
        taken, refs = refs[:count], refs[count:]
        return taken

    (own_ref,) = take(1)
    inputs = [take(count[0]) for count in counts]
    (all_ref,) = take(1)
    outputs = [take(count[1]) for count in counts]
    gather = PlaneGather(own_ref, all_ref, *take(3))
    buffers, held = [], {}
    for work, count in zip(works, counts):
        if work not in held:
            held[work] = take(count[2])
        buffers.append(held[work])

    def all_work():
        started = [work(*given, *wanted, *room) for work, given, wanted, room in zip(works, inputs, outputs, buffers)]
        for one in started:
            next(one)
        for one in started:
            yield from one

    going = all_work()

    def some(count):
        for _ in range(count):
            next(going, None)

    gather.start()
    some(paces[0])
    gather.first()
    some(paces[1])
    gather.second()
    finish(going)
    gather.finish()


def plane_gather(rows, collective_id=0, jobs=(), paces=(0, 0)):
    count, width = rows.shape
    hbm = pl.BlockSpec(memory_space=pl.ANY)
    scratch, held = gather_sems(), set()
    for work, _, _, _, _, buffers in jobs:
        if work not in held:
            held.add(work)
            scratch += buffers
    return pl.pallas_call(
        functools.partial(
            gather_kernel,
            [job[0] for job in jobs],
            [(len(job[1]), len(job[3]), len(job[5])) for job in jobs],
            paces,
        ),
        in_specs=[hbm] + [spec for job in jobs for spec in job[2]],
        out_specs=[hbm] + [spec for job in jobs for spec in job[4]],
        out_shape=[jax.ShapeDtypeStruct((8 * count, width), rows.dtype)] + [out for job in jobs for out in job[3]],
        scratch_shapes=scratch,
        compiler_params=pltpu.CompilerParams(
            collective_id=collective_id, has_side_effects=True, vmem_limit_bytes=(48 << 20) if jobs else None
        ),
        cost_estimate=small_cost(),
        name="plane_gather",
    )(rows, *[value for job in jobs for value in job[1]])


HBM = pl.BlockSpec(memory_space=pl.ANY)
VMEM = pl.BlockSpec(memory_space=pltpu.VMEM)
ROWS_TURNED = functools.partial(row_product, True)
ROWS_STRAIGHT = functools.partial(row_product, False)


def token_job(left, right):
    out = jax.ShapeDtypeStruct((left.shape[1], right.shape[1]), BF16)
    return token_product, [left, right], [HBM] * 2, [out], [HBM], product_buffers(right.shape[1])


def pair_job(left, first, second):
    columns = first.shape[1]
    out = jax.ShapeDtypeStruct((left.shape[1], columns), BF16)
    room = [
        pltpu.VMEM((2, TOKENS_AT_ONCE, LEFT_AT_ONCE), BF16),
        pltpu.VMEM((left.shape[0], 2 * columns), BF16),
        pltpu.VMEM((LEFT_AT_ONCE, 2 * columns), F32),
        pltpu.VMEM((LEFT_AT_ONCE, 2 * columns), BF16),
        pltpu.SemaphoreType.DMA((6,)),
    ]
    return pair_product, [left, first, second], [HBM] * 3, [out] * 2, [HBM] * 2, room


def cut_job(weights, parts):
    outs = [jax.ShapeDtypeStruct((w.shape[0], w.shape[1] // parts), w.dtype) for w in weights]
    room = [pltpu.VMEM((len(weights),) + outs[0].shape, BF16), pltpu.SemaphoreType.DMA((2, len(weights)))]
    return cut_columns, list(weights), [HBM] * len(weights), outs, [HBM] * len(weights), room


def row_job(left, right, turned):
    out = jax.ShapeDtypeStruct((left.shape[0], right.shape[0 if turned else 1]), BF16)
    work = ROWS_TURNED if turned else ROWS_STRAIGHT
    return work, [left, right], [HBM] * 2, [out], [HBM], row_product_buffers(right, turned)


def table_job(lengths, parents, tokens):
    outs = [jax.ShapeDtypeStruct((8, tokens), jnp.int32), jax.ShapeDtypeStruct((tokens, 128), jnp.int32)]
    outs += [jax.ShapeDtypeStruct((tokens, 128), F32)] * 2
    room = [pltpu.VMEM(out.shape, out.dtype) for out in outs[1:]]
    room += [pltpu.SemaphoreType.DMA((3, tokens // TABLE_ROWS))]
    return table_work, [lengths, parents, rope_freqs(128)], [VMEM] * 3, outs, [VMEM, HBM, HBM, HBM], room


def scatter_kernel(rows, offsets, jobs, *refs):
    parts = len(offsets)

    def take(count):
        nonlocal refs
        taken, refs = refs[:count], refs[count:]
        return taken

    a_refs, w_homes, lefts, rights = take(parts), take(parts), take(jobs), take(jobs)
    (out_ref,), products = take(1), take(jobs)
    core_out, core_in, first_in, next_in, sems = take(5)
    a_bufs, w_refs, (a_sems, w_sems), buffers = take(parts), take(parts), take(2), refs

    def work(job):
        if job < jobs:
            finish(token_product(lefts[job], rights[job], products[job], *buffers))

    x, core, row = plane_place()
    over_x, over_row, over_core = plane_neighbours(x, core, row)
    half = rows // 2
    width = out_ref.shape[1]
    chunks = width // COLS

    def place(piece, on_core):
        far_x, far_row, part = PIECES[piece]
        bx = x + far_x - 2 * far_x * x
        by = row + far_row - 2 * far_row * row
        return pl.ds(pl.multiple_of(((bx * 2 + on_core) * 2 + by) * rows + part * half, half), half)

    def columns(j):
        return pl.ds(pl.multiple_of(j * COLS, COLS), COLS)

    steps = [(0, True)]
    for piece in range(8):
        steps += [(piece + 1, True)] * (piece < 7) + [(piece, False)]

    def load(step):
        piece, partner_half = steps[step]
        taken = place(piece, 1 - core if partner_half else core)
        return [
            pltpu.make_async_copy(a_ref.at[taken], a_buf.at[step % 2], a_sems.at[step % 2, p])
            for p, (a_ref, a_buf) in enumerate(zip(a_refs, a_bufs))
        ]

    w_copies = [
        pltpu.make_async_copy(home.at[:, pl.ds(offset, w_ref.shape[1])], w_ref, w_sems.at[p])
        for p, (home, offset, w_ref) in enumerate(zip(w_homes, offsets, w_refs))
    ]
    loads = {0: load(0)}
    for copy in w_copies + loads[0]:
        copy.start()
    enter_plane((over_x, over_row, over_core))
    for copy in w_copies:
        copy.wait()

    def partial(slot, j):
        total = None
        for a_buf, w_ref in zip(a_bufs, w_refs):
            term = dot_t(a_buf[slot], w_ref[columns(j), :])
            total = term if total is None else total + term
        return total

    def remote(source, target, slot, device):
        return pltpu.make_async_remote_copy(
            src_ref=source, dst_ref=target, send_sem=sems.at[0, slot], recv_sem=sems.at[1, slot],
            device_id=device, device_id_type=MESH,
        )

    core_copies, first_copies, next_copies = [], [], []
    for step, (piece, partner_half) in enumerate(steps):
        for copy in loads[step]:
            copy.wait()
        if step + 1 < len(steps):
            loads[step + 1] = load(step + 1)
            for copy in loads[step + 1]:
                copy.start()
        if partner_half:

            @pl.loop(0, chunks)
            def _(j, step=step, piece=piece):
                core_out[piece, :, columns(j)] = partial(step % 2, j).astype(BF16)

            core_copies.append(remote(core_out.at[piece], core_in.at[piece], piece, over_core))
            core_copies[-1].start()
            continue
        core_copies[piece].wait_recv()

        @pl.loop(0, chunks)
        def _(j, step=step, piece=piece):
            total = partial(step % 2, j) + core_in[piece, :, columns(j)].astype(F32)
            core_in[piece, :, columns(j)] = total.astype(BF16)

        if piece < 4:
            first_copies.append(
                remote(core_in.at[piece], first_in.at[piece], 8 + piece, over_x if piece % 2 == 0 else over_row)
            )
            first_copies[-1].start()
    for part in range(2):
        first_copies[part].wait_recv()

        @pl.loop(0, chunks)
        def _(j, part=part):
            total = core_in[4 + part, :, columns(j)].astype(F32) + first_in[part, :, columns(j)].astype(F32)
            core_in[4 + part, :, columns(j)] = total.astype(BF16)

        next_copies.append(remote(core_in.at[4 + part], next_in.at[part], 12 + part, over_row if part == 0 else over_x))
        next_copies[-1].start()
    for job in range(jobs):
        work(job)
    for part in range(2):
        first_copies[2 + part].wait_recv()
        next_copies[part].wait_recv()

        @pl.loop(0, chunks)
        def _(j, part=part):
            total = core_in[6 + part, :, columns(j)].astype(F32) + first_in[2 + part, :, columns(j)].astype(F32)
            out_ref[pl.ds(part * half, half), columns(j)] = total + next_in[part, :, columns(j)].astype(F32)

    for copy in core_copies + first_copies + next_copies:
        copy.wait_send()


def plane_scatter(parts, weights, collective_id, jobs=(), offsets=None):
    count = parts[0].shape[0]
    width = weights[0].shape[0]
    rows = count // 8
    half = rows // 2
    vmem, hbm = pl.BlockSpec(memory_space=pltpu.VMEM), pl.BlockSpec(memory_space=pl.ANY)
    offsets = offsets or [0] * len(parts)
    lefts, rights = [left for left, _ in jobs], [right for _, right in jobs]
    return pl.pallas_call(
        functools.partial(scatter_kernel, rows, offsets, len(jobs)),
        in_specs=[hbm] * (2 * len(parts) + 2 * len(jobs)),
        out_specs=[vmem] + [hbm] * len(jobs),
        out_shape=[jax.ShapeDtypeStruct((rows, width), F32)]
        + [jax.ShapeDtypeStruct((left.shape[1], right.shape[1]), BF16) for left, right in jobs],
        scratch_shapes=[
            pltpu.VMEM((8, half, width), BF16),
            pltpu.VMEM((8, half, width), BF16),
            pltpu.VMEM((4, half, width), BF16),
            pltpu.VMEM((2, half, width), BF16),
            pltpu.SemaphoreType.DMA((2, 14)),
        ]
        + [pltpu.VMEM((2, half, a.shape[1]), BF16) for a in parts]
        + [pltpu.VMEM((width, a.shape[1]), BF16) for a in parts]
        + [pltpu.SemaphoreType.DMA((2, len(parts))), pltpu.SemaphoreType.DMA((len(parts),))]
        + (product_buffers(rights[0].shape[1]) if jobs else []),
        compiler_params=pltpu.CompilerParams(
            collective_id=collective_id, has_side_effects=True, vmem_limit_bytes=(58 if jobs else 52) << 20
        ),
        cost_estimate=small_cost(),
        name="plane_scatter",
    )(*parts, *weights, *lefts, *rights)


def gated_kernel(x_ref, grad_ref, gate_ref, up_ref, hidden_ref, gate_grad_ref, up_grad_ref):
    columns = gate_ref.shape[1]
    step = min(256, columns)
    together = min(2, columns // step)

    @pl.loop(0, columns // (step * together))
    def _(j):
        for part in range(together):
            taken = pl.ds(pl.multiple_of((j * together + part) * step, step), step)
            gate = dot_n(x_ref[...], gate_ref[:, taken])
            up = dot_n(x_ref[...], up_ref[:, taken])
            grad = grad_ref[:, taken].astype(F32)
            sigmoid = jax.nn.sigmoid(gate)
            silu = gate * sigmoid
            hidden_ref[:, taken] = (silu * up).astype(BF16)
            gate_grad_ref[:, taken] = (grad * up * sigmoid * (1.0 + gate * (1.0 - sigmoid))).astype(BF16)
            up_grad_ref[:, taken] = (grad * silu).astype(BF16)


def gated_rows(x, hidden_grad, w_gate, w_up):
    tokens, depth = x.shape
    columns = w_gate.shape[1]
    block = 512
    rows = pl.BlockSpec((block, columns), lambda i: (i, 0))
    weight = pl.BlockSpec((depth, columns), lambda i: (0, 0), pipeline_mode=pl.Buffered(1))
    out = jax.ShapeDtypeStruct((tokens, columns), BF16)
    return pl.pallas_call(
        gated_kernel,
        grid=(tokens // block,),
        in_specs=[pl.BlockSpec((block, depth), lambda i: (i, 0)), rows, weight, weight],
        out_specs=[rows] * 3,
        out_shape=[out] * 3,
        compiler_params=pltpu.CompilerParams(vmem_limit_bytes=48 << 20),
        cost_estimate=small_cost(),
        name="gated_rows",
    )(x, hidden_grad, w_gate, w_up)


def is_plane():
    return lax.axis_size("ctx") == 4 and lax.axis_size("tensor") == 2


def gather_rows(rows):
    return lax.all_gather(rows, GROUP, axis=0, tiled=True)


def scatter_rows(rows):
    return lax.psum_scatter(rows.astype(BF16), GROUP, scatter_dimension=0, tiled=True).astype(F32)


def gather_now(rows):
    return plane_gather(rows)[0] if is_plane() else gather_rows(rows)


def cut(weight):
    columns = weight.shape[1] // lax.axis_size("ctx")
    return lax.dynamic_slice_in_dim(weight, lax.axis_index("ctx") * columns, columns, 1)


def gather_with_tables(rows, lengths, parents, tokens, width, weights):
    if is_plane():
        jobs = [cut_job(weights, lax.axis_size("ctx")), table_job(lengths, parents, tokens)]
        got = plane_gather(rows, 8, jobs, (4, 4))
        return got[:1] + got[1 + len(weights) :], got[1 : 1 + len(weights)]
    segment, parent, depth = tree_tables(lengths[0], parents[0], tokens)
    return [gather_rows(rows), *lay_out(segment, parent), *rope_tables(depth, width)], [cut(w) for w in weights]


def gather_with_product(rows, left, right):
    if is_plane():
        return plane_gather(rows, 5, [row_job(left, right, False)], (4, 4))
    return gather_rows(rows), dot_n(left, right).astype(BF16)


def gather_with_three(rows, left, right, shared, first, second):
    if is_plane():
        return plane_gather(rows, 4, [row_job(left, right, True), pair_job(shared, first, second)], (8, 3))
    products = dot_t(left, right), dot_tn(shared, first), dot_tn(shared, second)
    return [gather_rows(rows)] + [product.astype(BF16) for product in products]


def product_scatter(parts, weights, collective_id, jobs=(), offsets=None):
    if is_plane():
        return plane_scatter(parts, weights, collective_id, jobs, offsets)
    offsets = offsets or [0] * len(parts)
    weights = [w[:, first : first + part.shape[1]] for part, w, first in zip(parts, weights, offsets)]
    rows = scatter_rows(dot_t(jnp.concatenate(parts, axis=1), jnp.concatenate(weights, axis=1)))
    return [rows] + [dot_tn(left, right).astype(BF16) for left, right in jobs]


def gather_weight(own):
    return lax.all_gather(own, "fsdp", axis=0, tiled=True)


def scatter_weight(grad):
    return lax.psum_scatter(grad.astype(BF16), "fsdp", scatter_dimension=0, tiled=True)


def swap_rows(part):
    size = lax.axis_size("ctx")
    return lax.all_to_all(part.reshape(size, part.shape[0] // size, -1), "ctx", split_axis=0, concat_axis=0)


def lay_side_by_side(got, count):
    columns = got.shape[2] // count
    return [
        jnp.concatenate([got[j, :, c * columns : (c + 1) * columns] for j in range(got.shape[0])], axis=1).astype(F32)
        for c in range(count)
    ]


def normalize(rows):
    norm_inv = lax.rsqrt(jnp.mean(rows * rows, axis=1, keepdims=True) + EPSILON)
    return (rows * norm_inv, norm_inv)


def norm_backward(grad_rows, scaled, norm_inv, gain):
    weighted = grad_rows * gain[None, :]
    inner = jnp.mean(weighted * scaled, axis=1, keepdims=True)
    return norm_inv * (weighted - scaled * inner)


def body(
    tokens_in,
    attn_gain,
    query_weight,
    key_weight,
    value_weight,
    output_weight,
    mlp_gain,
    gate_weight,
    up_weight,
    down_weight,
    seg_lengths,
    leaf_parent,
    cotangent,
):
    ctx = lax.axis_index("ctx")
    parts = lax.axis_size("ctx")
    tree_len = tokens_in.shape[0] * parts * lax.axis_size("tensor")
    width = query_weight.shape[1] // parts
    units = gate_weight.shape[1] // parts

    def mine(weight, columns):
        return lax.dynamic_slice_in_dim(weight, ctx * columns, columns, 1)

    x_rows = tokens_in.astype(F32)
    attn_scaled, attn_inv = normalize(x_rows)
    w_attn = gather_weight(
        jnp.concatenate([mine(w, width) for w in (query_weight, key_weight, value_weight, output_weight)], axis=1)
    )
    (attn_in, rows_table, cols_table, cosine, sine), cuts = gather_with_tables(
        (attn_scaled * attn_gain[None, :]).astype(BF16),
        seg_lengths,
        leaf_parent,
        tree_len,
        min(2 * HEAD_DIM, width),
        [gate_weight, down_weight, up_weight],
    )
    w_gate, w_down, w_up = [gather_weight(own) for own in cuts]
    w_qkv, w_out = w_attn[:, : 3 * width], w_attn[:, 3 * width :]

    qkv = jnp.dot(attn_in, w_qkv, preferred_element_type=F32)
    if is_plane():
        attn_out, lse, query_rows, key_rows, value_rows, cot_all = attention_forward(
            qkv, cosine, sine, rows_table, cols_table, width, cotangent
        )
    else:
        attn_out, lse, query_rows, key_rows, value_rows = attention_forward(
            qkv, cosine, sine, rows_table, cols_table, width
        )
        cot_all = gather_rows(cotangent)
    mid_rows = x_rows + product_scatter([attn_out], [w_attn], 1, (), [3 * width])[0]
    mlp_scaled, mlp_inv = normalize(mid_rows)
    mlp_own = (mlp_scaled * mlp_gain[None, :]).astype(BF16)
    mlp_in, hidden_grad = gather_with_product(mlp_own, cot_all, w_down)
    hidden, gate_rows_grad, up_rows_grad = gated_rows(mlp_in, hidden_grad, w_gate, w_up)

    mlp_in_grad, down_part = product_scatter(
        [gate_rows_grad, up_rows_grad], [w_gate, w_up], 3, [(cot_all, hidden)]
    )
    down_grad = scatter_weight(down_part)
    mid_grad = cotangent.astype(F32) + norm_backward(mlp_in_grad, mlp_scaled, mlp_inv, mlp_gain)
    mid_all, down_rows, up_part, gate_part = gather_with_three(
        mid_grad.astype(BF16), hidden, w_down, mlp_in, up_rows_grad, gate_rows_grad
    )
    up_grad = scatter_weight(up_part)
    gate_grad = scatter_weight(gate_part)

    out_heads_grad = jnp.dot(mid_all, w_out, preferred_element_type=F32).astype(BF16)
    output_grad = dot_tn(mid_all, attn_out).astype(BF16)
    out_heads_grad, down_grad = lax.optimization_barrier((out_heads_grad, down_grad))
    if is_plane():
        pre_grads, down_rows = attention_backward(
            query_rows, key_rows, value_rows, attn_out, out_heads_grad, lse, cosine, sine, rows_table, cols_table, down_rows
        )
    else:
        pre_grads = attention_backward(
            query_rows, key_rows, value_rows, attn_out, out_heads_grad, lse, cosine, sine, rows_table, cols_table
        )
        pre_grads = jnp.concatenate(pre_grads, axis=1)
        down_rows = scatter_rows(down_rows)
    block_out = (mid_rows + down_rows.astype(F32)).astype(BF16)
    pre_grads, up_grad, gate_grad, down_swapped = lax.optimization_barrier(
        (pre_grads, up_grad, gate_grad, swap_rows(down_grad))
    )
    swapped = swap_rows(jnp.concatenate([gate_grad, up_grad], axis=1))
    attn_part = jnp.concatenate([dot_tn(attn_in, pre_grads).astype(BF16), output_grad], axis=1)
    pre_grads, attn_part, swapped = lax.optimization_barrier((pre_grads, attn_part, swapped))
    attn_grad = scatter_weight(attn_part)
    (attn_in_grad,) = product_scatter([pre_grads], [w_attn], 2)
    attn_in_grad, attn_grad = lax.optimization_barrier((attn_in_grad, attn_grad))
    gate_out, up_out = lay_side_by_side(swapped, 2)
    (down_out,) = lay_side_by_side(down_swapped, 1)
    query_out, key_out, value_out, output_out = lay_side_by_side(swap_rows(attn_grad), 4)

    def gain_part(pairs, gain):
        held = query_out.shape[0]
        total = sum(
            jnp.sum(lax.dynamic_slice_in_dim(weight, ctx * held, held, 0).astype(F32) * grad, axis=1)
            for weight, grad in pairs
        )
        first = (lax.axis_index("fsdp") * parts + ctx) * held
        return total / lax.dynamic_slice_in_dim(gain, first, held, 0)

    sums = jnp.stack(
        [
            gain_part([(query_weight, query_out), (key_weight, key_out), (value_weight, value_out)], attn_gain),
            gain_part([(gate_weight, gate_out), (up_weight, up_out)], mlp_gain),
        ]
    )
    row, others = lax.axis_index("tensor"), lax.axis_size("tensor")
    kept = sums.shape[1] // others
    if others == 2:
        got = lax.ppermute(lax.dynamic_slice_in_dim(sums, (1 - row) * kept, kept, 1), "tensor", [(0, 1), (1, 0)])
        gain_grads = lax.dynamic_slice_in_dim(sums, row * kept, kept, 1) + got
    else:
        gain_grads = lax.dynamic_slice_in_dim(lax.psum(sums, "tensor"), row * kept, kept, 1)

    attn_back = norm_backward(attn_in_grad, attn_scaled, attn_inv, attn_gain)
    input_grad = (mid_grad + attn_back).astype(BF16)
    return (
        block_out,
        input_grad,
        gain_grads[0],
        query_out,
        key_out,
        value_out,
        output_out,
        gain_grads[1],
        gate_out,
        up_out,
        down_out,
    )


def solution(mesh):
    rows = P(("fsdp", "ctx", "tensor"), None)
    weight = P("fsdp", "tensor")
    gain = P(("fsdp", "ctx", "tensor"))
    grad = P(("fsdp", "ctx"), "tensor")
    in_specs = (
        rows, P(), weight, weight, weight, weight, P(), weight, weight, weight, P("fsdp", None), P("fsdp", None), rows,
    )
    out_specs = (rows, rows, gain, grad, grad, grad, grad, gain, grad, grad, grad)
    return jax.shard_map(body, mesh=mesh, in_specs=in_specs, out_specs=out_specs, check_vma=False)
```

```python
import functools

import jax
import jax.numpy as jnp
import numpy as np
from jax import lax
from jax.experimental import pallas as pl
from jax.experimental.pallas import tpu as pltpu
from jax.sharding import PartitionSpec as P

HEAD_DIM = 64
TRUNK = 2176
MOST_SEG = 128
ROPE_BASE = 130000.0
EPSILON = 1e-05
NEG_LARGE = -1e30
SCALE = HEAD_DIM ** (-0.5)

BQ = 512
BK = 512
GROUP = ("ctx", "tensor")

F32 = jnp.float32
BF16 = jnp.bfloat16


def pick_table(onehot, table):
    return jnp.sum(jnp.where(onehot, table[None, :], 0), axis=1)


def tree_tables(lengths_row, parent_row, tree_len):
    branches = lengths_row.shape[0] - parent_row.shape[0]
    ends = TRUNK + jnp.cumsum(lengths_row)
    starts = ends - lengths_row
    matches = parent_row[:, None] - 1 == jnp.arange(branches, dtype=jnp.int32)[None, :]
    parent_len = jnp.sum(jnp.where(matches, lengths_row[None, :branches], 0), axis=1)
    zero_one = jnp.zeros((1,), jnp.int32)
    seg_start = jnp.concatenate([zero_one, starts])
    seg_base = jnp.concatenate(
        [zero_one, jnp.full((branches,), TRUNK, jnp.int32), TRUNK + parent_len]
    )
    seg_parent = jnp.concatenate([zero_one, jnp.zeros((branches,), jnp.int32), parent_row])
    positions = jnp.arange(tree_len, dtype=jnp.int32)
    above = jnp.sum((ends[None, :] <= positions[:, None]).astype(jnp.int32), axis=1)
    segment = (positions >= TRUNK).astype(jnp.int32) + above
    onehot = segment[:, None] == jnp.arange(seg_start.shape[0], dtype=jnp.int32)[None, :]
    depth = positions - pick_table(onehot, seg_start) + pick_table(onehot, seg_base)
    parent = pick_table(onehot, seg_parent)
    return (segment, parent, depth)


def rope_freqs(width):
    half = HEAD_DIM // 2
    powers = -2.0 * (np.arange(width) % half) / HEAD_DIM
    return np.power(ROPE_BASE, powers).astype(np.float32)[None, :]


def rope_tables(depth, width):
    angles = depth.astype(F32)[:, None] * rope_freqs(width)
    sign = np.where(np.arange(width) % HEAD_DIM < HEAD_DIM // 2, -1.0, 1.0).astype(np.float32)
    return jnp.cos(angles), jnp.sin(angles) * sign[None, :]


def lay_out(segment, parent):
    both = jnp.stack([segment, parent])
    return jnp.pad(both, ((0, 6), (0, 0))), jnp.pad(both.T, ((0, 0), (0, 126)))


TABLE_ROWS = 512
TABLE_STEP = 64


def tables_at(positions, lengths, parents):
    leaves = parents.shape[1]
    branches = lengths.shape[1] - leaves
    zero = jnp.zeros_like(positions)
    segment = jnp.where(positions >= TRUNK, 1, 0)
    parent, depth = zero, positions
    end = jnp.full((1, 1), TRUNK, jnp.int32)
    starts = []
    for s in range(branches + leaves):
        start, end = end, end + lengths[:, s : s + 1]
        inside = (positions >= start) & (positions < end)
        base, above = jnp.full((1, 1), TRUNK, jnp.int32), jnp.zeros((1, 1), jnp.int32)
        if s >= branches:
            above = parents[:, s - branches : s - branches + 1]
            for b in range(branches):
                base = base + jnp.where(above == b + 1, lengths[:, b : b + 1], 0)
        segment = segment + jnp.where(positions >= end, 1, 0)
        parent = jnp.where(inside, above, parent)
        depth = jnp.where(inside, positions - start + base, depth)
    return segment, parent, depth


def sine_cosine(x):
    turns = jnp.floor(x * np.float32(2.0 / np.pi) + 0.5)
    r = x - turns * np.float32(1.5703125)
    r = r - turns * np.float32(4.837512969970703125e-4)
    r = r - turns * np.float32(7.549789954891882e-8)
    z = r * r
    sine = ((np.float32(-1.9515295891e-4) * z + np.float32(8.3321608736e-3)) * z - np.float32(1.6666654611e-1)) * z * r + r
    cosine = (
        (np.float32(2.443315711809948e-5) * z - np.float32(1.388731625493765e-3)) * z + np.float32(4.166664568298827e-2)
    ) * z * z - np.float32(0.5) * z + np.float32(1.0)
    quarter = turns.astype(jnp.int32) & 3
    odd = (quarter & 1) == 1
    first, second = jnp.where(odd, cosine, sine), jnp.where(odd, sine, cosine)
    return jnp.where(quarter >= 2, -first, first), jnp.where((quarter == 1) | (quarter == 2), -second, second)


def table_work(lengths, parents, freqs, rows_ref, cols_ref, cos_ref, sin_ref, cols_buf, cos_buf, sin_buf, sems):
    yield
    tokens = cos_ref.shape[0]
    shape = (8, tokens)
    segment, parent, _ = tables_at(lax.broadcasted_iota(jnp.int32, shape, 1), lengths, parents)
    line = lax.broadcasted_iota(jnp.int32, shape, 0)
    rows_ref[...] = jnp.where(line == 0, segment, jnp.where(line == 1, parent, 0))
    copies = []
    for chunk in range(tokens // TABLE_ROWS):
        rows = pl.ds(chunk * TABLE_ROWS, TABLE_ROWS)

        @pl.loop(0, TABLE_ROWS // TABLE_STEP)
        def _(j, chunk=chunk):
            first = pl.multiple_of(chunk * TABLE_ROWS + j * TABLE_STEP, TABLE_STEP)
            taken = pl.ds(first, TABLE_STEP)
            shape = (TABLE_STEP, 128)
            lane = lax.broadcasted_iota(jnp.int32, shape, 1)
            segment, parent, depth = tables_at(lax.broadcasted_iota(jnp.int32, shape, 0) + first, lengths, parents)
            cols_buf[taken, :] = jnp.where(lane == 0, segment, jnp.where(lane == 1, parent, 0))
            sine, cosine = sine_cosine(depth.astype(F32) * freqs[...])
            cos_buf[taken, :] = cosine
            sin_buf[taken, :] = jnp.where(lane % HEAD_DIM < HEAD_DIM // 2, -sine, sine)

        for kind, (source, target) in enumerate(((cols_buf, cols_ref), (cos_buf, cos_ref), (sin_buf, sin_ref))):
            copies.append(pltpu.make_async_copy(source.at[rows], target.at[rows], sems.at[kind, chunk]))
            copies[-1].start()
        yield
    for copy in copies:
        copy.wait()


MESH = pl.DeviceIdType.MESH


def plane_place():
    ctx, row = lax.axis_index("ctx"), lax.axis_index("tensor")
    x, core = ctx // 2, ctx % 2
    return x, core, row


def plane_neighbours(x, core, row):
    over_x = {"ctx": (1 - x) * 2 + core}
    over_core = {"ctx": x * 2 + 1 - core}
    over_row = {"tensor": 1 - row}
    return over_x, over_row, over_core


def enter_plane(neighbours):
    barrier = pltpu.get_barrier_semaphore()
    for device in neighbours:
        pl.semaphore_signal(barrier, inc=1, device_id=device, device_id_type=MESH)
    pl.semaphore_wait(barrier, 3)


PIECES = ((1, 1, 0), (1, 1, 1), (1, 0, 0), (0, 1, 1), (0, 1, 0), (1, 0, 1), (0, 0, 0), (0, 0, 1))
COLS = 512


class PlaneGather:
    def __init__(self, own_ref, all_ref, local_sem, send_sem, recv_sem):
        self.own_ref, self.all_ref, self.sems = own_ref, all_ref, (local_sem, send_sem, recv_sem)
        self.x, self.core, self.row = plane_place()
        self.devices = plane_neighbours(self.x, self.core, self.row)
        self.rows = own_ref.shape[0]

    def place(self, far_x, far_row, part):
        bx = self.x + far_x - 2 * far_x * self.x
        by = self.row + far_row - 2 * far_row * self.row
        half = self.rows // 2
        return pl.ds(pl.multiple_of(((bx * 2 + self.core) * 2 + by) * self.rows + part * half, half), half)

    def copy(self, slot):
        far_x, far_row, part, device = (
            (0, 0, 0, 1), (0, 0, 1, 1), (1, 0, 1, 1), (0, 0, 1, 0), (0, 0, 0, 0), (0, 1, 0, 0), (0, 0, 0, 2),
            (0, 0, 1, 2), (0, 1, 0, 2), (1, 0, 1, 2), (0, 1, 1, 2), (1, 0, 0, 2), (1, 1, 0, 2), (1, 1, 1, 2),
        )[slot]
        half = self.rows // 2
        target = self.place(far_x, far_row, part)
        own = far_x == 0 and far_row == 0
        source = self.own_ref.at[pl.ds(part * half, half)] if own else self.all_ref.at[target]
        return pltpu.make_async_remote_copy(
            src_ref=source, dst_ref=self.all_ref.at[target], send_sem=self.sems[1].at[slot],
            recv_sem=self.sems[2].at[slot], device_id=self.devices[device], device_id_type=MESH,
        )

    def local(self, part):
        half = self.rows // 2
        return pltpu.make_async_copy(
            self.own_ref.at[pl.ds(part * half, half)], self.all_ref.at[self.place(0, 0, part)], self.sems[0].at[part]
        )

    def start(self):
        enter_plane(self.devices)
        for slot in (0, 3, 1, 4, 6, 7):
            self.copy(slot).start()
        for part in range(2):
            self.local(part).start()

    def forward(self, got, slots):
        self.copy(got).wait_recv()
        for slot in slots:
            self.copy(slot).start()

    def first(self):
        self.forward(0, (5, 8))
        self.forward(3, (2, 9))

    def second(self):
        self.forward(1, (10,))
        self.forward(4, (11,))

    def finish(self):
        self.forward(5, (12,))
        self.forward(2, (13,))
        for slot in range(6, 14):
            self.copy(slot).wait_recv()
        for slot in range(14):
            self.copy(slot).wait_send()
        for part in range(2):
            self.local(part).wait()


def gather_sems():
    return [pltpu.SemaphoreType.DMA((2,)), pltpu.SemaphoreType.DMA((14,)), pltpu.SemaphoreType.DMA((14,))]


class PlaneScatter:
    def __init__(self, part_ref, out_ref, core_in, first_in, next_in, own, total, sems, own_sems):
        self.part_ref, self.out_ref, self.core_in, self.first_in, self.next_in = part_ref, out_ref, core_in, first_in, next_in
        self.own, self.total, self.sems, self.own_sems = own, total, sems, own_sems
        self.x, self.core, self.row = plane_place()
        self.devices = plane_neighbours(self.x, self.core, self.row)
        self.rows = part_ref.shape[0] // 8

    def place(self, piece, on_core):
        far_x, far_row, part = PIECES[piece]
        bx = self.x + far_x - 2 * far_x * self.x
        by = self.row + far_row - 2 * far_row * self.row
        half = self.rows // 2
        return pl.ds(pl.multiple_of(((bx * 2 + on_core) * 2 + by) * self.rows + part * half, half), half)

    def copy(self, slot):
        if slot < 8:
            source, target, device = self.part_ref.at[self.place(slot, 1 - self.core)], self.core_in.at[slot], 2
        elif slot < 12:
            source, target, device = self.core_in.at[slot - 8], self.first_in.at[slot - 8], slot % 2
        else:
            source, target, device = self.core_in.at[slot - 8], self.next_in.at[slot - 12], 1 - slot % 2
        return pltpu.make_async_remote_copy(
            src_ref=source, dst_ref=target, send_sem=self.sems.at[0, slot], recv_sem=self.sems.at[1, slot],
            device_id=self.devices[device], device_id_type=MESH,
        )

    def load(self, piece):
        return pltpu.make_async_copy(
            self.part_ref.at[self.place(piece, self.core)], self.own.at[piece % 4], self.own_sems.at[piece % 4]
        )

    def add(self, target, where, *others):
        @pl.loop(0, target.shape[-1] // COLS)
        def _(j):
            columns = pl.ds(pl.multiple_of(j * COLS, COLS), COLS)
            total = sum(ref[slot, :, columns].astype(F32) for ref, slot in others)
            target[where, :, columns] = total.astype(target.dtype)

    def start(self):
        enter_plane(self.devices)
        for slot in range(8):
            self.copy(slot).start()
        for piece in range(4):
            self.load(piece).start()

    def first(self):
        for piece in range(4):
            self.load(piece).wait()
            self.copy(piece).wait_recv()
            self.add(self.core_in, piece, (self.own, piece), (self.core_in, piece))
            self.copy(8 + piece).start()
        for piece in range(4, 8):
            self.load(piece).start()

    def second(self):
        for piece in range(4, 8):
            self.load(piece).wait()
            self.copy(piece).wait_recv()
            self.add(self.core_in, piece, (self.own, piece - 4), (self.core_in, piece))

    def third(self):
        for part in range(2):
            self.copy(8 + part).wait_recv()
            self.add(self.core_in, 4 + part, (self.core_in, 4 + part), (self.first_in, part))
            self.copy(12 + part).start()

    def finish(self):
        half = self.rows // 2
        for part in range(2):
            self.copy(10 + part).wait_recv()
            self.copy(12 + part).wait_recv()
            self.add(self.total, part, (self.core_in, 6 + part), (self.first_in, 2 + part), (self.next_in, part))
        stores = [
            pltpu.make_async_copy(
                self.total.at[part], self.out_ref.at[pl.ds(part * half, half)], self.own_sems.at[part]
            )
            for part in range(2)
        ]
        for store in stores:
            store.start()
        for slot in range(14):
            self.copy(slot).wait_send()
        for store in stores:
            store.wait()


def scatter_scratch(rows, width):
    half = rows // 2
    return [
        pltpu.VMEM((8, half, width), BF16),
        pltpu.VMEM((4, half, width), BF16),
        pltpu.VMEM((2, half, width), BF16),
        pltpu.VMEM((4, half, width), BF16),
        pltpu.VMEM((2, half, width), BF16),
        pltpu.SemaphoreType.DMA((2, 14)),
        pltpu.SemaphoreType.DMA((4,)),
    ]


def at_step(step, total, places):
    for place, phase in places:

        @pl.when(step == place)
        def _(phase=phase):
            phase()


def partner(x):
    half = HEAD_DIM // 2
    width = x.shape[1]
    if width == HEAD_DIM:
        return jnp.concatenate([x[:, half:], x[:, :half]], axis=1)
    lane = lax.broadcasted_iota(jnp.int32, x.shape, 1)
    ahead = pltpu.roll(x, width - half, 1)
    behind = pltpu.roll(x, half, 1)
    return jnp.where(lane % HEAD_DIM < half, ahead, behind)


def head_mask(shape, head):
    lane = lax.broadcasted_iota(jnp.int32, shape, 1)
    return lane // HEAD_DIM == head


def dot_t(a, b):
    return lax.dot_general(a, b, (((1,), (1,)), ((), ())), preferred_element_type=F32)


def dot_n(a, b):
    return lax.dot_general(a, b, (((1,), (0,)), ((), ())), preferred_element_type=F32)


def dot_tn(a, b):
    return lax.dot_general(a, b, (((0,), (0,)), ((), ())), preferred_element_type=F32)


def key_plan(i, tile):
    base = TRUNK // BK * BK
    branch_end = TRUNK + 4 * MOST_SEG
    first_tree = base // BQ
    mixed_end = -(-(branch_end + MOST_SEG) // BQ)
    chunks = jnp.minimum(i * BQ, base) // BK

    @pl.when(i < first_tree)
    def _():
        @pl.loop(0, chunks)
        def _(j):
            start = pl.multiple_of(j * BK, BK)
            tile(start, BK, 0, start)

    @pl.when(i >= first_tree)
    def _():
        tile(0, base, 0, 0)

    @pl.when(i < first_tree)
    def _():
        start = pl.multiple_of(chunks * BK, BK)
        tile(start, BK, 1, start)

    for block in range(first_tree, mixed_end):

        @pl.when(i == block)
        def _(block=block):
            tile(base, (block + 1) * BQ - base, 2, base)

    @pl.when(i >= mixed_end)
    def _():
        tile(base, branch_end - base, 3, base)
        tile(pl.multiple_of(i * BQ - MOST_SEG, MOST_SEG), BQ + MOST_SEG, 4, branch_end)


def most_keys():
    return TRUNK + 4 * MOST_SEG + BQ + MOST_SEG


def seen_mask(kind, q_at, k_at, seg_q, par_q, seg_k):
    if kind == 3:
        return (seg_k == 0) | (seg_k == par_q)
    causal = k_at <= q_at
    if kind == 1:
        return causal
    if kind == 4:
        return causal & (seg_k == seg_q)
    return causal & ((seg_k == 0) | (seg_k == seg_q) | (seg_k == par_q))


def fwd_kernel(heads, hosts, *refs):
    if not hosts:
        return fwd_work(heads, *refs)
    gather = PlaneGather(refs[7], refs[13], *refs[-3:])
    step, total = pl.program_id(0) * pl.num_programs(1) + pl.program_id(1), 16
    at_step(step, total, ((0, gather.start), (6, gather.first), (12, gather.second)))
    fwd_work(heads, *refs[:7], *refs[8:13], *refs[14:-3])
    at_step(step, total, ((total - 1, gather.finish),))


def fwd_work(
    heads, q_ref, k_ref, v_ref, cos_ref, sin_ref, rows_ref, cols_ref,
    o_ref, lse_ref, qr_ref, kr_ref, vr_ref, kt_ref, va_ref, s_ref, m_ref, acc_ref,
):
    i = pl.program_id(1)
    wide = 2 * HEAD_DIM

    @pl.when(i == 0)
    def _():
        @pl.loop(0, k_ref.shape[0] // BK)
        def _(j):
            rows = pl.ds(pl.multiple_of(j * BK, BK), BK)
            k = k_ref[rows, :]
            k = (k * cos_ref[rows, :] + partner(k) * sin_ref[rows, :]).astype(BF16)
            kr_ref[rows, :] = k
            kt_ref[:, rows] = jnp.transpose(k)
            v = v_ref[rows, :].astype(BF16)
            vr_ref[rows, :] = v
            if heads == 1:
                va_ref[0, rows, :] = jnp.concatenate([v, jnp.ones_like(v)], axis=1)
            else:
                for h in range(heads):
                    va_ref[h, rows, :] = jnp.where(head_mask(v.shape, h), v, jnp.ones_like(v))

    rows = pl.ds(pl.multiple_of(i * BQ, BQ), BQ)
    q = q_ref[...]
    q = (q * cos_ref[rows, :] + partner(q) * sin_ref[rows, :]).astype(BF16)
    qr_ref[...] = q
    q = q * jnp.asarray(SCALE, BF16)
    q_heads = [jnp.where(head_mask(q.shape, h), q, jnp.zeros_like(q)) for h in range(heads)]
    m_ref[...] = jnp.full_like(m_ref, NEG_LARGE)
    acc_ref[...] = jnp.zeros_like(acc_ref)

    def score_tile(start, width, kind, place):
        keys = pl.ds(start, width)
        k = kt_ref[:, keys]
        seen = None
        if kind != 0:
            shape = (BQ, width)
            seen = seen_mask(
                kind,
                lax.broadcasted_iota(jnp.int32, shape, 0) + i * BQ,
                lax.broadcasted_iota(jnp.int32, shape, 1) + start,
                cols_ref[:, 0:1], cols_ref[:, 1:2], rows_ref[0:1, keys],
            )
        for h in range(heads):
            s = dot_n(q_heads[h], k)
            if seen is not None:
                s = jnp.where(seen, s, NEG_LARGE)
            s_ref[h, :, pl.ds(place, width)] = s
            largest = m_ref[h]
            for c in range(width // 128):
                largest = jnp.maximum(largest, s[:, c * 128 : (c + 1) * 128])
            m_ref[h] = largest

    key_plan(i, score_tile)
    for h in range(heads):
        m_ref[h] = jnp.broadcast_to(jnp.max(m_ref[h], axis=1, keepdims=True), (BQ, 128))

    def value_tile(start, width, kind, place):
        keys = pl.ds(start, width)
        for h in range(heads):
            m = m_ref[h]
            parts = [
                jnp.exp(s_ref[h, :, pl.ds(place + c * 128, 128)] - m).astype(BF16) for c in range(width // 128)
            ]
            acc_ref[h] += dot_n(jnp.concatenate(parts, axis=1), va_ref[h, keys, :])

    key_plan(i, value_tile)
    out, lse = None, None
    for h in range(heads):
        acc = acc_ref[h]
        part = acc / pltpu.roll(acc, HEAD_DIM, 1)
        stat = m_ref[h] + jnp.log(jnp.broadcast_to(acc[:, (1 - h) * HEAD_DIM : (1 - h) * HEAD_DIM + 1], (BQ, wide)))
        mask = head_mask((BQ, wide), h)
        out = part if h == 0 else jnp.where(mask, part, out)
        lse = stat if h == 0 else jnp.where(mask, stat, lse)
    o_ref[...] = out[:, : heads * HEAD_DIM].astype(BF16)
    turned = jnp.transpose(lse)
    for h in range(heads):
        lse_ref[0, h : h + 1, :] = turned[h * HEAD_DIM : h * HEAD_DIM + 1, :]


def bwd_kernel(heads, hosts, *refs):
    if not hosts:
        return bwd_work(heads, *refs)
    scatter = PlaneScatter(refs[10], refs[12], *refs[-7:])
    step, total = pl.program_id(0) * pl.num_programs(1) + pl.program_id(1), 16
    at_step(
        step, total, ((0, scatter.start), (3, scatter.first), (5, scatter.second), (7, scatter.third))
    )
    bwd_work(heads, *refs[:10], *refs[13:-7], together=refs[11])
    at_step(step, total, ((total - 1, scatter.finish),))


def bwd_work(
    heads, q_ref, k_ref, v_ref, o_ref, do_ref, lse_ref, cos_ref, sin_ref, rows_ref, cols_ref,
    *refs, together=None,
):
    if together is None:
        dq_ref, dk_ref, dv_ref, dq_acc, dk_acc, dv_acc = refs
    else:
        dq_acc, dk_acc, dv_acc, dq_ref, dk_ref, dv_ref, out_sems = refs
    i = pl.program_id(1)

    def store(kind, source, rows, sem):
        groups, width = pl.num_programs(0), source.shape[1]
        columns = pl.ds(pl.multiple_of((kind * groups + pl.program_id(0)) * width, width), width)
        return pltpu.make_async_copy(source, together.at[rows, columns], out_sems.at[sem])

    @pl.when(i == 0)
    def _():
        dk_acc[...] = jnp.zeros_like(dk_acc)
        dv_acc[...] = jnp.zeros_like(dv_acc)

    q = q_ref[...]
    scaled = q * jnp.asarray(SCALE, BF16)
    do = do_ref[...]
    product = jnp.transpose(do.astype(F32) * o_ref[...].astype(F32))
    zero = jnp.zeros_like(q)
    masks = [head_mask(q.shape, h) for h in range(heads)]
    q_heads = [jnp.where(m, scaled, zero) for m in masks]
    do_heads = [jnp.where(m, do, zero) for m in masks]
    deltas = [
        jnp.sum(product[h * HEAD_DIM : (h + 1) * HEAD_DIM, :], axis=0, keepdims=True) for h in range(heads)
    ]
    lses = [lse_ref[0, h : h + 1, :] for h in range(heads)]
    q_turned = [jnp.transpose(x) for x in q_heads]
    do_turned = [jnp.transpose(x) for x in do_heads]
    q_stack = jnp.concatenate(q_heads, axis=0)
    do_stack = jnp.concatenate(do_heads, axis=0)
    dq_acc[...] = jnp.zeros_like(dq_acc)

    def tile(start, width, kind, place):
        keys = pl.ds(start, width)
        k = k_ref[keys, :]
        v = v_ref[keys, :]
        seen = None
        if kind != 0:
            shape = (width, BQ)
            seen = seen_mask(
                kind,
                lax.broadcasted_iota(jnp.int32, shape, 1) + i * BQ,
                lax.broadcasted_iota(jnp.int32, shape, 0) + start,
                rows_ref[0:1, :], rows_ref[1:2, :], cols_ref[keys, 0:1],
            )
        probs, grads, k_heads = [], [], []
        for h in range(heads):
            s = dot_n(k, q_turned[h])
            p = jnp.exp(s - lses[h])
            if seen is not None:
                p = jnp.where(seen, p, 0.0)
            dp = dot_n(v, do_turned[h])
            probs.append(p.astype(BF16))
            grads.append((p * (dp - deltas[h])).astype(BF16))
            k_heads.append(jnp.where(head_mask(k.shape, h), k, jnp.zeros_like(k)))
        grad_row = jnp.concatenate(grads, axis=1)
        dv_acc[keys, :] += dot_n(jnp.concatenate(probs, axis=1), do_stack)
        dk_acc[keys, :] += dot_n(grad_row, q_stack)
        dq_acc[...] += dot_tn(jnp.concatenate(grads, axis=0), jnp.concatenate(k_heads, axis=0))

    key_plan(i, tile)
    dq = dq_acc[...] * SCALE
    rows = pl.ds(pl.multiple_of(i * BQ, BQ), BQ)
    dq = (dq * cos_ref[rows, :] - partner(dq) * sin_ref[rows, :]).astype(BF16)
    if together is None:
        dq_ref[...] = dq
    else:
        step, last = pl.program_id(0) * pl.num_programs(1) + i, pl.num_programs(0) * pl.num_programs(1) - 1
        for slot in range(2):

            @pl.when(step % 2 == slot)
            def _(slot=slot):
                @pl.when(step >= 2)
                def _():
                    store(0, dq_ref.at[slot], rows, slot).wait()

                dq_ref[slot] = dq
                store(0, dq_ref.at[slot], rows, slot).start()

        @pl.when(step == last)
        def _():
            for slot in range(2):
                store(0, dq_ref.at[slot], rows, slot).wait()

    @pl.when(i == pl.num_programs(1) - 1)
    def _():
        @pl.loop(0, dk_acc.shape[0] // BK)
        def _(j):
            rows = pl.ds(pl.multiple_of(j * BK, BK), BK)
            dk = dk_acc[rows, :]
            dk_ref[rows, :] = (dk * cos_ref[rows, :] - partner(dk) * sin_ref[rows, :]).astype(BF16)
            dv_ref[rows, :] = dv_acc[rows, :].astype(BF16)

        if together is not None:
            every = pl.ds(0, dk_acc.shape[0])
            copies = [store(1, dk_ref, every, 2), store(2, dv_ref, every, 3)]
            for copy in copies:
                copy.start()
            for copy in copies:
                copy.wait()


def small_cost():
    return pl.CostEstimate(flops=1 << 20, bytes_accessed=1 << 20, transcendentals=0)


def attention_forward(qkv, cosine, sine, rows_table, cols_table, width, hosted=None):
    tree_len = qkv.shape[0]
    gw = min(2 * HEAD_DIM, width)
    groups, heads = width // gw, gw // HEAD_DIM
    row_block = pl.BlockSpec((BQ, gw), lambda g, i: (i, g))
    table = pl.BlockSpec((tree_len, gw), lambda g, i: (0, 0))
    full = pl.BlockSpec((tree_len, gw), lambda g, i: (0, g))
    act = jax.ShapeDtypeStruct((tree_len, width), BF16)
    if width % 128 == 0:
        queries, keys, values, step = qkv, qkv, qkv, groups
    else:
        queries, keys, values = jnp.split(qkv, 3, axis=1)
        step = 0
    hosts = hosted is not None
    hbm = pl.BlockSpec(memory_space=pl.ANY)
    return pl.pallas_call(
        functools.partial(fwd_kernel, heads, hosts),
        grid=(groups, tree_len // BQ),
        in_specs=[
            row_block,
            pl.BlockSpec((tree_len, gw), lambda g, i: (0, step + g)),
            pl.BlockSpec((tree_len, gw), lambda g, i: (0, 2 * step + g)),
            table,
            table,
            pl.BlockSpec((8, tree_len), lambda g, i: (0, 0)),
            pl.BlockSpec((BQ, 128), lambda g, i: (i, 0)),
        ]
        + [hbm] * hosts,
        out_specs=[row_block, pl.BlockSpec((1, heads, BQ), lambda g, i: (g, 0, i)), row_block, full, full] + [hbm] * hosts,
        out_shape=[act, jax.ShapeDtypeStruct((groups, heads, tree_len), F32), act, act, act]
        + ([jax.ShapeDtypeStruct((8 * hosted.shape[0], hosted.shape[1]), BF16)] if hosts else []),
        scratch_shapes=[
            pltpu.VMEM((gw, tree_len), BF16),
            pltpu.VMEM((heads, tree_len, 128), BF16),
            pltpu.VMEM((heads, BQ, most_keys()), F32),
            pltpu.VMEM((heads, BQ, 128), F32),
            pltpu.VMEM((heads, BQ, 128), F32),
        ]
        + (gather_sems() if hosts else []),
        compiler_params=pltpu.CompilerParams(
            vmem_limit_bytes=56 << 20, collective_id=6 if hosts else None, has_side_effects=hosts
        ),
        cost_estimate=small_cost(),
        name="tree_attention_forward",
    )(queries, keys, values, cosine, sine, rows_table, cols_table, *([hosted] if hosts else []))


def attention_backward(q, k, v, out, grad, lse, cosine, sine, rows_table, cols_table, hosted=None):
    tree_len, width = q.shape
    gw = min(2 * HEAD_DIM, width)
    groups, heads = width // gw, gw // HEAD_DIM
    row_block = pl.BlockSpec((BQ, gw), lambda g, i: (i, g))
    table = pl.BlockSpec((tree_len, gw), lambda g, i: (0, 0))
    full = pl.BlockSpec((tree_len, gw), lambda g, i: (0, g))
    act = jax.ShapeDtypeStruct((tree_len, width), BF16)
    hosts = hosted is not None
    hbm = pl.BlockSpec(memory_space=pl.ANY)
    return pl.pallas_call(
        functools.partial(bwd_kernel, heads, hosts),
        grid=(groups, tree_len // BQ),
        in_specs=[
            row_block, full, full, row_block, row_block,
            pl.BlockSpec((1, heads, BQ), lambda g, i: (g, 0, i)),
            table, table,
            pl.BlockSpec((8, BQ), lambda g, i: (0, i)),
            pl.BlockSpec((tree_len, 128), lambda g, i: (0, 0)),
        ]
        + [hbm] * hosts,
        out_specs=[hbm] * 2 if hosts else [row_block, full, full],
        out_shape=[
            jax.ShapeDtypeStruct((tree_len, 3 * width), BF16),
            jax.ShapeDtypeStruct((hosted.shape[0] // 8, hosted.shape[1]), BF16),
        ]
        if hosts
        else [act, act, act],
        scratch_shapes=[
            pltpu.VMEM((BQ, gw), F32),
            pltpu.VMEM((tree_len, gw), F32),
            pltpu.VMEM((tree_len, gw), F32),
        ]
        + (
            [pltpu.VMEM(shape, BF16) for shape in ((2, BQ, gw), (tree_len, gw), (tree_len, gw))]
            + [pltpu.SemaphoreType.DMA((4,))]
            + scatter_scratch(hosted.shape[0] // 8, hosted.shape[1])
            if hosts
            else []
        ),
        compiler_params=pltpu.CompilerParams(
            vmem_limit_bytes=60 << 20, collective_id=7 if hosts else None, has_side_effects=hosts
        ),
        cost_estimate=small_cost(),
        name="tree_attention_backward",
    )(q, k, v, out, grad, lse, cosine, sine, rows_table, cols_table, *([hosted] if hosts else []))


TOKENS_AT_ONCE = 2048
LEFT_AT_ONCE = 512
TOKEN_STEP = 1024
ROW_STEP = 1024


def product_buffers(columns):
    return [
        pltpu.VMEM((2, TOKENS_AT_ONCE, LEFT_AT_ONCE), BF16),
        pltpu.VMEM((2 * TOKENS_AT_ONCE, columns), BF16),
        pltpu.VMEM((LEFT_AT_ONCE, columns), F32),
        pltpu.VMEM((LEFT_AT_ONCE, columns), BF16),
        pltpu.SemaphoreType.DMA((4,)),
    ]


def token_product(left_ref, right_ref, out_ref, left_buf, right_buf, total, out_buf, sems):
    tokens = left_ref.shape[0]
    parts, groups = tokens // TOKENS_AT_ONCE, left_ref.shape[1] // LEFT_AT_ONCE

    def load(step):
        group, part = step // parts, step % parts
        source = left_ref.at[
            pl.ds(part * TOKENS_AT_ONCE, TOKENS_AT_ONCE), pl.ds(group * LEFT_AT_ONCE, LEFT_AT_ONCE)
        ]
        return pltpu.make_async_copy(source, left_buf.at[step % 2], sems.at[step % 2])

    def store(group):
        return pltpu.make_async_copy(out_buf, out_ref.at[pl.ds(group * LEFT_AT_ONCE, LEFT_AT_ONCE)], sems.at[3])

    whole = pltpu.make_async_copy(right_ref, right_buf, sems.at[2])
    whole.start()
    load(0).start()
    yield
    whole.wait()
    for group in range(groups):
        for part in range(parts):
            step = group * parts + part
            load(step).wait()
            if step + 1 < groups * parts:
                load(step + 1).start()
            if part == 0:
                total[...] = jnp.zeros_like(total)

            @pl.loop(0, TOKENS_AT_ONCE // TOKEN_STEP)
            def _(j, step=step, part=part):
                left = left_buf[step % 2, pl.ds(pl.multiple_of(j * TOKEN_STEP, TOKEN_STEP), TOKEN_STEP), :]
                right = right_buf[pl.ds(pl.multiple_of(part * TOKENS_AT_ONCE + j * TOKEN_STEP, TOKEN_STEP), TOKEN_STEP), :]
                total[...] += dot_tn(left, right)

        if group > 0:
            store(group - 1).wait()
        out_buf[...] = total[...].astype(BF16)
        store(group).start()
        yield
    store(groups - 1).wait()


def finish(product):
    for _ in product:
        pass


def pair_product(left_ref, first_ref, second_ref, out_first, out_second, left_buf, right_buf, total, out_buf, sems):
    tokens, columns = first_ref.shape
    parts, groups = tokens // TOKENS_AT_ONCE, left_ref.shape[1] // LEFT_AT_ONCE
    sides = [pl.ds(0, columns), pl.ds(columns, columns)]

    def load(step):
        group, part = step // parts, step % parts
        source = left_ref.at[
            pl.ds(part * TOKENS_AT_ONCE, TOKENS_AT_ONCE), pl.ds(group * LEFT_AT_ONCE, LEFT_AT_ONCE)
        ]
        return pltpu.make_async_copy(source, left_buf.at[step % 2], sems.at[step % 2])

    def stores(group):
        rows = pl.ds(group * LEFT_AT_ONCE, LEFT_AT_ONCE)
        return [
            pltpu.make_async_copy(out_buf.at[:, side], out_ref.at[rows], sems.at[4 + n])
            for n, (side, out_ref) in enumerate(zip(sides, (out_first, out_second)))
        ]

    wholes = [
        pltpu.make_async_copy(ref, right_buf.at[:, side], sems.at[2 + n])
        for n, (side, ref) in enumerate(zip(sides, (first_ref, second_ref)))
    ]
    load(0).start()
    for copy in wholes:
        copy.start()
    yield
    for copy in wholes:
        copy.wait()
    for group in range(groups):
        for part in range(parts):
            step = group * parts + part
            load(step).wait()
            if step + 1 < groups * parts:
                load(step + 1).start()
            if part == 0:
                total[...] = jnp.zeros_like(total)

            @pl.loop(0, TOKENS_AT_ONCE // TOKEN_STEP)
            def _(j, step=step, part=part):
                left = left_buf[step % 2, pl.ds(pl.multiple_of(j * TOKEN_STEP, TOKEN_STEP), TOKEN_STEP), :]
                right = right_buf[pl.ds(pl.multiple_of(part * TOKENS_AT_ONCE + j * TOKEN_STEP, TOKEN_STEP), TOKEN_STEP), :]
                total[...] += dot_tn(left, right)

        if group > 0:
            for copy in stores(group - 1):
                copy.wait()
        out_buf[...] = total[...].astype(BF16)
        for copy in stores(group):
            copy.start()
        yield
    for copy in stores(groups - 1):
        copy.wait()


def cut_columns(*refs):
    count = (len(refs) - 2) // 2
    sources, targets, (room, sems) = refs[:count], refs[count : 2 * count], refs[2 * count :]

    def inward(n):
        columns = targets[n].shape[1]
        taken = pl.ds(pl.multiple_of(lax.axis_index("ctx") * columns, columns), columns)
        return pltpu.make_async_copy(sources[n].at[:, taken], room.at[n], sems.at[0, n])

    def outward(n):
        return pltpu.make_async_copy(room.at[n], targets[n], sems.at[1, n])

    for n in range(count):
        inward(n).start()
    yield
    for n in range(count):
        inward(n).wait()
        outward(n).start()
    yield
    for n in range(count):
        outward(n).wait()


def row_product(turned, left_ref, right_ref, out_ref, left_buf, right_buf, out_buf, sems):
    groups = left_ref.shape[0] // LEFT_AT_ONCE

    def rows(group):
        return pl.ds(group * LEFT_AT_ONCE, LEFT_AT_ONCE)

    def load(group):
        return pltpu.make_async_copy(left_ref.at[rows(group)], left_buf.at[group % 2], sems.at[group % 2])

    def store(group):
        return pltpu.make_async_copy(out_buf.at[group % 2], out_ref.at[rows(group)], sems.at[3 + group % 2])

    whole = pltpu.make_async_copy(right_ref, right_buf, sems.at[2])
    whole.start()
    load(0).start()
    yield
    whole.wait()
    for group in range(groups):
        load(group).wait()
        if group + 1 < groups:
            load(group + 1).start()
        if group > 1:
            store(group - 2).wait()

        @pl.loop(0, out_ref.shape[1] // ROW_STEP)
        def _(j, group=group):
            columns = pl.ds(pl.multiple_of(j * ROW_STEP, ROW_STEP), ROW_STEP)
            if turned:
                part = dot_t(left_buf[group % 2], right_buf[columns, :])
            else:
                part = dot_n(left_buf[group % 2], right_buf[:, columns])
            out_buf[group % 2, :, columns] = part.astype(BF16)

        store(group).start()
        yield
    for group in range(max(0, groups - 2), groups):
        store(group).wait()


def row_product_buffers(right, turned):
    return [
        pltpu.VMEM((2, LEFT_AT_ONCE, right.shape[1 if turned else 0]), BF16),
        pltpu.VMEM(right.shape, BF16),
        pltpu.VMEM((2, LEFT_AT_ONCE, right.shape[0 if turned else 1]), BF16),
        pltpu.SemaphoreType.DMA((5,)),
    ]


def gather_kernel(works, counts, paces, *refs):
    def take(count):
        nonlocal refs
        taken, refs = refs[:count], refs[count:]
        return taken

    (own_ref,) = take(1)
    inputs = [take(count[0]) for count in counts]
    (all_ref,) = take(1)
    outputs = [take(count[1]) for count in counts]
    gather = PlaneGather(own_ref, all_ref, *take(3))
    buffers, held = [], {}
    for work, count in zip(works, counts):
        if work not in held:
            held[work] = take(count[2])
        buffers.append(held[work])

    def all_work():
        started = [work(*given, *wanted, *room) for work, given, wanted, room in zip(works, inputs, outputs, buffers)]
        for one in started:
            next(one)
        for one in started:
            yield from one

    going = all_work()

    def some(count):
        for _ in range(count):
            next(going, None)

    gather.start()
    some(paces[0])
    gather.first()
    some(paces[1])
    gather.second()
    finish(going)
    gather.finish()


def plane_gather(rows, collective_id=0, jobs=(), paces=(0, 0)):
    count, width = rows.shape
    hbm = pl.BlockSpec(memory_space=pl.ANY)
    scratch, held = gather_sems(), set()
    for work, _, _, _, _, buffers in jobs:
        if work not in held:
            held.add(work)
            scratch += buffers
    return pl.pallas_call(
        functools.partial(
            gather_kernel,
            [job[0] for job in jobs],
            [(len(job[1]), len(job[3]), len(job[5])) for job in jobs],
            paces,
        ),
        in_specs=[hbm] + [spec for job in jobs for spec in job[2]],
        out_specs=[hbm] + [spec for job in jobs for spec in job[4]],
        out_shape=[jax.ShapeDtypeStruct((8 * count, width), rows.dtype)] + [out for job in jobs for out in job[3]],
        scratch_shapes=scratch,
        compiler_params=pltpu.CompilerParams(
            collective_id=collective_id, has_side_effects=True, vmem_limit_bytes=(48 << 20) if jobs else None
        ),
        cost_estimate=small_cost(),
        name="plane_gather",
    )(rows, *[value for job in jobs for value in job[1]])


HBM = pl.BlockSpec(memory_space=pl.ANY)
VMEM = pl.BlockSpec(memory_space=pltpu.VMEM)
ROWS_TURNED = functools.partial(row_product, True)
ROWS_STRAIGHT = functools.partial(row_product, False)


def token_job(left, right):
    out = jax.ShapeDtypeStruct((left.shape[1], right.shape[1]), BF16)
    return token_product, [left, right], [HBM] * 2, [out], [HBM], product_buffers(right.shape[1])


def pair_job(left, first, second):
    columns = first.shape[1]
    out = jax.ShapeDtypeStruct((left.shape[1], columns), BF16)
    room = [
        pltpu.VMEM((2, TOKENS_AT_ONCE, LEFT_AT_ONCE), BF16),
        pltpu.VMEM((left.shape[0], 2 * columns), BF16),
        pltpu.VMEM((LEFT_AT_ONCE, 2 * columns), F32),
        pltpu.VMEM((LEFT_AT_ONCE, 2 * columns), BF16),
        pltpu.SemaphoreType.DMA((6,)),
    ]
    return pair_product, [left, first, second], [HBM] * 3, [out] * 2, [HBM] * 2, room


def cut_job(weights, parts):
    outs = [jax.ShapeDtypeStruct((w.shape[0], w.shape[1] // parts), w.dtype) for w in weights]
    room = [pltpu.VMEM((len(weights),) + outs[0].shape, BF16), pltpu.SemaphoreType.DMA((2, len(weights)))]
    return cut_columns, list(weights), [HBM] * len(weights), outs, [HBM] * len(weights), room


def row_job(left, right, turned):
    out = jax.ShapeDtypeStruct((left.shape[0], right.shape[0 if turned else 1]), BF16)
    work = ROWS_TURNED if turned else ROWS_STRAIGHT
    return work, [left, right], [HBM] * 2, [out], [HBM], row_product_buffers(right, turned)


def table_job(lengths, parents, tokens):
    outs = [jax.ShapeDtypeStruct((8, tokens), jnp.int32), jax.ShapeDtypeStruct((tokens, 128), jnp.int32)]
    outs += [jax.ShapeDtypeStruct((tokens, 128), F32)] * 2
    room = [pltpu.VMEM(out.shape, out.dtype) for out in outs[1:]]
    room += [pltpu.SemaphoreType.DMA((3, tokens // TABLE_ROWS))]
    return table_work, [lengths, parents, rope_freqs(128)], [VMEM] * 3, outs, [VMEM, HBM, HBM, HBM], room


def scatter_kernel(rows, offsets, jobs, *refs):
    parts = len(offsets)

    def take(count):
        nonlocal refs
        taken, refs = refs[:count], refs[count:]
        return taken

    a_refs, w_homes, lefts, rights = take(parts), take(parts), take(jobs), take(jobs)
    (out_ref,), products = take(1), take(jobs)
    core_out, core_in, first_in, next_in, sems = take(5)
    a_bufs, w_refs, (a_sems, w_sems), buffers = take(parts), take(parts), take(2), refs

    def work(job):
        if job < jobs:
            finish(token_product(lefts[job], rights[job], products[job], *buffers))

    x, core, row = plane_place()
    over_x, over_row, over_core = plane_neighbours(x, core, row)
    half = rows // 2
    width = out_ref.shape[1]
    chunks = width // COLS

    def place(piece, on_core):
        far_x, far_row, part = PIECES[piece]
        bx = x + far_x - 2 * far_x * x
        by = row + far_row - 2 * far_row * row
        return pl.ds(pl.multiple_of(((bx * 2 + on_core) * 2 + by) * rows + part * half, half), half)

    def columns(j):
        return pl.ds(pl.multiple_of(j * COLS, COLS), COLS)

    steps = [(0, True)]
    for piece in range(8):
        steps += [(piece + 1, True)] * (piece < 7) + [(piece, False)]

    def load(step):
        piece, partner_half = steps[step]
        taken = place(piece, 1 - core if partner_half else core)
        return [
            pltpu.make_async_copy(a_ref.at[taken], a_buf.at[step % 2], a_sems.at[step % 2, p])
            for p, (a_ref, a_buf) in enumerate(zip(a_refs, a_bufs))
        ]

    w_copies = [
        pltpu.make_async_copy(home.at[:, pl.ds(offset, w_ref.shape[1])], w_ref, w_sems.at[p])
        for p, (home, offset, w_ref) in enumerate(zip(w_homes, offsets, w_refs))
    ]
    loads = {0: load(0)}
    for copy in w_copies + loads[0]:
        copy.start()
    enter_plane((over_x, over_row, over_core))
    for copy in w_copies:
        copy.wait()

    def partial(slot, j):
        total = None
        for a_buf, w_ref in zip(a_bufs, w_refs):
            term = dot_t(a_buf[slot], w_ref[columns(j), :])
            total = term if total is None else total + term
        return total

    def remote(source, target, slot, device):
        return pltpu.make_async_remote_copy(
            src_ref=source, dst_ref=target, send_sem=sems.at[0, slot], recv_sem=sems.at[1, slot],
            device_id=device, device_id_type=MESH,
        )

    core_copies, first_copies, next_copies = [], [], []
    for step, (piece, partner_half) in enumerate(steps):
        for copy in loads[step]:
            copy.wait()
        if step + 1 < len(steps):
            loads[step + 1] = load(step + 1)
            for copy in loads[step + 1]:
                copy.start()
        if partner_half:

            @pl.loop(0, chunks)
            def _(j, step=step, piece=piece):
                core_out[piece, :, columns(j)] = partial(step % 2, j).astype(BF16)

            core_copies.append(remote(core_out.at[piece], core_in.at[piece], piece, over_core))
            core_copies[-1].start()
            continue
        core_copies[piece].wait_recv()

        @pl.loop(0, chunks)
        def _(j, step=step, piece=piece):
            total = partial(step % 2, j) + core_in[piece, :, columns(j)].astype(F32)
            core_in[piece, :, columns(j)] = total.astype(BF16)

        if piece < 4:
            first_copies.append(
                remote(core_in.at[piece], first_in.at[piece], 8 + piece, over_x if piece % 2 == 0 else over_row)
            )
            first_copies[-1].start()
    for part in range(2):
        first_copies[part].wait_recv()

        @pl.loop(0, chunks)
        def _(j, part=part):
            total = core_in[4 + part, :, columns(j)].astype(F32) + first_in[part, :, columns(j)].astype(F32)
            core_in[4 + part, :, columns(j)] = total.astype(BF16)

        next_copies.append(remote(core_in.at[4 + part], next_in.at[part], 12 + part, over_row if part == 0 else over_x))
        next_copies[-1].start()
    for job in range(jobs):
        work(job)
    for part in range(2):
        first_copies[2 + part].wait_recv()
        next_copies[part].wait_recv()

        @pl.loop(0, chunks)
        def _(j, part=part):
            total = core_in[6 + part, :, columns(j)].astype(F32) + first_in[2 + part, :, columns(j)].astype(F32)
            out_ref[pl.ds(part * half, half), columns(j)] = total + next_in[part, :, columns(j)].astype(F32)

    for copy in core_copies + first_copies + next_copies:
        copy.wait_send()


def plane_scatter(parts, weights, collective_id, jobs=(), offsets=None):
    count = parts[0].shape[0]
    width = weights[0].shape[0]
    rows = count // 8
    half = rows // 2
    vmem, hbm = pl.BlockSpec(memory_space=pltpu.VMEM), pl.BlockSpec(memory_space=pl.ANY)
    offsets = offsets or [0] * len(parts)
    lefts, rights = [left for left, _ in jobs], [right for _, right in jobs]
    return pl.pallas_call(
        functools.partial(scatter_kernel, rows, offsets, len(jobs)),
        in_specs=[hbm] * (2 * len(parts) + 2 * len(jobs)),
        out_specs=[vmem] + [hbm] * len(jobs),
        out_shape=[jax.ShapeDtypeStruct((rows, width), F32)]
        + [jax.ShapeDtypeStruct((left.shape[1], right.shape[1]), BF16) for left, right in jobs],
        scratch_shapes=[
            pltpu.VMEM((8, half, width), BF16),
            pltpu.VMEM((8, half, width), BF16),
            pltpu.VMEM((4, half, width), BF16),
            pltpu.VMEM((2, half, width), BF16),
            pltpu.SemaphoreType.DMA((2, 14)),
        ]
        + [pltpu.VMEM((2, half, a.shape[1]), BF16) for a in parts]
        + [pltpu.VMEM((width, a.shape[1]), BF16) for a in parts]
        + [pltpu.SemaphoreType.DMA((2, len(parts))), pltpu.SemaphoreType.DMA((len(parts),))]
        + (product_buffers(rights[0].shape[1]) if jobs else []),
        compiler_params=pltpu.CompilerParams(
            collective_id=collective_id, has_side_effects=True, vmem_limit_bytes=(58 if jobs else 52) << 20
        ),
        cost_estimate=small_cost(),
        name="plane_scatter",
    )(*parts, *weights, *lefts, *rights)


def gated_kernel(x_ref, grad_ref, gate_ref, up_ref, hidden_ref, gate_grad_ref, up_grad_ref):
    columns = gate_ref.shape[1]
    step = min(512, columns)
    together = min(2, columns // step)

    @pl.loop(0, columns // (step * together))
    def _(j):
        for part in range(together):
            taken = pl.ds(pl.multiple_of((j * together + part) * step, step), step)
            gate = dot_n(x_ref[...], gate_ref[:, taken])
            up = dot_n(x_ref[...], up_ref[:, taken])
            grad = grad_ref[:, taken].astype(F32)
            sigmoid = jax.nn.sigmoid(gate)
            silu = gate * sigmoid
            hidden_ref[:, taken] = (silu * up).astype(BF16)
            gate_grad_ref[:, taken] = (grad * up * (sigmoid + silu * (1.0 - sigmoid))).astype(BF16)
            up_grad_ref[:, taken] = (grad * silu).astype(BF16)


def gated_rows(x, hidden_grad, w_gate, w_up):
    tokens, depth = x.shape
    columns = w_gate.shape[1]
    block = 256
    rows = pl.BlockSpec((block, columns), lambda i: (i, 0))
    weight = pl.BlockSpec((depth, columns), lambda i: (0, 0), pipeline_mode=pl.Buffered(1))
    out = jax.ShapeDtypeStruct((tokens, columns), BF16)
    return pl.pallas_call(
        gated_kernel,
        grid=(tokens // block,),
        in_specs=[pl.BlockSpec((block, depth), lambda i: (i, 0)), rows, weight, weight],
        out_specs=[rows] * 3,
        out_shape=[out] * 3,
        compiler_params=pltpu.CompilerParams(vmem_limit_bytes=48 << 20),
        cost_estimate=small_cost(),
        name="gated_rows",
    )(x, hidden_grad, w_gate, w_up)


def heads_kernel(x_ref, w_ref, out_ref, heads_ref, grad_ref, total):
    i = pl.program_id(0)

    @pl.when(i == 0)
    def _():
        total[...] = jnp.zeros_like(total)

    heads_ref[...] = dot_n(x_ref[...], w_ref[...]).astype(BF16)
    total[...] += dot_tn(out_ref[...], x_ref[...])

    @pl.when(i == pl.num_programs(0) - 1)
    def _():
        grad_ref[...] = jnp.transpose(total[...]).astype(BF16)


def heads_and_output_grad(mid, w_attn, attn_out):
    tokens, depth = mid.shape
    width = attn_out.shape[1]
    if width % 128:
        return dot_n(mid, w_attn[:, 3 * width :]).astype(BF16), dot_tn(mid, attn_out).astype(BF16)
    block = 1024
    rows = pl.BlockSpec((block, width), lambda i: (i, 0))
    return pl.pallas_call(
        heads_kernel,
        grid=(tokens // block,),
        in_specs=[pl.BlockSpec((block, depth), lambda i: (i, 0)), pl.BlockSpec((depth, width), lambda i: (0, 3)), rows],
        out_specs=[rows, pl.BlockSpec((depth, width), lambda i: (0, 0))],
        out_shape=[jax.ShapeDtypeStruct((tokens, width), BF16), jax.ShapeDtypeStruct((depth, width), BF16)],
        scratch_shapes=[pltpu.VMEM((width, depth), F32)],
        compiler_params=pltpu.CompilerParams(vmem_limit_bytes=40 << 20),
        cost_estimate=small_cost(),
        name="heads_and_output_grad",
    )(mid, w_attn, attn_out)


def weight_grads_kernel(x_ref, pre_ref, output_ref, grad_ref, total):
    i = pl.program_id(0)
    width = pre_ref.shape[1]

    @pl.when(i == 0)
    def _():
        total[...] = jnp.zeros_like(total)

    total[...] += dot_tn(x_ref[...], pre_ref[...])

    @pl.when(i == pl.num_programs(0) - 1)
    def _():
        grad_ref[:, :width] = total[...].astype(BF16)
        grad_ref[:, width:] = output_ref[...]


def attention_weight_grads(attn_in, pre_grads, output_grad):
    tokens, depth = attn_in.shape
    width, last = pre_grads.shape[1], output_grad.shape[1]
    if width % 128 or last % 128:
        return jnp.concatenate([dot_tn(attn_in, pre_grads).astype(BF16), output_grad], axis=1)
    block = 1024
    return pl.pallas_call(
        weight_grads_kernel,
        grid=(tokens // block,),
        in_specs=[
            pl.BlockSpec((block, depth), lambda i: (i, 0)),
            pl.BlockSpec((block, width), lambda i: (i, 0)),
            pl.BlockSpec((depth, last), lambda i: (0, 0)),
        ],
        out_specs=pl.BlockSpec((depth, width + last), lambda i: (0, 0)),
        out_shape=jax.ShapeDtypeStruct((depth, width + last), BF16),
        scratch_shapes=[pltpu.VMEM((depth, width), F32)],
        compiler_params=pltpu.CompilerParams(vmem_limit_bytes=48 << 20),
        cost_estimate=small_cost(),
        name="attention_weight_grads",
    )(attn_in, pre_grads, output_grad)


def is_plane():
    return lax.axis_size("ctx") == 4 and lax.axis_size("tensor") == 2


def gather_rows(rows):
    return lax.all_gather(rows, GROUP, axis=0, tiled=True)


def scatter_rows(rows):
    return lax.psum_scatter(rows.astype(BF16), GROUP, scatter_dimension=0, tiled=True).astype(F32)


def gather_now(rows):
    return plane_gather(rows)[0] if is_plane() else gather_rows(rows)


def cut(weight):
    columns = weight.shape[1] // lax.axis_size("ctx")
    return lax.dynamic_slice_in_dim(weight, lax.axis_index("ctx") * columns, columns, 1)


def gather_with_tables(rows, lengths, parents, tokens, width, weights):
    if is_plane():
        jobs = [cut_job(weights, lax.axis_size("ctx")), table_job(lengths, parents, tokens)]
        got = plane_gather(rows, 8, jobs, (4, 4))
        return got[:1] + got[1 + len(weights) :], got[1 : 1 + len(weights)]
    segment, parent, depth = tree_tables(lengths[0], parents[0], tokens)
    return [gather_rows(rows), *lay_out(segment, parent), *rope_tables(depth, width)], [cut(w) for w in weights]


def gather_with_product(rows, left, right):
    if is_plane():
        return plane_gather(rows, 5, [row_job(left, right, False)], (4, 4))
    return gather_rows(rows), dot_n(left, right).astype(BF16)


def gather_with_three(rows, left, right, shared, first, second):
    if is_plane():
        return plane_gather(rows, 4, [row_job(left, right, True), pair_job(shared, first, second)], (8, 3))
    products = dot_t(left, right), dot_tn(shared, first), dot_tn(shared, second)
    return [gather_rows(rows)] + [product.astype(BF16) for product in products]


def product_scatter(parts, weights, collective_id, jobs=(), offsets=None):
    if is_plane():
        return plane_scatter(parts, weights, collective_id, jobs, offsets)
    offsets = offsets or [0] * len(parts)
    weights = [w[:, first : first + part.shape[1]] for part, w, first in zip(parts, weights, offsets)]
    rows = scatter_rows(dot_t(jnp.concatenate(parts, axis=1), jnp.concatenate(weights, axis=1)))
    return [rows] + [dot_tn(left, right).astype(BF16) for left, right in jobs]


def gather_weight(own):
    return lax.all_gather(own, "fsdp", axis=0, tiled=True)


def scatter_weight(grad):
    return lax.psum_scatter(grad.astype(BF16), "fsdp", scatter_dimension=0, tiled=True)


def swap_rows(part):
    size = lax.axis_size("ctx")
    return lax.all_to_all(part.reshape(size, part.shape[0] // size, -1), "ctx", split_axis=0, concat_axis=0)


def lay_side_by_side(got, count):
    columns = got.shape[2] // count
    return [
        jnp.concatenate([got[j, :, c * columns : (c + 1) * columns] for j in range(got.shape[0])], axis=1).astype(F32)
        for c in range(count)
    ]


def normalize(rows):
    norm_inv = lax.rsqrt(jnp.mean(rows * rows, axis=1, keepdims=True) + EPSILON)
    return (rows * norm_inv, norm_inv)


def norm_backward(grad_rows, scaled, norm_inv, gain):
    weighted = grad_rows * gain[None, :]
    inner = jnp.mean(weighted * scaled, axis=1, keepdims=True)
    return norm_inv * (weighted - scaled * inner)


def body(
    tokens_in,
    attn_gain,
    query_weight,
    key_weight,
    value_weight,
    output_weight,
    mlp_gain,
    gate_weight,
    up_weight,
    down_weight,
    seg_lengths,
    leaf_parent,
    cotangent,
):
    ctx = lax.axis_index("ctx")
    parts = lax.axis_size("ctx")
    tree_len = tokens_in.shape[0] * parts * lax.axis_size("tensor")
    width = query_weight.shape[1] // parts
    units = gate_weight.shape[1] // parts

    def mine(weight, columns):
        return lax.dynamic_slice_in_dim(weight, ctx * columns, columns, 1)

    x_rows = tokens_in.astype(F32)
    attn_scaled, attn_inv = normalize(x_rows)
    w_attn = gather_weight(
        jnp.concatenate([mine(w, width) for w in (query_weight, key_weight, value_weight, output_weight)], axis=1)
    )
    (attn_in, rows_table, cols_table, cosine, sine), cuts = gather_with_tables(
        (attn_scaled * attn_gain[None, :]).astype(BF16),
        seg_lengths,
        leaf_parent,
        tree_len,
        min(2 * HEAD_DIM, width),
        [gate_weight, down_weight, up_weight],
    )
    w_gate, w_down, w_up = [gather_weight(own) for own in cuts]
    w_qkv = w_attn[:, : 3 * width]

    qkv = jnp.dot(attn_in, w_qkv, preferred_element_type=F32)
    if is_plane():
        attn_out, lse, query_rows, key_rows, value_rows, cot_all = attention_forward(
            qkv, cosine, sine, rows_table, cols_table, width, cotangent
        )
    else:
        attn_out, lse, query_rows, key_rows, value_rows = attention_forward(
            qkv, cosine, sine, rows_table, cols_table, width
        )
        cot_all = gather_rows(cotangent)
    mid_rows = x_rows + product_scatter([attn_out], [w_attn], 1, (), [3 * width])[0]
    mlp_scaled, mlp_inv = normalize(mid_rows)
    mlp_own = (mlp_scaled * mlp_gain[None, :]).astype(BF16)
    mlp_in, hidden_grad = gather_with_product(mlp_own, cot_all, w_down)
    hidden, gate_rows_grad, up_rows_grad = gated_rows(mlp_in, hidden_grad, w_gate, w_up)

    mlp_in_grad, down_part = product_scatter(
        [gate_rows_grad, up_rows_grad], [w_gate, w_up], 3, [(cot_all, hidden)]
    )
    down_grad = scatter_weight(down_part)
    mid_grad = cotangent.astype(F32) + norm_backward(mlp_in_grad, mlp_scaled, mlp_inv, mlp_gain)
    mid_all, down_rows, up_part, gate_part = gather_with_three(
        mid_grad.astype(BF16), hidden, w_down, mlp_in, up_rows_grad, gate_rows_grad
    )
    up_grad = scatter_weight(up_part)
    gate_grad = scatter_weight(gate_part)

    out_heads_grad, output_grad = heads_and_output_grad(mid_all, w_attn, attn_out)
    out_heads_grad, down_grad = lax.optimization_barrier((out_heads_grad, down_grad))
    if is_plane():
        pre_grads, down_rows = attention_backward(
            query_rows, key_rows, value_rows, attn_out, out_heads_grad, lse, cosine, sine, rows_table, cols_table, down_rows
        )
    else:
        pre_grads = attention_backward(
            query_rows, key_rows, value_rows, attn_out, out_heads_grad, lse, cosine, sine, rows_table, cols_table
        )
        pre_grads = jnp.concatenate(pre_grads, axis=1)
        down_rows = scatter_rows(down_rows)
    block_out = (mid_rows + down_rows.astype(F32)).astype(BF16)
    pre_grads, up_grad, gate_grad, down_swapped = lax.optimization_barrier(
        (pre_grads, up_grad, gate_grad, swap_rows(down_grad))
    )
    swapped = swap_rows(jnp.concatenate([gate_grad, up_grad], axis=1))
    attn_part = attention_weight_grads(attn_in, pre_grads, output_grad)
    pre_grads, attn_part, swapped = lax.optimization_barrier((pre_grads, attn_part, swapped))
    attn_grad = scatter_weight(attn_part)
    (attn_in_grad,) = product_scatter([pre_grads], [w_attn], 2)
    attn_in_grad, attn_grad = lax.optimization_barrier((attn_in_grad, attn_grad))
    gate_out, up_out = lay_side_by_side(swapped, 2)
    (down_out,) = lay_side_by_side(down_swapped, 1)
    query_out, key_out, value_out, output_out = lay_side_by_side(swap_rows(attn_grad), 4)

    def gain_part(pairs, gain):
        held = query_out.shape[0]
        total = sum(
            jnp.sum(lax.dynamic_slice_in_dim(weight, ctx * held, held, 0).astype(F32) * grad, axis=1)
            for weight, grad in pairs
        )
        first = (lax.axis_index("fsdp") * parts + ctx) * held
        return total / lax.dynamic_slice_in_dim(gain, first, held, 0)

    sums = jnp.stack(
        [
            gain_part([(query_weight, query_out), (key_weight, key_out), (value_weight, value_out)], attn_gain),
            gain_part([(gate_weight, gate_out), (up_weight, up_out)], mlp_gain),
        ]
    )
    row, others = lax.axis_index("tensor"), lax.axis_size("tensor")
    kept = sums.shape[1] // others
    if others == 2:
        got = lax.ppermute(lax.dynamic_slice_in_dim(sums, (1 - row) * kept, kept, 1), "tensor", [(0, 1), (1, 0)])
        gain_grads = lax.dynamic_slice_in_dim(sums, row * kept, kept, 1) + got
    else:
        gain_grads = lax.dynamic_slice_in_dim(lax.psum(sums, "tensor"), row * kept, kept, 1)

    attn_back = norm_backward(attn_in_grad, attn_scaled, attn_inv, attn_gain)
    input_grad = (mid_grad + attn_back).astype(BF16)
    return (
        block_out,
        input_grad,
        gain_grads[0],
        query_out,
        key_out,
        value_out,
        output_out,
        gain_grads[1],
        gate_out,
        up_out,
        down_out,
    )


def solution(mesh):
    rows = P(("fsdp", "ctx", "tensor"), None)
    weight = P("fsdp", "tensor")
    gain = P(("fsdp", "ctx", "tensor"))
    grad = P(("fsdp", "ctx"), "tensor")
    in_specs = (
        rows, P(), weight, weight, weight, weight, P(), weight, weight, weight, P("fsdp", None), P("fsdp", None), rows,
    )
    out_specs = (rows, rows, gain, grad, grad, grad, grad, gain, grad, grad, grad)
    return jax.shard_map(body, mesh=mesh, in_specs=in_specs, out_specs=out_specs, check_vma=False)
```

```python
import functools

import jax
import jax.numpy as jnp
import numpy as np
from jax import lax
from jax.experimental import pallas as pl
from jax.experimental.pallas import tpu as pltpu
from jax.sharding import PartitionSpec as P

HEAD_DIM = 64
TRUNK = 2176
MOST_SEG = 128
ROPE_BASE = 130000.0
EPSILON = 1e-05
NEG_LARGE = -1e30
SCALE = HEAD_DIM ** (-0.5)

BQ = 512
BK = 512
GROUP = ("ctx", "tensor")

F32 = jnp.float32
BF16 = jnp.bfloat16


def pick_table(onehot, table):
    return jnp.sum(jnp.where(onehot, table[None, :], 0), axis=1)


def tree_tables(lengths_row, parent_row, tree_len):
    branches = lengths_row.shape[0] - parent_row.shape[0]
    ends = TRUNK + jnp.cumsum(lengths_row)
    starts = ends - lengths_row
    matches = parent_row[:, None] - 1 == jnp.arange(branches, dtype=jnp.int32)[None, :]
    parent_len = jnp.sum(jnp.where(matches, lengths_row[None, :branches], 0), axis=1)
    zero_one = jnp.zeros((1,), jnp.int32)
    seg_start = jnp.concatenate([zero_one, starts])
    seg_base = jnp.concatenate(
        [zero_one, jnp.full((branches,), TRUNK, jnp.int32), TRUNK + parent_len]
    )
    seg_parent = jnp.concatenate([zero_one, jnp.zeros((branches,), jnp.int32), parent_row])
    positions = jnp.arange(tree_len, dtype=jnp.int32)
    above = jnp.sum((ends[None, :] <= positions[:, None]).astype(jnp.int32), axis=1)
    segment = (positions >= TRUNK).astype(jnp.int32) + above
    onehot = segment[:, None] == jnp.arange(seg_start.shape[0], dtype=jnp.int32)[None, :]
    depth = positions - pick_table(onehot, seg_start) + pick_table(onehot, seg_base)
    parent = pick_table(onehot, seg_parent)
    return (segment, parent, depth)


def rope_freqs(width):
    half = HEAD_DIM // 2
    powers = -2.0 * (np.arange(width) % half) / HEAD_DIM
    return np.power(ROPE_BASE, powers).astype(np.float32)[None, :]


def rope_tables(depth, width):
    angles = depth.astype(F32)[:, None] * rope_freqs(width)
    sign = np.where(np.arange(width) % HEAD_DIM < HEAD_DIM // 2, -1.0, 1.0).astype(np.float32)
    return jnp.cos(angles), jnp.sin(angles) * sign[None, :]


def lay_out(segment, parent):
    both = jnp.stack([segment, parent])
    return jnp.pad(both, ((0, 6), (0, 0))), jnp.pad(both.T, ((0, 0), (0, 126)))


TABLE_ROWS = 512
TABLE_STEP = 64


def tables_at(positions, lengths, parents):
    leaves = parents.shape[1]
    branches = lengths.shape[1] - leaves
    zero = jnp.zeros_like(positions)
    segment = jnp.where(positions >= TRUNK, 1, 0)
    parent, depth = zero, positions
    end = jnp.full((1, 1), TRUNK, jnp.int32)
    starts = []
    for s in range(branches + leaves):
        start, end = end, end + lengths[:, s : s + 1]
        inside = (positions >= start) & (positions < end)
        base, above = jnp.full((1, 1), TRUNK, jnp.int32), jnp.zeros((1, 1), jnp.int32)
        if s >= branches:
            above = parents[:, s - branches : s - branches + 1]
            for b in range(branches):
                base = base + jnp.where(above == b + 1, lengths[:, b : b + 1], 0)
        segment = segment + jnp.where(positions >= end, 1, 0)
        parent = jnp.where(inside, above, parent)
        depth = jnp.where(inside, positions - start + base, depth)
    return segment, parent, depth


def sine_cosine(x):
    turns = jnp.floor(x * np.float32(2.0 / np.pi) + 0.5)
    r = x - turns * np.float32(1.5703125)
    r = r - turns * np.float32(4.837512969970703125e-4)
    r = r - turns * np.float32(7.549789954891882e-8)
    z = r * r
    sine = ((np.float32(-1.9515295891e-4) * z + np.float32(8.3321608736e-3)) * z - np.float32(1.6666654611e-1)) * z * r + r
    cosine = (
        (np.float32(2.443315711809948e-5) * z - np.float32(1.388731625493765e-3)) * z + np.float32(4.166664568298827e-2)
    ) * z * z - np.float32(0.5) * z + np.float32(1.0)
    quarter = turns.astype(jnp.int32) & 3
    odd = (quarter & 1) == 1
    first, second = jnp.where(odd, cosine, sine), jnp.where(odd, sine, cosine)
    return jnp.where(quarter >= 2, -first, first), jnp.where((quarter == 1) | (quarter == 2), -second, second)


def table_work(lengths, parents, freqs, rows_ref, cols_ref, cos_ref, sin_ref, cols_buf, cos_buf, sin_buf, sems):
    yield
    tokens = cos_ref.shape[0]
    shape = (8, tokens)
    segment, parent, _ = tables_at(lax.broadcasted_iota(jnp.int32, shape, 1), lengths, parents)
    line = lax.broadcasted_iota(jnp.int32, shape, 0)
    rows_ref[...] = jnp.where(line == 0, segment, jnp.where(line == 1, parent, 0))
    copies = []
    for chunk in range(tokens // TABLE_ROWS):
        rows = pl.ds(chunk * TABLE_ROWS, TABLE_ROWS)

        @pl.loop(0, TABLE_ROWS // TABLE_STEP)
        def _(j, chunk=chunk):
            first = pl.multiple_of(chunk * TABLE_ROWS + j * TABLE_STEP, TABLE_STEP)
            taken = pl.ds(first, TABLE_STEP)
            shape = (TABLE_STEP, 128)
            lane = lax.broadcasted_iota(jnp.int32, shape, 1)
            segment, parent, depth = tables_at(lax.broadcasted_iota(jnp.int32, shape, 0) + first, lengths, parents)
            cols_buf[taken, :] = jnp.where(lane == 0, segment, jnp.where(lane == 1, parent, 0))
            sine, cosine = sine_cosine(depth.astype(F32) * freqs[...])
            cos_buf[taken, :] = cosine
            sin_buf[taken, :] = jnp.where(lane % HEAD_DIM < HEAD_DIM // 2, -sine, sine)

        for kind, (source, target) in enumerate(((cols_buf, cols_ref), (cos_buf, cos_ref), (sin_buf, sin_ref))):
            copies.append(pltpu.make_async_copy(source.at[rows], target.at[rows], sems.at[kind, chunk]))
            copies[-1].start()
        yield
    for copy in copies:
        copy.wait()


MESH = pl.DeviceIdType.MESH


def plane_place():
    ctx, row = lax.axis_index("ctx"), lax.axis_index("tensor")
    x, core = ctx // 2, ctx % 2
    return x, core, row


def plane_neighbours(x, core, row):
    over_x = {"ctx": (1 - x) * 2 + core}
    over_core = {"ctx": x * 2 + 1 - core}
    over_row = {"tensor": 1 - row}
    return over_x, over_row, over_core


def enter_plane(neighbours):
    barrier = pltpu.get_barrier_semaphore()
    for device in neighbours:
        pl.semaphore_signal(barrier, inc=1, device_id=device, device_id_type=MESH)
    pl.semaphore_wait(barrier, 3)


PIECES = ((1, 1, 0), (1, 1, 1), (1, 0, 0), (0, 1, 1), (0, 1, 0), (1, 0, 1), (0, 0, 0), (0, 0, 1))
COLS = 512


class PlaneGather:
    def __init__(self, own_ref, all_ref, local_sem, send_sem, recv_sem):
        self.own_ref, self.all_ref, self.sems = own_ref, all_ref, (local_sem, send_sem, recv_sem)
        self.x, self.core, self.row = plane_place()
        self.devices = plane_neighbours(self.x, self.core, self.row)
        self.rows = own_ref.shape[0]

    def place(self, far_x, far_row, part):
        bx = self.x + far_x - 2 * far_x * self.x
        by = self.row + far_row - 2 * far_row * self.row
        half = self.rows // 2
        return pl.ds(pl.multiple_of(((bx * 2 + self.core) * 2 + by) * self.rows + part * half, half), half)

    def copy(self, slot):
        far_x, far_row, part, device = (
            (0, 0, 0, 1), (0, 0, 1, 1), (1, 0, 1, 1), (0, 0, 1, 0), (0, 0, 0, 0), (0, 1, 0, 0), (0, 0, 0, 2),
            (0, 0, 1, 2), (0, 1, 0, 2), (1, 0, 1, 2), (0, 1, 1, 2), (1, 0, 0, 2), (1, 1, 0, 2), (1, 1, 1, 2),
        )[slot]
        half = self.rows // 2
        target = self.place(far_x, far_row, part)
        own = far_x == 0 and far_row == 0
        source = self.own_ref.at[pl.ds(part * half, half)] if own else self.all_ref.at[target]
        return pltpu.make_async_remote_copy(
            src_ref=source, dst_ref=self.all_ref.at[target], send_sem=self.sems[1].at[slot],
            recv_sem=self.sems[2].at[slot], device_id=self.devices[device], device_id_type=MESH,
        )

    def local(self, part):
        half = self.rows // 2
        return pltpu.make_async_copy(
            self.own_ref.at[pl.ds(part * half, half)], self.all_ref.at[self.place(0, 0, part)], self.sems[0].at[part]
        )

    def start(self):
        enter_plane(self.devices)
        for slot in (0, 3, 1, 4, 6, 7):
            self.copy(slot).start()
        for part in range(2):
            self.local(part).start()

    def forward(self, got, slots):
        self.copy(got).wait_recv()
        for slot in slots:
            self.copy(slot).start()

    def first(self):
        self.forward(0, (5, 8))
        self.forward(3, (2, 9))

    def second(self):
        self.forward(1, (10,))
        self.forward(4, (11,))

    def finish(self):
        self.forward(5, (12,))
        self.forward(2, (13,))
        for slot in range(6, 14):
            self.copy(slot).wait_recv()
        for slot in range(14):
            self.copy(slot).wait_send()
        for part in range(2):
            self.local(part).wait()


def gather_sems():
    return [pltpu.SemaphoreType.DMA((2,)), pltpu.SemaphoreType.DMA((14,)), pltpu.SemaphoreType.DMA((14,))]


class PlaneScatter:
    def __init__(self, part_ref, out_ref, core_in, first_in, next_in, own, total, sems, own_sems):
        self.part_ref, self.out_ref, self.core_in, self.first_in, self.next_in = part_ref, out_ref, core_in, first_in, next_in
        self.own, self.total, self.sems, self.own_sems = own, total, sems, own_sems
        self.x, self.core, self.row = plane_place()
        self.devices = plane_neighbours(self.x, self.core, self.row)
        self.rows = part_ref.shape[0] // 8

    def place(self, piece, on_core):
        far_x, far_row, part = PIECES[piece]
        bx = self.x + far_x - 2 * far_x * self.x
        by = self.row + far_row - 2 * far_row * self.row
        half = self.rows // 2
        return pl.ds(pl.multiple_of(((bx * 2 + on_core) * 2 + by) * self.rows + part * half, half), half)

    def copy(self, slot):
        if slot < 8:
            source, target, device = self.part_ref.at[self.place(slot, 1 - self.core)], self.core_in.at[slot], 2
        elif slot < 12:
            source, target, device = self.core_in.at[slot - 8], self.first_in.at[slot - 8], slot % 2
        else:
            source, target, device = self.core_in.at[slot - 8], self.next_in.at[slot - 12], 1 - slot % 2
        return pltpu.make_async_remote_copy(
            src_ref=source, dst_ref=target, send_sem=self.sems.at[0, slot], recv_sem=self.sems.at[1, slot],
            device_id=self.devices[device], device_id_type=MESH,
        )

    def load(self, piece):
        return pltpu.make_async_copy(
            self.part_ref.at[self.place(piece, self.core)], self.own.at[piece % 4], self.own_sems.at[piece % 4]
        )

    def add(self, target, where, *others):
        @pl.loop(0, target.shape[-1] // COLS)
        def _(j):
            columns = pl.ds(pl.multiple_of(j * COLS, COLS), COLS)
            total = sum(ref[slot, :, columns].astype(F32) for ref, slot in others)
            target[where, :, columns] = total.astype(target.dtype)

    def start(self):
        enter_plane(self.devices)
        for slot in range(8):
            self.copy(slot).start()
        for piece in range(4):
            self.load(piece).start()

    def first(self):
        for piece in range(4):
            self.load(piece).wait()
            self.copy(piece).wait_recv()
            self.add(self.core_in, piece, (self.own, piece), (self.core_in, piece))
            self.copy(8 + piece).start()
        for piece in range(4, 8):
            self.load(piece).start()

    def second(self):
        for piece in range(4, 8):
            self.load(piece).wait()
            self.copy(piece).wait_recv()
            self.add(self.core_in, piece, (self.own, piece - 4), (self.core_in, piece))

    def third(self):
        for part in range(2):
            self.copy(8 + part).wait_recv()
            self.add(self.core_in, 4 + part, (self.core_in, 4 + part), (self.first_in, part))
            self.copy(12 + part).start()

    def finish(self):
        half = self.rows // 2
        for part in range(2):
            self.copy(10 + part).wait_recv()
            self.copy(12 + part).wait_recv()
            self.add(self.total, part, (self.core_in, 6 + part), (self.first_in, 2 + part), (self.next_in, part))
        stores = [
            pltpu.make_async_copy(
                self.total.at[part], self.out_ref.at[pl.ds(part * half, half)], self.own_sems.at[part]
            )
            for part in range(2)
        ]
        for store in stores:
            store.start()
        for slot in range(14):
            self.copy(slot).wait_send()
        for store in stores:
            store.wait()


def scatter_scratch(rows, width):
    half = rows // 2
    return [
        pltpu.VMEM((8, half, width), BF16),
        pltpu.VMEM((4, half, width), BF16),
        pltpu.VMEM((2, half, width), BF16),
        pltpu.VMEM((4, half, width), BF16),
        pltpu.VMEM((2, half, width), BF16),
        pltpu.SemaphoreType.DMA((2, 14)),
        pltpu.SemaphoreType.DMA((4,)),
    ]


def at_step(step, total, places):
    for place, phase in places:

        @pl.when(step == place)
        def _(phase=phase):
            phase()


def partner(x):
    half = HEAD_DIM // 2
    width = x.shape[1]
    if width == HEAD_DIM:
        return jnp.concatenate([x[:, half:], x[:, :half]], axis=1)
    lane = lax.broadcasted_iota(jnp.int32, x.shape, 1)
    ahead = pltpu.roll(x, width - half, 1)
    behind = pltpu.roll(x, half, 1)
    return jnp.where(lane % HEAD_DIM < half, ahead, behind)


def head_mask(shape, head):
    lane = lax.broadcasted_iota(jnp.int32, shape, 1)
    return lane // HEAD_DIM == head


def dot_t(a, b):
    return lax.dot_general(a, b, (((1,), (1,)), ((), ())), preferred_element_type=F32)


def dot_n(a, b):
    return lax.dot_general(a, b, (((1,), (0,)), ((), ())), preferred_element_type=F32)


def dot_tn(a, b):
    return lax.dot_general(a, b, (((0,), (0,)), ((), ())), preferred_element_type=F32)


def key_plan(i, tile):
    base = TRUNK // BK * BK
    branch_end = TRUNK + 4 * MOST_SEG
    first_tree = base // BQ
    mixed_end = -(-(branch_end + MOST_SEG) // BQ)
    chunks = jnp.minimum(i * BQ, base) // BK
    half = BQ // 2

    @pl.when(i < first_tree)
    def _():
        @pl.loop(0, chunks)
        def _(j):
            start = pl.multiple_of(j * BK, BK)
            tile(start, BK, 0, start, 0, BQ)

    @pl.when(i >= first_tree)
    def _():
        tile(0, base, 0, 0, 0, BQ)

    @pl.when(i < first_tree)
    def _():
        start = pl.multiple_of(chunks * BK, BK)
        for part in range(2):
            tile(start, (part + 1) * half, 1, start, part * half, half)

    for block in range(first_tree, mixed_end):

        @pl.when(i == block)
        def _(block=block):
            for part in range(2):
                tile(base, block * BQ + (part + 1) * half - base, 2, base, part * half, half)

    @pl.when(i >= mixed_end)
    def _():
        tile(base, branch_end - base, 3, base, 0, BQ)
        for part in range(2):
            start = pl.multiple_of(i * BQ + part * half - MOST_SEG, MOST_SEG)
            tile(start, half + MOST_SEG, 4, branch_end, part * half, half)


def most_keys():
    branch_end = TRUNK + 4 * MOST_SEG
    return max(branch_end + BQ // 2 + MOST_SEG, -(-(branch_end + MOST_SEG) // BQ) * BQ)


def seen_mask(kind, q_at, k_at, seg_q, par_q, seg_k):
    if kind == 3:
        return (seg_k == 0) | (seg_k == par_q)
    causal = k_at <= q_at
    if kind == 1:
        return causal
    if kind == 4:
        return causal & (seg_k == seg_q)
    return causal & ((seg_k == 0) | (seg_k == seg_q) | (seg_k == par_q))


def fwd_kernel(heads, hosts, *refs):
    if not hosts:
        return fwd_work(heads, *refs)
    gather = PlaneGather(refs[7], refs[13], *refs[-3:])
    step, total = pl.program_id(0) * pl.num_programs(1) + pl.program_id(1), 16
    at_step(step, total, ((0, gather.start), (6, gather.first), (12, gather.second)))
    fwd_work(heads, *refs[:7], *refs[8:13], *refs[14:-3])
    at_step(step, total, ((total - 1, gather.finish),))


def fwd_work(
    heads, q_ref, k_ref, v_ref, cos_ref, sin_ref, rows_ref, cols_ref,
    o_ref, lse_ref, qr_ref, kr_ref, vr_ref, kt_ref, va_ref, s_ref, m_ref, acc_ref,
):
    i = pl.program_id(1)
    wide = 2 * HEAD_DIM

    @pl.when(i == 0)
    def _():
        @pl.loop(0, k_ref.shape[0] // BK)
        def _(j):
            rows = pl.ds(pl.multiple_of(j * BK, BK), BK)
            k = k_ref[rows, :]
            k = (k * cos_ref[rows, :] + partner(k) * sin_ref[rows, :]).astype(BF16)
            kr_ref[rows, :] = k
            kt_ref[:, rows] = jnp.transpose(k)
            v = v_ref[rows, :].astype(BF16)
            vr_ref[rows, :] = v
            if heads == 1:
                va_ref[0, rows, :] = jnp.concatenate([v, jnp.ones_like(v)], axis=1)
            else:
                for h in range(heads):
                    va_ref[h, rows, :] = jnp.where(head_mask(v.shape, h), v, jnp.ones_like(v))

    rows = pl.ds(pl.multiple_of(i * BQ, BQ), BQ)
    q = q_ref[...]
    q = (q * cos_ref[rows, :] + partner(q) * sin_ref[rows, :]).astype(BF16)
    qr_ref[...] = q
    q = q * jnp.asarray(SCALE, BF16)
    q_heads = [jnp.where(head_mask(q.shape, h), q, jnp.zeros_like(q)) for h in range(heads)]
    m_ref[...] = jnp.full_like(m_ref, NEG_LARGE)
    acc_ref[...] = jnp.zeros_like(acc_ref)

    def score_tile(start, width, kind, place, first, count):
        keys, rows = pl.ds(start, width), slice(first, first + count)
        k = kt_ref[:, keys]
        seen = None
        if kind != 0:
            shape = (count, width)
            seen = seen_mask(
                kind,
                lax.broadcasted_iota(jnp.int32, shape, 0) + i * BQ + first,
                lax.broadcasted_iota(jnp.int32, shape, 1) + start,
                cols_ref[rows, 0:1], cols_ref[rows, 1:2], rows_ref[0:1, keys],
            )
        for h in range(heads):
            s = dot_n(q_heads[h][rows], k)
            if seen is not None:
                s = jnp.where(seen, s, NEG_LARGE)
            s_ref[h, rows, pl.ds(place, width)] = s
            largest = m_ref[h, rows]
            for c in range(width // 128):
                largest = jnp.maximum(largest, s[:, c * 128 : (c + 1) * 128])
            m_ref[h, rows] = largest

    key_plan(i, score_tile)
    for h in range(heads):
        m_ref[h] = jnp.broadcast_to(jnp.max(m_ref[h], axis=1, keepdims=True), (BQ, 128))

    def value_tile(start, width, kind, place, first, count):
        keys, rows = pl.ds(start, width), slice(first, first + count)
        for h in range(heads):
            m = m_ref[h, rows]
            parts = [
                jnp.exp(s_ref[h, rows, pl.ds(place + c * 128, 128)] - m).astype(BF16) for c in range(width // 128)
            ]
            acc_ref[h, rows] += dot_n(jnp.concatenate(parts, axis=1), va_ref[h, keys, :])

    key_plan(i, value_tile)
    out, lse = None, None
    for h in range(heads):
        acc = acc_ref[h]
        part = acc / pltpu.roll(acc, HEAD_DIM, 1)
        stat = m_ref[h] + jnp.log(jnp.broadcast_to(acc[:, (1 - h) * HEAD_DIM : (1 - h) * HEAD_DIM + 1], (BQ, wide)))
        mask = head_mask((BQ, wide), h)
        out = part if h == 0 else jnp.where(mask, part, out)
        lse = stat if h == 0 else jnp.where(mask, stat, lse)
    o_ref[...] = out[:, : heads * HEAD_DIM].astype(BF16)
    turned = jnp.transpose(lse)
    for h in range(heads):
        lse_ref[0, h : h + 1, :] = turned[h * HEAD_DIM : h * HEAD_DIM + 1, :]


def bwd_kernel(heads, hosts, *refs):
    if not hosts:
        return bwd_work(heads, *refs)
    scatter = PlaneScatter(refs[10], refs[12], *refs[-7:])
    step, total = pl.program_id(0) * pl.num_programs(1) + pl.program_id(1), 16
    at_step(
        step, total, ((0, scatter.start), (3, scatter.first), (5, scatter.second), (7, scatter.third))
    )
    bwd_work(heads, *refs[:10], *refs[13:-7], together=refs[11])
    at_step(step, total, ((total - 1, scatter.finish),))


def bwd_work(
    heads, q_ref, k_ref, v_ref, o_ref, do_ref, lse_ref, cos_ref, sin_ref, rows_ref, cols_ref,
    *refs, together=None,
):
    if together is None:
        dq_ref, dk_ref, dv_ref, dq_acc, dk_acc, dv_acc = refs
    else:
        dq_acc, dk_acc, dv_acc, dq_ref, dk_ref, dv_ref, out_sems = refs
    i = pl.program_id(1)

    def store(kind, source, rows, sem):
        groups, width = pl.num_programs(0), source.shape[1]
        columns = pl.ds(pl.multiple_of((kind * groups + pl.program_id(0)) * width, width), width)
        return pltpu.make_async_copy(source, together.at[rows, columns], out_sems.at[sem])

    @pl.when(i == 0)
    def _():
        dk_acc[...] = jnp.zeros_like(dk_acc)
        dv_acc[...] = jnp.zeros_like(dv_acc)

    q = q_ref[...]
    scaled = q * jnp.asarray(SCALE, BF16)
    do = do_ref[...]
    product = jnp.transpose(do.astype(F32) * o_ref[...].astype(F32))
    zero = jnp.zeros_like(q)
    masks = [head_mask(q.shape, h) for h in range(heads)]
    q_heads = [jnp.where(m, scaled, zero) for m in masks]
    do_heads = [jnp.where(m, do, zero) for m in masks]
    deltas = [
        jnp.sum(product[h * HEAD_DIM : (h + 1) * HEAD_DIM, :], axis=0, keepdims=True) for h in range(heads)
    ]
    lses = [lse_ref[0, h : h + 1, :] for h in range(heads)]
    q_turned = [jnp.transpose(x) for x in q_heads]
    do_turned = [jnp.transpose(x) for x in do_heads]
    dq_acc[...] = jnp.zeros_like(dq_acc)

    def tile(start, width, kind, place, first, count):
        keys, part = pl.ds(start, width), slice(first, first + count)
        k = k_ref[keys, :]
        v = v_ref[keys, :]
        seen = None
        if kind != 0:
            shape = (width, count)
            seen = seen_mask(
                kind,
                lax.broadcasted_iota(jnp.int32, shape, 1) + i * BQ + first,
                lax.broadcasted_iota(jnp.int32, shape, 0) + start,
                rows_ref[0:1, part], rows_ref[1:2, part], cols_ref[keys, 0:1],
            )
        probs, grads, k_heads = [], [], []
        for h in range(heads):
            s = dot_n(k, q_turned[h][:, part])
            p = jnp.exp(s - lses[h][:, part])
            if seen is not None:
                p = jnp.where(seen, p, 0.0)
            dp = dot_n(v, do_turned[h][:, part])
            probs.append(p.astype(BF16))
            grads.append((p * (dp - deltas[h][:, part])).astype(BF16))
            k_heads.append(jnp.where(head_mask(k.shape, h), k, jnp.zeros_like(k)))
        grad_row = jnp.concatenate(grads, axis=1)
        dv_acc[keys, :] += dot_n(jnp.concatenate(probs, axis=1), jnp.concatenate([x[part] for x in do_heads], axis=0))
        dk_acc[keys, :] += dot_n(grad_row, jnp.concatenate([x[part] for x in q_heads], axis=0))
        dq_acc[part, :] += dot_tn(jnp.concatenate(grads, axis=0), jnp.concatenate(k_heads, axis=0))

    key_plan(i, tile)
    dq = dq_acc[...] * SCALE
    rows = pl.ds(pl.multiple_of(i * BQ, BQ), BQ)
    dq = (dq * cos_ref[rows, :] - partner(dq) * sin_ref[rows, :]).astype(BF16)
    if together is None:
        dq_ref[...] = dq
    else:
        step, last = pl.program_id(0) * pl.num_programs(1) + i, pl.num_programs(0) * pl.num_programs(1) - 1
        for slot in range(2):

            @pl.when(step % 2 == slot)
            def _(slot=slot):
                @pl.when(step >= 2)
                def _():
                    store(0, dq_ref.at[slot], rows, slot).wait()

                dq_ref[slot] = dq
                store(0, dq_ref.at[slot], rows, slot).start()

        @pl.when(step == last)
        def _():
            for slot in range(2):
                store(0, dq_ref.at[slot], rows, slot).wait()

    @pl.when(i == pl.num_programs(1) - 1)
    def _():
        @pl.loop(0, dk_acc.shape[0] // BK)
        def _(j):
            rows = pl.ds(pl.multiple_of(j * BK, BK), BK)
            dk = dk_acc[rows, :]
            dk_ref[rows, :] = (dk * cos_ref[rows, :] - partner(dk) * sin_ref[rows, :]).astype(BF16)
            dv_ref[rows, :] = dv_acc[rows, :].astype(BF16)

        if together is not None:
            every = pl.ds(0, dk_acc.shape[0])
            copies = [store(1, dk_ref, every, 2), store(2, dv_ref, every, 3)]
            for copy in copies:
                copy.start()
            for copy in copies:
                copy.wait()


def small_cost():
    return pl.CostEstimate(flops=1 << 20, bytes_accessed=1 << 20, transcendentals=0)


def attention_forward(qkv, cosine, sine, rows_table, cols_table, width, hosted=None):
    tree_len = qkv.shape[0]
    gw = min(2 * HEAD_DIM, width)
    groups, heads = width // gw, gw // HEAD_DIM
    row_block = pl.BlockSpec((BQ, gw), lambda g, i: (i, g))
    table = pl.BlockSpec((tree_len, gw), lambda g, i: (0, 0))
    full = pl.BlockSpec((tree_len, gw), lambda g, i: (0, g))
    act = jax.ShapeDtypeStruct((tree_len, width), BF16)
    if width % 128 == 0:
        queries, keys, values, step = qkv, qkv, qkv, groups
    else:
        queries, keys, values = jnp.split(qkv, 3, axis=1)
        step = 0
    hosts = hosted is not None
    hbm = pl.BlockSpec(memory_space=pl.ANY)
    return pl.pallas_call(
        functools.partial(fwd_kernel, heads, hosts),
        grid=(groups, tree_len // BQ),
        in_specs=[
            row_block,
            pl.BlockSpec((tree_len, gw), lambda g, i: (0, step + g)),
            pl.BlockSpec((tree_len, gw), lambda g, i: (0, 2 * step + g)),
            table,
            table,
            pl.BlockSpec((8, tree_len), lambda g, i: (0, 0)),
            pl.BlockSpec((BQ, 128), lambda g, i: (i, 0)),
        ]
        + [hbm] * hosts,
        out_specs=[row_block, pl.BlockSpec((1, heads, BQ), lambda g, i: (g, 0, i)), row_block, full, full] + [hbm] * hosts,
        out_shape=[act, jax.ShapeDtypeStruct((groups, heads, tree_len), F32), act, act, act]
        + ([jax.ShapeDtypeStruct((8 * hosted.shape[0], hosted.shape[1]), BF16)] if hosts else []),
        scratch_shapes=[
            pltpu.VMEM((gw, tree_len), BF16),
            pltpu.VMEM((heads, tree_len, 128), BF16),
            pltpu.VMEM((heads, BQ, most_keys()), F32),
            pltpu.VMEM((heads, BQ, 128), F32),
            pltpu.VMEM((heads, BQ, 128), F32),
        ]
        + (gather_sems() if hosts else []),
        compiler_params=pltpu.CompilerParams(
            vmem_limit_bytes=60 << 20, collective_id=6 if hosts else None, has_side_effects=hosts
        ),
        cost_estimate=small_cost(),
        name="tree_attention_forward",
    )(queries, keys, values, cosine, sine, rows_table, cols_table, *([hosted] if hosts else []))


def attention_backward(q, k, v, out, grad, lse, cosine, sine, rows_table, cols_table, hosted=None):
    tree_len, width = q.shape
    gw = min(2 * HEAD_DIM, width)
    groups, heads = width // gw, gw // HEAD_DIM
    row_block = pl.BlockSpec((BQ, gw), lambda g, i: (i, g))
    table = pl.BlockSpec((tree_len, gw), lambda g, i: (0, 0))
    full = pl.BlockSpec((tree_len, gw), lambda g, i: (0, g))
    act = jax.ShapeDtypeStruct((tree_len, width), BF16)
    hosts = hosted is not None
    hbm = pl.BlockSpec(memory_space=pl.ANY)
    return pl.pallas_call(
        functools.partial(bwd_kernel, heads, hosts),
        grid=(groups, tree_len // BQ),
        in_specs=[
            row_block, full, full, row_block, row_block,
            pl.BlockSpec((1, heads, BQ), lambda g, i: (g, 0, i)),
            table, table,
            pl.BlockSpec((8, BQ), lambda g, i: (0, i)),
            pl.BlockSpec((tree_len, 128), lambda g, i: (0, 0)),
        ]
        + [hbm] * hosts,
        out_specs=[hbm] * 2 if hosts else [row_block, full, full],
        out_shape=[
            jax.ShapeDtypeStruct((tree_len, 3 * width), BF16),
            jax.ShapeDtypeStruct((hosted.shape[0] // 8, hosted.shape[1]), BF16),
        ]
        if hosts
        else [act, act, act],
        scratch_shapes=[
            pltpu.VMEM((BQ, gw), F32),
            pltpu.VMEM((tree_len, gw), F32),
            pltpu.VMEM((tree_len, gw), F32),
        ]
        + (
            [pltpu.VMEM(shape, BF16) for shape in ((2, BQ, gw), (tree_len, gw), (tree_len, gw))]
            + [pltpu.SemaphoreType.DMA((4,))]
            + scatter_scratch(hosted.shape[0] // 8, hosted.shape[1])
            if hosts
            else []
        ),
        compiler_params=pltpu.CompilerParams(
            vmem_limit_bytes=60 << 20, collective_id=7 if hosts else None, has_side_effects=hosts
        ),
        cost_estimate=small_cost(),
        name="tree_attention_backward",
    )(q, k, v, out, grad, lse, cosine, sine, rows_table, cols_table, *([hosted] if hosts else []))


TOKENS_AT_ONCE = 2048
LEFT_AT_ONCE = 512
TOKEN_STEP = 1024
ROW_STEP = 1024


def product_buffers(columns):
    return [
        pltpu.VMEM((2, TOKENS_AT_ONCE, LEFT_AT_ONCE), BF16),
        pltpu.VMEM((2 * TOKENS_AT_ONCE, columns), BF16),
        pltpu.VMEM((LEFT_AT_ONCE, columns), F32),
        pltpu.VMEM((LEFT_AT_ONCE, columns), BF16),
        pltpu.SemaphoreType.DMA((4,)),
    ]


def token_product(left_ref, right_ref, out_ref, left_buf, right_buf, total, out_buf, sems):
    tokens = left_ref.shape[0]
    parts, groups = tokens // TOKENS_AT_ONCE, left_ref.shape[1] // LEFT_AT_ONCE

    def load(step):
        group, part = step // parts, step % parts
        source = left_ref.at[
            pl.ds(part * TOKENS_AT_ONCE, TOKENS_AT_ONCE), pl.ds(group * LEFT_AT_ONCE, LEFT_AT_ONCE)
        ]
        return pltpu.make_async_copy(source, left_buf.at[step % 2], sems.at[step % 2])

    def store(group):
        return pltpu.make_async_copy(out_buf, out_ref.at[pl.ds(group * LEFT_AT_ONCE, LEFT_AT_ONCE)], sems.at[3])

    whole = pltpu.make_async_copy(right_ref, right_buf, sems.at[2])
    whole.start()
    load(0).start()
    yield
    whole.wait()
    for group in range(groups):
        for part in range(parts):
            step = group * parts + part
            load(step).wait()
            if step + 1 < groups * parts:
                load(step + 1).start()
            if part == 0:
                total[...] = jnp.zeros_like(total)

            @pl.loop(0, TOKENS_AT_ONCE // TOKEN_STEP)
            def _(j, step=step, part=part):
                left = left_buf[step % 2, pl.ds(pl.multiple_of(j * TOKEN_STEP, TOKEN_STEP), TOKEN_STEP), :]
                right = right_buf[pl.ds(pl.multiple_of(part * TOKENS_AT_ONCE + j * TOKEN_STEP, TOKEN_STEP), TOKEN_STEP), :]
                total[...] += dot_tn(left, right)

        if group > 0:
            store(group - 1).wait()
        out_buf[...] = total[...].astype(BF16)
        store(group).start()
        yield
    store(groups - 1).wait()


def finish(product):
    for _ in product:
        pass


def pair_product(left_ref, first_ref, second_ref, out_first, out_second, left_buf, right_buf, total, out_buf, sems):
    tokens, columns = first_ref.shape
    parts, groups = tokens // TOKENS_AT_ONCE, left_ref.shape[1] // LEFT_AT_ONCE
    sides = [pl.ds(0, columns), pl.ds(columns, columns)]

    def load(step):
        group, part = step // parts, step % parts
        source = left_ref.at[
            pl.ds(part * TOKENS_AT_ONCE, TOKENS_AT_ONCE), pl.ds(group * LEFT_AT_ONCE, LEFT_AT_ONCE)
        ]
        return pltpu.make_async_copy(source, left_buf.at[step % 2], sems.at[step % 2])

    def stores(group):
        rows = pl.ds(group * LEFT_AT_ONCE, LEFT_AT_ONCE)
        return [
            pltpu.make_async_copy(out_buf.at[:, side], out_ref.at[rows], sems.at[4 + n])
            for n, (side, out_ref) in enumerate(zip(sides, (out_first, out_second)))
        ]

    wholes = [
        pltpu.make_async_copy(ref, right_buf.at[:, side], sems.at[2 + n])
        for n, (side, ref) in enumerate(zip(sides, (first_ref, second_ref)))
    ]
    load(0).start()
    for copy in wholes:
        copy.start()
    yield
    for copy in wholes:
        copy.wait()
    for group in range(groups):
        for part in range(parts):
            step = group * parts + part
            load(step).wait()
            if step + 1 < groups * parts:
                load(step + 1).start()
            if part == 0:
                total[...] = jnp.zeros_like(total)

            @pl.loop(0, TOKENS_AT_ONCE // TOKEN_STEP)
            def _(j, step=step, part=part):
                left = left_buf[step % 2, pl.ds(pl.multiple_of(j * TOKEN_STEP, TOKEN_STEP), TOKEN_STEP), :]
                right = right_buf[pl.ds(pl.multiple_of(part * TOKENS_AT_ONCE + j * TOKEN_STEP, TOKEN_STEP), TOKEN_STEP), :]
                total[...] += dot_tn(left, right)

        if group > 0:
            for copy in stores(group - 1):
                copy.wait()
        out_buf[...] = total[...].astype(BF16)
        for copy in stores(group):
            copy.start()
        yield
    for copy in stores(groups - 1):
        copy.wait()


def cut_columns(*refs):
    count = (len(refs) - 2) // 2
    sources, targets, (room, sems) = refs[:count], refs[count : 2 * count], refs[2 * count :]

    def inward(n):
        columns = targets[n].shape[1]
        taken = pl.ds(pl.multiple_of(lax.axis_index("ctx") * columns, columns), columns)
        return pltpu.make_async_copy(sources[n].at[:, taken], room.at[n], sems.at[0, n])

    def outward(n):
        return pltpu.make_async_copy(room.at[n], targets[n], sems.at[1, n])

    for n in range(count):
        inward(n).start()
    yield
    for n in range(count):
        inward(n).wait()
        outward(n).start()
    yield
    for n in range(count):
        outward(n).wait()


def row_product(turned, left_ref, right_ref, out_ref, left_buf, right_buf, out_buf, sems):
    groups = left_ref.shape[0] // LEFT_AT_ONCE

    def rows(group):
        return pl.ds(group * LEFT_AT_ONCE, LEFT_AT_ONCE)

    def load(group):
        return pltpu.make_async_copy(left_ref.at[rows(group)], left_buf.at[group % 2], sems.at[group % 2])

    def store(group):
        return pltpu.make_async_copy(out_buf.at[group % 2], out_ref.at[rows(group)], sems.at[3 + group % 2])

    whole = pltpu.make_async_copy(right_ref, right_buf, sems.at[2])
    whole.start()
    load(0).start()
    yield
    whole.wait()
    for group in range(groups):
        load(group).wait()
        if group + 1 < groups:
            load(group + 1).start()
        if group > 1:
            store(group - 2).wait()

        @pl.loop(0, out_ref.shape[1] // ROW_STEP)
        def _(j, group=group):
            columns = pl.ds(pl.multiple_of(j * ROW_STEP, ROW_STEP), ROW_STEP)
            if turned:
                part = dot_t(left_buf[group % 2], right_buf[columns, :])
            else:
                part = dot_n(left_buf[group % 2], right_buf[:, columns])
            out_buf[group % 2, :, columns] = part.astype(BF16)

        store(group).start()
        yield
    for group in range(max(0, groups - 2), groups):
        store(group).wait()


def row_product_buffers(right, turned):
    return [
        pltpu.VMEM((2, LEFT_AT_ONCE, right.shape[1 if turned else 0]), BF16),
        pltpu.VMEM(right.shape, BF16),
        pltpu.VMEM((2, LEFT_AT_ONCE, right.shape[0 if turned else 1]), BF16),
        pltpu.SemaphoreType.DMA((5,)),
    ]


def gather_kernel(works, counts, paces, *refs):
    def take(count):
        nonlocal refs
        taken, refs = refs[:count], refs[count:]
        return taken

    (own_ref,) = take(1)
    inputs = [take(count[0]) for count in counts]
    (all_ref,) = take(1)
    outputs = [take(count[1]) for count in counts]
    gather = PlaneGather(own_ref, all_ref, *take(3))
    buffers, held = [], {}
    for work, count in zip(works, counts):
        if work not in held:
            held[work] = take(count[2])
        buffers.append(held[work])

    def all_work():
        started = [work(*given, *wanted, *room) for work, given, wanted, room in zip(works, inputs, outputs, buffers)]
        for one in started:
            next(one)
        for one in started:
            yield from one

    going = all_work()

    def some(count):
        for _ in range(count):
            next(going, None)

    gather.start()
    some(paces[0])
    gather.first()
    some(paces[1])
    gather.second()
    finish(going)
    gather.finish()


def plane_gather(rows, collective_id=0, jobs=(), paces=(0, 0)):
    count, width = rows.shape
    hbm = pl.BlockSpec(memory_space=pl.ANY)
    scratch, held = gather_sems(), set()
    for work, _, _, _, _, buffers in jobs:
        if work not in held:
            held.add(work)
            scratch += buffers
    return pl.pallas_call(
        functools.partial(
            gather_kernel,
            [job[0] for job in jobs],
            [(len(job[1]), len(job[3]), len(job[5])) for job in jobs],
            paces,
        ),
        in_specs=[hbm] + [spec for job in jobs for spec in job[2]],
        out_specs=[hbm] + [spec for job in jobs for spec in job[4]],
        out_shape=[jax.ShapeDtypeStruct((8 * count, width), rows.dtype)] + [out for job in jobs for out in job[3]],
        scratch_shapes=scratch,
        compiler_params=pltpu.CompilerParams(
            collective_id=collective_id, has_side_effects=True, vmem_limit_bytes=(60 << 20) if jobs else None
        ),
        cost_estimate=small_cost(),
        name="plane_gather",
    )(rows, *[value for job in jobs for value in job[1]])


HBM = pl.BlockSpec(memory_space=pl.ANY)
VMEM = pl.BlockSpec(memory_space=pltpu.VMEM)
ROWS_TURNED = functools.partial(row_product, True)
ROWS_STRAIGHT = functools.partial(row_product, False)


def token_job(left, right):
    out = jax.ShapeDtypeStruct((left.shape[1], right.shape[1]), BF16)
    return token_product, [left, right], [HBM] * 2, [out], [HBM], product_buffers(right.shape[1])


def pair_job(left, first, second):
    columns = first.shape[1]
    out = jax.ShapeDtypeStruct((left.shape[1], columns), BF16)
    room = [
        pltpu.VMEM((2, TOKENS_AT_ONCE, LEFT_AT_ONCE), BF16),
        pltpu.VMEM((left.shape[0], 2 * columns), BF16),
        pltpu.VMEM((LEFT_AT_ONCE, 2 * columns), F32),
        pltpu.VMEM((LEFT_AT_ONCE, 2 * columns), BF16),
        pltpu.SemaphoreType.DMA((6,)),
    ]
    return pair_product, [left, first, second], [HBM] * 3, [out] * 2, [HBM] * 2, room


def cut_job(weights, parts):
    outs = [jax.ShapeDtypeStruct((w.shape[0], w.shape[1] // parts), w.dtype) for w in weights]
    room = [pltpu.VMEM((len(weights),) + outs[0].shape, BF16), pltpu.SemaphoreType.DMA((2, len(weights)))]
    return cut_columns, list(weights), [HBM] * len(weights), outs, [HBM] * len(weights), room


def row_job(left, right, turned):
    out = jax.ShapeDtypeStruct((left.shape[0], right.shape[0 if turned else 1]), BF16)
    work = ROWS_TURNED if turned else ROWS_STRAIGHT
    return work, [left, right], [HBM] * 2, [out], [HBM], row_product_buffers(right, turned)


def table_job(lengths, parents, tokens):
    outs = [jax.ShapeDtypeStruct((8, tokens), jnp.int32), jax.ShapeDtypeStruct((tokens, 128), jnp.int32)]
    outs += [jax.ShapeDtypeStruct((tokens, 128), F32)] * 2
    room = [pltpu.VMEM(out.shape, out.dtype) for out in outs[1:]]
    room += [pltpu.SemaphoreType.DMA((3, tokens // TABLE_ROWS))]
    return table_work, [lengths, parents, rope_freqs(128)], [VMEM] * 3, outs, [VMEM, HBM, HBM, HBM], room


def scatter_kernel(rows, offsets, jobs, *refs):
    parts = len(offsets)

    def take(count):
        nonlocal refs
        taken, refs = refs[:count], refs[count:]
        return taken

    a_refs, w_homes, lefts, rights = take(parts), take(parts), take(jobs), take(jobs)
    (out_ref,), products = take(1), take(jobs)
    core_out, core_in, first_in, next_in, sems = take(5)
    a_bufs, w_refs, (a_sems, w_sems), buffers = take(parts), take(parts), take(2), refs

    def work(job):
        if job < jobs:
            finish(token_product(lefts[job], rights[job], products[job], *buffers))

    x, core, row = plane_place()
    over_x, over_row, over_core = plane_neighbours(x, core, row)
    half = rows // 2
    width = out_ref.shape[1]
    chunks = width // COLS

    def place(piece, on_core):
        far_x, far_row, part = PIECES[piece]
        bx = x + far_x - 2 * far_x * x
        by = row + far_row - 2 * far_row * row
        return pl.ds(pl.multiple_of(((bx * 2 + on_core) * 2 + by) * rows + part * half, half), half)

    def columns(j):
        return pl.ds(pl.multiple_of(j * COLS, COLS), COLS)

    steps = [(0, True)]
    for piece in range(8):
        steps += [(piece + 1, True)] * (piece < 7) + [(piece, False)]

    def load(step):
        piece, partner_half = steps[step]
        taken = place(piece, 1 - core if partner_half else core)
        return [
            pltpu.make_async_copy(a_ref.at[taken], a_buf.at[step % 2], a_sems.at[step % 2, p])
            for p, (a_ref, a_buf) in enumerate(zip(a_refs, a_bufs))
        ]

    w_copies = [
        pltpu.make_async_copy(home.at[:, pl.ds(offset, w_ref.shape[1])], w_ref, w_sems.at[p])
        for p, (home, offset, w_ref) in enumerate(zip(w_homes, offsets, w_refs))
    ]
    loads = {0: load(0)}
    for copy in w_copies + loads[0]:
        copy.start()
    enter_plane((over_x, over_row, over_core))
    for copy in w_copies:
        copy.wait()

    def partial(slot, j):
        total = None
        for a_buf, w_ref in zip(a_bufs, w_refs):
            term = dot_t(a_buf[slot], w_ref[columns(j), :])
            total = term if total is None else total + term
        return total

    def remote(source, target, slot, device):
        return pltpu.make_async_remote_copy(
            src_ref=source, dst_ref=target, send_sem=sems.at[0, slot], recv_sem=sems.at[1, slot],
            device_id=device, device_id_type=MESH,
        )

    core_copies, first_copies, next_copies = [], [], []
    for step, (piece, partner_half) in enumerate(steps):
        for copy in loads[step]:
            copy.wait()
        if step + 1 < len(steps):
            loads[step + 1] = load(step + 1)
            for copy in loads[step + 1]:
                copy.start()
        if partner_half:

            @pl.loop(0, chunks)
            def _(j, step=step, piece=piece):
                core_out[piece, :, columns(j)] = partial(step % 2, j).astype(BF16)

            core_copies.append(remote(core_out.at[piece], core_in.at[piece], piece, over_core))
            core_copies[-1].start()
            continue
        core_copies[piece].wait_recv()

        @pl.loop(0, chunks)
        def _(j, step=step, piece=piece):
            total = partial(step % 2, j) + core_in[piece, :, columns(j)].astype(F32)
            core_in[piece, :, columns(j)] = total.astype(BF16)

        if piece < 4:
            first_copies.append(
                remote(core_in.at[piece], first_in.at[piece], 8 + piece, over_x if piece % 2 == 0 else over_row)
            )
            first_copies[-1].start()
    for part in range(2):
        first_copies[part].wait_recv()

        @pl.loop(0, chunks)
        def _(j, part=part):
            total = core_in[4 + part, :, columns(j)].astype(F32) + first_in[part, :, columns(j)].astype(F32)
            core_in[4 + part, :, columns(j)] = total.astype(BF16)

        next_copies.append(remote(core_in.at[4 + part], next_in.at[part], 12 + part, over_row if part == 0 else over_x))
        next_copies[-1].start()
    for job in range(jobs):
        work(job)
    for part in range(2):
        first_copies[2 + part].wait_recv()
        next_copies[part].wait_recv()

        @pl.loop(0, chunks)
        def _(j, part=part):
            total = core_in[6 + part, :, columns(j)].astype(F32) + first_in[2 + part, :, columns(j)].astype(F32)
            out_ref[pl.ds(part * half, half), columns(j)] = total + next_in[part, :, columns(j)].astype(F32)

    for copy in core_copies + first_copies + next_copies:
        copy.wait_send()


def plane_scatter(parts, weights, collective_id, jobs=(), offsets=None):
    count = parts[0].shape[0]
    width = weights[0].shape[0]
    rows = count // 8
    half = rows // 2
    vmem, hbm = pl.BlockSpec(memory_space=pltpu.VMEM), pl.BlockSpec(memory_space=pl.ANY)
    offsets = offsets or [0] * len(parts)
    lefts, rights = [left for left, _ in jobs], [right for _, right in jobs]
    return pl.pallas_call(
        functools.partial(scatter_kernel, rows, offsets, len(jobs)),
        in_specs=[hbm] * (2 * len(parts) + 2 * len(jobs)),
        out_specs=[vmem] + [hbm] * len(jobs),
        out_shape=[jax.ShapeDtypeStruct((rows, width), F32)]
        + [jax.ShapeDtypeStruct((left.shape[1], right.shape[1]), BF16) for left, right in jobs],
        scratch_shapes=[
            pltpu.VMEM((8, half, width), BF16),
            pltpu.VMEM((8, half, width), BF16),
            pltpu.VMEM((4, half, width), BF16),
            pltpu.VMEM((2, half, width), BF16),
            pltpu.SemaphoreType.DMA((2, 14)),
        ]
        + [pltpu.VMEM((2, half, a.shape[1]), BF16) for a in parts]
        + [pltpu.VMEM((width, a.shape[1]), BF16) for a in parts]
        + [pltpu.SemaphoreType.DMA((2, len(parts))), pltpu.SemaphoreType.DMA((len(parts),))]
        + (product_buffers(rights[0].shape[1]) if jobs else []),
        compiler_params=pltpu.CompilerParams(
            collective_id=collective_id, has_side_effects=True, vmem_limit_bytes=60 << 20
        ),
        cost_estimate=small_cost(),
        name="plane_scatter",
    )(*parts, *weights, *lefts, *rights)


def gated_kernel(x_ref, grad_ref, gate_ref, up_ref, hidden_ref, gate_grad_ref, up_grad_ref):
    columns = gate_ref.shape[1]
    step = min(512, columns)
    together = min(2, columns // step)

    @pl.loop(0, columns // (step * together))
    def _(j):
        for part in range(together):
            taken = pl.ds(pl.multiple_of((j * together + part) * step, step), step)
            gate = dot_n(x_ref[...], gate_ref[:, taken])
            up = dot_n(x_ref[...], up_ref[:, taken])
            grad = grad_ref[:, taken].astype(F32)
            sigmoid = jax.nn.sigmoid(gate)
            silu = gate * sigmoid
            hidden_ref[:, taken] = (silu * up).astype(BF16)
            gate_grad_ref[:, taken] = (grad * up * (sigmoid + silu * (1.0 - sigmoid))).astype(BF16)
            up_grad_ref[:, taken] = (grad * silu).astype(BF16)


def gated_rows(x, hidden_grad, w_gate, w_up):
    tokens, depth = x.shape
    columns = w_gate.shape[1]
    block = 256
    rows = pl.BlockSpec((block, columns), lambda i: (i, 0))
    weight = pl.BlockSpec((depth, columns), lambda i: (0, 0), pipeline_mode=pl.Buffered(1))
    out = jax.ShapeDtypeStruct((tokens, columns), BF16)
    return pl.pallas_call(
        gated_kernel,
        grid=(tokens // block,),
        in_specs=[pl.BlockSpec((block, depth), lambda i: (i, 0)), rows, weight, weight],
        out_specs=[rows] * 3,
        out_shape=[out] * 3,
        compiler_params=pltpu.CompilerParams(vmem_limit_bytes=60 << 20),
        cost_estimate=small_cost(),
        name="gated_rows",
    )(x, hidden_grad, w_gate, w_up)


def heads_kernel(x_ref, w_ref, out_ref, heads_ref, grad_ref, total):
    i = pl.program_id(0)

    @pl.when(i == 0)
    def _():
        total[...] = jnp.zeros_like(total)

    heads_ref[...] = dot_n(x_ref[...], w_ref[...]).astype(BF16)
    total[...] += dot_tn(out_ref[...], x_ref[...])

    @pl.when(i == pl.num_programs(0) - 1)
    def _():
        grad_ref[...] = jnp.transpose(total[...]).astype(BF16)


def heads_and_output_grad(mid, w_attn, attn_out):
    tokens, depth = mid.shape
    width = attn_out.shape[1]
    if width % 128:
        return dot_n(mid, w_attn[:, 3 * width :]).astype(BF16), dot_tn(mid, attn_out).astype(BF16)
    block = 1024
    rows = pl.BlockSpec((block, width), lambda i: (i, 0))
    return pl.pallas_call(
        heads_kernel,
        grid=(tokens // block,),
        in_specs=[pl.BlockSpec((block, depth), lambda i: (i, 0)), pl.BlockSpec((depth, width), lambda i: (0, 3)), rows],
        out_specs=[rows, pl.BlockSpec((depth, width), lambda i: (0, 0))],
        out_shape=[jax.ShapeDtypeStruct((tokens, width), BF16), jax.ShapeDtypeStruct((depth, width), BF16)],
        scratch_shapes=[pltpu.VMEM((width, depth), F32)],
        compiler_params=pltpu.CompilerParams(vmem_limit_bytes=60 << 20),
        cost_estimate=small_cost(),
        name="heads_and_output_grad",
    )(mid, w_attn, attn_out)


def weight_grads_kernel(x_ref, pre_ref, output_ref, grad_ref, total):
    i = pl.program_id(0)
    width = pre_ref.shape[1]

    @pl.when(i == 0)
    def _():
        total[...] = jnp.zeros_like(total)

    total[...] += dot_tn(x_ref[...], pre_ref[...])

    @pl.when(i == pl.num_programs(0) - 1)
    def _():
        grad_ref[:, :width] = total[...].astype(BF16)
        grad_ref[:, width:] = output_ref[...]


def attention_weight_grads(attn_in, pre_grads, output_grad):
    tokens, depth = attn_in.shape
    width, last = pre_grads.shape[1], output_grad.shape[1]
    if width % 128 or last % 128:
        return jnp.concatenate([dot_tn(attn_in, pre_grads).astype(BF16), output_grad], axis=1)
    block = 1024
    return pl.pallas_call(
        weight_grads_kernel,
        grid=(tokens // block,),
        in_specs=[
            pl.BlockSpec((block, depth), lambda i: (i, 0)),
            pl.BlockSpec((block, width), lambda i: (i, 0)),
            pl.BlockSpec((depth, last), lambda i: (0, 0)),
        ],
        out_specs=pl.BlockSpec((depth, width + last), lambda i: (0, 0)),
        out_shape=jax.ShapeDtypeStruct((depth, width + last), BF16),
        scratch_shapes=[pltpu.VMEM((depth, width), F32)],
        compiler_params=pltpu.CompilerParams(vmem_limit_bytes=60 << 20),
        cost_estimate=small_cost(),
        name="attention_weight_grads",
    )(attn_in, pre_grads, output_grad)


def is_plane():
    return lax.axis_size("ctx") == 4 and lax.axis_size("tensor") == 2


def gather_rows(rows):
    return lax.all_gather(rows, GROUP, axis=0, tiled=True)


def scatter_rows(rows):
    return lax.psum_scatter(rows.astype(BF16), GROUP, scatter_dimension=0, tiled=True).astype(F32)


def gather_now(rows):
    return plane_gather(rows)[0] if is_plane() else gather_rows(rows)


def cut(weight):
    columns = weight.shape[1] // lax.axis_size("ctx")
    return lax.dynamic_slice_in_dim(weight, lax.axis_index("ctx") * columns, columns, 1)


def gather_with_tables(rows, lengths, parents, tokens, width, weights):
    if is_plane():
        jobs = [cut_job(weights, lax.axis_size("ctx")), table_job(lengths, parents, tokens)]
        got = plane_gather(rows, 8, jobs, (4, 4))
        return got[:1] + got[1 + len(weights) :], got[1 : 1 + len(weights)]
    segment, parent, depth = tree_tables(lengths[0], parents[0], tokens)
    return [gather_rows(rows), *lay_out(segment, parent), *rope_tables(depth, width)], [cut(w) for w in weights]


def gather_with_product(rows, left, right):
    if is_plane():
        return plane_gather(rows, 5, [row_job(left, right, False)], (4, 4))
    return gather_rows(rows), dot_n(left, right).astype(BF16)


def gather_with_three(rows, left, right, shared, first, second):
    if is_plane():
        return plane_gather(rows, 4, [row_job(left, right, True), pair_job(shared, first, second)], (8, 3))
    products = dot_t(left, right), dot_tn(shared, first), dot_tn(shared, second)
    return [gather_rows(rows)] + [product.astype(BF16) for product in products]


def product_scatter(parts, weights, collective_id, jobs=(), offsets=None):
    if is_plane():
        return plane_scatter(parts, weights, collective_id, jobs, offsets)
    offsets = offsets or [0] * len(parts)
    weights = [w[:, first : first + part.shape[1]] for part, w, first in zip(parts, weights, offsets)]
    rows = scatter_rows(dot_t(jnp.concatenate(parts, axis=1), jnp.concatenate(weights, axis=1)))
    return [rows] + [dot_tn(left, right).astype(BF16) for left, right in jobs]


def gather_weight(own):
    return lax.all_gather(own, "fsdp", axis=0, tiled=True)


def scatter_weight(grad):
    return lax.psum_scatter(grad.astype(BF16), "fsdp", scatter_dimension=0, tiled=True)


def swap_rows(part):
    size = lax.axis_size("ctx")
    return lax.all_to_all(part.reshape(size, part.shape[0] // size, -1), "ctx", split_axis=0, concat_axis=0)


def lay_side_by_side(got, count):
    columns = got.shape[2] // count
    return [
        jnp.concatenate([got[j, :, c * columns : (c + 1) * columns] for j in range(got.shape[0])], axis=1).astype(F32)
        for c in range(count)
    ]


def normalize(rows):
    norm_inv = lax.rsqrt(jnp.mean(rows * rows, axis=1, keepdims=True) + EPSILON)
    return (rows * norm_inv, norm_inv)


def norm_backward(grad_rows, scaled, norm_inv, gain):
    weighted = grad_rows * gain[None, :]
    inner = jnp.mean(weighted * scaled, axis=1, keepdims=True)
    return norm_inv * (weighted - scaled * inner)


def body(
    tokens_in,
    attn_gain,
    query_weight,
    key_weight,
    value_weight,
    output_weight,
    mlp_gain,
    gate_weight,
    up_weight,
    down_weight,
    seg_lengths,
    leaf_parent,
    cotangent,
):
    ctx = lax.axis_index("ctx")
    parts = lax.axis_size("ctx")
    tree_len = tokens_in.shape[0] * parts * lax.axis_size("tensor")
    width = query_weight.shape[1] // parts
    units = gate_weight.shape[1] // parts

    def mine(weight, columns):
        return lax.dynamic_slice_in_dim(weight, ctx * columns, columns, 1)

    x_rows = tokens_in.astype(F32)
    attn_scaled, attn_inv = normalize(x_rows)
    w_attn = gather_weight(
        jnp.concatenate([mine(w, width) for w in (query_weight, key_weight, value_weight, output_weight)], axis=1)
    )
    (attn_in, rows_table, cols_table, cosine, sine), cuts = gather_with_tables(
        (attn_scaled * attn_gain[None, :]).astype(BF16),
        seg_lengths,
        leaf_parent,
        tree_len,
        min(2 * HEAD_DIM, width),
        [gate_weight, down_weight, up_weight],
    )
    w_gate, w_down, w_up = [gather_weight(own) for own in cuts]
    w_qkv = w_attn[:, : 3 * width]

    qkv = jnp.dot(attn_in, w_qkv, preferred_element_type=F32)
    if is_plane():
        attn_out, lse, query_rows, key_rows, value_rows, cot_all = attention_forward(
            qkv, cosine, sine, rows_table, cols_table, width, cotangent
        )
    else:
        attn_out, lse, query_rows, key_rows, value_rows = attention_forward(
            qkv, cosine, sine, rows_table, cols_table, width
        )
        cot_all = gather_rows(cotangent)
    mid_rows = x_rows + product_scatter([attn_out], [w_attn], 1, (), [3 * width])[0]
    mlp_scaled, mlp_inv = normalize(mid_rows)
    mlp_own = (mlp_scaled * mlp_gain[None, :]).astype(BF16)
    mlp_in, hidden_grad = gather_with_product(mlp_own, cot_all, w_down)
    hidden, gate_rows_grad, up_rows_grad = gated_rows(mlp_in, hidden_grad, w_gate, w_up)

    mlp_in_grad, down_part = product_scatter(
        [gate_rows_grad, up_rows_grad], [w_gate, w_up], 3, [(cot_all, hidden)]
    )
    down_grad = scatter_weight(down_part)
    mid_grad = cotangent.astype(F32) + norm_backward(mlp_in_grad, mlp_scaled, mlp_inv, mlp_gain)
    mid_all, down_rows, up_part, gate_part = gather_with_three(
        mid_grad.astype(BF16), hidden, w_down, mlp_in, up_rows_grad, gate_rows_grad
    )
    up_grad = scatter_weight(up_part)
    gate_grad = scatter_weight(gate_part)

    out_heads_grad, output_grad = heads_and_output_grad(mid_all, w_attn, attn_out)
    out_heads_grad, down_grad = lax.optimization_barrier((out_heads_grad, down_grad))
    if is_plane():
        pre_grads, down_rows = attention_backward(
            query_rows, key_rows, value_rows, attn_out, out_heads_grad, lse, cosine, sine, rows_table, cols_table, down_rows
        )
    else:
        pre_grads = attention_backward(
            query_rows, key_rows, value_rows, attn_out, out_heads_grad, lse, cosine, sine, rows_table, cols_table
        )
        pre_grads = jnp.concatenate(pre_grads, axis=1)
        down_rows = scatter_rows(down_rows)
    block_out = (mid_rows + down_rows.astype(F32)).astype(BF16)
    pre_grads, up_grad, gate_grad, down_swapped = lax.optimization_barrier(
        (pre_grads, up_grad, gate_grad, swap_rows(down_grad))
    )
    swapped = swap_rows(jnp.concatenate([gate_grad, up_grad], axis=1))
    attn_part = attention_weight_grads(attn_in, pre_grads, output_grad)
    pre_grads, attn_part, swapped = lax.optimization_barrier((pre_grads, attn_part, swapped))
    attn_grad = scatter_weight(attn_part)
    (attn_in_grad,) = product_scatter([pre_grads], [w_attn], 2)
    attn_in_grad, attn_grad = lax.optimization_barrier((attn_in_grad, attn_grad))
    gate_out, up_out = lay_side_by_side(swapped, 2)
    (down_out,) = lay_side_by_side(down_swapped, 1)
    query_out, key_out, value_out, output_out = lay_side_by_side(swap_rows(attn_grad), 4)

    def gain_part(pairs, gain):
        held = query_out.shape[0]
        total = sum(
            jnp.sum(lax.dynamic_slice_in_dim(weight, ctx * held, held, 0).astype(F32) * grad, axis=1)
            for weight, grad in pairs
        )
        first = (lax.axis_index("fsdp") * parts + ctx) * held
        return total / lax.dynamic_slice_in_dim(gain, first, held, 0)

    sums = jnp.stack(
        [
            gain_part([(query_weight, query_out), (key_weight, key_out), (value_weight, value_out)], attn_gain),
            gain_part([(gate_weight, gate_out), (up_weight, up_out)], mlp_gain),
        ]
    )
    row, others = lax.axis_index("tensor"), lax.axis_size("tensor")
    kept = sums.shape[1] // others
    if others == 2:
        got = lax.ppermute(lax.dynamic_slice_in_dim(sums, (1 - row) * kept, kept, 1), "tensor", [(0, 1), (1, 0)])
        gain_grads = lax.dynamic_slice_in_dim(sums, row * kept, kept, 1) + got
    else:
        gain_grads = lax.dynamic_slice_in_dim(lax.psum(sums, "tensor"), row * kept, kept, 1)

    attn_back = norm_backward(attn_in_grad, attn_scaled, attn_inv, attn_gain)
    input_grad = (mid_grad + attn_back).astype(BF16)
    return (
        block_out,
        input_grad,
        gain_grads[0],
        query_out,
        key_out,
        value_out,
        output_out,
        gain_grads[1],
        gate_out,
        up_out,
        down_out,
    )


def solution(mesh):
    rows = P(("fsdp", "ctx", "tensor"), None)
    weight = P("fsdp", "tensor")
    gain = P(("fsdp", "ctx", "tensor"))
    grad = P(("fsdp", "ctx"), "tensor")
    in_specs = (
        rows, P(), weight, weight, weight, weight, P(), weight, weight, weight, P("fsdp", None), P("fsdp", None), rows,
    )
    out_specs = (rows, rows, gain, grad, grad, grad, grad, gain, grad, grad, grad)
    return jax.shard_map(body, mesh=mesh, in_specs=in_specs, out_specs=out_specs, check_vma=False)
```

```python
import functools

import jax
import jax.numpy as jnp
import numpy as np
from jax import lax
from jax.experimental import pallas as pl
from jax.experimental.pallas import tpu as pltpu
from jax.sharding import PartitionSpec as P

HEAD_DIM = 64
TRUNK = 2176
MOST_SEG = 128
ROPE_BASE = 130000.0
EPSILON = 1e-05
NEG_LARGE = -1e30
SCALE = HEAD_DIM ** (-0.5)

BQ = 512
BK = 512
GROUP = ("ctx", "tensor")

F32 = jnp.float32
BF16 = jnp.bfloat16


def pick_table(onehot, table):
    return jnp.sum(jnp.where(onehot, table[None, :], 0), axis=1)


def tree_tables(lengths_row, parent_row, tree_len):
    branches = lengths_row.shape[0] - parent_row.shape[0]
    ends = TRUNK + jnp.cumsum(lengths_row)
    starts = ends - lengths_row
    matches = parent_row[:, None] - 1 == jnp.arange(branches, dtype=jnp.int32)[None, :]
    parent_len = jnp.sum(jnp.where(matches, lengths_row[None, :branches], 0), axis=1)
    zero_one = jnp.zeros((1,), jnp.int32)
    seg_start = jnp.concatenate([zero_one, starts])
    seg_base = jnp.concatenate(
        [zero_one, jnp.full((branches,), TRUNK, jnp.int32), TRUNK + parent_len]
    )
    seg_parent = jnp.concatenate([zero_one, jnp.zeros((branches,), jnp.int32), parent_row])
    positions = jnp.arange(tree_len, dtype=jnp.int32)
    above = jnp.sum((ends[None, :] <= positions[:, None]).astype(jnp.int32), axis=1)
    segment = (positions >= TRUNK).astype(jnp.int32) + above
    onehot = segment[:, None] == jnp.arange(seg_start.shape[0], dtype=jnp.int32)[None, :]
    depth = positions - pick_table(onehot, seg_start) + pick_table(onehot, seg_base)
    parent = pick_table(onehot, seg_parent)
    return (segment, parent, depth)


def rope_freqs(width):
    half = HEAD_DIM // 2
    powers = -2.0 * (np.arange(width) % half) / HEAD_DIM
    return np.power(ROPE_BASE, powers).astype(np.float32)[None, :]


def rope_tables(depth, width):
    angles = depth.astype(F32)[:, None] * rope_freqs(width)
    sign = np.where(np.arange(width) % HEAD_DIM < HEAD_DIM // 2, -1.0, 1.0).astype(np.float32)
    return jnp.cos(angles), jnp.sin(angles) * sign[None, :]


def lay_out(segment, parent):
    both = jnp.stack([segment, parent])
    return jnp.pad(both, ((0, 6), (0, 0))), jnp.pad(both.T, ((0, 0), (0, 126)))


TABLE_ROWS = 512
TABLE_STEP = 64


def tables_at(positions, lengths, parents):
    leaves = parents.shape[1]
    branches = lengths.shape[1] - leaves
    zero = jnp.zeros_like(positions)
    segment = jnp.where(positions >= TRUNK, 1, 0)
    parent, depth = zero, positions
    end = jnp.full((1, 1), TRUNK, jnp.int32)
    starts = []
    for s in range(branches + leaves):
        start, end = end, end + lengths[:, s : s + 1]
        inside = (positions >= start) & (positions < end)
        base, above = jnp.full((1, 1), TRUNK, jnp.int32), jnp.zeros((1, 1), jnp.int32)
        if s >= branches:
            above = parents[:, s - branches : s - branches + 1]
            for b in range(branches):
                base = base + jnp.where(above == b + 1, lengths[:, b : b + 1], 0)
        segment = segment + jnp.where(positions >= end, 1, 0)
        parent = jnp.where(inside, above, parent)
        depth = jnp.where(inside, positions - start + base, depth)
    return segment, parent, depth


def sine_cosine(x):
    turns = jnp.floor(x * np.float32(2.0 / np.pi) + 0.5)
    r = x - turns * np.float32(1.5703125)
    r = r - turns * np.float32(4.837512969970703125e-4)
    r = r - turns * np.float32(7.549789954891882e-8)
    z = r * r
    sine = ((np.float32(-1.9515295891e-4) * z + np.float32(8.3321608736e-3)) * z - np.float32(1.6666654611e-1)) * z * r + r
    cosine = (
        (np.float32(2.443315711809948e-5) * z - np.float32(1.388731625493765e-3)) * z + np.float32(4.166664568298827e-2)
    ) * z * z - np.float32(0.5) * z + np.float32(1.0)
    quarter = turns.astype(jnp.int32) & 3
    odd = (quarter & 1) == 1
    first, second = jnp.where(odd, cosine, sine), jnp.where(odd, sine, cosine)
    return jnp.where(quarter >= 2, -first, first), jnp.where((quarter == 1) | (quarter == 2), -second, second)


def table_work(lengths, parents, freqs, rows_ref, cols_ref, cos_ref, sin_ref, cols_buf, cos_buf, sin_buf, sems):
    yield
    tokens = cos_ref.shape[0]
    shape = (8, tokens)
    segment, parent, _ = tables_at(lax.broadcasted_iota(jnp.int32, shape, 1), lengths, parents)
    line = lax.broadcasted_iota(jnp.int32, shape, 0)
    rows_ref[...] = jnp.where(line == 0, segment, jnp.where(line == 1, parent, 0))
    copies = []
    for chunk in range(tokens // TABLE_ROWS):
        rows = pl.ds(chunk * TABLE_ROWS, TABLE_ROWS)

        @pl.loop(0, TABLE_ROWS // TABLE_STEP)
        def _(j, chunk=chunk):
            first = pl.multiple_of(chunk * TABLE_ROWS + j * TABLE_STEP, TABLE_STEP)
            taken = pl.ds(first, TABLE_STEP)
            shape = (TABLE_STEP, 128)
            lane = lax.broadcasted_iota(jnp.int32, shape, 1)
            segment, parent, depth = tables_at(lax.broadcasted_iota(jnp.int32, shape, 0) + first, lengths, parents)
            cols_buf[taken, :] = jnp.where(lane == 0, segment, jnp.where(lane == 1, parent, 0))
            sine, cosine = sine_cosine(depth.astype(F32) * freqs[...])
            cos_buf[taken, :] = cosine
            sin_buf[taken, :] = jnp.where(lane % HEAD_DIM < HEAD_DIM // 2, -sine, sine)

        for kind, (source, target) in enumerate(((cols_buf, cols_ref), (cos_buf, cos_ref), (sin_buf, sin_ref))):
            copies.append(pltpu.make_async_copy(source.at[rows], target.at[rows], sems.at[kind, chunk]))
            copies[-1].start()
        yield
    for copy in copies:
        copy.wait()


MESH = pl.DeviceIdType.MESH


def plane_place():
    ctx, row = lax.axis_index("ctx"), lax.axis_index("tensor")
    x, core = ctx // 2, ctx % 2
    return x, core, row


def plane_neighbours(x, core, row):
    over_x = {"ctx": (1 - x) * 2 + core}
    over_core = {"ctx": x * 2 + 1 - core}
    over_row = {"tensor": 1 - row}
    return over_x, over_row, over_core


def enter_plane(neighbours):
    barrier = pltpu.get_barrier_semaphore()
    for device in neighbours:
        pl.semaphore_signal(barrier, inc=1, device_id=device, device_id_type=MESH)
    pl.semaphore_wait(barrier, 3)


PIECES = ((1, 1, 0), (1, 1, 1), (1, 0, 0), (0, 1, 1), (0, 1, 0), (1, 0, 1), (0, 0, 0), (0, 0, 1))
COLS = 512


class PlaneGather:
    def __init__(self, own_ref, all_ref, local_sem, send_sem, recv_sem):
        self.own_ref, self.all_ref, self.sems = own_ref, all_ref, (local_sem, send_sem, recv_sem)
        self.x, self.core, self.row = plane_place()
        self.devices = plane_neighbours(self.x, self.core, self.row)
        self.rows = own_ref.shape[0]

    def place(self, far_x, far_row, part):
        bx = self.x + far_x - 2 * far_x * self.x
        by = self.row + far_row - 2 * far_row * self.row
        half = self.rows // 2
        return pl.ds(pl.multiple_of(((bx * 2 + self.core) * 2 + by) * self.rows + part * half, half), half)

    def copy(self, slot):
        far_x, far_row, part, device = (
            (0, 0, 0, 1), (0, 0, 1, 1), (1, 0, 1, 1), (0, 0, 1, 0), (0, 0, 0, 0), (0, 1, 0, 0), (0, 0, 0, 2),
            (0, 0, 1, 2), (0, 1, 0, 2), (1, 0, 1, 2), (0, 1, 1, 2), (1, 0, 0, 2), (1, 1, 0, 2), (1, 1, 1, 2),
        )[slot]
        half = self.rows // 2
        target = self.place(far_x, far_row, part)
        own = far_x == 0 and far_row == 0
        source = self.own_ref.at[pl.ds(part * half, half)] if own else self.all_ref.at[target]
        return pltpu.make_async_remote_copy(
            src_ref=source, dst_ref=self.all_ref.at[target], send_sem=self.sems[1].at[slot],
            recv_sem=self.sems[2].at[slot], device_id=self.devices[device], device_id_type=MESH,
        )

    def local(self, part):
        half = self.rows // 2
        return pltpu.make_async_copy(
            self.own_ref.at[pl.ds(part * half, half)], self.all_ref.at[self.place(0, 0, part)], self.sems[0].at[part]
        )

    def start(self):
        enter_plane(self.devices)
        for slot in (0, 3, 1, 4, 6, 7):
            self.copy(slot).start()
        for part in range(2):
            self.local(part).start()

    def forward(self, got, slots):
        self.copy(got).wait_recv()
        for slot in slots:
            self.copy(slot).start()

    def first(self):
        self.forward(0, (5, 8))
        self.forward(3, (2, 9))

    def second(self):
        self.forward(1, (10,))
        self.forward(4, (11,))

    def finish(self):
        self.forward(5, (12,))
        self.forward(2, (13,))
        for slot in range(6, 14):
            self.copy(slot).wait_recv()
        for slot in range(14):
            self.copy(slot).wait_send()
        for part in range(2):
            self.local(part).wait()


def gather_sems():
    return [pltpu.SemaphoreType.DMA((2,)), pltpu.SemaphoreType.DMA((14,)), pltpu.SemaphoreType.DMA((14,))]


class PlaneScatter:
    def __init__(self, part_ref, out_ref, core_in, first_in, next_in, own, total, sems, own_sems):
        self.part_ref, self.out_ref, self.core_in, self.first_in, self.next_in = part_ref, out_ref, core_in, first_in, next_in
        self.own, self.total, self.sems, self.own_sems = own, total, sems, own_sems
        self.x, self.core, self.row = plane_place()
        self.devices = plane_neighbours(self.x, self.core, self.row)
        self.rows = part_ref.shape[0] // 8

    def place(self, piece, on_core):
        far_x, far_row, part = PIECES[piece]
        bx = self.x + far_x - 2 * far_x * self.x
        by = self.row + far_row - 2 * far_row * self.row
        half = self.rows // 2
        return pl.ds(pl.multiple_of(((bx * 2 + on_core) * 2 + by) * self.rows + part * half, half), half)

    def copy(self, slot):
        if slot < 8:
            source, target, device = self.part_ref.at[self.place(slot, 1 - self.core)], self.core_in.at[slot], 2
        elif slot < 12:
            source, target, device = self.core_in.at[slot - 8], self.first_in.at[slot - 8], slot % 2
        else:
            source, target, device = self.core_in.at[slot - 8], self.next_in.at[slot - 12], 1 - slot % 2
        return pltpu.make_async_remote_copy(
            src_ref=source, dst_ref=target, send_sem=self.sems.at[0, slot], recv_sem=self.sems.at[1, slot],
            device_id=self.devices[device], device_id_type=MESH,
        )

    def load(self, piece):
        return pltpu.make_async_copy(
            self.part_ref.at[self.place(piece, self.core)], self.own.at[piece % 4], self.own_sems.at[piece % 4]
        )

    def add(self, target, where, *others):
        @pl.loop(0, target.shape[-1] // COLS)
        def _(j):
            columns = pl.ds(pl.multiple_of(j * COLS, COLS), COLS)
            total = sum(ref[slot, :, columns].astype(F32) for ref, slot in others)
            target[where, :, columns] = total.astype(target.dtype)

    def start(self):
        enter_plane(self.devices)
        for slot in range(8):
            self.copy(slot).start()
        for piece in range(4):
            self.load(piece).start()

    def first(self):
        for piece in range(4):
            self.load(piece).wait()
            self.copy(piece).wait_recv()
            self.add(self.core_in, piece, (self.own, piece), (self.core_in, piece))
            self.copy(8 + piece).start()
        for piece in range(4, 8):
            self.load(piece).start()

    def second(self):
        for piece in range(4, 8):
            self.load(piece).wait()
            self.copy(piece).wait_recv()
            self.add(self.core_in, piece, (self.own, piece - 4), (self.core_in, piece))

    def third(self):
        for part in range(2):
            self.copy(8 + part).wait_recv()
            self.add(self.core_in, 4 + part, (self.core_in, 4 + part), (self.first_in, part))
            self.copy(12 + part).start()

    def finish(self):
        half = self.rows // 2
        for part in range(2):
            self.copy(10 + part).wait_recv()
            self.copy(12 + part).wait_recv()
            self.add(self.total, part, (self.core_in, 6 + part), (self.first_in, 2 + part), (self.next_in, part))
        stores = [
            pltpu.make_async_copy(
                self.total.at[part], self.out_ref.at[pl.ds(part * half, half)], self.own_sems.at[part]
            )
            for part in range(2)
        ]
        for store in stores:
            store.start()
        for slot in range(14):
            self.copy(slot).wait_send()
        for store in stores:
            store.wait()


def scatter_scratch(rows, width):
    half = rows // 2
    return [
        pltpu.VMEM((8, half, width), BF16),
        pltpu.VMEM((4, half, width), BF16),
        pltpu.VMEM((2, half, width), BF16),
        pltpu.VMEM((4, half, width), BF16),
        pltpu.VMEM((2, half, width), BF16),
        pltpu.SemaphoreType.DMA((2, 14)),
        pltpu.SemaphoreType.DMA((4,)),
    ]


def at_step(step, total, places):
    for place, phase in places:

        @pl.when(step == place)
        def _(phase=phase):
            phase()


def partner(x):
    half = HEAD_DIM // 2
    width = x.shape[1]
    if width == HEAD_DIM:
        return jnp.concatenate([x[:, half:], x[:, :half]], axis=1)
    lane = lax.broadcasted_iota(jnp.int32, x.shape, 1)
    ahead = pltpu.roll(x, width - half, 1)
    behind = pltpu.roll(x, half, 1)
    return jnp.where(lane % HEAD_DIM < half, ahead, behind)


def head_mask(shape, head):
    lane = lax.broadcasted_iota(jnp.int32, shape, 1)
    return lane // HEAD_DIM == head


def dot_t(a, b):
    return lax.dot_general(a, b, (((1,), (1,)), ((), ())), preferred_element_type=F32)


def dot_n(a, b):
    return lax.dot_general(a, b, (((1,), (0,)), ((), ())), preferred_element_type=F32)


def dot_tn(a, b):
    return lax.dot_general(a, b, (((0,), (0,)), ((), ())), preferred_element_type=F32)


def key_plan(i, tile):
    base = TRUNK // BK * BK
    branch_end = TRUNK + 4 * MOST_SEG
    first_tree = base // BQ
    mixed_end = -(-(branch_end + MOST_SEG) // BQ)
    chunks = jnp.minimum(i * BQ, base) // BK
    half = BQ // 2

    @pl.when(i < first_tree)
    def _():
        @pl.loop(0, chunks)
        def _(j):
            start = pl.multiple_of(j * BK, BK)
            tile(start, BK, 0, start, 0, BQ)

    @pl.when(i >= first_tree)
    def _():
        tile(0, base, 0, 0, 0, BQ)

    @pl.when(i < first_tree)
    def _():
        start = pl.multiple_of(chunks * BK, BK)
        for part in range(2):
            tile(start, (part + 1) * half, 1, start, part * half, half)

    for block in range(first_tree, mixed_end):

        @pl.when(i == block)
        def _(block=block):
            for part in range(2):
                tile(base, block * BQ + (part + 1) * half - base, 2, base, part * half, half)

    @pl.when(i >= mixed_end)
    def _():
        tile(base, branch_end - base, 3, base, 0, BQ)
        for part in range(2):
            start = pl.multiple_of(i * BQ + part * half - MOST_SEG, MOST_SEG)
            tile(start, half + MOST_SEG, 4, branch_end, part * half, half)


def most_keys():
    branch_end = TRUNK + 4 * MOST_SEG
    return max(branch_end + BQ // 2 + MOST_SEG, -(-(branch_end + MOST_SEG) // BQ) * BQ)


def seen_mask(kind, q_at, k_at, seg_q, par_q, seg_k):
    if kind == 3:
        return (seg_k == 0) | (seg_k == par_q)
    causal = k_at <= q_at
    if kind == 1:
        return causal
    if kind == 4:
        return causal & (seg_k == seg_q)
    return causal & ((seg_k == 0) | (seg_k == seg_q) | (seg_k == par_q))


def fwd_kernel(heads, hosts, *refs):
    if not hosts:
        return fwd_work(heads, *refs)
    gather = PlaneGather(refs[7], refs[13], *refs[-3:])
    step, total = pl.program_id(0) * pl.num_programs(1) + pl.program_id(1), 16
    at_step(step, total, ((0, gather.start), (6, gather.first), (12, gather.second)))
    fwd_work(heads, *refs[:7], *refs[8:13], *refs[14:-3])
    at_step(step, total, ((total - 1, gather.finish),))


def fwd_work(
    heads, q_ref, k_ref, v_ref, cos_ref, sin_ref, rows_ref, cols_ref,
    o_ref, lse_ref, qr_ref, kr_ref, vr_ref, kt_ref, va_ref, s_ref, m_ref, acc_ref,
):
    i = pl.program_id(1)
    wide = 2 * HEAD_DIM

    @pl.when(i == 0)
    def _():
        @pl.loop(0, k_ref.shape[0] // BK)
        def _(j):
            rows = pl.ds(pl.multiple_of(j * BK, BK), BK)
            k = k_ref[rows, :]
            k = (k * cos_ref[rows, :] + partner(k) * sin_ref[rows, :]).astype(BF16)
            kr_ref[rows, :] = k
            kt_ref[:, rows] = jnp.transpose(k)
            v = v_ref[rows, :].astype(BF16)
            vr_ref[rows, :] = v
            if heads == 1:
                va_ref[0, rows, :] = jnp.concatenate([v, jnp.ones_like(v)], axis=1)
            else:
                for h in range(heads):
                    va_ref[h, rows, :] = jnp.where(head_mask(v.shape, h), v, jnp.ones_like(v))

    rows = pl.ds(pl.multiple_of(i * BQ, BQ), BQ)
    q = q_ref[...]
    q = (q * cos_ref[rows, :] + partner(q) * sin_ref[rows, :]).astype(BF16)
    qr_ref[...] = q
    q = q * jnp.asarray(SCALE, BF16)
    q_heads = [jnp.where(head_mask(q.shape, h), q, jnp.zeros_like(q)) for h in range(heads)]
    m_ref[...] = jnp.full_like(m_ref, NEG_LARGE)
    acc_ref[...] = jnp.zeros_like(acc_ref)

    def score_tile(start, width, kind, place, first, count):
        keys, rows = pl.ds(start, width), slice(first, first + count)
        k = kt_ref[:, keys]
        seen = None
        if kind != 0:
            shape = (count, width)
            seen = seen_mask(
                kind,
                lax.broadcasted_iota(jnp.int32, shape, 0) + i * BQ + first,
                lax.broadcasted_iota(jnp.int32, shape, 1) + start,
                cols_ref[rows, 0:1], cols_ref[rows, 1:2], rows_ref[0:1, keys],
            )
        for h in range(heads):
            s = dot_n(q_heads[h][rows], k)
            if seen is not None:
                s = jnp.where(seen, s, NEG_LARGE)
            s_ref[h, rows, pl.ds(place, width)] = s
            largest = m_ref[h, rows]
            for c in range(width // 128):
                largest = jnp.maximum(largest, s[:, c * 128 : (c + 1) * 128])
            m_ref[h, rows] = largest

    key_plan(i, score_tile)
    for h in range(heads):
        m_ref[h] = jnp.broadcast_to(jnp.max(m_ref[h], axis=1, keepdims=True), (BQ, 128))

    def value_tile(start, width, kind, place, first, count):
        keys, rows = pl.ds(start, width), slice(first, first + count)
        for h in range(heads):
            m = m_ref[h, rows]
            parts = [
                jnp.exp(s_ref[h, rows, pl.ds(place + c * 128, 128)] - m).astype(BF16) for c in range(width // 128)
            ]
            acc_ref[h, rows] += dot_n(jnp.concatenate(parts, axis=1), va_ref[h, keys, :])

    key_plan(i, value_tile)
    out, lse = None, None
    for h in range(heads):
        acc = acc_ref[h]
        part = acc / pltpu.roll(acc, HEAD_DIM, 1)
        stat = m_ref[h] + jnp.log(jnp.broadcast_to(acc[:, (1 - h) * HEAD_DIM : (1 - h) * HEAD_DIM + 1], (BQ, wide)))
        mask = head_mask((BQ, wide), h)
        out = part if h == 0 else jnp.where(mask, part, out)
        lse = stat if h == 0 else jnp.where(mask, stat, lse)
    o_ref[...] = out[:, : heads * HEAD_DIM].astype(BF16)
    turned = jnp.transpose(lse)
    for h in range(heads):
        lse_ref[0, h : h + 1, :] = turned[h * HEAD_DIM : h * HEAD_DIM + 1, :]


def bwd_kernel(heads, hosts, *refs):
    if not hosts:
        return bwd_work(heads, *refs)
    scatter = PlaneScatter(refs[10], refs[12], *refs[-7:])
    step, total = pl.program_id(0) * pl.num_programs(1) + pl.program_id(1), 16
    at_step(
        step, total, ((0, scatter.start), (3, scatter.first), (5, scatter.second), (7, scatter.third))
    )
    bwd_work(heads, *refs[:10], *refs[13:-7], together=refs[11])
    at_step(step, total, ((total - 1, scatter.finish),))


def bwd_work(
    heads, q_ref, k_ref, v_ref, o_ref, do_ref, lse_ref, cos_ref, sin_ref, rows_ref, cols_ref,
    *refs, together=None,
):
    if together is None:
        dq_ref, dk_ref, dv_ref, dq_acc, dk_acc, dv_acc = refs
    else:
        dq_acc, dk_acc, dv_acc, dq_ref, dk_ref, dv_ref, out_sems = refs
    i = pl.program_id(1)

    def store(kind, source, rows, sem):
        groups, width = pl.num_programs(0), source.shape[1]
        columns = pl.ds(pl.multiple_of((kind * groups + pl.program_id(0)) * width, width), width)
        return pltpu.make_async_copy(source, together.at[rows, columns], out_sems.at[sem])

    @pl.when(i == 0)
    def _():
        dk_acc[...] = jnp.zeros_like(dk_acc)
        dv_acc[...] = jnp.zeros_like(dv_acc)

    q = q_ref[...]
    scaled = q * jnp.asarray(SCALE, BF16)
    do = do_ref[...]
    product = jnp.transpose(do.astype(F32) * o_ref[...].astype(F32))
    zero = jnp.zeros_like(q)
    masks = [head_mask(q.shape, h) for h in range(heads)]
    q_heads = [jnp.where(m, scaled, zero) for m in masks]
    do_heads = [jnp.where(m, do, zero) for m in masks]
    deltas = [
        jnp.sum(product[h * HEAD_DIM : (h + 1) * HEAD_DIM, :], axis=0, keepdims=True) for h in range(heads)
    ]
    lses = [lse_ref[0, h : h + 1, :] for h in range(heads)]
    q_turned = [jnp.transpose(x) for x in q_heads]
    do_turned = [jnp.transpose(x) for x in do_heads]
    dq_acc[...] = jnp.zeros_like(dq_acc)

    def tile(start, width, kind, place, first, count):
        keys, part = pl.ds(start, width), slice(first, first + count)
        k = k_ref[keys, :]
        v = v_ref[keys, :]
        seen = None
        if kind != 0:
            shape = (width, count)
            seen = seen_mask(
                kind,
                lax.broadcasted_iota(jnp.int32, shape, 1) + i * BQ + first,
                lax.broadcasted_iota(jnp.int32, shape, 0) + start,
                rows_ref[0:1, part], rows_ref[1:2, part], cols_ref[keys, 0:1],
            )
        probs, grads, k_heads = [], [], []
        for h in range(heads):
            s = dot_n(k, q_turned[h][:, part])
            p = jnp.exp(s - lses[h][:, part])
            if seen is not None:
                p = jnp.where(seen, p, 0.0)
            dp = dot_n(v, do_turned[h][:, part])
            probs.append(p.astype(BF16))
            grads.append((p * (dp - deltas[h][:, part])).astype(BF16))
            k_heads.append(jnp.where(head_mask(k.shape, h), k, jnp.zeros_like(k)))
        grad_row = jnp.concatenate(grads, axis=1)
        dv_acc[keys, :] += dot_n(jnp.concatenate(probs, axis=1), jnp.concatenate([x[part] for x in do_heads], axis=0))
        dk_acc[keys, :] += dot_n(grad_row, jnp.concatenate([x[part] for x in q_heads], axis=0))
        dq_acc[part, :] += dot_tn(jnp.concatenate(grads, axis=0), jnp.concatenate(k_heads, axis=0))

    key_plan(i, tile)
    dq = dq_acc[...] * SCALE
    rows = pl.ds(pl.multiple_of(i * BQ, BQ), BQ)
    dq = (dq * cos_ref[rows, :] - partner(dq) * sin_ref[rows, :]).astype(BF16)
    if together is None:
        dq_ref[...] = dq
    else:
        step, last = pl.program_id(0) * pl.num_programs(1) + i, pl.num_programs(0) * pl.num_programs(1) - 1
        for slot in range(2):

            @pl.when(step % 2 == slot)
            def _(slot=slot):
                @pl.when(step >= 2)
                def _():
                    store(0, dq_ref.at[slot], rows, slot).wait()

                dq_ref[slot] = dq
                store(0, dq_ref.at[slot], rows, slot).start()

        @pl.when(step == last)
        def _():
            for slot in range(2):
                store(0, dq_ref.at[slot], rows, slot).wait()

    @pl.when(i == pl.num_programs(1) - 1)
    def _():
        @pl.loop(0, dk_acc.shape[0] // BK)
        def _(j):
            rows = pl.ds(pl.multiple_of(j * BK, BK), BK)
            dk = dk_acc[rows, :]
            dk_ref[rows, :] = (dk * cos_ref[rows, :] - partner(dk) * sin_ref[rows, :]).astype(BF16)
            dv_ref[rows, :] = dv_acc[rows, :].astype(BF16)

        if together is not None:
            every = pl.ds(0, dk_acc.shape[0])
            copies = [store(1, dk_ref, every, 2), store(2, dv_ref, every, 3)]
            for copy in copies:
                copy.start()
            for copy in copies:
                copy.wait()


def small_cost():
    return pl.CostEstimate(flops=1 << 20, bytes_accessed=1 << 20, transcendentals=0)


def attention_forward(qkv, cosine, sine, rows_table, cols_table, width, hosted=None):
    tree_len = qkv.shape[0]
    gw = min(2 * HEAD_DIM, width)
    groups, heads = width // gw, gw // HEAD_DIM
    row_block = pl.BlockSpec((BQ, gw), lambda g, i: (i, g))
    table = pl.BlockSpec((tree_len, gw), lambda g, i: (0, 0))
    full = pl.BlockSpec((tree_len, gw), lambda g, i: (0, g))
    act = jax.ShapeDtypeStruct((tree_len, width), BF16)
    if width % 128 == 0:
        queries, keys, values, step = qkv, qkv, qkv, groups
    else:
        queries, keys, values = jnp.split(qkv, 3, axis=1)
        step = 0
    hosts = hosted is not None
    hbm = pl.BlockSpec(memory_space=pl.ANY)
    return pl.pallas_call(
        functools.partial(fwd_kernel, heads, hosts),
        grid=(groups, tree_len // BQ),
        in_specs=[
            row_block,
            pl.BlockSpec((tree_len, gw), lambda g, i: (0, step + g)),
            pl.BlockSpec((tree_len, gw), lambda g, i: (0, 2 * step + g)),
            table,
            table,
            pl.BlockSpec((8, tree_len), lambda g, i: (0, 0)),
            pl.BlockSpec((BQ, 128), lambda g, i: (i, 0)),
        ]
        + [hbm] * hosts,
        out_specs=[row_block, pl.BlockSpec((1, heads, BQ), lambda g, i: (g, 0, i)), row_block, full, full] + [hbm] * hosts,
        out_shape=[act, jax.ShapeDtypeStruct((groups, heads, tree_len), F32), act, act, act]
        + ([jax.ShapeDtypeStruct((8 * hosted.shape[0], hosted.shape[1]), BF16)] if hosts else []),
        scratch_shapes=[
            pltpu.VMEM((gw, tree_len), BF16),
            pltpu.VMEM((heads, tree_len, 128), BF16),
            pltpu.VMEM((heads, BQ, most_keys()), F32),
            pltpu.VMEM((heads, BQ, 128), F32),
            pltpu.VMEM((heads, BQ, 128), F32),
        ]
        + (gather_sems() if hosts else []),
        compiler_params=pltpu.CompilerParams(
            vmem_limit_bytes=60 << 20, collective_id=6 if hosts else None, has_side_effects=hosts
        ),
        cost_estimate=small_cost(),
        name="tree_attention_forward",
    )(queries, keys, values, cosine, sine, rows_table, cols_table, *([hosted] if hosts else []))


def attention_backward(q, k, v, out, grad, lse, cosine, sine, rows_table, cols_table, hosted=None):
    tree_len, width = q.shape
    gw = min(2 * HEAD_DIM, width)
    groups, heads = width // gw, gw // HEAD_DIM
    row_block = pl.BlockSpec((BQ, gw), lambda g, i: (i, g))
    table = pl.BlockSpec((tree_len, gw), lambda g, i: (0, 0))
    full = pl.BlockSpec((tree_len, gw), lambda g, i: (0, g))
    act = jax.ShapeDtypeStruct((tree_len, width), BF16)
    hosts = hosted is not None
    hbm = pl.BlockSpec(memory_space=pl.ANY)
    return pl.pallas_call(
        functools.partial(bwd_kernel, heads, hosts),
        grid=(groups, tree_len // BQ),
        in_specs=[
            row_block, full, full, row_block, row_block,
            pl.BlockSpec((1, heads, BQ), lambda g, i: (g, 0, i)),
            table, table,
            pl.BlockSpec((8, BQ), lambda g, i: (0, i)),
            pl.BlockSpec((tree_len, 128), lambda g, i: (0, 0)),
        ]
        + [hbm] * hosts,
        out_specs=[hbm] * 2 if hosts else [row_block, full, full],
        out_shape=[
            jax.ShapeDtypeStruct((tree_len, 3 * width), BF16),
            jax.ShapeDtypeStruct((hosted.shape[0] // 8, hosted.shape[1]), BF16),
        ]
        if hosts
        else [act, act, act],
        scratch_shapes=[
            pltpu.VMEM((BQ, gw), F32),
            pltpu.VMEM((tree_len, gw), F32),
            pltpu.VMEM((tree_len, gw), F32),
        ]
        + (
            [pltpu.VMEM(shape, BF16) for shape in ((2, BQ, gw), (tree_len, gw), (tree_len, gw))]
            + [pltpu.SemaphoreType.DMA((4,))]
            + scatter_scratch(hosted.shape[0] // 8, hosted.shape[1])
            if hosts
            else []
        ),
        compiler_params=pltpu.CompilerParams(
            vmem_limit_bytes=60 << 20, collective_id=7 if hosts else None, has_side_effects=hosts
        ),
        cost_estimate=small_cost(),
        name="tree_attention_backward",
    )(q, k, v, out, grad, lse, cosine, sine, rows_table, cols_table, *([hosted] if hosts else []))


TOKENS_AT_ONCE = 2048
LEFT_AT_ONCE = 512
TOKEN_STEP = 1024
ROW_STEP = 1024


def product_buffers(columns):
    return [
        pltpu.VMEM((2, TOKENS_AT_ONCE, LEFT_AT_ONCE), BF16),
        pltpu.VMEM((2 * TOKENS_AT_ONCE, columns), BF16),
        pltpu.VMEM((LEFT_AT_ONCE, columns), F32),
        pltpu.VMEM((LEFT_AT_ONCE, columns), BF16),
        pltpu.SemaphoreType.DMA((4,)),
    ]


def token_product(left_ref, right_ref, out_ref, left_buf, right_buf, total, out_buf, sems):
    tokens = left_ref.shape[0]
    parts, groups = tokens // TOKENS_AT_ONCE, left_ref.shape[1] // LEFT_AT_ONCE

    def load(step):
        group, part = step // parts, step % parts
        source = left_ref.at[
            pl.ds(part * TOKENS_AT_ONCE, TOKENS_AT_ONCE), pl.ds(group * LEFT_AT_ONCE, LEFT_AT_ONCE)
        ]
        return pltpu.make_async_copy(source, left_buf.at[step % 2], sems.at[step % 2])

    def store(group):
        return pltpu.make_async_copy(out_buf, out_ref.at[pl.ds(group * LEFT_AT_ONCE, LEFT_AT_ONCE)], sems.at[3])

    whole = pltpu.make_async_copy(right_ref, right_buf, sems.at[2])
    whole.start()
    load(0).start()
    yield
    whole.wait()
    for group in range(groups):
        for part in range(parts):
            step = group * parts + part
            load(step).wait()
            if step + 1 < groups * parts:
                load(step + 1).start()
            if part == 0:
                total[...] = jnp.zeros_like(total)

            @pl.loop(0, TOKENS_AT_ONCE // TOKEN_STEP)
            def _(j, step=step, part=part):
                left = left_buf[step % 2, pl.ds(pl.multiple_of(j * TOKEN_STEP, TOKEN_STEP), TOKEN_STEP), :]
                right = right_buf[pl.ds(pl.multiple_of(part * TOKENS_AT_ONCE + j * TOKEN_STEP, TOKEN_STEP), TOKEN_STEP), :]
                total[...] += dot_tn(left, right)

        if group > 0:
            store(group - 1).wait()
        out_buf[...] = total[...].astype(BF16)
        store(group).start()
        yield
    store(groups - 1).wait()


def finish(product):
    for _ in product:
        pass


def pair_product(left_ref, first_ref, second_ref, out_first, out_second, left_buf, right_buf, total, out_buf, sems):
    tokens, columns = first_ref.shape
    parts, groups = tokens // TOKENS_AT_ONCE, left_ref.shape[1] // LEFT_AT_ONCE
    sides = [pl.ds(0, columns), pl.ds(columns, columns)]

    def load(step):
        group, part = step // parts, step % parts
        source = left_ref.at[
            pl.ds(part * TOKENS_AT_ONCE, TOKENS_AT_ONCE), pl.ds(group * LEFT_AT_ONCE, LEFT_AT_ONCE)
        ]
        return pltpu.make_async_copy(source, left_buf.at[step % 2], sems.at[step % 2])

    def stores(group):
        rows = pl.ds(group * LEFT_AT_ONCE, LEFT_AT_ONCE)
        return [
            pltpu.make_async_copy(out_buf.at[:, side], out_ref.at[rows], sems.at[4 + n])
            for n, (side, out_ref) in enumerate(zip(sides, (out_first, out_second)))
        ]

    wholes = [
        pltpu.make_async_copy(ref, right_buf.at[:, side], sems.at[2 + n])
        for n, (side, ref) in enumerate(zip(sides, (first_ref, second_ref)))
    ]
    load(0).start()
    for copy in wholes:
        copy.start()
    yield
    for copy in wholes:
        copy.wait()
    for group in range(groups):
        for part in range(parts):
            step = group * parts + part
            load(step).wait()
            if step + 1 < groups * parts:
                load(step + 1).start()
            if part == 0:
                total[...] = jnp.zeros_like(total)

            @pl.loop(0, TOKENS_AT_ONCE // TOKEN_STEP)
            def _(j, step=step, part=part):
                left = left_buf[step % 2, pl.ds(pl.multiple_of(j * TOKEN_STEP, TOKEN_STEP), TOKEN_STEP), :]
                right = right_buf[pl.ds(pl.multiple_of(part * TOKENS_AT_ONCE + j * TOKEN_STEP, TOKEN_STEP), TOKEN_STEP), :]
                total[...] += dot_tn(left, right)

        if group > 0:
            for copy in stores(group - 1):
                copy.wait()
        out_buf[...] = total[...].astype(BF16)
        for copy in stores(group):
            copy.start()
        yield
    for copy in stores(groups - 1):
        copy.wait()


def cut_columns(*refs):
    count = (len(refs) - 2) // 2
    sources, targets, (room, sems) = refs[:count], refs[count : 2 * count], refs[2 * count :]

    def inward(n):
        columns = targets[n].shape[1]
        taken = pl.ds(pl.multiple_of(lax.axis_index("ctx") * columns, columns), columns)
        return pltpu.make_async_copy(sources[n].at[:, taken], room.at[n], sems.at[0, n])

    def outward(n):
        return pltpu.make_async_copy(room.at[n], targets[n], sems.at[1, n])

    for n in range(count):
        inward(n).start()
    yield
    for n in range(count):
        inward(n).wait()
        outward(n).start()
    yield
    for n in range(count):
        outward(n).wait()


def row_product(turned, left_ref, right_ref, out_ref, left_buf, right_buf, out_buf, sems):
    groups = left_ref.shape[0] // LEFT_AT_ONCE

    def rows(group):
        return pl.ds(group * LEFT_AT_ONCE, LEFT_AT_ONCE)

    def load(group):
        return pltpu.make_async_copy(left_ref.at[rows(group)], left_buf.at[group % 2], sems.at[group % 2])

    def store(group):
        return pltpu.make_async_copy(out_buf.at[group % 2], out_ref.at[rows(group)], sems.at[3 + group % 2])

    whole = pltpu.make_async_copy(right_ref, right_buf, sems.at[2])
    whole.start()
    load(0).start()
    yield
    whole.wait()
    for group in range(groups):
        load(group).wait()
        if group + 1 < groups:
            load(group + 1).start()
        if group > 1:
            store(group - 2).wait()

        @pl.loop(0, out_ref.shape[1] // ROW_STEP)
        def _(j, group=group):
            columns = pl.ds(pl.multiple_of(j * ROW_STEP, ROW_STEP), ROW_STEP)
            if turned:
                part = dot_t(left_buf[group % 2], right_buf[columns, :])
            else:
                part = dot_n(left_buf[group % 2], right_buf[:, columns])
            out_buf[group % 2, :, columns] = part.astype(BF16)

        store(group).start()
        yield
    for group in range(max(0, groups - 2), groups):
        store(group).wait()


def row_product_buffers(right, turned):
    return [
        pltpu.VMEM((2, LEFT_AT_ONCE, right.shape[1 if turned else 0]), BF16),
        pltpu.VMEM(right.shape, BF16),
        pltpu.VMEM((2, LEFT_AT_ONCE, right.shape[0 if turned else 1]), BF16),
        pltpu.SemaphoreType.DMA((5,)),
    ]


def gather_kernel(works, counts, paces, *refs):
    def take(count):
        nonlocal refs
        taken, refs = refs[:count], refs[count:]
        return taken

    (own_ref,) = take(1)
    inputs = [take(count[0]) for count in counts]
    (all_ref,) = take(1)
    outputs = [take(count[1]) for count in counts]
    gather = PlaneGather(own_ref, all_ref, *take(3))
    buffers, held = [], {}
    for work, count in zip(works, counts):
        if work not in held:
            held[work] = take(count[2])
        buffers.append(held[work])

    def all_work():
        started = [work(*given, *wanted, *room) for work, given, wanted, room in zip(works, inputs, outputs, buffers)]
        for one in started:
            next(one)
        for one in started:
            yield from one

    going = all_work()

    def some(count):
        for _ in range(count):
            next(going, None)

    gather.start()
    some(paces[0])
    gather.first()
    some(paces[1])
    gather.second()
    finish(going)
    gather.finish()


def plane_gather(rows, collective_id=0, jobs=(), paces=(0, 0)):
    count, width = rows.shape
    hbm = pl.BlockSpec(memory_space=pl.ANY)
    scratch, held = gather_sems(), set()
    for work, _, _, _, _, buffers in jobs:
        if work not in held:
            held.add(work)
            scratch += buffers
    return pl.pallas_call(
        functools.partial(
            gather_kernel,
            [job[0] for job in jobs],
            [(len(job[1]), len(job[3]), len(job[5])) for job in jobs],
            paces,
        ),
        in_specs=[hbm] + [spec for job in jobs for spec in job[2]],
        out_specs=[hbm] + [spec for job in jobs for spec in job[4]],
        out_shape=[jax.ShapeDtypeStruct((8 * count, width), rows.dtype)] + [out for job in jobs for out in job[3]],
        scratch_shapes=scratch,
        compiler_params=pltpu.CompilerParams(
            collective_id=collective_id, has_side_effects=True, vmem_limit_bytes=(60 << 20) if jobs else None
        ),
        cost_estimate=small_cost(),
        name="plane_gather",
    )(rows, *[value for job in jobs for value in job[1]])


HBM = pl.BlockSpec(memory_space=pl.ANY)
VMEM = pl.BlockSpec(memory_space=pltpu.VMEM)
ROWS_TURNED = functools.partial(row_product, True)
ROWS_STRAIGHT = functools.partial(row_product, False)


def token_job(left, right):
    out = jax.ShapeDtypeStruct((left.shape[1], right.shape[1]), BF16)
    return token_product, [left, right], [HBM] * 2, [out], [HBM], product_buffers(right.shape[1])


def pair_job(left, first, second):
    columns = first.shape[1]
    out = jax.ShapeDtypeStruct((left.shape[1], columns), BF16)
    room = [
        pltpu.VMEM((2, TOKENS_AT_ONCE, LEFT_AT_ONCE), BF16),
        pltpu.VMEM((left.shape[0], 2 * columns), BF16),
        pltpu.VMEM((LEFT_AT_ONCE, 2 * columns), F32),
        pltpu.VMEM((LEFT_AT_ONCE, 2 * columns), BF16),
        pltpu.SemaphoreType.DMA((6,)),
    ]
    return pair_product, [left, first, second], [HBM] * 3, [out] * 2, [HBM] * 2, room


def cut_job(weights, parts):
    outs = [jax.ShapeDtypeStruct((w.shape[0], w.shape[1] // parts), w.dtype) for w in weights]
    room = [pltpu.VMEM((len(weights),) + outs[0].shape, BF16), pltpu.SemaphoreType.DMA((2, len(weights)))]
    return cut_columns, list(weights), [HBM] * len(weights), outs, [HBM] * len(weights), room


def row_job(left, right, turned):
    out = jax.ShapeDtypeStruct((left.shape[0], right.shape[0 if turned else 1]), BF16)
    work = ROWS_TURNED if turned else ROWS_STRAIGHT
    return work, [left, right], [HBM] * 2, [out], [HBM], row_product_buffers(right, turned)


def table_job(lengths, parents, tokens):
    outs = [jax.ShapeDtypeStruct((8, tokens), jnp.int32), jax.ShapeDtypeStruct((tokens, 128), jnp.int32)]
    outs += [jax.ShapeDtypeStruct((tokens, 128), F32)] * 2
    room = [pltpu.VMEM(out.shape, out.dtype) for out in outs[1:]]
    room += [pltpu.SemaphoreType.DMA((3, tokens // TABLE_ROWS))]
    return table_work, [lengths, parents, rope_freqs(128)], [VMEM] * 3, outs, [VMEM, HBM, HBM, HBM], room


def scatter_kernel(rows, offsets, jobs, *refs):
    parts = len(offsets)

    def take(count):
        nonlocal refs
        taken, refs = refs[:count], refs[count:]
        return taken

    a_refs, w_homes, lefts, rights = take(parts), take(parts), take(jobs), take(jobs)
    (out_ref,), products = take(1), take(jobs)
    core_out, core_in, first_in, next_in, sems = take(5)
    a_bufs, w_refs, (a_sems, w_sems), buffers = take(parts), take(parts), take(2), refs

    def work(job):
        if job < jobs:
            finish(token_product(lefts[job], rights[job], products[job], *buffers))

    x, core, row = plane_place()
    over_x, over_row, over_core = plane_neighbours(x, core, row)
    half = rows // 2
    width = out_ref.shape[1]
    chunks = width // COLS

    def place(piece, on_core):
        far_x, far_row, part = PIECES[piece]
        bx = x + far_x - 2 * far_x * x
        by = row + far_row - 2 * far_row * row
        return pl.ds(pl.multiple_of(((bx * 2 + on_core) * 2 + by) * rows + part * half, half), half)

    def columns(j):
        return pl.ds(pl.multiple_of(j * COLS, COLS), COLS)

    steps = [(0, True)]
    for piece in range(8):
        steps += [(piece + 1, True)] * (piece < 7) + [(piece, False)]

    def load(step):
        piece, partner_half = steps[step]
        taken = place(piece, 1 - core if partner_half else core)
        return [
            pltpu.make_async_copy(a_ref.at[taken], a_buf.at[step % 2], a_sems.at[step % 2, p])
            for p, (a_ref, a_buf) in enumerate(zip(a_refs, a_bufs))
        ]

    w_copies = [
        pltpu.make_async_copy(home.at[:, pl.ds(offset, w_ref.shape[1])], w_ref, w_sems.at[p])
        for p, (home, offset, w_ref) in enumerate(zip(w_homes, offsets, w_refs))
    ]
    loads = {0: load(0)}
    for copy in w_copies + loads[0]:
        copy.start()
    enter_plane((over_x, over_row, over_core))
    for copy in w_copies:
        copy.wait()

    def partial(slot, j):
        total = None
        for a_buf, w_ref in zip(a_bufs, w_refs):
            term = dot_t(a_buf[slot], w_ref[columns(j), :])
            total = term if total is None else total + term
        return total

    def remote(source, target, slot, device):
        return pltpu.make_async_remote_copy(
            src_ref=source, dst_ref=target, send_sem=sems.at[0, slot], recv_sem=sems.at[1, slot],
            device_id=device, device_id_type=MESH,
        )

    core_copies, first_copies, next_copies = [], [], []
    for step, (piece, partner_half) in enumerate(steps):
        for copy in loads[step]:
            copy.wait()
        if step + 1 < len(steps):
            loads[step + 1] = load(step + 1)
            for copy in loads[step + 1]:
                copy.start()
        if partner_half:

            @pl.loop(0, chunks)
            def _(j, step=step, piece=piece):
                core_out[piece, :, columns(j)] = partial(step % 2, j).astype(BF16)

            core_copies.append(remote(core_out.at[piece], core_in.at[piece], piece, over_core))
            core_copies[-1].start()
            continue
        core_copies[piece].wait_recv()

        @pl.loop(0, chunks)
        def _(j, step=step, piece=piece):
            total = partial(step % 2, j) + core_in[piece, :, columns(j)].astype(F32)
            core_in[piece, :, columns(j)] = total.astype(BF16)

        if piece < 4:
            first_copies.append(
                remote(core_in.at[piece], first_in.at[piece], 8 + piece, over_x if piece % 2 == 0 else over_row)
            )
            first_copies[-1].start()
    for part in range(2):
        first_copies[part].wait_recv()

        @pl.loop(0, chunks)
        def _(j, part=part):
            total = core_in[4 + part, :, columns(j)].astype(F32) + first_in[part, :, columns(j)].astype(F32)
            core_in[4 + part, :, columns(j)] = total.astype(BF16)

        next_copies.append(remote(core_in.at[4 + part], next_in.at[part], 12 + part, over_row if part == 0 else over_x))
        next_copies[-1].start()
    for job in range(jobs):
        work(job)
    for part in range(2):
        first_copies[2 + part].wait_recv()
        next_copies[part].wait_recv()

        @pl.loop(0, chunks)
        def _(j, part=part):
            total = core_in[6 + part, :, columns(j)].astype(F32) + first_in[2 + part, :, columns(j)].astype(F32)
            out_ref[pl.ds(part * half, half), columns(j)] = total + next_in[part, :, columns(j)].astype(F32)

    for copy in core_copies + first_copies + next_copies:
        copy.wait_send()


def plane_scatter(parts, weights, collective_id, jobs=(), offsets=None):
    count = parts[0].shape[0]
    width = weights[0].shape[0]
    rows = count // 8
    half = rows // 2
    vmem, hbm = pl.BlockSpec(memory_space=pltpu.VMEM), pl.BlockSpec(memory_space=pl.ANY)
    offsets = offsets or [0] * len(parts)
    lefts, rights = [left for left, _ in jobs], [right for _, right in jobs]
    return pl.pallas_call(
        functools.partial(scatter_kernel, rows, offsets, len(jobs)),
        in_specs=[hbm] * (2 * len(parts) + 2 * len(jobs)),
        out_specs=[vmem] + [hbm] * len(jobs),
        out_shape=[jax.ShapeDtypeStruct((rows, width), F32)]
        + [jax.ShapeDtypeStruct((left.shape[1], right.shape[1]), BF16) for left, right in jobs],
        scratch_shapes=[
            pltpu.VMEM((8, half, width), BF16),
            pltpu.VMEM((8, half, width), BF16),
            pltpu.VMEM((4, half, width), BF16),
            pltpu.VMEM((2, half, width), BF16),
            pltpu.SemaphoreType.DMA((2, 14)),
        ]
        + [pltpu.VMEM((2, half, a.shape[1]), BF16) for a in parts]
        + [pltpu.VMEM((width, a.shape[1]), BF16) for a in parts]
        + [pltpu.SemaphoreType.DMA((2, len(parts))), pltpu.SemaphoreType.DMA((len(parts),))]
        + (product_buffers(rights[0].shape[1]) if jobs else []),
        compiler_params=pltpu.CompilerParams(
            collective_id=collective_id, has_side_effects=True, vmem_limit_bytes=60 << 20
        ),
        cost_estimate=small_cost(),
        name="plane_scatter",
    )(*parts, *weights, *lefts, *rights)


def gated_kernel(x_ref, grad_ref, gate_ref, up_ref, hidden_ref, gate_grad_ref, up_grad_ref):
    columns = gate_ref.shape[1]
    step = min(512, columns)
    together = min(2, columns // step)

    @pl.loop(0, columns // (step * together))
    def _(j):
        for part in range(together):
            taken = pl.ds(pl.multiple_of((j * together + part) * step, step), step)
            gate = dot_n(x_ref[...], gate_ref[:, taken])
            up = dot_n(x_ref[...], up_ref[:, taken])
            grad = grad_ref[:, taken].astype(F32)
            sigmoid = jax.nn.sigmoid(gate)
            silu = gate * sigmoid
            hidden_ref[:, taken] = (silu * up).astype(BF16)
            gate_grad_ref[:, taken] = (grad * up * (sigmoid + silu * (1.0 - sigmoid))).astype(BF16)
            up_grad_ref[:, taken] = (grad * silu).astype(BF16)


def gated_rows(x, hidden_grad, w_gate, w_up):
    tokens, depth = x.shape
    columns = w_gate.shape[1]
    block = 256
    rows = pl.BlockSpec((block, columns), lambda i: (i, 0))
    weight = pl.BlockSpec((depth, columns), lambda i: (0, 0), pipeline_mode=pl.Buffered(1))
    out = jax.ShapeDtypeStruct((tokens, columns), BF16)
    return pl.pallas_call(
        gated_kernel,
        grid=(tokens // block,),
        in_specs=[pl.BlockSpec((block, depth), lambda i: (i, 0)), rows, weight, weight],
        out_specs=[rows] * 3,
        out_shape=[out] * 3,
        compiler_params=pltpu.CompilerParams(vmem_limit_bytes=60 << 20),
        cost_estimate=small_cost(),
        name="gated_rows",
    )(x, hidden_grad, w_gate, w_up)


def heads_kernel(x_ref, w_ref, out_ref, heads_ref, grad_ref, total):
    i = pl.program_id(0)

    @pl.when(i == 0)
    def _():
        total[...] = jnp.zeros_like(total)

    heads_ref[...] = dot_n(x_ref[...], w_ref[...]).astype(BF16)
    total[...] += dot_tn(out_ref[...], x_ref[...])

    @pl.when(i == pl.num_programs(0) - 1)
    def _():
        grad_ref[...] = jnp.transpose(total[...]).astype(BF16)


def heads_and_output_grad(mid, w_attn, attn_out):
    tokens, depth = mid.shape
    width = attn_out.shape[1]
    if width % 128:
        return dot_n(mid, w_attn[:, 3 * width :]).astype(BF16), dot_tn(mid, attn_out).astype(BF16)
    block = 1024
    rows = pl.BlockSpec((block, width), lambda i: (i, 0))
    return pl.pallas_call(
        heads_kernel,
        grid=(tokens // block,),
        in_specs=[pl.BlockSpec((block, depth), lambda i: (i, 0)), pl.BlockSpec((depth, width), lambda i: (0, 3)), rows],
        out_specs=[rows, pl.BlockSpec((depth, width), lambda i: (0, 0))],
        out_shape=[jax.ShapeDtypeStruct((tokens, width), BF16), jax.ShapeDtypeStruct((depth, width), BF16)],
        scratch_shapes=[pltpu.VMEM((width, depth), F32)],
        compiler_params=pltpu.CompilerParams(vmem_limit_bytes=60 << 20),
        cost_estimate=small_cost(),
        name="heads_and_output_grad",
    )(mid, w_attn, attn_out)


def weight_grads_kernel(x_ref, pre_ref, output_ref, grad_ref, total):
    i = pl.program_id(0)
    width = pre_ref.shape[1]

    @pl.when(i == 0)
    def _():
        total[...] = jnp.zeros_like(total)

    total[...] += dot_tn(x_ref[...], pre_ref[...])

    @pl.when(i == pl.num_programs(0) - 1)
    def _():
        grad_ref[:, :width] = total[...].astype(BF16)
        grad_ref[:, width:] = output_ref[...]


def attention_weight_grads(attn_in, pre_grads, output_grad):
    tokens, depth = attn_in.shape
    width, last = pre_grads.shape[1], output_grad.shape[1]
    if width % 128 or last % 128:
        return jnp.concatenate([dot_tn(attn_in, pre_grads).astype(BF16), output_grad], axis=1)
    block = 1024
    return pl.pallas_call(
        weight_grads_kernel,
        grid=(tokens // block,),
        in_specs=[
            pl.BlockSpec((block, depth), lambda i: (i, 0)),
            pl.BlockSpec((block, width), lambda i: (i, 0)),
            pl.BlockSpec((depth, last), lambda i: (0, 0)),
        ],
        out_specs=pl.BlockSpec((depth, width + last), lambda i: (0, 0)),
        out_shape=jax.ShapeDtypeStruct((depth, width + last), BF16),
        scratch_shapes=[pltpu.VMEM((depth, width), F32)],
        compiler_params=pltpu.CompilerParams(vmem_limit_bytes=60 << 20),
        cost_estimate=small_cost(),
        name="attention_weight_grads",
    )(attn_in, pre_grads, output_grad)


def is_plane():
    return lax.axis_size("ctx") == 4 and lax.axis_size("tensor") == 2


def gather_rows(rows):
    return lax.all_gather(rows, GROUP, axis=0, tiled=True)


def scatter_rows(rows):
    return lax.psum_scatter(rows.astype(BF16), GROUP, scatter_dimension=0, tiled=True).astype(F32)


def gather_now(rows):
    return plane_gather(rows)[0] if is_plane() else gather_rows(rows)


def cut(weight):
    columns = weight.shape[1] // lax.axis_size("ctx")
    return lax.dynamic_slice_in_dim(weight, lax.axis_index("ctx") * columns, columns, 1)


def gather_with_tables(rows, lengths, parents, tokens, width, weights):
    if is_plane():
        jobs = [cut_job(weights, lax.axis_size("ctx")), table_job(lengths, parents, tokens)]
        got = plane_gather(rows, 8, jobs, (4, 4))
        return got[:1] + got[1 + len(weights) :], got[1 : 1 + len(weights)]
    segment, parent, depth = tree_tables(lengths[0], parents[0], tokens)
    return [gather_rows(rows), *lay_out(segment, parent), *rope_tables(depth, width)], [cut(w) for w in weights]


def gather_with_product(rows, left, right):
    if is_plane():
        return plane_gather(rows, 5, [row_job(left, right, False)], (4, 4))
    return gather_rows(rows), dot_n(left, right).astype(BF16)


def gather_with_three(rows, left, right, shared, first, second):
    if is_plane():
        return plane_gather(rows, 4, [row_job(left, right, True), pair_job(shared, first, second)], (8, 3))
    products = dot_t(left, right), dot_tn(shared, first), dot_tn(shared, second)
    return [gather_rows(rows)] + [product.astype(BF16) for product in products]


def product_scatter(parts, weights, collective_id, jobs=(), offsets=None):
    if is_plane():
        return plane_scatter(parts, weights, collective_id, jobs, offsets)
    offsets = offsets or [0] * len(parts)
    weights = [w[:, first : first + part.shape[1]] for part, w, first in zip(parts, weights, offsets)]
    rows = scatter_rows(dot_t(jnp.concatenate(parts, axis=1), jnp.concatenate(weights, axis=1)))
    return [rows] + [dot_tn(left, right).astype(BF16) for left, right in jobs]


def gather_weight(own):
    return lax.all_gather(own, "fsdp", axis=0, tiled=True)


def scatter_weight(grad):
    return lax.psum_scatter(grad.astype(BF16), "fsdp", scatter_dimension=0, tiled=True)


def swap_rows(part):
    size = lax.axis_size("ctx")
    return lax.all_to_all(part.reshape(size, part.shape[0] // size, -1), "ctx", split_axis=0, concat_axis=0)


def lay_side_by_side(got, count):
    columns = got.shape[2] // count
    return [
        jnp.concatenate([got[j, :, c * columns : (c + 1) * columns] for j in range(got.shape[0])], axis=1).astype(F32)
        for c in range(count)
    ]


def normalize(rows):
    norm_inv = lax.rsqrt(jnp.mean(rows * rows, axis=1, keepdims=True) + EPSILON)
    return (rows * norm_inv, norm_inv)


def norm_backward(grad_rows, scaled, norm_inv, gain):
    weighted = grad_rows * gain[None, :]
    inner = jnp.mean(weighted * scaled, axis=1, keepdims=True)
    return norm_inv * (weighted - scaled * inner)


def body(
    tokens_in,
    attn_gain,
    query_weight,
    key_weight,
    value_weight,
    output_weight,
    mlp_gain,
    gate_weight,
    up_weight,
    down_weight,
    seg_lengths,
    leaf_parent,
    cotangent,
):
    ctx = lax.axis_index("ctx")
    parts = lax.axis_size("ctx")
    tree_len = tokens_in.shape[0] * parts * lax.axis_size("tensor")
    width = query_weight.shape[1] // parts
    units = gate_weight.shape[1] // parts

    def mine(weight, columns):
        return lax.dynamic_slice_in_dim(weight, ctx * columns, columns, 1)

    x_rows = tokens_in.astype(F32)
    attn_scaled, attn_inv = normalize(x_rows)
    w_attn = gather_weight(
        jnp.concatenate([mine(w, width) for w in (query_weight, key_weight, value_weight, output_weight)], axis=1)
    )
    (attn_in, rows_table, cols_table, cosine, sine), cuts = gather_with_tables(
        (attn_scaled * attn_gain[None, :]).astype(BF16),
        seg_lengths,
        leaf_parent,
        tree_len,
        min(2 * HEAD_DIM, width),
        [gate_weight, down_weight, up_weight],
    )
    w_gate, w_down, w_up = [gather_weight(own) for own in cuts]
    w_qkv = w_attn[:, : 3 * width]

    qkv = jnp.dot(attn_in, w_qkv, preferred_element_type=F32)
    if is_plane():
        attn_out, lse, query_rows, key_rows, value_rows, cot_all = attention_forward(
            qkv, cosine, sine, rows_table, cols_table, width, cotangent
        )
    else:
        attn_out, lse, query_rows, key_rows, value_rows = attention_forward(
            qkv, cosine, sine, rows_table, cols_table, width
        )
        cot_all = gather_rows(cotangent)
    mid_rows = x_rows + product_scatter([attn_out], [w_attn], 1, (), [3 * width])[0]
    mlp_scaled, mlp_inv = normalize(mid_rows)
    mlp_own = (mlp_scaled * mlp_gain[None, :]).astype(BF16)
    mlp_in, hidden_grad = gather_with_product(mlp_own, cot_all, w_down)
    hidden, gate_rows_grad, up_rows_grad = gated_rows(mlp_in, hidden_grad, w_gate, w_up)

    mlp_in_grad, down_part = product_scatter(
        [gate_rows_grad, up_rows_grad], [w_gate, w_up], 3, [(cot_all, hidden)]
    )
    down_grad = scatter_weight(down_part)
    mid_grad = cotangent.astype(F32) + norm_backward(mlp_in_grad, mlp_scaled, mlp_inv, mlp_gain)
    mid_all, down_rows, up_part, gate_part = gather_with_three(
        mid_grad.astype(BF16), hidden, w_down, mlp_in, up_rows_grad, gate_rows_grad
    )
    up_grad = scatter_weight(up_part)
    gate_grad = scatter_weight(gate_part)

    out_heads_grad, output_grad = heads_and_output_grad(mid_all, w_attn, attn_out)
    out_heads_grad, down_grad = lax.optimization_barrier((out_heads_grad, down_grad))
    if is_plane():
        pre_grads, down_rows = attention_backward(
            query_rows, key_rows, value_rows, attn_out, out_heads_grad, lse, cosine, sine, rows_table, cols_table, down_rows
        )
    else:
        pre_grads = attention_backward(
            query_rows, key_rows, value_rows, attn_out, out_heads_grad, lse, cosine, sine, rows_table, cols_table
        )
        pre_grads = jnp.concatenate(pre_grads, axis=1)
        down_rows = scatter_rows(down_rows)
    block_out = (mid_rows + down_rows.astype(F32)).astype(BF16)
    pre_grads, up_grad, down_swapped = lax.optimization_barrier((pre_grads, up_grad, swap_rows(down_grad)))
    up_swapped = swap_rows(up_grad)
    attn_part = attention_weight_grads(attn_in, pre_grads, output_grad)
    pre_grads, attn_part, up_swapped, gate_grad = lax.optimization_barrier(
        (pre_grads, attn_part, up_swapped, gate_grad)
    )
    gate_swapped = swap_rows(gate_grad)
    attn_grad = scatter_weight(attn_part)
    (attn_in_grad,) = product_scatter([pre_grads], [w_attn], 2)
    attn_in_grad, attn_grad = lax.optimization_barrier((attn_in_grad, attn_grad))
    (gate_out,), (up_out,), (down_out,) = [lay_side_by_side(got, 1) for got in (gate_swapped, up_swapped, down_swapped)]
    query_out, key_out, value_out, output_out = lay_side_by_side(swap_rows(attn_grad), 4)

    def gain_part(pairs, gain):
        held = query_out.shape[0]
        total = sum(
            jnp.sum(lax.dynamic_slice_in_dim(weight, ctx * held, held, 0).astype(F32) * grad, axis=1)
            for weight, grad in pairs
        )
        first = (lax.axis_index("fsdp") * parts + ctx) * held
        return total / lax.dynamic_slice_in_dim(gain, first, held, 0)

    sums = jnp.stack(
        [
            gain_part([(query_weight, query_out), (key_weight, key_out), (value_weight, value_out)], attn_gain),
            gain_part([(gate_weight, gate_out), (up_weight, up_out)], mlp_gain),
        ]
    )
    row, others = lax.axis_index("tensor"), lax.axis_size("tensor")
    kept = sums.shape[1] // others
    if others == 2:
        got = lax.ppermute(lax.dynamic_slice_in_dim(sums, (1 - row) * kept, kept, 1), "tensor", [(0, 1), (1, 0)])
        gain_grads = lax.dynamic_slice_in_dim(sums, row * kept, kept, 1) + got
    else:
        gain_grads = lax.dynamic_slice_in_dim(lax.psum(sums, "tensor"), row * kept, kept, 1)

    attn_back = norm_backward(attn_in_grad, attn_scaled, attn_inv, attn_gain)
    input_grad = (mid_grad + attn_back).astype(BF16)
    return (
        block_out,
        input_grad,
        gain_grads[0],
        query_out,
        key_out,
        value_out,
        output_out,
        gain_grads[1],
        gate_out,
        up_out,
        down_out,
    )


def solution(mesh):
    rows = P(("fsdp", "ctx", "tensor"), None)
    weight = P("fsdp", "tensor")
    gain = P(("fsdp", "ctx", "tensor"))
    grad = P(("fsdp", "ctx"), "tensor")
    in_specs = (
        rows, P(), weight, weight, weight, weight, P(), weight, weight, weight, P("fsdp", None), P("fsdp", None), rows,
    )
    out_specs = (rows, rows, gain, grad, grad, grad, grad, gain, grad, grad, grad)
    return jax.shard_map(body, mesh=mesh, in_specs=in_specs, out_specs=out_specs, check_vma=False)
```

```python
import functools

import jax
import jax.numpy as jnp
import numpy as np
from jax import lax
from jax.experimental import pallas as pl
from jax.experimental.pallas import tpu as pltpu
from jax.sharding import PartitionSpec as P

HEAD_DIM = 64
TRUNK = 2176
MOST_SEG = 128
ROPE_BASE = 130000.0
EPSILON = 1e-05
NEG_LARGE = -1e30
SCALE = HEAD_DIM ** (-0.5)

BQ = 512
BK = 512
GROUP = ("ctx", "tensor")

F32 = jnp.float32
BF16 = jnp.bfloat16


def pick_table(onehot, table):
    return jnp.sum(jnp.where(onehot, table[None, :], 0), axis=1)


def tree_tables(lengths_row, parent_row, tree_len):
    branches = lengths_row.shape[0] - parent_row.shape[0]
    ends = TRUNK + jnp.cumsum(lengths_row)
    starts = ends - lengths_row
    matches = parent_row[:, None] - 1 == jnp.arange(branches, dtype=jnp.int32)[None, :]
    parent_len = jnp.sum(jnp.where(matches, lengths_row[None, :branches], 0), axis=1)
    zero_one = jnp.zeros((1,), jnp.int32)
    seg_start = jnp.concatenate([zero_one, starts])
    seg_base = jnp.concatenate(
        [zero_one, jnp.full((branches,), TRUNK, jnp.int32), TRUNK + parent_len]
    )
    seg_parent = jnp.concatenate([zero_one, jnp.zeros((branches,), jnp.int32), parent_row])
    positions = jnp.arange(tree_len, dtype=jnp.int32)
    above = jnp.sum((ends[None, :] <= positions[:, None]).astype(jnp.int32), axis=1)
    segment = (positions >= TRUNK).astype(jnp.int32) + above
    onehot = segment[:, None] == jnp.arange(seg_start.shape[0], dtype=jnp.int32)[None, :]
    depth = positions - pick_table(onehot, seg_start) + pick_table(onehot, seg_base)
    parent = pick_table(onehot, seg_parent)
    return (segment, parent, depth)


def rope_freqs(width):
    half = HEAD_DIM // 2
    powers = -2.0 * (np.arange(width) % half) / HEAD_DIM
    return np.power(ROPE_BASE, powers).astype(np.float32)[None, :]


def rope_tables(depth, width):
    angles = depth.astype(F32)[:, None] * rope_freqs(width)
    sign = np.where(np.arange(width) % HEAD_DIM < HEAD_DIM // 2, -1.0, 1.0).astype(np.float32)
    return jnp.cos(angles), jnp.sin(angles) * sign[None, :]


def lay_out(segment, parent):
    both = jnp.stack([segment, parent])
    return jnp.pad(both, ((0, 6), (0, 0))), jnp.pad(both.T, ((0, 0), (0, 126)))


TABLE_ROWS = 512
TABLE_STEP = 64


def tables_at(positions, lengths, parents):
    leaves = parents.shape[1]
    branches = lengths.shape[1] - leaves
    zero = jnp.zeros_like(positions)
    segment = jnp.where(positions >= TRUNK, 1, 0)
    parent, depth = zero, positions
    end = jnp.full((1, 1), TRUNK, jnp.int32)
    starts = []
    for s in range(branches + leaves):
        start, end = end, end + lengths[:, s : s + 1]
        inside = (positions >= start) & (positions < end)
        base, above = jnp.full((1, 1), TRUNK, jnp.int32), jnp.zeros((1, 1), jnp.int32)
        if s >= branches:
            above = parents[:, s - branches : s - branches + 1]
            for b in range(branches):
                base = base + jnp.where(above == b + 1, lengths[:, b : b + 1], 0)
        segment = segment + jnp.where(positions >= end, 1, 0)
        parent = jnp.where(inside, above, parent)
        depth = jnp.where(inside, positions - start + base, depth)
    return segment, parent, depth


def sine_cosine(x):
    turns = jnp.floor(x * np.float32(2.0 / np.pi) + 0.5)
    r = x - turns * np.float32(1.5703125)
    r = r - turns * np.float32(4.837512969970703125e-4)
    r = r - turns * np.float32(7.549789954891882e-8)
    z = r * r
    sine = ((np.float32(-1.9515295891e-4) * z + np.float32(8.3321608736e-3)) * z - np.float32(1.6666654611e-1)) * z * r + r
    cosine = (
        (np.float32(2.443315711809948e-5) * z - np.float32(1.388731625493765e-3)) * z + np.float32(4.166664568298827e-2)
    ) * z * z - np.float32(0.5) * z + np.float32(1.0)
    quarter = turns.astype(jnp.int32) & 3
    odd = (quarter & 1) == 1
    first, second = jnp.where(odd, cosine, sine), jnp.where(odd, sine, cosine)
    return jnp.where(quarter >= 2, -first, first), jnp.where((quarter == 1) | (quarter == 2), -second, second)


def table_work(lengths, parents, freqs, rows_ref, cols_ref, cos_ref, sin_ref, cols_buf, cos_buf, sin_buf, sems):
    yield
    tokens = cos_ref.shape[0]
    shape = (8, tokens)
    segment, parent, _ = tables_at(lax.broadcasted_iota(jnp.int32, shape, 1), lengths, parents)
    line = lax.broadcasted_iota(jnp.int32, shape, 0)
    rows_ref[...] = jnp.where(line == 0, segment, jnp.where(line == 1, parent, 0))
    copies = []
    for chunk in range(tokens // TABLE_ROWS):
        rows = pl.ds(chunk * TABLE_ROWS, TABLE_ROWS)

        @pl.loop(0, TABLE_ROWS // TABLE_STEP)
        def _(j, chunk=chunk):
            first = pl.multiple_of(chunk * TABLE_ROWS + j * TABLE_STEP, TABLE_STEP)
            taken = pl.ds(first, TABLE_STEP)
            shape = (TABLE_STEP, 128)
            lane = lax.broadcasted_iota(jnp.int32, shape, 1)
            segment, parent, depth = tables_at(lax.broadcasted_iota(jnp.int32, shape, 0) + first, lengths, parents)
            cols_buf[taken, :] = jnp.where(lane == 0, segment, jnp.where(lane == 1, parent, 0))
            sine, cosine = sine_cosine(depth.astype(F32) * freqs[...])
            cos_buf[taken, :] = cosine
            sin_buf[taken, :] = jnp.where(lane % HEAD_DIM < HEAD_DIM // 2, -sine, sine)

        for kind, (source, target) in enumerate(((cols_buf, cols_ref), (cos_buf, cos_ref), (sin_buf, sin_ref))):
            copies.append(pltpu.make_async_copy(source.at[rows], target.at[rows], sems.at[kind, chunk]))
            copies[-1].start()
        yield
    for copy in copies:
        copy.wait()


MESH = pl.DeviceIdType.MESH


def plane_place():
    ctx, row = lax.axis_index("ctx"), lax.axis_index("tensor")
    x, core = ctx // 2, ctx % 2
    return x, core, row


def plane_neighbours(x, core, row):
    over_x = {"ctx": (1 - x) * 2 + core}
    over_core = {"ctx": x * 2 + 1 - core}
    over_row = {"tensor": 1 - row}
    return over_x, over_row, over_core


def enter_plane(neighbours):
    barrier = pltpu.get_barrier_semaphore()
    for device in neighbours:
        pl.semaphore_signal(barrier, inc=1, device_id=device, device_id_type=MESH)
    pl.semaphore_wait(barrier, 3)


PIECES = ((1, 1, 0), (1, 1, 1), (1, 0, 0), (0, 1, 1), (0, 1, 0), (1, 0, 1), (0, 0, 0), (0, 0, 1))
COLS = 512


class PlaneGather:
    def __init__(self, own_ref, all_ref, local_sem, send_sem, recv_sem):
        self.own_ref, self.all_ref, self.sems = own_ref, all_ref, (local_sem, send_sem, recv_sem)
        self.x, self.core, self.row = plane_place()
        self.devices = plane_neighbours(self.x, self.core, self.row)
        self.rows = own_ref.shape[0]

    def place(self, far_x, far_row, part):
        bx = self.x + far_x - 2 * far_x * self.x
        by = self.row + far_row - 2 * far_row * self.row
        half = self.rows // 2
        return pl.ds(pl.multiple_of(((bx * 2 + self.core) * 2 + by) * self.rows + part * half, half), half)

    def copy(self, slot):
        far_x, far_row, part, device = (
            (0, 0, 0, 1), (0, 0, 1, 1), (1, 0, 1, 1), (0, 0, 1, 0), (0, 0, 0, 0), (0, 1, 0, 0), (0, 0, 0, 2),
            (0, 0, 1, 2), (0, 1, 0, 2), (1, 0, 1, 2), (0, 1, 1, 2), (1, 0, 0, 2), (1, 1, 0, 2), (1, 1, 1, 2),
        )[slot]
        half = self.rows // 2
        target = self.place(far_x, far_row, part)
        own = far_x == 0 and far_row == 0
        source = self.own_ref.at[pl.ds(part * half, half)] if own else self.all_ref.at[target]
        return pltpu.make_async_remote_copy(
            src_ref=source, dst_ref=self.all_ref.at[target], send_sem=self.sems[1].at[slot],
            recv_sem=self.sems[2].at[slot], device_id=self.devices[device], device_id_type=MESH,
        )

    def local(self, part):
        half = self.rows // 2
        return pltpu.make_async_copy(
            self.own_ref.at[pl.ds(part * half, half)], self.all_ref.at[self.place(0, 0, part)], self.sems[0].at[part]
        )

    def start(self):
        enter_plane(self.devices)
        for slot in (0, 3, 1, 4, 6, 7):
            self.copy(slot).start()
        for part in range(2):
            self.local(part).start()

    def forward(self, got, slots):
        self.copy(got).wait_recv()
        for slot in slots:
            self.copy(slot).start()

    def first(self):
        self.forward(0, (5, 8))
        self.forward(3, (2, 9))

    def second(self):
        self.forward(1, (10,))
        self.forward(4, (11,))

    def finish(self):
        self.forward(5, (12,))
        self.forward(2, (13,))
        for slot in range(6, 14):
            self.copy(slot).wait_recv()
        for slot in range(14):
            self.copy(slot).wait_send()
        for part in range(2):
            self.local(part).wait()


def gather_sems():
    return [pltpu.SemaphoreType.DMA((2,)), pltpu.SemaphoreType.DMA((14,)), pltpu.SemaphoreType.DMA((14,))]


class PlaneScatter:
    def __init__(self, part_ref, out_ref, core_in, first_in, next_in, own, total, sems, own_sems):
        self.part_ref, self.out_ref, self.core_in, self.first_in, self.next_in = part_ref, out_ref, core_in, first_in, next_in
        self.own, self.total, self.sems, self.own_sems = own, total, sems, own_sems
        self.x, self.core, self.row = plane_place()
        self.devices = plane_neighbours(self.x, self.core, self.row)
        self.rows = part_ref.shape[0] // 8

    def place(self, piece, on_core):
        far_x, far_row, part = PIECES[piece]
        bx = self.x + far_x - 2 * far_x * self.x
        by = self.row + far_row - 2 * far_row * self.row
        half = self.rows // 2
        return pl.ds(pl.multiple_of(((bx * 2 + on_core) * 2 + by) * self.rows + part * half, half), half)

    def copy(self, slot):
        if slot < 8:
            source, target, device = self.part_ref.at[self.place(slot, 1 - self.core)], self.core_in.at[slot], 2
        elif slot < 12:
            source, target, device = self.core_in.at[slot - 8], self.first_in.at[slot - 8], slot % 2
        else:
            source, target, device = self.core_in.at[slot - 8], self.next_in.at[slot - 12], 1 - slot % 2
        return pltpu.make_async_remote_copy(
            src_ref=source, dst_ref=target, send_sem=self.sems.at[0, slot], recv_sem=self.sems.at[1, slot],
            device_id=self.devices[device], device_id_type=MESH,
        )

    def load(self, piece):
        return pltpu.make_async_copy(
            self.part_ref.at[self.place(piece, self.core)], self.own.at[piece % 4], self.own_sems.at[piece % 4]
        )

    def add(self, target, where, *others):
        @pl.loop(0, target.shape[-1] // COLS)
        def _(j):
            columns = pl.ds(pl.multiple_of(j * COLS, COLS), COLS)
            total = sum(ref[slot, :, columns].astype(F32) for ref, slot in others)
            target[where, :, columns] = total.astype(target.dtype)

    def start(self):
        enter_plane(self.devices)
        for slot in range(8):
            self.copy(slot).start()
        for piece in range(4):
            self.load(piece).start()

    def first(self):
        for piece in range(4):
            self.load(piece).wait()
            self.copy(piece).wait_recv()
            self.add(self.core_in, piece, (self.own, piece), (self.core_in, piece))
            self.copy(8 + piece).start()
        for piece in range(4, 8):
            self.load(piece).start()

    def second(self):
        for piece in range(4, 8):
            self.load(piece).wait()
            self.copy(piece).wait_recv()
            self.add(self.core_in, piece, (self.own, piece - 4), (self.core_in, piece))

    def third(self):
        for part in range(2):
            self.copy(8 + part).wait_recv()
            self.add(self.core_in, 4 + part, (self.core_in, 4 + part), (self.first_in, part))
            self.copy(12 + part).start()

    def finish(self):
        half = self.rows // 2
        for part in range(2):
            self.copy(10 + part).wait_recv()
            self.copy(12 + part).wait_recv()
            self.add(self.total, part, (self.core_in, 6 + part), (self.first_in, 2 + part), (self.next_in, part))
        stores = [
            pltpu.make_async_copy(
                self.total.at[part], self.out_ref.at[pl.ds(part * half, half)], self.own_sems.at[part]
            )
            for part in range(2)
        ]
        for store in stores:
            store.start()
        for slot in range(14):
            self.copy(slot).wait_send()
        for store in stores:
            store.wait()


def scatter_scratch(rows, width):
    half = rows // 2
    return [
        pltpu.VMEM((8, half, width), BF16),
        pltpu.VMEM((4, half, width), BF16),
        pltpu.VMEM((2, half, width), BF16),
        pltpu.VMEM((4, half, width), BF16),
        pltpu.VMEM((2, half, width), BF16),
        pltpu.SemaphoreType.DMA((2, 14)),
        pltpu.SemaphoreType.DMA((4,)),
    ]


def at_step(step, total, places):
    for place, phase in places:

        @pl.when(step == place)
        def _(phase=phase):
            phase()


def partner(x):
    half = HEAD_DIM // 2
    width = x.shape[1]
    if width == HEAD_DIM:
        return jnp.concatenate([x[:, half:], x[:, :half]], axis=1)
    lane = lax.broadcasted_iota(jnp.int32, x.shape, 1)
    ahead = pltpu.roll(x, width - half, 1)
    behind = pltpu.roll(x, half, 1)
    return jnp.where(lane % HEAD_DIM < half, ahead, behind)


def head_mask(shape, head):
    lane = lax.broadcasted_iota(jnp.int32, shape, 1)
    return lane // HEAD_DIM == head


def dot_t(a, b):
    return lax.dot_general(a, b, (((1,), (1,)), ((), ())), preferred_element_type=F32)


def dot_n(a, b):
    return lax.dot_general(a, b, (((1,), (0,)), ((), ())), preferred_element_type=F32)


def dot_tn(a, b):
    return lax.dot_general(a, b, (((0,), (0,)), ((), ())), preferred_element_type=F32)


def key_plan(i, tile):
    base = TRUNK // BK * BK
    branch_end = TRUNK + 4 * MOST_SEG
    first_tree = base // BQ
    mixed_end = -(-(branch_end + MOST_SEG) // BQ)
    chunks = jnp.minimum(i * BQ, base) // BK
    half = BQ // 2

    @pl.when(i < first_tree)
    def _():
        @pl.loop(0, chunks)
        def _(j):
            start = pl.multiple_of(j * BK, BK)
            tile(start, BK, 0, start, 0, BQ)

    @pl.when(i >= first_tree)
    def _():
        tile(0, base, 0, 0, 0, BQ)

    @pl.when(i < first_tree)
    def _():
        start = pl.multiple_of(chunks * BK, BK)
        for part in range(2):
            tile(start, (part + 1) * half, 1, start, part * half, half)

    for block in range(first_tree, mixed_end):

        @pl.when(i == block)
        def _(block=block):
            for part in range(2):
                tile(base, block * BQ + (part + 1) * half - base, 2, base, part * half, half)

    @pl.when(i >= mixed_end)
    def _():
        tile(base, branch_end - base, 3, base, 0, BQ)
        for part in range(2):
            start = pl.multiple_of(i * BQ + part * half - MOST_SEG, MOST_SEG)
            tile(start, half + MOST_SEG, 4, branch_end, part * half, half)


def most_keys():
    branch_end = TRUNK + 4 * MOST_SEG
    return max(branch_end + BQ // 2 + MOST_SEG, -(-(branch_end + MOST_SEG) // BQ) * BQ)


def seen_mask(kind, q_at, k_at, seg_q, par_q, seg_k):
    if kind == 3:
        return (seg_k == 0) | (seg_k == par_q)
    causal = k_at <= q_at
    if kind == 1:
        return causal
    if kind == 4:
        return causal & (seg_k == seg_q)
    return causal & ((seg_k == 0) | (seg_k == seg_q) | (seg_k == par_q))


def fwd_kernel(heads, hosts, *refs):
    if not hosts:
        return fwd_work(heads, *refs)
    gather = PlaneGather(refs[7], refs[13], *refs[-3:])
    step, total = pl.program_id(0) * pl.num_programs(1) + pl.program_id(1), 16
    at_step(step, total, ((0, gather.start), (6, gather.first), (12, gather.second)))
    fwd_work(heads, *refs[:7], *refs[8:13], *refs[14:-3])
    at_step(step, total, ((total - 1, gather.finish),))


def fwd_work(
    heads, q_ref, k_ref, v_ref, cos_ref, sin_ref, rows_ref, cols_ref,
    o_ref, lse_ref, qr_ref, kr_ref, vr_ref, kt_ref, va_ref, s_ref, m_ref, acc_ref,
):
    i = pl.program_id(1)
    wide = 2 * HEAD_DIM

    @pl.when(i == 0)
    def _():
        @pl.loop(0, k_ref.shape[0] // BK)
        def _(j):
            rows = pl.ds(pl.multiple_of(j * BK, BK), BK)
            k = k_ref[rows, :]
            k = (k * cos_ref[rows, :] + partner(k) * sin_ref[rows, :]).astype(BF16)
            kr_ref[rows, :] = k
            kt_ref[:, rows] = jnp.transpose(k)
            v = v_ref[rows, :].astype(BF16)
            vr_ref[rows, :] = v
            if heads == 1:
                va_ref[0, rows, :] = jnp.concatenate([v, jnp.ones_like(v)], axis=1)
            else:
                for h in range(heads):
                    va_ref[h, rows, :] = jnp.where(head_mask(v.shape, h), v, jnp.ones_like(v))

    rows = pl.ds(pl.multiple_of(i * BQ, BQ), BQ)
    q = q_ref[...]
    q = (q * cos_ref[rows, :] + partner(q) * sin_ref[rows, :]).astype(BF16)
    qr_ref[...] = q
    q = q * jnp.asarray(SCALE, BF16)
    q_heads = [jnp.where(head_mask(q.shape, h), q, jnp.zeros_like(q)) for h in range(heads)]
    m_ref[...] = jnp.full_like(m_ref, NEG_LARGE)
    acc_ref[...] = jnp.zeros_like(acc_ref)

    def score_tile(start, width, kind, place, first, count):
        keys, rows = pl.ds(start, width), slice(first, first + count)
        k = kt_ref[:, keys]
        seen = None
        if kind != 0:
            shape = (count, width)
            seen = seen_mask(
                kind,
                lax.broadcasted_iota(jnp.int32, shape, 0) + i * BQ + first,
                lax.broadcasted_iota(jnp.int32, shape, 1) + start,
                cols_ref[rows, 0:1], cols_ref[rows, 1:2], rows_ref[0:1, keys],
            )
        for h in range(heads):
            s = dot_n(q_heads[h][rows], k)
            if seen is not None:
                s = jnp.where(seen, s, NEG_LARGE)
            s_ref[h, rows, pl.ds(place, width)] = s
            largest = m_ref[h, rows]
            for c in range(width // 128):
                largest = jnp.maximum(largest, s[:, c * 128 : (c + 1) * 128])
            m_ref[h, rows] = largest

    key_plan(i, score_tile)
    for h in range(heads):
        m_ref[h] = jnp.broadcast_to(jnp.max(m_ref[h], axis=1, keepdims=True), (BQ, 128))

    def value_tile(start, width, kind, place, first, count):
        keys, rows = pl.ds(start, width), slice(first, first + count)
        for h in range(heads):
            m = m_ref[h, rows]
            parts = [
                jnp.exp(s_ref[h, rows, pl.ds(place + c * 128, 128)] - m).astype(BF16) for c in range(width // 128)
            ]
            acc_ref[h, rows] += dot_n(jnp.concatenate(parts, axis=1), va_ref[h, keys, :])

    key_plan(i, value_tile)
    out, lse = None, None
    for h in range(heads):
        acc = acc_ref[h]
        part = acc / pltpu.roll(acc, HEAD_DIM, 1)
        stat = m_ref[h] + jnp.log(jnp.broadcast_to(acc[:, (1 - h) * HEAD_DIM : (1 - h) * HEAD_DIM + 1], (BQ, wide)))
        mask = head_mask((BQ, wide), h)
        out = part if h == 0 else jnp.where(mask, part, out)
        lse = stat if h == 0 else jnp.where(mask, stat, lse)
    o_ref[...] = out[:, : heads * HEAD_DIM].astype(BF16)
    turned = jnp.transpose(lse)
    for h in range(heads):
        lse_ref[0, h : h + 1, :] = turned[h * HEAD_DIM : h * HEAD_DIM + 1, :]


def bwd_kernel(heads, hosts, *refs):
    if not hosts:
        return bwd_work(heads, *refs)
    scatter = PlaneScatter(refs[10], refs[12], *refs[-7:])
    step, total = pl.program_id(0) * pl.num_programs(1) + pl.program_id(1), 16
    at_step(
        step, total, ((0, scatter.start), (3, scatter.first), (5, scatter.second), (7, scatter.third))
    )
    bwd_work(heads, *refs[:10], *refs[13:-7], together=refs[11])
    at_step(step, total, ((total - 1, scatter.finish),))


def bwd_work(
    heads, q_ref, k_ref, v_ref, o_ref, do_ref, lse_ref, cos_ref, sin_ref, rows_ref, cols_ref,
    *refs, together=None,
):
    if together is None:
        dq_ref, dk_ref, dv_ref, dq_acc, dk_acc, dv_acc = refs
    else:
        dq_acc, dk_acc, dv_acc, dq_ref, dk_ref, dv_ref, out_sems = refs
    i = pl.program_id(1)

    def store(kind, source, rows, sem):
        groups, width = pl.num_programs(0), source.shape[1]
        columns = pl.ds(pl.multiple_of((kind * groups + pl.program_id(0)) * width, width), width)
        return pltpu.make_async_copy(source, together.at[rows, columns], out_sems.at[sem])

    @pl.when(i == 0)
    def _():
        dk_acc[...] = jnp.zeros_like(dk_acc)
        dv_acc[...] = jnp.zeros_like(dv_acc)

    q = q_ref[...]
    scaled = q * jnp.asarray(SCALE, BF16)
    do = do_ref[...]
    product = jnp.transpose(do.astype(F32) * o_ref[...].astype(F32))
    zero = jnp.zeros_like(q)
    masks = [head_mask(q.shape, h) for h in range(heads)]
    q_heads = [jnp.where(m, scaled, zero) for m in masks]
    do_heads = [jnp.where(m, do, zero) for m in masks]
    deltas = [
        jnp.sum(product[h * HEAD_DIM : (h + 1) * HEAD_DIM, :], axis=0, keepdims=True) for h in range(heads)
    ]
    lses = [lse_ref[0, h : h + 1, :] for h in range(heads)]
    q_turned = [jnp.transpose(x) for x in q_heads]
    do_turned = [jnp.transpose(x) for x in do_heads]
    dq_acc[...] = jnp.zeros_like(dq_acc)

    def tile(start, width, kind, place, first, count):
        keys, part = pl.ds(start, width), slice(first, first + count)
        k = k_ref[keys, :]
        v = v_ref[keys, :]
        seen = None
        if kind != 0:
            shape = (width, count)
            seen = seen_mask(
                kind,
                lax.broadcasted_iota(jnp.int32, shape, 1) + i * BQ + first,
                lax.broadcasted_iota(jnp.int32, shape, 0) + start,
                rows_ref[0:1, part], rows_ref[1:2, part], cols_ref[keys, 0:1],
            )
        probs, grads, k_heads = [], [], []
        for h in range(heads):
            s = dot_n(k, q_turned[h][:, part])
            p = jnp.exp(s - lses[h][:, part])
            if seen is not None:
                p = jnp.where(seen, p, 0.0)
            dp = dot_n(v, do_turned[h][:, part])
            probs.append(p.astype(BF16))
            grads.append((p * (dp - deltas[h][:, part])).astype(BF16))
            k_heads.append(jnp.where(head_mask(k.shape, h), k, jnp.zeros_like(k)))
        grad_row = jnp.concatenate(grads, axis=1)
        dv_acc[keys, :] += dot_n(jnp.concatenate(probs, axis=1), jnp.concatenate([x[part] for x in do_heads], axis=0))
        dk_acc[keys, :] += dot_n(grad_row, jnp.concatenate([x[part] for x in q_heads], axis=0))
        dq_acc[part, :] += dot_tn(jnp.concatenate(grads, axis=0), jnp.concatenate(k_heads, axis=0))

    key_plan(i, tile)
    dq = dq_acc[...] * SCALE
    rows = pl.ds(pl.multiple_of(i * BQ, BQ), BQ)
    dq = (dq * cos_ref[rows, :] - partner(dq) * sin_ref[rows, :]).astype(BF16)
    if together is None:
        dq_ref[...] = dq
    else:
        step, last = pl.program_id(0) * pl.num_programs(1) + i, pl.num_programs(0) * pl.num_programs(1) - 1
        for slot in range(2):

            @pl.when(step % 2 == slot)
            def _(slot=slot):
                @pl.when(step >= 2)
                def _():
                    store(0, dq_ref.at[slot], rows, slot).wait()

                dq_ref[slot] = dq
                store(0, dq_ref.at[slot], rows, slot).start()

        @pl.when(step == last)
        def _():
            for slot in range(2):
                store(0, dq_ref.at[slot], rows, slot).wait()

    @pl.when(i == pl.num_programs(1) - 1)
    def _():
        @pl.loop(0, dk_acc.shape[0] // BK)
        def _(j):
            rows = pl.ds(pl.multiple_of(j * BK, BK), BK)
            dk = dk_acc[rows, :]
            dk_ref[rows, :] = (dk * cos_ref[rows, :] - partner(dk) * sin_ref[rows, :]).astype(BF16)
            dv_ref[rows, :] = dv_acc[rows, :].astype(BF16)

        if together is not None:
            every = pl.ds(0, dk_acc.shape[0])
            copies = [store(1, dk_ref, every, 2), store(2, dv_ref, every, 3)]
            for copy in copies:
                copy.start()
            for copy in copies:
                copy.wait()


def small_cost():
    return pl.CostEstimate(flops=1 << 20, bytes_accessed=1 << 20, transcendentals=0)


def attention_forward(qkv, cosine, sine, rows_table, cols_table, width, hosted=None):
    tree_len = qkv.shape[0]
    gw = min(2 * HEAD_DIM, width)
    groups, heads = width // gw, gw // HEAD_DIM
    row_block = pl.BlockSpec((BQ, gw), lambda g, i: (i, g))
    table = pl.BlockSpec((tree_len, gw), lambda g, i: (0, 0))
    full = pl.BlockSpec((tree_len, gw), lambda g, i: (0, g))
    act = jax.ShapeDtypeStruct((tree_len, width), BF16)
    if width % 128 == 0:
        queries, keys, values, step = qkv, qkv, qkv, groups
    else:
        queries, keys, values = jnp.split(qkv, 3, axis=1)
        step = 0
    hosts = hosted is not None
    hbm = pl.BlockSpec(memory_space=pl.ANY)
    return pl.pallas_call(
        functools.partial(fwd_kernel, heads, hosts),
        grid=(groups, tree_len // BQ),
        in_specs=[
            row_block,
            pl.BlockSpec((tree_len, gw), lambda g, i: (0, step + g)),
            pl.BlockSpec((tree_len, gw), lambda g, i: (0, 2 * step + g)),
            table,
            table,
            pl.BlockSpec((8, tree_len), lambda g, i: (0, 0)),
            pl.BlockSpec((BQ, 128), lambda g, i: (i, 0)),
        ]
        + [hbm] * hosts,
        out_specs=[row_block, pl.BlockSpec((1, heads, BQ), lambda g, i: (g, 0, i)), row_block, full, full] + [hbm] * hosts,
        out_shape=[act, jax.ShapeDtypeStruct((groups, heads, tree_len), F32), act, act, act]
        + ([jax.ShapeDtypeStruct((8 * hosted.shape[0], hosted.shape[1]), BF16)] if hosts else []),
        scratch_shapes=[
            pltpu.VMEM((gw, tree_len), BF16),
            pltpu.VMEM((heads, tree_len, 128), BF16),
            pltpu.VMEM((heads, BQ, most_keys()), F32),
            pltpu.VMEM((heads, BQ, 128), F32),
            pltpu.VMEM((heads, BQ, 128), F32),
        ]
        + (gather_sems() if hosts else []),
        compiler_params=pltpu.CompilerParams(
            vmem_limit_bytes=60 << 20, collective_id=6 if hosts else None, has_side_effects=hosts
        ),
        cost_estimate=small_cost(),
        name="tree_attention_forward",
    )(queries, keys, values, cosine, sine, rows_table, cols_table, *([hosted] if hosts else []))


def attention_backward(q, k, v, out, grad, lse, cosine, sine, rows_table, cols_table, hosted=None):
    tree_len, width = q.shape
    gw = min(2 * HEAD_DIM, width)
    groups, heads = width // gw, gw // HEAD_DIM
    row_block = pl.BlockSpec((BQ, gw), lambda g, i: (i, g))
    table = pl.BlockSpec((tree_len, gw), lambda g, i: (0, 0))
    full = pl.BlockSpec((tree_len, gw), lambda g, i: (0, g))
    act = jax.ShapeDtypeStruct((tree_len, width), BF16)
    hosts = hosted is not None
    hbm = pl.BlockSpec(memory_space=pl.ANY)
    return pl.pallas_call(
        functools.partial(bwd_kernel, heads, hosts),
        grid=(groups, tree_len // BQ),
        in_specs=[
            row_block, full, full, row_block, row_block,
            pl.BlockSpec((1, heads, BQ), lambda g, i: (g, 0, i)),
            table, table,
            pl.BlockSpec((8, BQ), lambda g, i: (0, i)),
            pl.BlockSpec((tree_len, 128), lambda g, i: (0, 0)),
        ]
        + [hbm] * hosts,
        out_specs=[hbm] * 2 if hosts else [row_block, full, full],
        out_shape=[
            jax.ShapeDtypeStruct((tree_len, 3 * width), BF16),
            jax.ShapeDtypeStruct((hosted.shape[0] // 8, hosted.shape[1]), BF16),
        ]
        if hosts
        else [act, act, act],
        scratch_shapes=[
            pltpu.VMEM((BQ, gw), F32),
            pltpu.VMEM((tree_len, gw), F32),
            pltpu.VMEM((tree_len, gw), F32),
        ]
        + (
            [pltpu.VMEM(shape, BF16) for shape in ((2, BQ, gw), (tree_len, gw), (tree_len, gw))]
            + [pltpu.SemaphoreType.DMA((4,))]
            + scatter_scratch(hosted.shape[0] // 8, hosted.shape[1])
            if hosts
            else []
        ),
        compiler_params=pltpu.CompilerParams(
            vmem_limit_bytes=60 << 20, collective_id=7 if hosts else None, has_side_effects=hosts
        ),
        cost_estimate=small_cost(),
        name="tree_attention_backward",
    )(q, k, v, out, grad, lse, cosine, sine, rows_table, cols_table, *([hosted] if hosts else []))


TOKENS_AT_ONCE = 2048
LEFT_AT_ONCE = 512
TOKEN_STEP = 1024
ROW_STEP = 1024


def product_buffers(columns):
    return [
        pltpu.VMEM((2, TOKENS_AT_ONCE, LEFT_AT_ONCE), BF16),
        pltpu.VMEM((2 * TOKENS_AT_ONCE, columns), BF16),
        pltpu.VMEM((LEFT_AT_ONCE, columns), F32),
        pltpu.VMEM((LEFT_AT_ONCE, columns), BF16),
        pltpu.SemaphoreType.DMA((4,)),
    ]


def token_product(left_ref, right_ref, out_ref, left_buf, right_buf, total, out_buf, sems):
    tokens = left_ref.shape[0]
    parts, groups = tokens // TOKENS_AT_ONCE, left_ref.shape[1] // LEFT_AT_ONCE

    def load(step):
        group, part = step // parts, step % parts
        source = left_ref.at[
            pl.ds(part * TOKENS_AT_ONCE, TOKENS_AT_ONCE), pl.ds(group * LEFT_AT_ONCE, LEFT_AT_ONCE)
        ]
        return pltpu.make_async_copy(source, left_buf.at[step % 2], sems.at[step % 2])

    def store(group):
        return pltpu.make_async_copy(out_buf, out_ref.at[pl.ds(group * LEFT_AT_ONCE, LEFT_AT_ONCE)], sems.at[3])

    whole = pltpu.make_async_copy(right_ref, right_buf, sems.at[2])
    whole.start()
    load(0).start()
    yield
    whole.wait()
    for group in range(groups):
        for part in range(parts):
            step = group * parts + part
            load(step).wait()
            if step + 1 < groups * parts:
                load(step + 1).start()
            if part == 0:
                total[...] = jnp.zeros_like(total)

            @pl.loop(0, TOKENS_AT_ONCE // TOKEN_STEP)
            def _(j, step=step, part=part):
                left = left_buf[step % 2, pl.ds(pl.multiple_of(j * TOKEN_STEP, TOKEN_STEP), TOKEN_STEP), :]
                right = right_buf[pl.ds(pl.multiple_of(part * TOKENS_AT_ONCE + j * TOKEN_STEP, TOKEN_STEP), TOKEN_STEP), :]
                total[...] += dot_tn(left, right)

        if group > 0:
            store(group - 1).wait()
        out_buf[...] = total[...].astype(BF16)
        store(group).start()
        yield
    store(groups - 1).wait()


def finish(product):
    for _ in product:
        pass


def pair_product(left_ref, first_ref, second_ref, out_first, out_second, left_buf, right_buf, total, out_buf, sems):
    tokens, columns = first_ref.shape
    parts, groups = tokens // TOKENS_AT_ONCE, left_ref.shape[1] // LEFT_AT_ONCE
    sides = [pl.ds(0, columns), pl.ds(columns, columns)]

    def load(step):
        group, part = step // parts, step % parts
        source = left_ref.at[
            pl.ds(part * TOKENS_AT_ONCE, TOKENS_AT_ONCE), pl.ds(group * LEFT_AT_ONCE, LEFT_AT_ONCE)
        ]
        return pltpu.make_async_copy(source, left_buf.at[step % 2], sems.at[step % 2])

    def stores(group):
        rows = pl.ds(group * LEFT_AT_ONCE, LEFT_AT_ONCE)
        return [
            pltpu.make_async_copy(out_buf.at[:, side], out_ref.at[rows], sems.at[4 + n])
            for n, (side, out_ref) in enumerate(zip(sides, (out_first, out_second)))
        ]

    wholes = [
        pltpu.make_async_copy(ref, right_buf.at[:, side], sems.at[2 + n])
        for n, (side, ref) in enumerate(zip(sides, (first_ref, second_ref)))
    ]
    load(0).start()
    for copy in wholes:
        copy.start()
    yield
    for copy in wholes:
        copy.wait()
    for group in range(groups):
        for part in range(parts):
            step = group * parts + part
            load(step).wait()
            if step + 1 < groups * parts:
                load(step + 1).start()
            if part == 0:
                total[...] = jnp.zeros_like(total)

            @pl.loop(0, TOKENS_AT_ONCE // TOKEN_STEP)
            def _(j, step=step, part=part):
                left = left_buf[step % 2, pl.ds(pl.multiple_of(j * TOKEN_STEP, TOKEN_STEP), TOKEN_STEP), :]
                right = right_buf[pl.ds(pl.multiple_of(part * TOKENS_AT_ONCE + j * TOKEN_STEP, TOKEN_STEP), TOKEN_STEP), :]
                total[...] += dot_tn(left, right)

        if group > 0:
            for copy in stores(group - 1):
                copy.wait()
        out_buf[...] = total[...].astype(BF16)
        for copy in stores(group):
            copy.start()
        yield
    for copy in stores(groups - 1):
        copy.wait()


def cut_columns(*refs):
    count = (len(refs) - 2) // 2
    sources, targets, (room, sems) = refs[:count], refs[count : 2 * count], refs[2 * count :]

    def inward(n):
        columns = targets[n].shape[1]
        taken = pl.ds(pl.multiple_of(lax.axis_index("ctx") * columns, columns), columns)
        return pltpu.make_async_copy(sources[n].at[:, taken], room.at[n], sems.at[0, n])

    def outward(n):
        return pltpu.make_async_copy(room.at[n], targets[n], sems.at[1, n])

    for n in range(count):
        inward(n).start()
    yield
    for n in range(count):
        inward(n).wait()
        outward(n).start()
    yield
    for n in range(count):
        outward(n).wait()


def row_product(turned, left_ref, right_ref, out_ref, left_buf, right_buf, out_buf, sems):
    groups = left_ref.shape[0] // LEFT_AT_ONCE

    def rows(group):
        return pl.ds(group * LEFT_AT_ONCE, LEFT_AT_ONCE)

    def load(group):
        return pltpu.make_async_copy(left_ref.at[rows(group)], left_buf.at[group % 2], sems.at[group % 2])

    def store(group):
        return pltpu.make_async_copy(out_buf.at[group % 2], out_ref.at[rows(group)], sems.at[3 + group % 2])

    whole = pltpu.make_async_copy(right_ref, right_buf, sems.at[2])
    whole.start()
    load(0).start()
    yield
    whole.wait()
    for group in range(groups):
        load(group).wait()
        if group + 1 < groups:
            load(group + 1).start()
        if group > 1:
            store(group - 2).wait()

        @pl.loop(0, out_ref.shape[1] // ROW_STEP)
        def _(j, group=group):
            columns = pl.ds(pl.multiple_of(j * ROW_STEP, ROW_STEP), ROW_STEP)
            if turned:
                part = dot_t(left_buf[group % 2], right_buf[columns, :])
            else:
                part = dot_n(left_buf[group % 2], right_buf[:, columns])
            out_buf[group % 2, :, columns] = part.astype(BF16)

        store(group).start()
        yield
    for group in range(max(0, groups - 2), groups):
        store(group).wait()


def row_product_buffers(right, turned):
    return [
        pltpu.VMEM((2, LEFT_AT_ONCE, right.shape[1 if turned else 0]), BF16),
        pltpu.VMEM(right.shape, BF16),
        pltpu.VMEM((2, LEFT_AT_ONCE, right.shape[0 if turned else 1]), BF16),
        pltpu.SemaphoreType.DMA((5,)),
    ]


def gather_kernel(works, counts, paces, *refs):
    def take(count):
        nonlocal refs
        taken, refs = refs[:count], refs[count:]
        return taken

    (own_ref,) = take(1)
    inputs = [take(count[0]) for count in counts]
    (all_ref,) = take(1)
    outputs = [take(count[1]) for count in counts]
    gather = PlaneGather(own_ref, all_ref, *take(3))
    buffers, held = [], {}
    for work, count in zip(works, counts):
        if work not in held:
            held[work] = take(count[2])
        buffers.append(held[work])

    def all_work():
        started = [work(*given, *wanted, *room) for work, given, wanted, room in zip(works, inputs, outputs, buffers)]
        for one in started:
            next(one)
        for one in started:
            yield from one

    going = all_work()

    def some(count):
        for _ in range(count):
            next(going, None)

    gather.start()
    some(paces[0])
    gather.first()
    some(paces[1])
    gather.second()
    finish(going)
    gather.finish()


def plane_gather(rows, collective_id=0, jobs=(), paces=(0, 0)):
    count, width = rows.shape
    hbm = pl.BlockSpec(memory_space=pl.ANY)
    scratch, held = gather_sems(), set()
    for work, _, _, _, _, buffers in jobs:
        if work not in held:
            held.add(work)
            scratch += buffers
    return pl.pallas_call(
        functools.partial(
            gather_kernel,
            [job[0] for job in jobs],
            [(len(job[1]), len(job[3]), len(job[5])) for job in jobs],
            paces,
        ),
        in_specs=[hbm] + [spec for job in jobs for spec in job[2]],
        out_specs=[hbm] + [spec for job in jobs for spec in job[4]],
        out_shape=[jax.ShapeDtypeStruct((8 * count, width), rows.dtype)] + [out for job in jobs for out in job[3]],
        scratch_shapes=scratch,
        compiler_params=pltpu.CompilerParams(
            collective_id=collective_id, has_side_effects=True, vmem_limit_bytes=(60 << 20) if jobs else None
        ),
        cost_estimate=small_cost(),
        name="plane_gather",
    )(rows, *[value for job in jobs for value in job[1]])


HBM = pl.BlockSpec(memory_space=pl.ANY)
VMEM = pl.BlockSpec(memory_space=pltpu.VMEM)
ROWS_TURNED = functools.partial(row_product, True)
ROWS_STRAIGHT = functools.partial(row_product, False)


def token_job(left, right):
    out = jax.ShapeDtypeStruct((left.shape[1], right.shape[1]), BF16)
    return token_product, [left, right], [HBM] * 2, [out], [HBM], product_buffers(right.shape[1])


def pair_job(left, first, second):
    columns = first.shape[1]
    out = jax.ShapeDtypeStruct((left.shape[1], columns), BF16)
    room = [
        pltpu.VMEM((2, TOKENS_AT_ONCE, LEFT_AT_ONCE), BF16),
        pltpu.VMEM((left.shape[0], 2 * columns), BF16),
        pltpu.VMEM((LEFT_AT_ONCE, 2 * columns), F32),
        pltpu.VMEM((LEFT_AT_ONCE, 2 * columns), BF16),
        pltpu.SemaphoreType.DMA((6,)),
    ]
    return pair_product, [left, first, second], [HBM] * 3, [out] * 2, [HBM] * 2, room


def cut_job(weights, parts):
    outs = [jax.ShapeDtypeStruct((w.shape[0], w.shape[1] // parts), w.dtype) for w in weights]
    room = [pltpu.VMEM((len(weights),) + outs[0].shape, BF16), pltpu.SemaphoreType.DMA((2, len(weights)))]
    return cut_columns, list(weights), [HBM] * len(weights), outs, [HBM] * len(weights), room


def row_job(left, right, turned):
    out = jax.ShapeDtypeStruct((left.shape[0], right.shape[0 if turned else 1]), BF16)
    work = ROWS_TURNED if turned else ROWS_STRAIGHT
    return work, [left, right], [HBM] * 2, [out], [HBM], row_product_buffers(right, turned)


def table_job(lengths, parents, tokens):
    outs = [jax.ShapeDtypeStruct((8, tokens), jnp.int32), jax.ShapeDtypeStruct((tokens, 128), jnp.int32)]
    outs += [jax.ShapeDtypeStruct((tokens, 128), F32)] * 2
    room = [pltpu.VMEM(out.shape, out.dtype) for out in outs[1:]]
    room += [pltpu.SemaphoreType.DMA((3, tokens // TABLE_ROWS))]
    return table_work, [lengths, parents, rope_freqs(128)], [VMEM] * 3, outs, [VMEM, HBM, HBM, HBM], room


def scatter_kernel(rows, offsets, jobs, *refs):
    parts = len(offsets)

    def take(count):
        nonlocal refs
        taken, refs = refs[:count], refs[count:]
        return taken

    a_refs, w_homes, lefts, rights = take(parts), take(parts), take(jobs), take(jobs)
    (out_ref,), products = take(1), take(jobs)
    core_out, core_in, first_in, next_in, sems = take(5)
    a_bufs, w_refs, (a_sems, w_sems), buffers = take(parts), take(parts), take(2), refs

    def work(job):
        if job < jobs:
            finish(token_product(lefts[job], rights[job], products[job], *buffers))

    x, core, row = plane_place()
    over_x, over_row, over_core = plane_neighbours(x, core, row)
    half = rows // 2
    width = out_ref.shape[1]
    chunks = width // COLS

    def place(piece, on_core):
        far_x, far_row, part = PIECES[piece]
        bx = x + far_x - 2 * far_x * x
        by = row + far_row - 2 * far_row * row
        return pl.ds(pl.multiple_of(((bx * 2 + on_core) * 2 + by) * rows + part * half, half), half)

    def columns(j):
        return pl.ds(pl.multiple_of(j * COLS, COLS), COLS)

    steps = [(0, True)]
    for piece in range(8):
        steps += [(piece + 1, True)] * (piece < 7) + [(piece, False)]

    def load(step):
        piece, partner_half = steps[step]
        taken = place(piece, 1 - core if partner_half else core)
        return [
            pltpu.make_async_copy(a_ref.at[taken], a_buf.at[step % 2], a_sems.at[step % 2, p])
            for p, (a_ref, a_buf) in enumerate(zip(a_refs, a_bufs))
        ]

    w_copies = [
        pltpu.make_async_copy(home.at[:, pl.ds(offset, w_ref.shape[1])], w_ref, w_sems.at[p])
        for p, (home, offset, w_ref) in enumerate(zip(w_homes, offsets, w_refs))
    ]
    loads = {0: load(0)}
    for copy in w_copies + loads[0]:
        copy.start()
    enter_plane((over_x, over_row, over_core))
    for copy in w_copies:
        copy.wait()

    def partial(slot, j):
        total = None
        for a_buf, w_ref in zip(a_bufs, w_refs):
            term = dot_t(a_buf[slot], w_ref[columns(j), :])
            total = term if total is None else total + term
        return total

    def remote(source, target, slot, device):
        return pltpu.make_async_remote_copy(
            src_ref=source, dst_ref=target, send_sem=sems.at[0, slot], recv_sem=sems.at[1, slot],
            device_id=device, device_id_type=MESH,
        )

    core_copies, first_copies, next_copies = [], [], []
    for step, (piece, partner_half) in enumerate(steps):
        for copy in loads[step]:
            copy.wait()
        if step + 1 < len(steps):
            loads[step + 1] = load(step + 1)
            for copy in loads[step + 1]:
                copy.start()
        if partner_half:

            @pl.loop(0, chunks)
            def _(j, step=step, piece=piece):
                core_out[piece, :, columns(j)] = partial(step % 2, j).astype(BF16)

            core_copies.append(remote(core_out.at[piece], core_in.at[piece], piece, over_core))
            core_copies[-1].start()
            continue
        core_copies[piece].wait_recv()

        @pl.loop(0, chunks)
        def _(j, step=step, piece=piece):
            total = partial(step % 2, j) + core_in[piece, :, columns(j)].astype(F32)
            core_in[piece, :, columns(j)] = total.astype(BF16)

        if piece < 4:
            first_copies.append(
                remote(core_in.at[piece], first_in.at[piece], 8 + piece, over_x if piece % 2 == 0 else over_row)
            )
            first_copies[-1].start()
    for part in range(2):
        first_copies[part].wait_recv()

        @pl.loop(0, chunks)
        def _(j, part=part):
            total = core_in[4 + part, :, columns(j)].astype(F32) + first_in[part, :, columns(j)].astype(F32)
            core_in[4 + part, :, columns(j)] = total.astype(BF16)

        next_copies.append(remote(core_in.at[4 + part], next_in.at[part], 12 + part, over_row if part == 0 else over_x))
        next_copies[-1].start()
    for job in range(jobs):
        work(job)
    for part in range(2):
        first_copies[2 + part].wait_recv()
        next_copies[part].wait_recv()

        @pl.loop(0, chunks)
        def _(j, part=part):
            total = core_in[6 + part, :, columns(j)].astype(F32) + first_in[2 + part, :, columns(j)].astype(F32)
            out_ref[pl.ds(part * half, half), columns(j)] = total + next_in[part, :, columns(j)].astype(F32)

    for copy in core_copies + first_copies + next_copies:
        copy.wait_send()


def plane_scatter(parts, weights, collective_id, jobs=(), offsets=None):
    count = parts[0].shape[0]
    width = weights[0].shape[0]
    rows = count // 8
    half = rows // 2
    vmem, hbm = pl.BlockSpec(memory_space=pltpu.VMEM), pl.BlockSpec(memory_space=pl.ANY)
    offsets = offsets or [0] * len(parts)
    lefts, rights = [left for left, _ in jobs], [right for _, right in jobs]
    return pl.pallas_call(
        functools.partial(scatter_kernel, rows, offsets, len(jobs)),
        in_specs=[hbm] * (2 * len(parts) + 2 * len(jobs)),
        out_specs=[vmem] + [hbm] * len(jobs),
        out_shape=[jax.ShapeDtypeStruct((rows, width), F32)]
        + [jax.ShapeDtypeStruct((left.shape[1], right.shape[1]), BF16) for left, right in jobs],
        scratch_shapes=[
            pltpu.VMEM((8, half, width), BF16),
            pltpu.VMEM((8, half, width), BF16),
            pltpu.VMEM((4, half, width), BF16),
            pltpu.VMEM((2, half, width), BF16),
            pltpu.SemaphoreType.DMA((2, 14)),
        ]
        + [pltpu.VMEM((2, half, a.shape[1]), BF16) for a in parts]
        + [pltpu.VMEM((width, a.shape[1]), BF16) for a in parts]
        + [pltpu.SemaphoreType.DMA((2, len(parts))), pltpu.SemaphoreType.DMA((len(parts),))]
        + (product_buffers(rights[0].shape[1]) if jobs else []),
        compiler_params=pltpu.CompilerParams(
            collective_id=collective_id, has_side_effects=True, vmem_limit_bytes=60 << 20
        ),
        cost_estimate=small_cost(),
        name="plane_scatter",
    )(*parts, *weights, *lefts, *rights)


def gated_kernel(x_ref, grad_ref, gate_ref, up_ref, hidden_ref, gate_grad_ref, up_grad_ref):
    columns = gate_ref.shape[1]
    step = min(512, columns)
    together = min(2, columns // step)

    @pl.loop(0, columns // (step * together))
    def _(j):
        for part in range(together):
            taken = pl.ds(pl.multiple_of((j * together + part) * step, step), step)
            gate = dot_n(x_ref[...], gate_ref[:, taken])
            up = dot_n(x_ref[...], up_ref[:, taken])
            grad = grad_ref[:, taken].astype(F32)
            sigmoid = jax.nn.sigmoid(gate)
            silu = gate * sigmoid
            hidden_ref[:, taken] = (silu * up).astype(BF16)
            gate_grad_ref[:, taken] = (grad * up * (sigmoid + silu * (1.0 - sigmoid))).astype(BF16)
            up_grad_ref[:, taken] = (grad * silu).astype(BF16)


def gated_rows(x, hidden_grad, w_gate, w_up):
    tokens, depth = x.shape
    columns = w_gate.shape[1]
    block = 256
    rows = pl.BlockSpec((block, columns), lambda i: (i, 0))
    weight = pl.BlockSpec((depth, columns), lambda i: (0, 0), pipeline_mode=pl.Buffered(1))
    out = jax.ShapeDtypeStruct((tokens, columns), BF16)
    return pl.pallas_call(
        gated_kernel,
        grid=(tokens // block,),
        in_specs=[pl.BlockSpec((block, depth), lambda i: (i, 0)), rows, weight, weight],
        out_specs=[rows] * 3,
        out_shape=[out] * 3,
        compiler_params=pltpu.CompilerParams(vmem_limit_bytes=60 << 20),
        cost_estimate=small_cost(),
        name="gated_rows",
    )(x, hidden_grad, w_gate, w_up)


def heads_kernel(x_ref, w_ref, out_ref, heads_ref, grad_ref, total):
    i = pl.program_id(0)

    @pl.when(i == 0)
    def _():
        total[...] = jnp.zeros_like(total)

    heads_ref[...] = dot_n(x_ref[...], w_ref[...]).astype(BF16)
    total[...] += dot_tn(out_ref[...], x_ref[...])

    @pl.when(i == pl.num_programs(0) - 1)
    def _():
        grad_ref[...] = jnp.transpose(total[...]).astype(BF16)


def heads_and_output_grad(mid, w_attn, attn_out):
    tokens, depth = mid.shape
    width = attn_out.shape[1]
    if width % 128:
        return dot_n(mid, w_attn[:, 3 * width :]).astype(BF16), dot_tn(mid, attn_out).astype(BF16)
    block = 1024
    rows = pl.BlockSpec((block, width), lambda i: (i, 0))
    return pl.pallas_call(
        heads_kernel,
        grid=(tokens // block,),
        in_specs=[pl.BlockSpec((block, depth), lambda i: (i, 0)), pl.BlockSpec((depth, width), lambda i: (0, 3)), rows],
        out_specs=[rows, pl.BlockSpec((depth, width), lambda i: (0, 0))],
        out_shape=[jax.ShapeDtypeStruct((tokens, width), BF16), jax.ShapeDtypeStruct((depth, width), BF16)],
        scratch_shapes=[pltpu.VMEM((width, depth), F32)],
        compiler_params=pltpu.CompilerParams(vmem_limit_bytes=60 << 20),
        cost_estimate=small_cost(),
        name="heads_and_output_grad",
    )(mid, w_attn, attn_out)


def weight_grads_kernel(x_ref, pre_ref, output_ref, grad_ref, total):
    i = pl.program_id(0)
    width = pre_ref.shape[1]

    @pl.when(i == 0)
    def _():
        total[...] = jnp.zeros_like(total)

    total[...] += dot_tn(x_ref[...], pre_ref[...])

    @pl.when(i == pl.num_programs(0) - 1)
    def _():
        grad_ref[:, :width] = total[...].astype(BF16)
        grad_ref[:, width:] = output_ref[...]


def attention_weight_grads(attn_in, pre_grads, output_grad):
    tokens, depth = attn_in.shape
    width, last = pre_grads.shape[1], output_grad.shape[1]
    if width % 128 or last % 128:
        return jnp.concatenate([dot_tn(attn_in, pre_grads).astype(BF16), output_grad], axis=1)
    block = 1024
    return pl.pallas_call(
        weight_grads_kernel,
        grid=(tokens // block,),
        in_specs=[
            pl.BlockSpec((block, depth), lambda i: (i, 0)),
            pl.BlockSpec((block, width), lambda i: (i, 0)),
            pl.BlockSpec((depth, last), lambda i: (0, 0)),
        ],
        out_specs=pl.BlockSpec((depth, width + last), lambda i: (0, 0)),
        out_shape=jax.ShapeDtypeStruct((depth, width + last), BF16),
        scratch_shapes=[pltpu.VMEM((depth, width), F32)],
        compiler_params=pltpu.CompilerParams(vmem_limit_bytes=60 << 20),
        cost_estimate=small_cost(),
        name="attention_weight_grads",
    )(attn_in, pre_grads, output_grad)


def is_plane():
    return lax.axis_size("ctx") == 4 and lax.axis_size("tensor") == 2


def gather_rows(rows):
    return lax.all_gather(rows, GROUP, axis=0, tiled=True)


def scatter_rows(rows):
    return lax.psum_scatter(rows.astype(BF16), GROUP, scatter_dimension=0, tiled=True).astype(F32)


def gather_now(rows):
    return plane_gather(rows)[0] if is_plane() else gather_rows(rows)


def cut(weight):
    columns = weight.shape[1] // lax.axis_size("ctx")
    return lax.dynamic_slice_in_dim(weight, lax.axis_index("ctx") * columns, columns, 1)


def gather_with_tables(rows, lengths, parents, tokens, width, weights):
    if is_plane():
        jobs = [cut_job(weights, lax.axis_size("ctx")), table_job(lengths, parents, tokens)]
        got = plane_gather(rows, 8, jobs, (4, 4))
        return got[:1] + got[1 + len(weights) :], got[1 : 1 + len(weights)]
    segment, parent, depth = tree_tables(lengths[0], parents[0], tokens)
    return [gather_rows(rows), *lay_out(segment, parent), *rope_tables(depth, width)], [cut(w) for w in weights]


def gather_with_product(rows, left, right):
    if is_plane():
        return plane_gather(rows, 5, [row_job(left, right, False)], (4, 4))
    return gather_rows(rows), dot_n(left, right).astype(BF16)


def gather_with_three(rows, left, right, shared, first, second):
    if is_plane():
        return plane_gather(rows, 4, [row_job(left, right, True), pair_job(shared, first, second)], (8, 3))
    products = dot_t(left, right), dot_tn(shared, first), dot_tn(shared, second)
    return [gather_rows(rows)] + [product.astype(BF16) for product in products]


def product_scatter(parts, weights, collective_id, jobs=(), offsets=None):
    if is_plane():
        return plane_scatter(parts, weights, collective_id, jobs, offsets)
    offsets = offsets or [0] * len(parts)
    weights = [w[:, first : first + part.shape[1]] for part, w, first in zip(parts, weights, offsets)]
    rows = scatter_rows(dot_t(jnp.concatenate(parts, axis=1), jnp.concatenate(weights, axis=1)))
    return [rows] + [dot_tn(left, right).astype(BF16) for left, right in jobs]


def gather_weight(own):
    return lax.all_gather(own, "fsdp", axis=0, tiled=True)


def scatter_weight(grad):
    return lax.psum_scatter(grad.astype(BF16), "fsdp", scatter_dimension=0, tiled=True)


def swap_rows(part):
    size = lax.axis_size("ctx")
    return lax.all_to_all(part.reshape(size, part.shape[0] // size, -1), "ctx", split_axis=0, concat_axis=0)


def lay_side_by_side(got, count):
    columns = got.shape[2] // count
    return [
        jnp.concatenate([got[j, :, c * columns : (c + 1) * columns] for j in range(got.shape[0])], axis=1).astype(F32)
        for c in range(count)
    ]


def lay_out_kernel(plan, weighted, ctx_ref, *refs):
    inputs = refs[: max(source for source, _ in plan) + 1]
    refs = refs[len(inputs) :]
    weights, outs, sums_ref, total = refs[:weighted], refs[weighted:-2], refs[-2], refs[-1]
    j = pl.program_id(0)

    @pl.when(j == 0)
    def _():
        total[...] = jnp.zeros_like(total)

    for n, ((source, first), out_ref) in enumerate(zip(plan, outs)):
        columns = out_ref.shape[1]
        grad = inputs[source][0, :, first : first + columns].astype(F32)
        out_ref[...] = grad
        if n < weighted:
            product = grad * weights[n][...].astype(F32)
            part = product[:, :128]
            for c in range(1, columns // 128):
                part = part + product[:, c * 128 : (c + 1) * 128]
            total[...] += part

    @pl.when(j == pl.num_programs(0) - 1)
    def _():
        column = jnp.sum(total[...], axis=1, keepdims=True)
        sums_ref[...] = jnp.transpose(jnp.broadcast_to(column, total.shape))[:8]


def lay_out_grads(swapped, count, weights):
    size, rows = swapped[0].shape[:2]
    columns = swapped[0].shape[2] // count
    if columns % 128 or rows != 128:
        outs = [out for got in swapped for out in lay_side_by_side(got, count)]
        ctx = lax.axis_index("ctx")
        held = [lax.dynamic_slice_in_dim(weight, ctx * rows, rows, 0).astype(F32) for weight in weights]
        return outs, sum(jnp.sum(weight * out, axis=1) for weight, out in zip(held, outs))
    plan = [(n, c * columns) for n in range(len(swapped)) for c in range(count)]
    result = pl.pallas_call(
        functools.partial(lay_out_kernel, plan, len(weights)),
        grid_spec=pltpu.PrefetchScalarGridSpec(
            num_scalar_prefetch=1,
            grid=(size,),
            in_specs=[pl.BlockSpec((1, rows, count * columns), lambda j, ctx: (j, 0, 0)) for _ in swapped]
            + [pl.BlockSpec((rows, columns), lambda j, ctx: (ctx[0], j)) for _ in weights],
            out_specs=[pl.BlockSpec((rows, columns), lambda j, ctx: (0, j)) for _ in plan]
            + [pl.BlockSpec((8, rows), lambda j, ctx: (0, 0))],
            scratch_shapes=[pltpu.VMEM((rows, 128), F32)],
        ),
        out_shape=[jax.ShapeDtypeStruct((rows, size * columns), F32) for _ in plan]
        + [jax.ShapeDtypeStruct((8, rows), F32)],
        compiler_params=pltpu.CompilerParams(vmem_limit_bytes=60 << 20),
        cost_estimate=small_cost(),
        name="lay_out_grads",
    )(lax.axis_index("ctx").reshape(1).astype(jnp.int32), *swapped, *weights)
    return result[:-1], result[-1][0]


def normalize(rows):
    norm_inv = lax.rsqrt(jnp.mean(rows * rows, axis=1, keepdims=True) + EPSILON)
    return (rows * norm_inv, norm_inv)


def norm_backward(grad_rows, scaled, norm_inv, gain):
    weighted = grad_rows * gain[None, :]
    inner = jnp.mean(weighted * scaled, axis=1, keepdims=True)
    return norm_inv * (weighted - scaled * inner)


def body(
    tokens_in,
    attn_gain,
    query_weight,
    key_weight,
    value_weight,
    output_weight,
    mlp_gain,
    gate_weight,
    up_weight,
    down_weight,
    seg_lengths,
    leaf_parent,
    cotangent,
):
    ctx = lax.axis_index("ctx")
    parts = lax.axis_size("ctx")
    tree_len = tokens_in.shape[0] * parts * lax.axis_size("tensor")
    width = query_weight.shape[1] // parts
    units = gate_weight.shape[1] // parts

    def mine(weight, columns):
        return lax.dynamic_slice_in_dim(weight, ctx * columns, columns, 1)

    x_rows = tokens_in.astype(F32)
    attn_scaled, attn_inv = normalize(x_rows)
    w_attn = gather_weight(
        jnp.concatenate([mine(w, width) for w in (query_weight, key_weight, value_weight, output_weight)], axis=1)
    )
    (attn_in, rows_table, cols_table, cosine, sine), cuts = gather_with_tables(
        (attn_scaled * attn_gain[None, :]).astype(BF16),
        seg_lengths,
        leaf_parent,
        tree_len,
        min(2 * HEAD_DIM, width),
        [gate_weight, down_weight, up_weight],
    )
    w_gate, w_down, w_up = [gather_weight(own) for own in cuts]
    w_qkv = w_attn[:, : 3 * width]

    qkv = jnp.dot(attn_in, w_qkv, preferred_element_type=F32)
    if is_plane():
        attn_out, lse, query_rows, key_rows, value_rows, cot_all = attention_forward(
            qkv, cosine, sine, rows_table, cols_table, width, cotangent
        )
    else:
        attn_out, lse, query_rows, key_rows, value_rows = attention_forward(
            qkv, cosine, sine, rows_table, cols_table, width
        )
        cot_all = gather_rows(cotangent)
    mid_rows = x_rows + product_scatter([attn_out], [w_attn], 1, (), [3 * width])[0]
    mlp_scaled, mlp_inv = normalize(mid_rows)
    mlp_own = (mlp_scaled * mlp_gain[None, :]).astype(BF16)
    mlp_in, hidden_grad = gather_with_product(mlp_own, cot_all, w_down)
    hidden, gate_rows_grad, up_rows_grad = gated_rows(mlp_in, hidden_grad, w_gate, w_up)

    mlp_in_grad, down_part = product_scatter(
        [gate_rows_grad, up_rows_grad], [w_gate, w_up], 3, [(cot_all, hidden)]
    )
    down_grad = scatter_weight(down_part)
    mid_grad = cotangent.astype(F32) + norm_backward(mlp_in_grad, mlp_scaled, mlp_inv, mlp_gain)
    mid_all, down_rows, up_part, gate_part = gather_with_three(
        mid_grad.astype(BF16), hidden, w_down, mlp_in, up_rows_grad, gate_rows_grad
    )
    up_grad = scatter_weight(up_part)
    gate_grad = scatter_weight(gate_part)

    out_heads_grad, output_grad = heads_and_output_grad(mid_all, w_attn, attn_out)
    out_heads_grad, down_grad = lax.optimization_barrier((out_heads_grad, down_grad))
    if is_plane():
        pre_grads, down_rows = attention_backward(
            query_rows, key_rows, value_rows, attn_out, out_heads_grad, lse, cosine, sine, rows_table, cols_table, down_rows
        )
    else:
        pre_grads = attention_backward(
            query_rows, key_rows, value_rows, attn_out, out_heads_grad, lse, cosine, sine, rows_table, cols_table
        )
        pre_grads = jnp.concatenate(pre_grads, axis=1)
        down_rows = scatter_rows(down_rows)
    block_out = (mid_rows + down_rows.astype(F32)).astype(BF16)
    pre_grads, up_grad, down_swapped = lax.optimization_barrier((pre_grads, up_grad, swap_rows(down_grad)))
    up_swapped = swap_rows(up_grad)
    attn_part = attention_weight_grads(attn_in, pre_grads, output_grad)
    pre_grads, attn_part, up_swapped, gate_grad = lax.optimization_barrier(
        (pre_grads, attn_part, up_swapped, gate_grad)
    )
    gate_swapped = swap_rows(gate_grad)
    attn_grad = scatter_weight(attn_part)
    (attn_in_grad,) = product_scatter([pre_grads], [w_attn], 2)
    attn_in_grad, attn_grad = lax.optimization_barrier((attn_in_grad, attn_grad))
    (gate_out, up_out, down_out), mlp_sums = lay_out_grads(
        [gate_swapped, up_swapped, down_swapped], 1, [gate_weight, up_weight]
    )
    attn_back = norm_backward(attn_in_grad, attn_scaled, attn_inv, attn_gain)
    input_grad = (mid_grad + attn_back).astype(BF16)
    attn_swapped, input_grad, mlp_sums = lax.optimization_barrier((swap_rows(attn_grad), input_grad, mlp_sums))
    (query_out, key_out, value_out, output_out), attn_sums = lay_out_grads(
        [attn_swapped], 4, [query_weight, key_weight, value_weight]
    )

    held = query_out.shape[0]
    first = (lax.axis_index("fsdp") * parts + ctx) * held
    sums = jnp.stack(
        [
            total / lax.dynamic_slice_in_dim(gain, first, held, 0)
            for total, gain in ((attn_sums, attn_gain), (mlp_sums, mlp_gain))
        ]
    )
    row, others = lax.axis_index("tensor"), lax.axis_size("tensor")
    kept = sums.shape[1] // others
    if others == 2:
        got = lax.ppermute(lax.dynamic_slice_in_dim(sums, (1 - row) * kept, kept, 1), "tensor", [(0, 1), (1, 0)])
        gain_grads = lax.dynamic_slice_in_dim(sums, row * kept, kept, 1) + got
    else:
        gain_grads = lax.dynamic_slice_in_dim(lax.psum(sums, "tensor"), row * kept, kept, 1)

    return (
        block_out,
        input_grad,
        gain_grads[0],
        query_out,
        key_out,
        value_out,
        output_out,
        gain_grads[1],
        gate_out,
        up_out,
        down_out,
    )


def solution(mesh):
    rows = P(("fsdp", "ctx", "tensor"), None)
    weight = P("fsdp", "tensor")
    gain = P(("fsdp", "ctx", "tensor"))
    grad = P(("fsdp", "ctx"), "tensor")
    in_specs = (
        rows, P(), weight, weight, weight, weight, P(), weight, weight, weight, P("fsdp", None), P("fsdp", None), rows,
    )
    out_specs = (rows, rows, gain, grad, grad, grad, grad, gain, grad, grad, grad)
    return jax.shard_map(body, mesh=mesh, in_specs=in_specs, out_specs=out_specs, check_vma=False)
```

```python
import functools

import jax
import jax.numpy as jnp
import numpy as np
from jax import lax
from jax.experimental import pallas as pl
from jax.experimental.pallas import tpu as pltpu
from jax.sharding import PartitionSpec as P

HEAD_DIM = 64
TRUNK = 2176
MOST_SEG = 128
ROPE_BASE = 130000.0
EPSILON = 1e-05
NEG_LARGE = -1e30
SCALE = HEAD_DIM ** (-0.5)

BQ = 512
BK = 512
GROUP = ("ctx", "tensor")

F32 = jnp.float32
BF16 = jnp.bfloat16


def pick_table(onehot, table):
    return jnp.sum(jnp.where(onehot, table[None, :], 0), axis=1)


def tree_tables(lengths_row, parent_row, tree_len):
    branches = lengths_row.shape[0] - parent_row.shape[0]
    ends = TRUNK + jnp.cumsum(lengths_row)
    starts = ends - lengths_row
    matches = parent_row[:, None] - 1 == jnp.arange(branches, dtype=jnp.int32)[None, :]
    parent_len = jnp.sum(jnp.where(matches, lengths_row[None, :branches], 0), axis=1)
    zero_one = jnp.zeros((1,), jnp.int32)
    seg_start = jnp.concatenate([zero_one, starts])
    seg_base = jnp.concatenate(
        [zero_one, jnp.full((branches,), TRUNK, jnp.int32), TRUNK + parent_len]
    )
    seg_parent = jnp.concatenate([zero_one, jnp.zeros((branches,), jnp.int32), parent_row])
    positions = jnp.arange(tree_len, dtype=jnp.int32)
    above = jnp.sum((ends[None, :] <= positions[:, None]).astype(jnp.int32), axis=1)
    segment = (positions >= TRUNK).astype(jnp.int32) + above
    onehot = segment[:, None] == jnp.arange(seg_start.shape[0], dtype=jnp.int32)[None, :]
    depth = positions - pick_table(onehot, seg_start) + pick_table(onehot, seg_base)
    parent = pick_table(onehot, seg_parent)
    return (segment, parent, depth)


def rope_freqs(width):
    half = HEAD_DIM // 2
    powers = -2.0 * (np.arange(width) % half) / HEAD_DIM
    return np.power(ROPE_BASE, powers).astype(np.float32)[None, :]


def rope_tables(depth, width):
    angles = depth.astype(F32)[:, None] * rope_freqs(width)
    sign = np.where(np.arange(width) % HEAD_DIM < HEAD_DIM // 2, -1.0, 1.0).astype(np.float32)
    return jnp.cos(angles), jnp.sin(angles) * sign[None, :]


def lay_out(segment, parent):
    both = jnp.stack([segment, parent])
    return jnp.pad(both, ((0, 6), (0, 0))), jnp.pad(both.T, ((0, 0), (0, 126)))


TABLE_ROWS = 512
TABLE_STEP = 64


def tables_at(positions, lengths, parents):
    leaves = parents.shape[1]
    branches = lengths.shape[1] - leaves
    zero = jnp.zeros_like(positions)
    segment = jnp.where(positions >= TRUNK, 1, 0)
    parent, depth = zero, positions
    end = jnp.full((1, 1), TRUNK, jnp.int32)
    starts = []
    for s in range(branches + leaves):
        start, end = end, end + lengths[:, s : s + 1]
        inside = (positions >= start) & (positions < end)
        base, above = jnp.full((1, 1), TRUNK, jnp.int32), jnp.zeros((1, 1), jnp.int32)
        if s >= branches:
            above = parents[:, s - branches : s - branches + 1]
            for b in range(branches):
                base = base + jnp.where(above == b + 1, lengths[:, b : b + 1], 0)
        segment = segment + jnp.where(positions >= end, 1, 0)
        parent = jnp.where(inside, above, parent)
        depth = jnp.where(inside, positions - start + base, depth)
    return segment, parent, depth


def sine_cosine(x):
    turns = jnp.floor(x * np.float32(2.0 / np.pi) + 0.5)
    r = x - turns * np.float32(1.5703125)
    r = r - turns * np.float32(4.837512969970703125e-4)
    r = r - turns * np.float32(7.549789954891882e-8)
    z = r * r
    sine = ((np.float32(-1.9515295891e-4) * z + np.float32(8.3321608736e-3)) * z - np.float32(1.6666654611e-1)) * z * r + r
    cosine = (
        (np.float32(2.443315711809948e-5) * z - np.float32(1.388731625493765e-3)) * z + np.float32(4.166664568298827e-2)
    ) * z * z - np.float32(0.5) * z + np.float32(1.0)
    quarter = turns.astype(jnp.int32) & 3
    odd = (quarter & 1) == 1
    first, second = jnp.where(odd, cosine, sine), jnp.where(odd, sine, cosine)
    return jnp.where(quarter >= 2, -first, first), jnp.where((quarter == 1) | (quarter == 2), -second, second)


def table_work(lengths, parents, freqs, rows_ref, cols_ref, cos_ref, sin_ref, cols_buf, cos_buf, sin_buf, sems):
    yield
    tokens = cos_ref.shape[0]
    shape = (8, tokens)
    segment, parent, _ = tables_at(lax.broadcasted_iota(jnp.int32, shape, 1), lengths, parents)
    line = lax.broadcasted_iota(jnp.int32, shape, 0)
    rows_ref[...] = jnp.where(line == 0, segment, jnp.where(line == 1, parent, 0))
    copies = []
    for chunk in range(tokens // TABLE_ROWS):
        rows = pl.ds(chunk * TABLE_ROWS, TABLE_ROWS)

        @pl.loop(0, TABLE_ROWS // TABLE_STEP)
        def _(j, chunk=chunk):
            first = pl.multiple_of(chunk * TABLE_ROWS + j * TABLE_STEP, TABLE_STEP)
            taken = pl.ds(first, TABLE_STEP)
            shape = (TABLE_STEP, 128)
            lane = lax.broadcasted_iota(jnp.int32, shape, 1)
            segment, parent, depth = tables_at(lax.broadcasted_iota(jnp.int32, shape, 0) + first, lengths, parents)
            cols_buf[taken, :] = jnp.where(lane == 0, segment, jnp.where(lane == 1, parent, 0))
            sine, cosine = sine_cosine(depth.astype(F32) * freqs[...])
            cos_buf[taken, :] = cosine
            sin_buf[taken, :] = jnp.where(lane % HEAD_DIM < HEAD_DIM // 2, -sine, sine)

        for kind, (source, target) in enumerate(((cols_buf, cols_ref), (cos_buf, cos_ref), (sin_buf, sin_ref))):
            copies.append(pltpu.make_async_copy(source.at[rows], target.at[rows], sems.at[kind, chunk]))
            copies[-1].start()
        yield
    for copy in copies:
        copy.wait()


MESH = pl.DeviceIdType.MESH


def plane_place():
    ctx, row = lax.axis_index("ctx"), lax.axis_index("tensor")
    x, core = ctx // 2, ctx % 2
    return x, core, row


def plane_neighbours(x, core, row):
    over_x = {"ctx": (1 - x) * 2 + core}
    over_core = {"ctx": x * 2 + 1 - core}
    over_row = {"tensor": 1 - row}
    return over_x, over_row, over_core


def enter_plane(neighbours):
    barrier = pltpu.get_barrier_semaphore()
    for device in neighbours:
        pl.semaphore_signal(barrier, inc=1, device_id=device, device_id_type=MESH)
    pl.semaphore_wait(barrier, 3)


PIECES = ((1, 1, 0), (1, 1, 1), (1, 0, 0), (0, 1, 1), (0, 1, 0), (1, 0, 1), (0, 0, 0), (0, 0, 1))
COLS = 512


class PlaneGather:
    def __init__(self, own_ref, all_ref, local_sem, send_sem, recv_sem):
        self.own_ref, self.all_ref, self.sems = own_ref, all_ref, (local_sem, send_sem, recv_sem)
        self.x, self.core, self.row = plane_place()
        self.devices = plane_neighbours(self.x, self.core, self.row)
        self.rows = own_ref.shape[0]

    def place(self, far_x, far_row, part):
        bx = self.x + far_x - 2 * far_x * self.x
        by = self.row + far_row - 2 * far_row * self.row
        half = self.rows // 2
        return pl.ds(pl.multiple_of(((bx * 2 + self.core) * 2 + by) * self.rows + part * half, half), half)

    def copy(self, slot):
        far_x, far_row, part, device = (
            (0, 0, 0, 1), (0, 0, 1, 1), (1, 0, 1, 1), (0, 0, 1, 0), (0, 0, 0, 0), (0, 1, 0, 0), (0, 0, 0, 2),
            (0, 0, 1, 2), (0, 1, 0, 2), (1, 0, 1, 2), (0, 1, 1, 2), (1, 0, 0, 2), (1, 1, 0, 2), (1, 1, 1, 2),
        )[slot]
        half = self.rows // 2
        target = self.place(far_x, far_row, part)
        own = far_x == 0 and far_row == 0
        source = self.own_ref.at[pl.ds(part * half, half)] if own else self.all_ref.at[target]
        return pltpu.make_async_remote_copy(
            src_ref=source, dst_ref=self.all_ref.at[target], send_sem=self.sems[1].at[slot],
            recv_sem=self.sems[2].at[slot], device_id=self.devices[device], device_id_type=MESH,
        )

    def local(self, part):
        half = self.rows // 2
        return pltpu.make_async_copy(
            self.own_ref.at[pl.ds(part * half, half)], self.all_ref.at[self.place(0, 0, part)], self.sems[0].at[part]
        )

    def start(self):
        enter_plane(self.devices)
        for slot in (0, 3, 1, 4, 6, 7):
            self.copy(slot).start()
        for part in range(2):
            self.local(part).start()

    def forward(self, got, slots):
        self.copy(got).wait_recv()
        for slot in slots:
            self.copy(slot).start()

    def first(self):
        self.forward(0, (5, 8))
        self.forward(3, (2, 9))

    def second(self):
        self.forward(1, (10,))
        self.forward(4, (11,))

    def finish(self):
        self.forward(5, (12,))
        self.forward(2, (13,))
        for slot in range(6, 14):
            self.copy(slot).wait_recv()
        for slot in range(14):
            self.copy(slot).wait_send()
        for part in range(2):
            self.local(part).wait()


def gather_sems():
    return [pltpu.SemaphoreType.DMA((2,)), pltpu.SemaphoreType.DMA((14,)), pltpu.SemaphoreType.DMA((14,))]


class PlaneScatter:
    def __init__(self, part_ref, out_ref, core_in, first_in, next_in, own, total, sems, own_sems):
        self.part_ref, self.out_ref, self.core_in, self.first_in, self.next_in = part_ref, out_ref, core_in, first_in, next_in
        self.own, self.total, self.sems, self.own_sems = own, total, sems, own_sems
        self.x, self.core, self.row = plane_place()
        self.devices = plane_neighbours(self.x, self.core, self.row)
        self.rows = part_ref.shape[0] // 8

    def place(self, piece, on_core):
        far_x, far_row, part = PIECES[piece]
        bx = self.x + far_x - 2 * far_x * self.x
        by = self.row + far_row - 2 * far_row * self.row
        half = self.rows // 2
        return pl.ds(pl.multiple_of(((bx * 2 + on_core) * 2 + by) * self.rows + part * half, half), half)

    def copy(self, slot):
        if slot < 8:
            source, target, device = self.part_ref.at[self.place(slot, 1 - self.core)], self.core_in.at[slot], 2
        elif slot < 12:
            source, target, device = self.core_in.at[slot - 8], self.first_in.at[slot - 8], slot % 2
        else:
            source, target, device = self.core_in.at[slot - 8], self.next_in.at[slot - 12], 1 - slot % 2
        return pltpu.make_async_remote_copy(
            src_ref=source, dst_ref=target, send_sem=self.sems.at[0, slot], recv_sem=self.sems.at[1, slot],
            device_id=self.devices[device], device_id_type=MESH,
        )

    def load(self, piece):
        return pltpu.make_async_copy(
            self.part_ref.at[self.place(piece, self.core)], self.own.at[piece % 4], self.own_sems.at[piece % 4]
        )

    def add(self, target, where, *others):
        @pl.loop(0, target.shape[-1] // COLS)
        def _(j):
            columns = pl.ds(pl.multiple_of(j * COLS, COLS), COLS)
            total = sum(ref[slot, :, columns].astype(F32) for ref, slot in others)
            target[where, :, columns] = total.astype(target.dtype)

    def start(self):
        enter_plane(self.devices)
        for slot in range(8):
            self.copy(slot).start()
        for piece in range(4):
            self.load(piece).start()

    def first(self):
        for piece in range(4):
            self.load(piece).wait()
            self.copy(piece).wait_recv()
            self.add(self.core_in, piece, (self.own, piece), (self.core_in, piece))
            self.copy(8 + piece).start()
        for piece in range(4, 8):
            self.load(piece).start()

    def second(self):
        for piece in range(4, 8):
            self.load(piece).wait()
            self.copy(piece).wait_recv()
            self.add(self.core_in, piece, (self.own, piece - 4), (self.core_in, piece))

    def third(self):
        for part in range(2):
            self.copy(8 + part).wait_recv()
            self.add(self.core_in, 4 + part, (self.core_in, 4 + part), (self.first_in, part))
            self.copy(12 + part).start()

    def finish(self):
        half = self.rows // 2
        for part in range(2):
            self.copy(10 + part).wait_recv()
            self.copy(12 + part).wait_recv()
            self.add(self.total, part, (self.core_in, 6 + part), (self.first_in, 2 + part), (self.next_in, part))
        stores = [
            pltpu.make_async_copy(
                self.total.at[part], self.out_ref.at[pl.ds(part * half, half)], self.own_sems.at[part]
            )
            for part in range(2)
        ]
        for store in stores:
            store.start()
        for slot in range(14):
            self.copy(slot).wait_send()
        for store in stores:
            store.wait()


def scatter_scratch(rows, width):
    half = rows // 2
    return [
        pltpu.VMEM((8, half, width), BF16),
        pltpu.VMEM((4, half, width), BF16),
        pltpu.VMEM((2, half, width), BF16),
        pltpu.VMEM((4, half, width), BF16),
        pltpu.VMEM((2, half, width), BF16),
        pltpu.SemaphoreType.DMA((2, 14)),
        pltpu.SemaphoreType.DMA((4,)),
    ]


def at_step(step, total, places):
    for place, phase in places:

        @pl.when(step == place)
        def _(phase=phase):
            phase()


def partner(x):
    half = HEAD_DIM // 2
    width = x.shape[1]
    if width == HEAD_DIM:
        return jnp.concatenate([x[:, half:], x[:, :half]], axis=1)
    lane = lax.broadcasted_iota(jnp.int32, x.shape, 1)
    ahead = pltpu.roll(x, width - half, 1)
    behind = pltpu.roll(x, half, 1)
    return jnp.where(lane % HEAD_DIM < half, ahead, behind)


def head_mask(shape, head):
    lane = lax.broadcasted_iota(jnp.int32, shape, 1)
    return lane // HEAD_DIM == head


def dot_t(a, b):
    return lax.dot_general(a, b, (((1,), (1,)), ((), ())), preferred_element_type=F32)


def dot_n(a, b):
    return lax.dot_general(a, b, (((1,), (0,)), ((), ())), preferred_element_type=F32)


def dot_tn(a, b):
    return lax.dot_general(a, b, (((0,), (0,)), ((), ())), preferred_element_type=F32)


def key_plan(i, tile):
    base = TRUNK // BK * BK
    branch_end = TRUNK + 4 * MOST_SEG
    first_tree = base // BQ
    mixed_end = -(-(branch_end + MOST_SEG) // BQ)
    chunks = jnp.minimum(i * BQ, base) // BK
    half = BQ // 2

    @pl.when(i < first_tree)
    def _():
        @pl.loop(0, chunks)
        def _(j):
            start = pl.multiple_of(j * BK, BK)
            tile(start, BK, 0, start, 0, BQ)

    @pl.when(i >= first_tree)
    def _():
        tile(0, base, 0, 0, 0, BQ)

    @pl.when(i < first_tree)
    def _():
        start = pl.multiple_of(chunks * BK, BK)
        for part in range(2):
            tile(start, (part + 1) * half, 1, start, part * half, half)

    for block in range(first_tree, mixed_end):

        @pl.when(i == block)
        def _(block=block):
            for part in range(2):
                tile(base, block * BQ + (part + 1) * half - base, 2, base, part * half, half)

    @pl.when(i >= mixed_end)
    def _():
        tile(base, branch_end - base, 3, base, 0, BQ)
        for part in range(2):
            start = pl.multiple_of(i * BQ + part * half - MOST_SEG, MOST_SEG)
            tile(start, half + MOST_SEG, 4, branch_end, part * half, half)


def most_keys():
    branch_end = TRUNK + 4 * MOST_SEG
    return max(branch_end + BQ // 2 + MOST_SEG, -(-(branch_end + MOST_SEG) // BQ) * BQ)


def seen_mask(kind, q_at, k_at, seg_q, par_q, seg_k):
    if kind == 3:
        return (seg_k == 0) | (seg_k == par_q)
    causal = k_at <= q_at
    if kind == 1:
        return causal
    if kind == 4:
        return causal & (seg_k == seg_q)
    return causal & ((seg_k == 0) | (seg_k == seg_q) | (seg_k == par_q))


def fwd_kernel(heads, hosts, *refs):
    if not hosts:
        return fwd_work(heads, *refs)
    gather = PlaneGather(refs[7], refs[13], *refs[-3:])
    step, total = pl.program_id(0) * pl.num_programs(1) + pl.program_id(1), 16
    at_step(step, total, ((0, gather.start), (6, gather.first), (12, gather.second)))
    fwd_work(heads, *refs[:7], *refs[8:13], *refs[14:-3])
    at_step(step, total, ((total - 1, gather.finish),))


def fwd_work(
    heads, q_ref, k_ref, v_ref, cos_ref, sin_ref, rows_ref, cols_ref,
    o_ref, lse_ref, qr_ref, kr_ref, vr_ref, kt_ref, va_ref, s_ref, m_ref, acc_ref,
):
    i = pl.program_id(1)
    wide = 2 * HEAD_DIM

    @pl.when(i == 0)
    def _():
        @pl.loop(0, k_ref.shape[0] // BK)
        def _(j):
            rows = pl.ds(pl.multiple_of(j * BK, BK), BK)
            k = k_ref[rows, :]
            k = (k * cos_ref[rows, :] + partner(k) * sin_ref[rows, :]).astype(BF16)
            kr_ref[rows, :] = k
            kt_ref[:, rows] = jnp.transpose(k)
            v = v_ref[rows, :].astype(BF16)
            vr_ref[rows, :] = v
            if heads == 1:
                va_ref[0, rows, :] = jnp.concatenate([v, jnp.ones_like(v)], axis=1)
            else:
                for h in range(heads):
                    va_ref[h, rows, :] = jnp.where(head_mask(v.shape, h), v, jnp.ones_like(v))

    rows = pl.ds(pl.multiple_of(i * BQ, BQ), BQ)
    q = q_ref[...]
    q = (q * cos_ref[rows, :] + partner(q) * sin_ref[rows, :]).astype(BF16)
    qr_ref[...] = q
    q = q * jnp.asarray(SCALE, BF16)
    q_heads = [jnp.where(head_mask(q.shape, h), q, jnp.zeros_like(q)) for h in range(heads)]
    m_ref[...] = jnp.full_like(m_ref, NEG_LARGE)
    acc_ref[...] = jnp.zeros_like(acc_ref)

    def score_tile(start, width, kind, place, first, count):
        keys, rows = pl.ds(start, width), slice(first, first + count)
        k = kt_ref[:, keys]
        seen = None
        if kind != 0:
            shape = (count, width)
            seen = seen_mask(
                kind,
                lax.broadcasted_iota(jnp.int32, shape, 0) + i * BQ + first,
                lax.broadcasted_iota(jnp.int32, shape, 1) + start,
                cols_ref[rows, 0:1], cols_ref[rows, 1:2], rows_ref[0:1, keys],
            )
        for h in range(heads):
            s = dot_n(q_heads[h][rows], k)
            if seen is not None:
                s = jnp.where(seen, s, NEG_LARGE)
            s_ref[h, rows, pl.ds(place, width)] = s
            largest = m_ref[h, rows]
            for c in range(width // 128):
                largest = jnp.maximum(largest, s[:, c * 128 : (c + 1) * 128])
            m_ref[h, rows] = largest

    key_plan(i, score_tile)
    for h in range(heads):
        m_ref[h] = jnp.broadcast_to(jnp.max(m_ref[h], axis=1, keepdims=True), (BQ, 128))

    def value_tile(start, width, kind, place, first, count):
        keys, rows = pl.ds(start, width), slice(first, first + count)
        for h in range(heads):
            m = m_ref[h, rows]
            parts = [
                jnp.exp(s_ref[h, rows, pl.ds(place + c * 128, 128)] - m).astype(BF16) for c in range(width // 128)
            ]
            acc_ref[h, rows] += dot_n(jnp.concatenate(parts, axis=1), va_ref[h, keys, :])

    key_plan(i, value_tile)
    out, lse = None, None
    for h in range(heads):
        acc = acc_ref[h]
        part = acc / pltpu.roll(acc, HEAD_DIM, 1)
        stat = m_ref[h] + jnp.log(jnp.broadcast_to(acc[:, (1 - h) * HEAD_DIM : (1 - h) * HEAD_DIM + 1], (BQ, wide)))
        mask = head_mask((BQ, wide), h)
        out = part if h == 0 else jnp.where(mask, part, out)
        lse = stat if h == 0 else jnp.where(mask, stat, lse)
    o_ref[...] = out[:, : heads * HEAD_DIM].astype(BF16)
    turned = jnp.transpose(lse)
    for h in range(heads):
        lse_ref[0, h : h + 1, :] = turned[h * HEAD_DIM : h * HEAD_DIM + 1, :]


def bwd_kernel(heads, hosts, *refs):
    if not hosts:
        return bwd_work(heads, *refs)
    scatter = PlaneScatter(refs[10], refs[12], *refs[-7:])
    step, total = pl.program_id(0) * pl.num_programs(1) + pl.program_id(1), 16
    at_step(
        step, total, ((0, scatter.start), (3, scatter.first), (5, scatter.second), (7, scatter.third))
    )
    bwd_work(heads, *refs[:10], *refs[13:-7], together=refs[11])
    at_step(step, total, ((total - 1, scatter.finish),))


def bwd_work(
    heads, q_ref, k_ref, v_ref, o_ref, do_ref, lse_ref, cos_ref, sin_ref, rows_ref, cols_ref,
    *refs, together=None,
):
    if together is None:
        dq_ref, dk_ref, dv_ref, dq_acc, dk_acc, dv_acc = refs
    else:
        dq_acc, dk_acc, dv_acc, dq_ref, dk_ref, dv_ref, out_sems = refs
    i = pl.program_id(1)

    def store(kind, source, rows, sem):
        groups, width = pl.num_programs(0), source.shape[1]
        columns = pl.ds(pl.multiple_of((kind * groups + pl.program_id(0)) * width, width), width)
        return pltpu.make_async_copy(source, together.at[rows, columns], out_sems.at[sem])

    @pl.when(i == 0)
    def _():
        dk_acc[...] = jnp.zeros_like(dk_acc)
        dv_acc[...] = jnp.zeros_like(dv_acc)

    q = q_ref[...]
    scaled = q * jnp.asarray(SCALE, BF16)
    do = do_ref[...]
    product = jnp.transpose(do.astype(F32) * o_ref[...].astype(F32))
    zero = jnp.zeros_like(q)
    masks = [head_mask(q.shape, h) for h in range(heads)]
    q_heads = [jnp.where(m, scaled, zero) for m in masks]
    do_heads = [jnp.where(m, do, zero) for m in masks]
    deltas = [
        jnp.sum(product[h * HEAD_DIM : (h + 1) * HEAD_DIM, :], axis=0, keepdims=True) for h in range(heads)
    ]
    lses = [lse_ref[0, h : h + 1, :] for h in range(heads)]
    q_turned = [jnp.transpose(x) for x in q_heads]
    do_turned = [jnp.transpose(x) for x in do_heads]
    dq_acc[...] = jnp.zeros_like(dq_acc)

    def tile(start, width, kind, place, first, count):
        keys, part = pl.ds(start, width), slice(first, first + count)
        k = k_ref[keys, :]
        v = v_ref[keys, :]
        seen = None
        if kind != 0:
            shape = (width, count)
            seen = seen_mask(
                kind,
                lax.broadcasted_iota(jnp.int32, shape, 1) + i * BQ + first,
                lax.broadcasted_iota(jnp.int32, shape, 0) + start,
                rows_ref[0:1, part], rows_ref[1:2, part], cols_ref[keys, 0:1],
            )
        probs, grads, k_heads = [], [], []
        for h in range(heads):
            s = dot_n(k, q_turned[h][:, part])
            p = jnp.exp(s - lses[h][:, part])
            if seen is not None:
                p = jnp.where(seen, p, 0.0)
            dp = dot_n(v, do_turned[h][:, part])
            probs.append(p.astype(BF16))
            grads.append((p * (dp - deltas[h][:, part])).astype(BF16))
            k_heads.append(jnp.where(head_mask(k.shape, h), k, jnp.zeros_like(k)))
        grad_row = jnp.concatenate(grads, axis=1)
        dv_acc[keys, :] += dot_n(jnp.concatenate(probs, axis=1), jnp.concatenate([x[part] for x in do_heads], axis=0))
        dk_acc[keys, :] += dot_n(grad_row, jnp.concatenate([x[part] for x in q_heads], axis=0))
        dq_acc[part, :] += dot_tn(jnp.concatenate(grads, axis=0), jnp.concatenate(k_heads, axis=0))

    key_plan(i, tile)
    dq = dq_acc[...] * SCALE
    rows = pl.ds(pl.multiple_of(i * BQ, BQ), BQ)
    dq = (dq * cos_ref[rows, :] - partner(dq) * sin_ref[rows, :]).astype(BF16)
    if together is None:
        dq_ref[...] = dq
    else:
        step, last = pl.program_id(0) * pl.num_programs(1) + i, pl.num_programs(0) * pl.num_programs(1) - 1
        for slot in range(2):

            @pl.when(step % 2 == slot)
            def _(slot=slot):
                @pl.when(step >= 2)
                def _():
                    store(0, dq_ref.at[slot], rows, slot).wait()

                dq_ref[slot] = dq
                store(0, dq_ref.at[slot], rows, slot).start()

        @pl.when(step == last)
        def _():
            for slot in range(2):
                store(0, dq_ref.at[slot], rows, slot).wait()

    @pl.when(i == pl.num_programs(1) - 1)
    def _():
        @pl.loop(0, dk_acc.shape[0] // BK)
        def _(j):
            rows = pl.ds(pl.multiple_of(j * BK, BK), BK)
            dk = dk_acc[rows, :]
            dk_ref[rows, :] = (dk * cos_ref[rows, :] - partner(dk) * sin_ref[rows, :]).astype(BF16)
            dv_ref[rows, :] = dv_acc[rows, :].astype(BF16)

        if together is not None:
            every = pl.ds(0, dk_acc.shape[0])
            copies = [store(1, dk_ref, every, 2), store(2, dv_ref, every, 3)]
            for copy in copies:
                copy.start()
            for copy in copies:
                copy.wait()


def small_cost():
    return pl.CostEstimate(flops=1 << 20, bytes_accessed=1 << 20, transcendentals=0)


def attention_forward(qkv, cosine, sine, rows_table, cols_table, width, hosted=None):
    tree_len = qkv.shape[0]
    gw = min(2 * HEAD_DIM, width)
    groups, heads = width // gw, gw // HEAD_DIM
    row_block = pl.BlockSpec((BQ, gw), lambda g, i: (i, g))
    table = pl.BlockSpec((tree_len, gw), lambda g, i: (0, 0))
    full = pl.BlockSpec((tree_len, gw), lambda g, i: (0, g))
    act = jax.ShapeDtypeStruct((tree_len, width), BF16)
    if width % 128 == 0:
        queries, keys, values, step = qkv, qkv, qkv, groups
    else:
        queries, keys, values = jnp.split(qkv, 3, axis=1)
        step = 0
    hosts = hosted is not None
    hbm = pl.BlockSpec(memory_space=pl.ANY)
    return pl.pallas_call(
        functools.partial(fwd_kernel, heads, hosts),
        grid=(groups, tree_len // BQ),
        in_specs=[
            row_block,
            pl.BlockSpec((tree_len, gw), lambda g, i: (0, step + g)),
            pl.BlockSpec((tree_len, gw), lambda g, i: (0, 2 * step + g)),
            table,
            table,
            pl.BlockSpec((8, tree_len), lambda g, i: (0, 0)),
            pl.BlockSpec((BQ, 128), lambda g, i: (i, 0)),
        ]
        + [hbm] * hosts,
        out_specs=[row_block, pl.BlockSpec((1, heads, BQ), lambda g, i: (g, 0, i)), row_block, full, full] + [hbm] * hosts,
        out_shape=[act, jax.ShapeDtypeStruct((groups, heads, tree_len), F32), act, act, act]
        + ([jax.ShapeDtypeStruct((8 * hosted.shape[0], hosted.shape[1]), BF16)] if hosts else []),
        scratch_shapes=[
            pltpu.VMEM((gw, tree_len), BF16),
            pltpu.VMEM((heads, tree_len, 128), BF16),
            pltpu.VMEM((heads, BQ, most_keys()), F32),
            pltpu.VMEM((heads, BQ, 128), F32),
            pltpu.VMEM((heads, BQ, 128), F32),
        ]
        + (gather_sems() if hosts else []),
        compiler_params=pltpu.CompilerParams(
            vmem_limit_bytes=60 << 20, collective_id=6 if hosts else None, has_side_effects=hosts
        ),
        cost_estimate=small_cost(),
        name="tree_attention_forward",
    )(queries, keys, values, cosine, sine, rows_table, cols_table, *([hosted] if hosts else []))


def attention_backward(q, k, v, out, grad, lse, cosine, sine, rows_table, cols_table, hosted=None):
    tree_len, width = q.shape
    gw = min(2 * HEAD_DIM, width)
    groups, heads = width // gw, gw // HEAD_DIM
    row_block = pl.BlockSpec((BQ, gw), lambda g, i: (i, g))
    table = pl.BlockSpec((tree_len, gw), lambda g, i: (0, 0))
    full = pl.BlockSpec((tree_len, gw), lambda g, i: (0, g))
    act = jax.ShapeDtypeStruct((tree_len, width), BF16)
    hosts = hosted is not None
    hbm = pl.BlockSpec(memory_space=pl.ANY)
    return pl.pallas_call(
        functools.partial(bwd_kernel, heads, hosts),
        grid=(groups, tree_len // BQ),
        in_specs=[
            row_block, full, full, row_block, row_block,
            pl.BlockSpec((1, heads, BQ), lambda g, i: (g, 0, i)),
            table, table,
            pl.BlockSpec((8, BQ), lambda g, i: (0, i)),
            pl.BlockSpec((tree_len, 128), lambda g, i: (0, 0)),
        ]
        + [hbm] * hosts,
        out_specs=[hbm] * 2 if hosts else [row_block, full, full],
        out_shape=[
            jax.ShapeDtypeStruct((tree_len, 3 * width), BF16),
            jax.ShapeDtypeStruct((hosted.shape[0] // 8, hosted.shape[1]), BF16),
        ]
        if hosts
        else [act, act, act],
        scratch_shapes=[
            pltpu.VMEM((BQ, gw), F32),
            pltpu.VMEM((tree_len, gw), F32),
            pltpu.VMEM((tree_len, gw), F32),
        ]
        + (
            [pltpu.VMEM(shape, BF16) for shape in ((2, BQ, gw), (tree_len, gw), (tree_len, gw))]
            + [pltpu.SemaphoreType.DMA((4,))]
            + scatter_scratch(hosted.shape[0] // 8, hosted.shape[1])
            if hosts
            else []
        ),
        compiler_params=pltpu.CompilerParams(
            vmem_limit_bytes=60 << 20, collective_id=7 if hosts else None, has_side_effects=hosts
        ),
        cost_estimate=small_cost(),
        name="tree_attention_backward",
    )(q, k, v, out, grad, lse, cosine, sine, rows_table, cols_table, *([hosted] if hosts else []))


TOKENS_AT_ONCE = 2048
LEFT_AT_ONCE = 512
TOKEN_STEP = 1024
ROW_STEP = 1024


def product_buffers(columns):
    return [
        pltpu.VMEM((2, TOKENS_AT_ONCE, LEFT_AT_ONCE), BF16),
        pltpu.VMEM((2 * TOKENS_AT_ONCE, columns), BF16),
        pltpu.VMEM((LEFT_AT_ONCE, columns), F32),
        pltpu.VMEM((LEFT_AT_ONCE, columns), BF16),
        pltpu.SemaphoreType.DMA((4,)),
    ]


def token_product(left_ref, right_ref, out_ref, left_buf, right_buf, total, out_buf, sems):
    tokens = left_ref.shape[0]
    parts, groups = tokens // TOKENS_AT_ONCE, left_ref.shape[1] // LEFT_AT_ONCE

    def load(step):
        group, part = step // parts, step % parts
        source = left_ref.at[
            pl.ds(part * TOKENS_AT_ONCE, TOKENS_AT_ONCE), pl.ds(group * LEFT_AT_ONCE, LEFT_AT_ONCE)
        ]
        return pltpu.make_async_copy(source, left_buf.at[step % 2], sems.at[step % 2])

    def store(group):
        return pltpu.make_async_copy(out_buf, out_ref.at[pl.ds(group * LEFT_AT_ONCE, LEFT_AT_ONCE)], sems.at[3])

    whole = pltpu.make_async_copy(right_ref, right_buf, sems.at[2])
    whole.start()
    load(0).start()
    yield
    whole.wait()
    for group in range(groups):
        for part in range(parts):
            step = group * parts + part
            load(step).wait()
            if step + 1 < groups * parts:
                load(step + 1).start()
            if part == 0:
                total[...] = jnp.zeros_like(total)

            @pl.loop(0, TOKENS_AT_ONCE // TOKEN_STEP)
            def _(j, step=step, part=part):
                left = left_buf[step % 2, pl.ds(pl.multiple_of(j * TOKEN_STEP, TOKEN_STEP), TOKEN_STEP), :]
                right = right_buf[pl.ds(pl.multiple_of(part * TOKENS_AT_ONCE + j * TOKEN_STEP, TOKEN_STEP), TOKEN_STEP), :]
                total[...] += dot_tn(left, right)

        if group > 0:
            store(group - 1).wait()
        out_buf[...] = total[...].astype(BF16)
        store(group).start()
        yield
    store(groups - 1).wait()


def finish(product):
    for _ in product:
        pass


def pair_product(left_ref, first_ref, second_ref, out_first, out_second, left_buf, right_buf, total, out_buf, sems):
    tokens, columns = first_ref.shape
    parts, groups = tokens // TOKENS_AT_ONCE, left_ref.shape[1] // LEFT_AT_ONCE
    sides = [pl.ds(0, columns), pl.ds(columns, columns)]

    def load(step):
        group, part = step // parts, step % parts
        source = left_ref.at[
            pl.ds(part * TOKENS_AT_ONCE, TOKENS_AT_ONCE), pl.ds(group * LEFT_AT_ONCE, LEFT_AT_ONCE)
        ]
        return pltpu.make_async_copy(source, left_buf.at[step % 2], sems.at[step % 2])

    def stores(group):
        rows = pl.ds(group * LEFT_AT_ONCE, LEFT_AT_ONCE)
        return [
            pltpu.make_async_copy(out_buf.at[:, side], out_ref.at[rows], sems.at[4 + n])
            for n, (side, out_ref) in enumerate(zip(sides, (out_first, out_second)))
        ]

    wholes = [
        pltpu.make_async_copy(ref, right_buf.at[:, side], sems.at[2 + n])
        for n, (side, ref) in enumerate(zip(sides, (first_ref, second_ref)))
    ]
    load(0).start()
    for copy in wholes:
        copy.start()
    yield
    for copy in wholes:
        copy.wait()
    for group in range(groups):
        for part in range(parts):
            step = group * parts + part
            load(step).wait()
            if step + 1 < groups * parts:
                load(step + 1).start()
            if part == 0:
                total[...] = jnp.zeros_like(total)

            @pl.loop(0, TOKENS_AT_ONCE // TOKEN_STEP)
            def _(j, step=step, part=part):
                left = left_buf[step % 2, pl.ds(pl.multiple_of(j * TOKEN_STEP, TOKEN_STEP), TOKEN_STEP), :]
                right = right_buf[pl.ds(pl.multiple_of(part * TOKENS_AT_ONCE + j * TOKEN_STEP, TOKEN_STEP), TOKEN_STEP), :]
                total[...] += dot_tn(left, right)

        if group > 0:
            for copy in stores(group - 1):
                copy.wait()
        out_buf[...] = total[...].astype(BF16)
        for copy in stores(group):
            copy.start()
        yield
    for copy in stores(groups - 1):
        copy.wait()


def cut_columns(*refs):
    count = (len(refs) - 2) // 2
    sources, targets, (room, sems) = refs[:count], refs[count : 2 * count], refs[2 * count :]

    def inward(n):
        columns = targets[n].shape[1]
        taken = pl.ds(pl.multiple_of(lax.axis_index("ctx") * columns, columns), columns)
        return pltpu.make_async_copy(sources[n].at[:, taken], room.at[n], sems.at[0, n])

    def outward(n):
        return pltpu.make_async_copy(room.at[n], targets[n], sems.at[1, n])

    for n in range(count):
        inward(n).start()
    yield
    for n in range(count):
        inward(n).wait()
        outward(n).start()
    yield
    for n in range(count):
        outward(n).wait()


def row_product(turned, left_ref, right_ref, out_ref, left_buf, right_buf, out_buf, sems):
    groups = left_ref.shape[0] // LEFT_AT_ONCE

    def rows(group):
        return pl.ds(group * LEFT_AT_ONCE, LEFT_AT_ONCE)

    def load(group):
        return pltpu.make_async_copy(left_ref.at[rows(group)], left_buf.at[group % 2], sems.at[group % 2])

    def store(group):
        return pltpu.make_async_copy(out_buf.at[group % 2], out_ref.at[rows(group)], sems.at[3 + group % 2])

    whole = pltpu.make_async_copy(right_ref, right_buf, sems.at[2])
    whole.start()
    load(0).start()
    yield
    whole.wait()
    for group in range(groups):
        load(group).wait()
        if group + 1 < groups:
            load(group + 1).start()
        if group > 1:
            store(group - 2).wait()

        @pl.loop(0, out_ref.shape[1] // ROW_STEP)
        def _(j, group=group):
            columns = pl.ds(pl.multiple_of(j * ROW_STEP, ROW_STEP), ROW_STEP)
            if turned:
                part = dot_t(left_buf[group % 2], right_buf[columns, :])
            else:
                part = dot_n(left_buf[group % 2], right_buf[:, columns])
            out_buf[group % 2, :, columns] = part.astype(BF16)

        store(group).start()
        yield
    for group in range(max(0, groups - 2), groups):
        store(group).wait()


def row_product_buffers(right, turned):
    return [
        pltpu.VMEM((2, LEFT_AT_ONCE, right.shape[1 if turned else 0]), BF16),
        pltpu.VMEM(right.shape, BF16),
        pltpu.VMEM((2, LEFT_AT_ONCE, right.shape[0 if turned else 1]), BF16),
        pltpu.SemaphoreType.DMA((5,)),
    ]


def gather_kernel(works, counts, paces, *refs):
    def take(count):
        nonlocal refs
        taken, refs = refs[:count], refs[count:]
        return taken

    (own_ref,) = take(1)
    inputs = [take(count[0]) for count in counts]
    (all_ref,) = take(1)
    outputs = [take(count[1]) for count in counts]
    gather = PlaneGather(own_ref, all_ref, *take(3))
    buffers, held = [], {}
    for work, count in zip(works, counts):
        if work not in held:
            held[work] = take(count[2])
        buffers.append(held[work])

    def all_work():
        started = [work(*given, *wanted, *room) for work, given, wanted, room in zip(works, inputs, outputs, buffers)]
        for one in started:
            next(one)
        for one in started:
            yield from one

    going = all_work()

    def some(count):
        for _ in range(count):
            next(going, None)

    gather.start()
    some(paces[0])
    gather.first()
    some(paces[1])
    gather.second()
    finish(going)
    gather.finish()


def plane_gather(rows, collective_id=0, jobs=(), paces=(0, 0)):
    count, width = rows.shape
    hbm = pl.BlockSpec(memory_space=pl.ANY)
    scratch, held = gather_sems(), set()
    for work, _, _, _, _, buffers in jobs:
        if work not in held:
            held.add(work)
            scratch += buffers
    return pl.pallas_call(
        functools.partial(
            gather_kernel,
            [job[0] for job in jobs],
            [(len(job[1]), len(job[3]), len(job[5])) for job in jobs],
            paces,
        ),
        in_specs=[hbm] + [spec for job in jobs for spec in job[2]],
        out_specs=[hbm] + [spec for job in jobs for spec in job[4]],
        out_shape=[jax.ShapeDtypeStruct((8 * count, width), rows.dtype)] + [out for job in jobs for out in job[3]],
        scratch_shapes=scratch,
        compiler_params=pltpu.CompilerParams(
            collective_id=collective_id, has_side_effects=True, vmem_limit_bytes=(60 << 20) if jobs else None
        ),
        cost_estimate=small_cost(),
        name="plane_gather",
    )(rows, *[value for job in jobs for value in job[1]])


HBM = pl.BlockSpec(memory_space=pl.ANY)
VMEM = pl.BlockSpec(memory_space=pltpu.VMEM)
ROWS_TURNED = functools.partial(row_product, True)
ROWS_STRAIGHT = functools.partial(row_product, False)


def token_job(left, right):
    out = jax.ShapeDtypeStruct((left.shape[1], right.shape[1]), BF16)
    return token_product, [left, right], [HBM] * 2, [out], [HBM], product_buffers(right.shape[1])


def pair_job(left, first, second):
    columns = first.shape[1]
    out = jax.ShapeDtypeStruct((left.shape[1], columns), BF16)
    room = [
        pltpu.VMEM((2, TOKENS_AT_ONCE, LEFT_AT_ONCE), BF16),
        pltpu.VMEM((left.shape[0], 2 * columns), BF16),
        pltpu.VMEM((LEFT_AT_ONCE, 2 * columns), F32),
        pltpu.VMEM((LEFT_AT_ONCE, 2 * columns), BF16),
        pltpu.SemaphoreType.DMA((6,)),
    ]
    return pair_product, [left, first, second], [HBM] * 3, [out] * 2, [HBM] * 2, room


def cut_job(weights, parts):
    outs = [jax.ShapeDtypeStruct((w.shape[0], w.shape[1] // parts), w.dtype) for w in weights]
    room = [pltpu.VMEM((len(weights),) + outs[0].shape, BF16), pltpu.SemaphoreType.DMA((2, len(weights)))]
    return cut_columns, list(weights), [HBM] * len(weights), outs, [HBM] * len(weights), room


def row_job(left, right, turned):
    out = jax.ShapeDtypeStruct((left.shape[0], right.shape[0 if turned else 1]), BF16)
    work = ROWS_TURNED if turned else ROWS_STRAIGHT
    return work, [left, right], [HBM] * 2, [out], [HBM], row_product_buffers(right, turned)


def table_job(lengths, parents, tokens):
    outs = [jax.ShapeDtypeStruct((8, tokens), jnp.int32), jax.ShapeDtypeStruct((tokens, 128), jnp.int32)]
    outs += [jax.ShapeDtypeStruct((tokens, 128), F32)] * 2
    room = [pltpu.VMEM(out.shape, out.dtype) for out in outs[1:]]
    room += [pltpu.SemaphoreType.DMA((3, tokens // TABLE_ROWS))]
    return table_work, [lengths, parents, rope_freqs(128)], [VMEM] * 3, outs, [VMEM, HBM, HBM, HBM], room


def scatter_kernel(rows, offsets, jobs, *refs):
    parts = len(offsets)

    def take(count):
        nonlocal refs
        taken, refs = refs[:count], refs[count:]
        return taken

    a_refs, w_homes, lefts, rights = take(parts), take(parts), take(jobs), take(jobs)
    (out_ref,), products = take(1), take(jobs)
    core_out, core_in, first_in, next_in, sems = take(5)
    a_bufs, w_refs, (a_sems, w_sems), buffers = take(parts), take(parts), take(2), refs

    def work(job):
        if job < jobs:
            finish(token_product(lefts[job], rights[job], products[job], *buffers))

    x, core, row = plane_place()
    over_x, over_row, over_core = plane_neighbours(x, core, row)
    half = rows // 2
    width = out_ref.shape[1]
    chunks = width // COLS

    def place(piece, on_core):
        far_x, far_row, part = PIECES[piece]
        bx = x + far_x - 2 * far_x * x
        by = row + far_row - 2 * far_row * row
        return pl.ds(pl.multiple_of(((bx * 2 + on_core) * 2 + by) * rows + part * half, half), half)

    def columns(j):
        return pl.ds(pl.multiple_of(j * COLS, COLS), COLS)

    steps = [(0, True)]
    for piece in range(8):
        steps += [(piece + 1, True)] * (piece < 7) + [(piece, False)]

    def load(step):
        piece, partner_half = steps[step]
        taken = place(piece, 1 - core if partner_half else core)
        return [
            pltpu.make_async_copy(a_ref.at[taken], a_buf.at[step % 2], a_sems.at[step % 2, p])
            for p, (a_ref, a_buf) in enumerate(zip(a_refs, a_bufs))
        ]

    w_copies = [
        pltpu.make_async_copy(home.at[:, pl.ds(offset, w_ref.shape[1])], w_ref, w_sems.at[p])
        for p, (home, offset, w_ref) in enumerate(zip(w_homes, offsets, w_refs))
    ]
    loads = {0: load(0)}
    for copy in w_copies + loads[0]:
        copy.start()
    enter_plane((over_x, over_row, over_core))
    for copy in w_copies:
        copy.wait()

    def partial(slot, j):
        total = None
        for a_buf, w_ref in zip(a_bufs, w_refs):
            term = dot_t(a_buf[slot], w_ref[columns(j), :])
            total = term if total is None else total + term
        return total

    def remote(source, target, slot, device):
        return pltpu.make_async_remote_copy(
            src_ref=source, dst_ref=target, send_sem=sems.at[0, slot], recv_sem=sems.at[1, slot],
            device_id=device, device_id_type=MESH,
        )

    core_copies, first_copies, next_copies = [], [], []
    for step, (piece, partner_half) in enumerate(steps):
        for copy in loads[step]:
            copy.wait()
        if step + 1 < len(steps):
            loads[step + 1] = load(step + 1)
            for copy in loads[step + 1]:
                copy.start()
        if partner_half:

            @pl.loop(0, chunks)
            def _(j, step=step, piece=piece):
                core_out[piece, :, columns(j)] = partial(step % 2, j).astype(BF16)

            core_copies.append(remote(core_out.at[piece], core_in.at[piece], piece, over_core))
            core_copies[-1].start()
            continue
        core_copies[piece].wait_recv()

        @pl.loop(0, chunks)
        def _(j, step=step, piece=piece):
            total = partial(step % 2, j) + core_in[piece, :, columns(j)].astype(F32)
            core_in[piece, :, columns(j)] = total.astype(BF16)

        if piece < 4:
            first_copies.append(
                remote(core_in.at[piece], first_in.at[piece], 8 + piece, over_x if piece % 2 == 0 else over_row)
            )
            first_copies[-1].start()
    for part in range(2):
        first_copies[part].wait_recv()

        @pl.loop(0, chunks)
        def _(j, part=part):
            total = core_in[4 + part, :, columns(j)].astype(F32) + first_in[part, :, columns(j)].astype(F32)
            core_in[4 + part, :, columns(j)] = total.astype(BF16)

        next_copies.append(remote(core_in.at[4 + part], next_in.at[part], 12 + part, over_row if part == 0 else over_x))
        next_copies[-1].start()
    for job in range(jobs):
        work(job)
    for part in range(2):
        first_copies[2 + part].wait_recv()
        next_copies[part].wait_recv()

        @pl.loop(0, chunks)
        def _(j, part=part):
            total = core_in[6 + part, :, columns(j)].astype(F32) + first_in[2 + part, :, columns(j)].astype(F32)
            out_ref[pl.ds(part * half, half), columns(j)] = total + next_in[part, :, columns(j)].astype(F32)

    for copy in core_copies + first_copies + next_copies:
        copy.wait_send()


def plane_scatter(parts, weights, collective_id, jobs=(), offsets=None):
    count = parts[0].shape[0]
    width = weights[0].shape[0]
    rows = count // 8
    half = rows // 2
    vmem, hbm = pl.BlockSpec(memory_space=pltpu.VMEM), pl.BlockSpec(memory_space=pl.ANY)
    offsets = offsets or [0] * len(parts)
    lefts, rights = [left for left, _ in jobs], [right for _, right in jobs]
    return pl.pallas_call(
        functools.partial(scatter_kernel, rows, offsets, len(jobs)),
        in_specs=[hbm] * (2 * len(parts) + 2 * len(jobs)),
        out_specs=[vmem] + [hbm] * len(jobs),
        out_shape=[jax.ShapeDtypeStruct((rows, width), F32)]
        + [jax.ShapeDtypeStruct((left.shape[1], right.shape[1]), BF16) for left, right in jobs],
        scratch_shapes=[
            pltpu.VMEM((8, half, width), BF16),
            pltpu.VMEM((8, half, width), BF16),
            pltpu.VMEM((4, half, width), BF16),
            pltpu.VMEM((2, half, width), BF16),
            pltpu.SemaphoreType.DMA((2, 14)),
        ]
        + [pltpu.VMEM((2, half, a.shape[1]), BF16) for a in parts]
        + [pltpu.VMEM((width, a.shape[1]), BF16) for a in parts]
        + [pltpu.SemaphoreType.DMA((2, len(parts))), pltpu.SemaphoreType.DMA((len(parts),))]
        + (product_buffers(rights[0].shape[1]) if jobs else []),
        compiler_params=pltpu.CompilerParams(
            collective_id=collective_id, has_side_effects=True, vmem_limit_bytes=60 << 20
        ),
        cost_estimate=small_cost(),
        name="plane_scatter",
    )(*parts, *weights, *lefts, *rights)


def gated_kernel(x_ref, grad_ref, gate_ref, up_ref, hidden_ref, gate_grad_ref, up_grad_ref):
    columns = gate_ref.shape[1]
    step = min(512, columns)
    together = min(2, columns // step)

    @pl.loop(0, columns // (step * together))
    def _(j):
        for part in range(together):
            taken = pl.ds(pl.multiple_of((j * together + part) * step, step), step)
            gate = dot_n(x_ref[...], gate_ref[:, taken])
            up = dot_n(x_ref[...], up_ref[:, taken])
            grad = grad_ref[:, taken].astype(F32)
            sigmoid = jax.nn.sigmoid(gate)
            silu = gate * sigmoid
            hidden_ref[:, taken] = (silu * up).astype(BF16)
            gate_grad_ref[:, taken] = (grad * up * (sigmoid + silu * (1.0 - sigmoid))).astype(BF16)
            up_grad_ref[:, taken] = (grad * silu).astype(BF16)


def gated_rows(x, hidden_grad, w_gate, w_up):
    tokens, depth = x.shape
    columns = w_gate.shape[1]
    block = 256
    rows = pl.BlockSpec((block, columns), lambda i: (i, 0))
    weight = pl.BlockSpec((depth, columns), lambda i: (0, 0), pipeline_mode=pl.Buffered(1))
    out = jax.ShapeDtypeStruct((tokens, columns), BF16)
    return pl.pallas_call(
        gated_kernel,
        grid=(tokens // block,),
        in_specs=[pl.BlockSpec((block, depth), lambda i: (i, 0)), rows, weight, weight],
        out_specs=[rows] * 3,
        out_shape=[out] * 3,
        compiler_params=pltpu.CompilerParams(vmem_limit_bytes=60 << 20),
        cost_estimate=small_cost(),
        name="gated_rows",
    )(x, hidden_grad, w_gate, w_up)


def heads_kernel(x_ref, w_ref, out_ref, heads_ref, grad_ref, total):
    i = pl.program_id(0)

    @pl.when(i == 0)
    def _():
        total[...] = jnp.zeros_like(total)

    heads_ref[...] = dot_n(x_ref[...], w_ref[...]).astype(BF16)
    total[...] += dot_tn(out_ref[...], x_ref[...])

    @pl.when(i == pl.num_programs(0) - 1)
    def _():
        grad_ref[...] = jnp.transpose(total[...]).astype(BF16)


def heads_and_output_grad(mid, w_attn, attn_out):
    tokens, depth = mid.shape
    width = attn_out.shape[1]
    if width % 128:
        return dot_n(mid, w_attn[:, 3 * width :]).astype(BF16), dot_tn(mid, attn_out).astype(BF16)
    block = 1024
    rows = pl.BlockSpec((block, width), lambda i: (i, 0))
    return pl.pallas_call(
        heads_kernel,
        grid=(tokens // block,),
        in_specs=[pl.BlockSpec((block, depth), lambda i: (i, 0)), pl.BlockSpec((depth, width), lambda i: (0, 3)), rows],
        out_specs=[rows, pl.BlockSpec((depth, width), lambda i: (0, 0))],
        out_shape=[jax.ShapeDtypeStruct((tokens, width), BF16), jax.ShapeDtypeStruct((depth, width), BF16)],
        scratch_shapes=[pltpu.VMEM((width, depth), F32)],
        compiler_params=pltpu.CompilerParams(vmem_limit_bytes=60 << 20),
        cost_estimate=small_cost(),
        name="heads_and_output_grad",
    )(mid, w_attn, attn_out)


def weight_grads_kernel(x_ref, pre_ref, output_ref, grad_ref, total):
    i = pl.program_id(0)
    width = pre_ref.shape[1]

    @pl.when(i == 0)
    def _():
        total[...] = jnp.zeros_like(total)

    total[...] += dot_tn(x_ref[...], pre_ref[...])

    @pl.when(i == pl.num_programs(0) - 1)
    def _():
        grad_ref[:, :width] = total[...].astype(BF16)
        grad_ref[:, width:] = output_ref[...]


def attention_weight_grads(attn_in, pre_grads, output_grad):
    tokens, depth = attn_in.shape
    width, last = pre_grads.shape[1], output_grad.shape[1]
    if width % 128 or last % 128:
        return jnp.concatenate([dot_tn(attn_in, pre_grads).astype(BF16), output_grad], axis=1)
    block = 1024
    return pl.pallas_call(
        weight_grads_kernel,
        grid=(tokens // block,),
        in_specs=[
            pl.BlockSpec((block, depth), lambda i: (i, 0)),
            pl.BlockSpec((block, width), lambda i: (i, 0)),
            pl.BlockSpec((depth, last), lambda i: (0, 0)),
        ],
        out_specs=pl.BlockSpec((depth, width + last), lambda i: (0, 0)),
        out_shape=jax.ShapeDtypeStruct((depth, width + last), BF16),
        scratch_shapes=[pltpu.VMEM((depth, width), F32)],
        compiler_params=pltpu.CompilerParams(vmem_limit_bytes=60 << 20),
        cost_estimate=small_cost(),
        name="attention_weight_grads",
    )(attn_in, pre_grads, output_grad)


def is_plane():
    return lax.axis_size("ctx") == 4 and lax.axis_size("tensor") == 2


def gather_rows(rows):
    return lax.all_gather(rows, GROUP, axis=0, tiled=True)


def scatter_rows(rows):
    return lax.psum_scatter(rows.astype(BF16), GROUP, scatter_dimension=0, tiled=True).astype(F32)


def gather_now(rows):
    return plane_gather(rows)[0] if is_plane() else gather_rows(rows)


def cut(weight):
    columns = weight.shape[1] // lax.axis_size("ctx")
    return lax.dynamic_slice_in_dim(weight, lax.axis_index("ctx") * columns, columns, 1)


def gather_with_tables(rows, lengths, parents, tokens, width, weights):
    if is_plane():
        jobs = [cut_job(weights, lax.axis_size("ctx")), table_job(lengths, parents, tokens)]
        got = plane_gather(rows, 8, jobs, (4, 4))
        return got[:1] + got[1 + len(weights) :], got[1 : 1 + len(weights)]
    segment, parent, depth = tree_tables(lengths[0], parents[0], tokens)
    return [gather_rows(rows), *lay_out(segment, parent), *rope_tables(depth, width)], [cut(w) for w in weights]


def gather_with_product(rows, left, right):
    if is_plane():
        return plane_gather(rows, 5, [row_job(left, right, False)], (4, 4))
    return gather_rows(rows), dot_n(left, right).astype(BF16)


def gather_with_three(rows, left, right, shared, first, second):
    if is_plane():
        return plane_gather(rows, 4, [row_job(left, right, True), pair_job(shared, first, second)], (8, 3))
    products = dot_t(left, right), dot_tn(shared, first), dot_tn(shared, second)
    return [gather_rows(rows)] + [product.astype(BF16) for product in products]


def product_scatter(parts, weights, collective_id, jobs=(), offsets=None):
    if is_plane():
        return plane_scatter(parts, weights, collective_id, jobs, offsets)
    offsets = offsets or [0] * len(parts)
    weights = [w[:, first : first + part.shape[1]] for part, w, first in zip(parts, weights, offsets)]
    rows = scatter_rows(dot_t(jnp.concatenate(parts, axis=1), jnp.concatenate(weights, axis=1)))
    return [rows] + [dot_tn(left, right).astype(BF16) for left, right in jobs]


def gather_weight(own):
    return lax.all_gather(own, "fsdp", axis=0, tiled=True)


def scatter_weight(grad):
    return lax.psum_scatter(grad.astype(BF16), "fsdp", scatter_dimension=0, tiled=True)


def swap_rows(part):
    size = lax.axis_size("ctx")
    return lax.all_to_all(part.reshape(size, part.shape[0] // size, -1), "ctx", split_axis=0, concat_axis=0)


def lay_side_by_side(got, count):
    columns = got.shape[2] // count
    return [
        jnp.concatenate([got[j, :, c * columns : (c + 1) * columns] for j in range(got.shape[0])], axis=1).astype(F32)
        for c in range(count)
    ]


def lay_out_kernel(plan, weighted, ctx_ref, *refs):
    inputs = refs[: max(source for source, _ in plan) + 1]
    refs = refs[len(inputs) :]
    weights, outs, sums_ref, total = refs[:weighted], refs[weighted:-2], refs[-2], refs[-1]
    j = pl.program_id(0)

    @pl.when(j == 0)
    def _():
        total[...] = jnp.zeros_like(total)

    for n, ((source, first), out_ref) in enumerate(zip(plan, outs)):
        columns = out_ref.shape[1]
        grad = inputs[source][0, :, first : first + columns].astype(F32)
        out_ref[...] = grad
        if n < weighted:
            product = grad * weights[n][...].astype(F32)
            part = product[:, :128]
            for c in range(1, columns // 128):
                part = part + product[:, c * 128 : (c + 1) * 128]
            total[...] += part

    @pl.when(j == pl.num_programs(0) - 1)
    def _():
        column = jnp.sum(total[...], axis=1, keepdims=True)
        sums_ref[...] = jnp.transpose(jnp.broadcast_to(column, total.shape))[:8]


def lay_out_grads(swapped, count, weights):
    size, rows = swapped[0].shape[:2]
    columns = swapped[0].shape[2] // count
    if columns % 128 or rows != 128:
        outs = [out for got in swapped for out in lay_side_by_side(got, count)]
        ctx = lax.axis_index("ctx")
        held = [lax.dynamic_slice_in_dim(weight, ctx * rows, rows, 0).astype(F32) for weight in weights]
        return outs, sum(jnp.sum(weight * out, axis=1) for weight, out in zip(held, outs))
    plan = [(n, c * columns) for n in range(len(swapped)) for c in range(count)]
    result = pl.pallas_call(
        functools.partial(lay_out_kernel, plan, len(weights)),
        grid_spec=pltpu.PrefetchScalarGridSpec(
            num_scalar_prefetch=1,
            grid=(size,),
            in_specs=[pl.BlockSpec((1, rows, count * columns), lambda j, ctx: (j, 0, 0)) for _ in swapped]
            + [pl.BlockSpec((rows, columns), lambda j, ctx: (ctx[0], j)) for _ in weights],
            out_specs=[pl.BlockSpec((rows, columns), lambda j, ctx: (0, j)) for _ in plan]
            + [pl.BlockSpec((8, rows), lambda j, ctx: (0, 0))],
            scratch_shapes=[pltpu.VMEM((rows, 128), F32)],
        ),
        out_shape=[jax.ShapeDtypeStruct((rows, size * columns), F32) for _ in plan]
        + [jax.ShapeDtypeStruct((8, rows), F32)],
        compiler_params=pltpu.CompilerParams(vmem_limit_bytes=60 << 20),
        cost_estimate=small_cost(),
        name="lay_out_grads",
    )(lax.axis_index("ctx").reshape(1).astype(jnp.int32), *swapped, *weights)
    return result[:-1], result[-1][0]


def normalize(rows):
    norm_inv = lax.rsqrt(jnp.mean(rows * rows, axis=1, keepdims=True) + EPSILON)
    return (rows * norm_inv, norm_inv)


def norm_backward(grad_rows, scaled, norm_inv, gain):
    weighted = grad_rows * gain[None, :]
    inner = jnp.mean(weighted * scaled, axis=1, keepdims=True)
    return norm_inv * (weighted - scaled * inner)


def body(
    tokens_in,
    attn_gain,
    query_weight,
    key_weight,
    value_weight,
    output_weight,
    mlp_gain,
    gate_weight,
    up_weight,
    down_weight,
    seg_lengths,
    leaf_parent,
    cotangent,
):
    ctx = lax.axis_index("ctx")
    parts = lax.axis_size("ctx")
    tree_len = tokens_in.shape[0] * parts * lax.axis_size("tensor")
    width = query_weight.shape[1] // parts
    units = gate_weight.shape[1] // parts

    def mine(weight, columns):
        return lax.dynamic_slice_in_dim(weight, ctx * columns, columns, 1)

    x_rows = tokens_in.astype(F32)
    attn_scaled, attn_inv = normalize(x_rows)
    w_attn = gather_weight(
        jnp.concatenate([mine(w, width) for w in (query_weight, key_weight, value_weight, output_weight)], axis=1)
    )
    (attn_in, rows_table, cols_table, cosine, sine), cuts = gather_with_tables(
        (attn_scaled * attn_gain[None, :]).astype(BF16),
        seg_lengths,
        leaf_parent,
        tree_len,
        min(2 * HEAD_DIM, width),
        [gate_weight, down_weight, up_weight],
    )
    w_gate, w_down, w_up = [gather_weight(own) for own in cuts]
    w_qkv = w_attn[:, : 3 * width]

    qkv = jnp.dot(attn_in, w_qkv, preferred_element_type=F32)
    if is_plane():
        attn_out, lse, query_rows, key_rows, value_rows, cot_all = attention_forward(
            qkv, cosine, sine, rows_table, cols_table, width, cotangent
        )
    else:
        attn_out, lse, query_rows, key_rows, value_rows = attention_forward(
            qkv, cosine, sine, rows_table, cols_table, width
        )
        cot_all = gather_rows(cotangent)
    mid_rows = x_rows + product_scatter([attn_out], [w_attn], 1, (), [3 * width])[0]
    mlp_scaled, mlp_inv = normalize(mid_rows)
    mlp_own = (mlp_scaled * mlp_gain[None, :]).astype(BF16)
    mlp_in, hidden_grad = gather_with_product(mlp_own, cot_all, w_down)
    hidden, gate_rows_grad, up_rows_grad = gated_rows(mlp_in, hidden_grad, w_gate, w_up)

    mlp_in_grad, down_part = product_scatter(
        [gate_rows_grad, up_rows_grad], [w_gate, w_up], 3, [(cot_all, hidden)]
    )
    down_grad = scatter_weight(down_part)
    mid_grad = cotangent.astype(F32) + norm_backward(mlp_in_grad, mlp_scaled, mlp_inv, mlp_gain)
    mid_all, down_rows, up_part, gate_part = gather_with_three(
        mid_grad.astype(BF16), hidden, w_down, mlp_in, up_rows_grad, gate_rows_grad
    )
    up_grad = scatter_weight(up_part)
    gate_grad = scatter_weight(gate_part)

    out_heads_grad, output_grad = heads_and_output_grad(mid_all, w_attn, attn_out)
    out_heads_grad, down_grad = lax.optimization_barrier((out_heads_grad, down_grad))
    if is_plane():
        pre_grads, down_rows = attention_backward(
            query_rows, key_rows, value_rows, attn_out, out_heads_grad, lse, cosine, sine, rows_table, cols_table, down_rows
        )
    else:
        pre_grads = attention_backward(
            query_rows, key_rows, value_rows, attn_out, out_heads_grad, lse, cosine, sine, rows_table, cols_table
        )
        pre_grads = jnp.concatenate(pre_grads, axis=1)
        down_rows = scatter_rows(down_rows)
    block_out = (mid_rows + down_rows.astype(F32)).astype(BF16)
    pre_grads, up_grad, down_swapped = lax.optimization_barrier((pre_grads, up_grad, swap_rows(down_grad)))
    up_swapped = swap_rows(up_grad)
    attn_part = attention_weight_grads(attn_in, pre_grads, output_grad)
    pre_grads, attn_part, up_swapped, gate_grad = lax.optimization_barrier(
        (pre_grads, attn_part, up_swapped, gate_grad)
    )
    gate_swapped = swap_rows(gate_grad)
    attn_grad = scatter_weight(attn_part)
    (attn_in_grad,) = product_scatter([pre_grads], [w_attn], 2)
    attn_in_grad, attn_grad = lax.optimization_barrier((attn_in_grad, attn_grad))
    attn_back = norm_backward(attn_in_grad, attn_scaled, attn_inv, attn_gain)
    input_grad = (mid_grad + attn_back).astype(BF16)
    gate_swapped, input_grad = lax.optimization_barrier((gate_swapped, input_grad))
    (gate_out, up_out, down_out), mlp_sums = lay_out_grads(
        [gate_swapped, up_swapped, down_swapped], 1, [gate_weight, up_weight]
    )
    attn_swapped, input_grad, mlp_sums = lax.optimization_barrier((swap_rows(attn_grad), input_grad, mlp_sums))
    (query_out, key_out, value_out, output_out), attn_sums = lay_out_grads(
        [attn_swapped], 4, [query_weight, key_weight, value_weight]
    )

    held = query_out.shape[0]
    first = (lax.axis_index("fsdp") * parts + ctx) * held
    sums = jnp.stack(
        [
            total / lax.dynamic_slice_in_dim(gain, first, held, 0)
            for total, gain in ((attn_sums, attn_gain), (mlp_sums, mlp_gain))
        ]
    )
    row, others = lax.axis_index("tensor"), lax.axis_size("tensor")
    kept = sums.shape[1] // others
    if others == 2:
        got = lax.ppermute(lax.dynamic_slice_in_dim(sums, (1 - row) * kept, kept, 1), "tensor", [(0, 1), (1, 0)])
        gain_grads = lax.dynamic_slice_in_dim(sums, row * kept, kept, 1) + got
    else:
        gain_grads = lax.dynamic_slice_in_dim(lax.psum(sums, "tensor"), row * kept, kept, 1)

    return (
        block_out,
        input_grad,
        gain_grads[0],
        query_out,
        key_out,
        value_out,
        output_out,
        gain_grads[1],
        gate_out,
        up_out,
        down_out,
    )


def solution(mesh):
    rows = P(("fsdp", "ctx", "tensor"), None)
    weight = P("fsdp", "tensor")
    gain = P(("fsdp", "ctx", "tensor"))
    grad = P(("fsdp", "ctx"), "tensor")
    in_specs = (
        rows, P(), weight, weight, weight, weight, P(), weight, weight, weight, P("fsdp", None), P("fsdp", None), rows,
    )
    out_specs = (rows, rows, gain, grad, grad, grad, grad, gain, grad, grad, grad)
    return jax.shard_map(body, mesh=mesh, in_specs=in_specs, out_specs=out_specs, check_vma=False)
```
